32 devices in a mesh: grp: 4 (over y, core), lat: 2 (over x), lon: 4 (over z).
Axes of the slice: x: 2, y: 2, z: 4, core: 2. Of those that a mesh axis runs over, the one named last changes fastest.
Arguments:
- layer_source_tensor: bfloat16 [8, 32, 64, 768], P(('grp', 'lat'), None, 'lon'), may hold values from -6 to 6
- horizon_class: int32 [8], P(('grp', 'lat')), may hold values from 0 to 23
- field_selector: int32 [8, 69], P(('grp', 'lat')), may hold values 0 or 1
- model_predictions: bfloat16 [8, 32, 64, 2, 4416], P(('grp', 'lat'), None, 'lon'), may hold values from -6 to 6
- loss_sensitivity: bfloat16 [8, 32, 64, 4416], P(('grp', 'lat'), None, 'lon'), may hold values from -6 to 6
- initial_standardize_gain: float32 [768], replicated, may hold values from 0.5 to 1.5
- initial_standardize_shift: float32 [768], replicated, may hold values from -1.75 to 1.75
- horizon_vectors: float32 [24, 768], replicated, may hold values from -3 to 3
- projection_triple_matrix: bfloat16 [768, 2304], replicated, may hold values from -0.21875 to 0.21875
- context_projector_matrix: bfloat16 [768, 768], replicated, may hold values from -4 to 4
- later_standardize_gain: float32 [768], replicated, may hold values from 0.5 to 1.5
- later_standardize_shift: float32 [768], replicated, may hold values from -1.75 to 1.75
- expand_matrix: bfloat16 [768, 3072], replicated, may hold values from -0.21875 to 0.21875
- expand_shift_vector: float32 [3072], replicated, may hold values from -1.75 to 1.75
- shrink_matrix: bfloat16 [3072, 768], replicated, may hold values from -0.109375 to 0.109375
- shrink_shift_vector: float32 [768], replicated, may hold values from -1.75 to 1.75
- mixing_predictor_matrix: bfloat16 [768, 138], replicated, may hold values from -0.09375 to 0.09375
- shift_predictor_matrix: bfloat16 [768, 69], replicated, may hold values from -0.09375 to 0.09375
Outputs:
- blended: bfloat16 [8, 32, 64, 4416], P(('grp', 'lat'), None, 'lon')
- x_grad: float32 [8, 32, 64, 768], P(('grp', 'lat'), None, 'lon')
- ln1_gain_grad: float32 [768], P(('lat', 'lon'))
- ln1_bias_grad: float32 [768], P(('lat', 'lon'))
- lead_table_grad: float32 [24, 768], P(None, ('lat', 'lon'))
- w_qkv_grad: float32 [768, 2304], P(('lat', 'lon'))
- w_out_grad: float32 [768, 768], P(('lat', 'lon'))
- ln2_gain_grad: float32 [768], P(('lat', 'lon'))
- ln2_bias_grad: float32 [768], P(('lat', 'lon'))
- w_up_grad: float32 [768, 3072], P(('lat', 'lon'))
- b_up_grad: float32 [3072], P(('lat', 'lon'))
- w_down_grad: float32 [3072, 768], P(('lat', 'lon'))
- b_down_grad: float32 [768], P(('lat', 'lon'))
- w_gate_grad: float32 [768, 138], P(('lat', 'lon'))
- w_bias_grad: float32 [768, 69], P(('lat', 'lon'))
The draws below stay inside these ranges and needn't reach their ends.
Inputs may be any that keep to these rules, and one draw needn't show every extreme that they name: `field_selector`: 1 where a channel is blended, 0 where it takes the first expert's forecast.
All inputs are finite; a program needn't handle non-finite values. No bound on the sum of `field_selector` on one device may be relied on, other than what follows from the above.
Results may differ from the reference program's by a relative error of at most 0.018.
The reference program's roundings to bfloat16 on the way count: a program that leaves them out, or rounds other values in their place, can miss the bound.
Values may be sent and summed in bfloat16 or wider, within the bound.
No kernel may reach another device: no remote copies, remote signals or barrier semaphores. Data moves between devices by JAX's collectives and lax.ppermute only.
A program may use at most 704 MiB of HBM per device.

```python
import jax
import jax.numpy as jnp
from jax import lax

D = 768
H = 12
DH = 64
FF = 3072
MODEL_NUMBER = 2
RESULT_FIELDS = 69
TILE_AREA = 64
LEADS = 24
TILE_DOWNWARD = 32
TILE_ACROSS = 64
SNAPSHOT_NUMBER = 8


def with_ends(values, stream_key, least, top_value):
    longest = values.shape.index(max(values.shape))
    spots = []
    for shift in (0, 1):
        where = [jax.random.randint(jax.random.fold_in(stream_key, axis), (), 0, length) for axis, length in enumerate(values.shape)]
        where[longest] = (where[longest] + shift) % values.shape[longest]
        spots.append(tuple(where))
    return values.at[spots[0]].set(least).at[spots[1]].set(top_value)


def level_of(key, shape, split, smallest, top_value):
    def one(dim, blocks):
        heights = jax.random.uniform(jax.random.fold_in(jax.random.fold_in(key, 6), dim), (blocks,), jnp.float32, smallest / len(split), top_value / len(split))
        return jnp.repeat(jnp.exp(heights), shape[dim] // blocks).reshape((-1,) + (1,) * (len(shape) - dim - 1))

    level = one(*split[0])
    for cut in split[1:]:
        level = level * one(*cut)
    return level


def noise(rng, extent, spread, bound, cuts=(), kind=jnp.bfloat16):
    level = level_of(rng, extent, cuts, -0.22, 0.18) if cuts else 1.0
    array = jax.random.normal(rng, extent, jnp.float32) * spread * level
    return jnp.minimum(jnp.maximum(array, -bound), bound).astype(kind)


def setup_inputs(seed: int = 0) -> dict:
    arg_keys = jax.random.split(jax.random.key(seed), 19)
    layer_source_tensor = noise(arg_keys[0], (SNAPSHOT_NUMBER, TILE_DOWNWARD, TILE_ACROSS, D), 1.0, 6.0, ((0, 8), (2, 4)))
    horizon_class = with_ends(jax.random.randint(arg_keys[1], (SNAPSHOT_NUMBER,), 0, LEADS), jax.random.fold_in(arg_keys[1], 1), 0, LEADS - 1).astype(jnp.int32)
    field_selector = with_ends((jax.random.randint(arg_keys[2], (SNAPSHOT_NUMBER, RESULT_FIELDS), 0, 4) < 3).astype(jnp.int32), jax.random.fold_in(arg_keys[2], 1), 0, 1)
    model_predictions = noise(arg_keys[3], (SNAPSHOT_NUMBER, TILE_DOWNWARD, TILE_ACROSS, MODEL_NUMBER, RESULT_FIELDS * TILE_AREA), 1.0, 6.0, ((0, 8), (2, 4)))
    loss_sensitivity = noise(arg_keys[4], (SNAPSHOT_NUMBER, TILE_DOWNWARD, TILE_ACROSS, RESULT_FIELDS * TILE_AREA), 1.0, 6.0, ((0, 8), (2, 4)))
    initial_standardize_gain = jnp.clip(1.0 + 0.1 * jax.random.normal(arg_keys[5], (D,), jnp.float32), 0.5, 1.5)
    initial_standardize_shift = noise(arg_keys[6], (D,), 0.3, 1.75, (), jnp.float32)
    horizon_vectors = noise(arg_keys[7], (LEADS, D), 0.5, 3.0, (), jnp.float32)
    projection_triple_matrix = noise(arg_keys[8], (D, 3 * D), D ** -0.5, 0.21875)
    context_projector_matrix = noise(arg_keys[9], (D, D), (0.45 * TILE_DOWNWARD ** 0.5 * TILE_ACROSS ** 0.5 * D ** -0.5), 4.0)
    later_standardize_gain = jnp.clip(1.0 + 0.1 * jax.random.normal(arg_keys[10], (D,), jnp.float32), 0.5, 1.5)
    later_standardize_shift = noise(arg_keys[11], (D,), 0.3, 1.75, (), jnp.float32)
    expand_matrix = noise(arg_keys[12], (D, FF), D ** -0.5, 0.21875)
    expand_shift_vector = noise(arg_keys[13], (FF,), 0.3, 1.75, (), jnp.float32)
    shrink_matrix = noise(arg_keys[14], (FF, D), FF ** -0.5, 0.109375)
    shrink_shift_vector = noise(arg_keys[15], (D,), 0.3, 1.75, (), jnp.float32)
    mixing_predictor_matrix = noise(arg_keys[16], (D, MODEL_NUMBER * RESULT_FIELDS), (0.45 * D ** -0.5), 0.09375)
    shift_predictor_matrix = noise(arg_keys[17], (D, RESULT_FIELDS), (0.4 * D ** -0.5), 0.09375)
    return {"layer_source_tensor": layer_source_tensor, "horizon_class": horizon_class, "field_selector": field_selector, "model_predictions": model_predictions, "loss_sensitivity": loss_sensitivity, "initial_standardize_gain": initial_standardize_gain, "initial_standardize_shift": initial_standardize_shift, "horizon_vectors": horizon_vectors, "projection_triple_matrix": projection_triple_matrix, "context_projector_matrix": context_projector_matrix, "later_standardize_gain": later_standardize_gain, "later_standardize_shift": later_standardize_shift, "expand_matrix": expand_matrix, "expand_shift_vector": expand_shift_vector, "shrink_matrix": shrink_matrix, "shrink_shift_vector": shrink_shift_vector, "mixing_predictor_matrix": mixing_predictor_matrix, "shift_predictor_matrix": shift_predictor_matrix}


EPSILON = 1e-06
HIGH = lax.Precision.HIGHEST

@jax.custom_vjp
def low(v):
    return lax.optimization_barrier(v.astype(jnp.bfloat16)).astype(jnp.float32)

@jax.custom_vjp
def low_back(v):
    return v

def low_keep(v):
    return (low(v), None)

def low_pass(kept, grad):
    return (grad,)

def back_keep(v):
    return (v, None)

def back_low(kept, grad):
    return (low(grad),)
low.defvjp(low_keep, low_pass)
low_back.defvjp(back_keep, back_low)

def matmul(left, right):
    return jnp.dot(left, right, precision=HIGH)

def layer_norm(values, gain, shift):
    centred = values - lax.optimization_barrier(jnp.mean(values, axis=-1, keepdims=True))
    inverse = lax.rsqrt(lax.optimization_barrier(jnp.mean(centred * centred, axis=-1, keepdims=True)) + EPSILON)
    return centred * inverse * gain + shift

def evaluate_each_snapshot(learnable_tensors, lines_each_snapshot, horizon_vector_entry, selector_field_line, prediction_each_snapshot):
    initial_standardize_gain, initial_standardize_shift, horizon_vectors, projection_triple_matrix, context_projector_matrix, later_standardize_gain, later_standardize_shift, expand_matrix, expand_shift_vector, shrink_matrix, shrink_shift_vector, mixing_predictor_matrix, shift_predictor_matrix = learnable_tensors
    tile_sequence = lines_each_snapshot.shape[0]
    mixed = low(layer_norm(lines_each_snapshot, initial_standardize_gain, initial_standardize_shift) + jnp.dot(horizon_vector_entry, horizon_vectors, precision=HIGH)[None, :])
    qkv = low_back(low(matmul(mixed, projection_triple_matrix)))
    queries = qkv[:, :D].reshape(tile_sequence, H, DH)
    keys = qkv[:, D:2 * D].reshape(tile_sequence, H, DH)
    values = qkv[:, 2 * D:].reshape(tile_sequence, H, DH)
    scores = low_back(jnp.einsum('qhd,khd->hqk', queries, keys, precision=HIGH) * 0.125)
    attn_weights = low(jax.nn.softmax(scores, axis=-1))
    attended = jnp.einsum('hqk,khd->qhd', attn_weights, values, precision=HIGH).reshape(tile_sequence, D)
    attended = low_back(low(attended))
    residual = lines_each_snapshot + low_back(matmul(attended, context_projector_matrix))
    hidden = low(layer_norm(residual, later_standardize_gain, later_standardize_shift))
    up_proj = low_back(matmul(hidden, expand_matrix) + expand_shift_vector)
    activation = low(jax.nn.gelu(up_proj, approximate=True))
    final = residual + low_back(matmul(activation, shrink_matrix) + shrink_shift_vector)
    final_low = low(final)
    logits = low_back(matmul(final_low, mixing_predictor_matrix)).reshape(tile_sequence, MODEL_NUMBER, RESULT_FIELDS)
    additive_shift = low_back(matmul(final_low, shift_predictor_matrix))
    model_mixing_share = jax.nn.softmax(logits, axis=1)
    prediction_amount = prediction_each_snapshot.reshape(tile_sequence, MODEL_NUMBER, RESULT_FIELDS, TILE_AREA)
    combined_prediction = lax.optimization_barrier(jnp.sum(model_mixing_share[:, :, :, None] * prediction_amount, axis=1)) + additive_shift[:, :, None]
    combining_selector = selector_field_line[None, :, None]
    return (combining_selector * combined_prediction + (1.0 - combining_selector) * prediction_amount[:, 0]).reshape(tile_sequence, RESULT_FIELDS * TILE_AREA)

def reference(layer_source_tensor, horizon_class, field_selector, model_predictions, loss_sensitivity, initial_standardize_gain, initial_standardize_shift, horizon_vectors, projection_triple_matrix, context_projector_matrix, later_standardize_gain, later_standardize_shift, expand_matrix, expand_shift_vector, shrink_matrix, shrink_shift_vector, mixing_predictor_matrix, shift_predictor_matrix):
    learnable_tensors = tuple((snapshot_entry.astype(jnp.float32) for snapshot_entry in (initial_standardize_gain, initial_standardize_shift, horizon_vectors, projection_triple_matrix, context_projector_matrix, later_standardize_gain, later_standardize_shift, expand_matrix, expand_shift_vector, shrink_matrix, shrink_shift_vector, mixing_predictor_matrix, shift_predictor_matrix)))
    snapshot_group = layer_source_tensor.shape[0]
    tile_sequence = TILE_DOWNWARD * TILE_ACROSS
    inputs = layer_source_tensor.astype(jnp.float32).reshape(snapshot_group, tile_sequence, D)
    horizon_onehot = (horizon_class[:, None] == jnp.arange(LEADS, dtype=jnp.int32)[None, :]).astype(jnp.float32)
    snapshot_selectors = field_selector.astype(jnp.float32)
    prediction_amount = model_predictions.astype(jnp.float32).reshape(snapshot_group, tile_sequence, MODEL_NUMBER, RESULT_FIELDS * TILE_AREA)
    iteration_body = jax.checkpoint(evaluate_each_snapshot)

    def run(received_sources, received_learnables):

        def iteration_number(iteration_state, snapshot_entry):
            lines_each_snapshot, horizon_vector_entry, selector_field_line, prediction_each_snapshot = snapshot_entry
            return (iteration_state, iteration_body(received_learnables, lines_each_snapshot, horizon_vector_entry, selector_field_line, prediction_each_snapshot))
        discarded_entry, gathered_results_pile = lax.scan(iteration_number, jnp.zeros((), jnp.float32), (received_sources, horizon_onehot, snapshot_selectors, prediction_amount))
        return gathered_results_pile
    gathered_results_pile, pullback = jax.vjp(run, inputs, learnable_tensors)
    grad_inputs, grad_params = pullback(loss_sensitivity.astype(jnp.float32).reshape(snapshot_group, tile_sequence, RESULT_FIELDS * TILE_AREA))
    blended = gathered_results_pile.astype(jnp.bfloat16).reshape(snapshot_group, TILE_DOWNWARD, TILE_ACROSS, RESULT_FIELDS * TILE_AREA)
    x_grad = grad_inputs.reshape(snapshot_group, TILE_DOWNWARD, TILE_ACROSS, D)
    return (blended, x_grad, grad_params[0], grad_params[1], grad_params[2], grad_params[3], grad_params[4], grad_params[5], grad_params[6], grad_params[7], grad_params[8], grad_params[9], grad_params[10], grad_params[11], grad_params[12])
```

```python
import functools
import math

import jax
import jax.numpy as jnp
from jax import lax
from jax.experimental import pallas as pl
from jax.experimental.pallas import tpu as pltpu
from jax.sharding import PartitionSpec as P

H = 12
DH = 64
RESULT_FIELDS = 69
TILE_AREA = 64
LEADS = 24
EPSILON = 1e-06
HIGH = lax.Precision.HIGHEST
SCALE = 0.125
SCALE_TWO = SCALE * math.log2(math.e)
NN = (((1,), (0,)), ((), ()))
NT = (((1,), (1,)), ((), ()))
TN = (((0,), (0,)), ((), ()))
BF = jnp.bfloat16
F32 = jnp.float32
PARAMS = pltpu.CompilerParams(vmem_limit_bytes=60 * 1024 * 1024)


def dot(left, right, dims=NN):
    return lax.dot_general(left, right, dims, preferred_element_type=F32)


def attend_kernel(count, chained, final, *refs):
    q_ref = refs[0]
    k_refs = refs[1 : 1 + count]
    v_refs = refs[1 + count : 1 + 2 * count]
    o_ref, l_ref = refs[-2:]
    outs = []
    for h in range(2):
        part = slice(h * DH, h * DH + DH)
        q = q_ref[0, :, part]
        scores = [dot(k[0, :, part], q, NT) for k in k_refs]
        top = functools.reduce(
            jnp.maximum, [jnp.max(s, axis=0, keepdims=True) for s in scores]
        )
        top = top * SCALE_TWO
        total = None
        mixed = None
        for s, v in zip(scores, v_refs):
            raised = jnp.exp2(s * SCALE_TWO - top)
            some = jnp.sum(raised, axis=0, keepdims=True)
            term = dot(v[0, :, part], raised.astype(BF), TN)
            total = some if total is None else total + some
            mixed = term if mixed is None else mixed + term
        mixed = mixed * (1.0 / total)
        log = top + jnp.log2(total)
        if chained:
            before_ref, before_log_ref = refs[1 + 2 * count : 3 + 2 * count]
            before = before_log_ref[0, 0, h : h + 1, :]
            high = jnp.maximum(before, log)
            joint = high + jnp.log2(jnp.exp2(before - high) + jnp.exp2(log - high))
            mixed = mixed * jnp.exp2(log - joint) + before_ref[0, part, :] * jnp.exp2(
                before - joint
            )
            log = joint
        l_ref[0, 0, h : h + 1, :] = log
        if final:
            outs.append(mixed)
        else:
            o_ref[0, part, :] = mixed
    if final:
        o_ref[0] = jnp.concatenate(outs, axis=0).T.astype(BF)


def attend(queries, shards, before, final):
    frames, rows, width = queries.shape
    count = len(shards)
    keys = shards[0].shape[1]
    pairs = width // 128
    turned = pl.BlockSpec((1, 128, rows), lambda f, p: (f, p, 0))
    row = pl.BlockSpec((1, rows, 128), lambda f, p: (f, 0, p))
    log = pl.BlockSpec((1, 1, 2, rows), lambda f, p: (f, p, 0, 0))
    chained = before is not None
    return pl.pallas_call(
        functools.partial(attend_kernel, count, chained, final),
        grid=(frames, pairs),
        in_specs=[row]
        + [pl.BlockSpec((1, keys, 128), lambda f, p: (f, 0, p))] * count
        + [pl.BlockSpec((1, keys, 128), lambda f, p: (f, 0, p + pairs))] * count
        + ([turned, log] if chained else []),
        out_specs=[row if final else turned, log],
        out_shape=[
            jax.ShapeDtypeStruct((frames, rows, width), BF)
            if final
            else jax.ShapeDtypeStruct((frames, width, rows), F32),
            jax.ShapeDtypeStruct((frames, pairs, 2, rows), F32),
        ],
        compiler_params=PARAMS,
        name="attend",
        cost_estimate=pl.CostEstimate(
            flops=16 * frames * rows * count * keys * width,
            transcendentals=frames * rows * count * keys * H,
            bytes_accessed=4 * frames * count * keys * width + 4 * frames * rows * width,
        ),
    )(queries, *shards, *shards, *(before if chained else ()))


def column_sums(total, values):
    normed, _ = layer_norm(values.astype(F32))
    return jnp.concatenate(
        (
            jnp.sum(total * normed, axis=0, keepdims=True),
            jnp.sum(total, axis=0, keepdims=True),
        )
    )


def attend_back_kernel(first, last, *refs):
    q_ref, g_ref, o_ref, l_ref, k_ref, v_ref, wk_ref, wv_ref, x_ref = refs[:9]
    rest = refs[9:]
    if not first:
        before_ref, rest = rest[0], rest[1:]
    if last:
        wq_ref, own_ref = rest[:2]
        dq_ref, dk_ref, dv_ref, term_ref, sums_ref, qterm_ref, qsums_ref, acc_ref, qacc_ref = rest[2:]
    else:
        dq_ref, dk_ref, dv_ref, term_ref, sums_ref, acc_ref = rest
    pair = pl.program_id(1)
    key_terms = []
    value_terms = []
    query_terms = []
    for h in range(2):
        part = slice(h * DH, h * DH + DH)
        q = q_ref[0, :, part]
        g = g_ref[0, :, part]
        k = k_ref[0, :, part]
        v = v_ref[0, :, part]
        product = g.astype(F32) * o_ref[0, :, part].astype(F32)
        high, low = split_two(product)
        ones = jnp.ones((8, DH), BF)
        delta = (dot(ones, high, NT) + dot(ones, low, NT))[0:1]
        probs = jnp.exp2(dot(k, q, NT) * SCALE_TWO - l_ref[0, 0, h : h + 1, :])
        grad_probs = dot(v, g, NT)
        grad_scores = (probs * (grad_probs - delta)).astype(BF)
        value_terms.append(dot(probs.astype(BF), g))
        key_terms.append(dot(grad_scores, q))
        grad_query = dot(k, grad_scores, TN) * SCALE
        if not first:
            grad_query = grad_query + before_ref[0, part, :]
        query_terms.append(grad_query)
    grad_key = (jnp.concatenate(key_terms, axis=1) * SCALE).astype(BF)
    grad_value = jnp.concatenate(value_terms, axis=1).astype(BF)
    grad_query = jnp.concatenate(query_terms, axis=0).astype(dq_ref.dtype)
    dk_ref[0] = grad_key
    dv_ref[0] = grad_value
    dq_ref[0] = grad_query

    def collect(total_ref, value):
        @pl.when(pair == 0)
        def _():
            total_ref[...] = value

        @pl.when(pair > 0)
        def _():
            total_ref[...] += value

    collect(acc_ref, dot(grad_key, wk_ref[...], NT) + dot(grad_value, wv_ref[...], NT))
    if last:
        collect(qacc_ref, dot(grad_query, wq_ref[...], (((0,), (1,)), ((), ()))))

    @pl.when(pair == pl.num_programs(1) - 1)
    def _():
        total = acc_ref[...]
        term_ref[0] = total.astype(term_ref.dtype)
        sums_ref[0] = column_sums(total, x_ref[0])
        if last:
            total = qacc_ref[...]
            qterm_ref[0] = total
            qsums_ref[0] = column_sums(total, own_ref[0])


def attend_back(queries, grad_out, out, logs, shard, weights, source, before, own):
    frames, rows, width = queries.shape
    keys = shard.shape[1]
    pairs = width // 128
    first = before is None
    last = own is not None
    row = pl.BlockSpec((1, rows, 128), lambda f, p: (f, 0, p))
    key = pl.BlockSpec((1, keys, 128), lambda f, p: (f, 0, p))
    value = pl.BlockSpec((1, keys, 128), lambda f, p: (f, 0, p + pairs))
    turned = pl.BlockSpec((1, 128, rows), lambda f, p: (f, p, 0))
    log = pl.BlockSpec((1, 1, 2, rows), lambda f, p: (f, p, 0, 0))

    def columns(group):
        return pl.BlockSpec((width, 128), lambda f, p: (0, p + group * pairs))

    def whole(*shape):
        return pl.BlockSpec((1,) + shape, lambda f, p: (f, 0, 0))

    in_specs = [row, row, row, log, key, value, columns(1), columns(2), whole(keys, width)]
    operands = [queries, grad_out, out, logs, shard, shard, weights, weights, source]
    aliases = {}
    if not first:
        if not last:
            aliases = {len(operands): 0}
        in_specs.append(turned)
        operands.append(before)
    out_specs = [turned, key, key, whole(keys, width), whole(2, width)]
    out_shape = [
        jax.ShapeDtypeStruct((frames, width, rows), BF if last else F32),
        jax.ShapeDtypeStruct((frames, keys, width), BF),
        jax.ShapeDtypeStruct((frames, keys, width), BF),
        jax.ShapeDtypeStruct((frames, keys, width), F32 if last else BF),
        jax.ShapeDtypeStruct((frames, 2, width), F32),
    ]
    scratch = [pltpu.VMEM((keys, width), F32)]
    if last:
        in_specs += [columns(0), whole(rows, width)]
        operands += [weights, own]
        out_specs += [whole(rows, width), whole(2, width)]
        out_shape += [
            jax.ShapeDtypeStruct((frames, rows, width), F32),
            jax.ShapeDtypeStruct((frames, 2, width), F32),
        ]
        scratch.append(pltpu.VMEM((rows, width), F32))
    return pl.pallas_call(
        functools.partial(attend_back_kernel, first, last),
        grid=(frames, pairs),
        in_specs=in_specs,
        out_specs=out_specs,
        out_shape=out_shape,
        scratch_shapes=scratch,
        input_output_aliases=aliases,
        compiler_params=PARAMS,
        name="attend_back",
        cost_estimate=pl.CostEstimate(
            flops=50 * frames * rows * keys * width,
            transcendentals=frames * rows * keys * H,
            bytes_accessed=2 * frames * width * (3 * rows + 4 * keys) + 8 * frames * rows * width,
        ),
    )(*operands)


def deal(place, result, mine_ref, sent_ref):
    halves = result.reshape(mine_ref.shape[0], 2, *mine_ref.shape[1:]).astype(BF)
    low = halves[:, 0]
    high = halves[:, 1]
    even = place == 0
    mine_ref[...] = jnp.where(even, low, high)
    sent_ref[...] = jnp.where(even, high, low)


def early_grads_kernel(
    place_ref, h_ref, a_ref, f_ref, up_ref, attn_ref, head_ref, vec_ref, mine_ref, sent_ref, turn_ref
):
    step = pl.program_id(0)
    last = pl.num_programs(0) - 1
    place = place_ref[0]
    wide = up_ref.shape[1]

    @pl.when(step == 0)
    def _():
        turn_ref[...] = h_ref[...].T

    @pl.when(step < last - 1)
    def _():
        deal(place, dot(turn_ref[...], up_ref[...]), mine_ref, sent_ref)

    @pl.when(step == last - 1)
    def _():
        turned = a_ref[...].T
        turn_ref[...] = turned
        deal(place, dot(turned, attn_ref[:, :wide]), mine_ref, sent_ref)

    @pl.when(step == last)
    def _():
        out = dot(turn_ref[...], attn_ref[:, wide:])
        heads = dot(f_ref[...].T, head_ref[...]) + vec_ref[...]
        deal(place, jnp.concatenate((out, heads), axis=1), mine_ref, sent_ref)


def early_grads(place, hidden, attended, final, up, attn, heads, vectors):
    rows, width = hidden.shape
    wide = 512
    steps = up.shape[1] // wide + 2
    count = width // 96

    def whole(values):
        return pl.BlockSpec(values.shape, lambda i: (0, 0))

    out = pl.BlockSpec((count, 48, wide), lambda i: (0, 0, i))
    return pl.pallas_call(
        early_grads_kernel,
        grid=(steps,),
        in_specs=[
            pl.BlockSpec(memory_space=pltpu.SMEM),
            whole(hidden),
            whole(attended),
            whole(final),
            pl.BlockSpec((rows, wide), lambda i: (0, jnp.minimum(i, steps - 3))),
            whole(attn),
            whole(heads),
            whole(vectors),
        ],
        out_specs=[out, out],
        out_shape=[jax.ShapeDtypeStruct((count, 48, wide * steps), BF)] * 2,
        scratch_shapes=[pltpu.VMEM((width, rows), BF)],
        compiler_params=PARAMS,
        name="early_grads",
        cost_estimate=pl.CostEstimate(
            flops=2 * rows * width * wide * steps,
            transcendentals=0,
            bytes_accessed=2 * rows * wide * steps + 2 * width * wide * steps,
        ),
    )(place, hidden, attended, final, up, attn, heads, vectors)


def down_grads_kernel(place_ref, act_ref, down_ref, mine_ref, sent_ref):
    deal(place_ref[0], dot(act_ref[...], down_ref[...], TN), mine_ref, sent_ref)


def down_grads(place, activation, down):
    rows, width = down.shape
    block = activation.shape[1] // 8
    out = pl.BlockSpec((1, block // 2, width), lambda i: (i, 0, 0))
    return pl.pallas_call(
        down_grads_kernel,
        grid=(8,),
        in_specs=[
            pl.BlockSpec(memory_space=pltpu.SMEM),
            pl.BlockSpec((rows, block), lambda i: (0, i)),
            pl.BlockSpec((rows, width), lambda i: (0, 0)),
        ],
        out_specs=[out, out],
        out_shape=[jax.ShapeDtypeStruct((8, block // 2, width), BF)] * 2,
        compiler_params=PARAMS,
        name="down_grads",
        cost_estimate=pl.CostEstimate(
            flops=16 * rows * width * block,
            transcendentals=0,
            bytes_accessed=16 * rows * block + 16 * width * block,
        ),
    )(place, activation, down)


def late_grads_kernel(count, place_ref, *refs):
    mixed_refs = refs[:count]
    query_ref = refs[count]
    key_refs = refs[count + 1 : 2 * count + 1]
    value_refs = refs[2 * count + 1 : 3 * count + 1]
    vec_ref, mine_ref, sent_ref, turn_ref = refs[3 * count + 1 :]
    step = pl.program_id(0)
    third = (pl.num_programs(0) - 1) // 3
    place = place_ref[0]

    @pl.when(step == 0)
    def _():
        for s in range(count):
            turn_ref[s] = mixed_refs[s][...].T

    @pl.when(step < third)
    def _():
        deal(place, dot(turn_ref[0], query_ref[...], NT), mine_ref, sent_ref)

    def joint(parts):
        return sum(dot(turn_ref[s], parts[s][...]) for s in range(count))

    @pl.when((step >= third) & (step < 2 * third))
    def _():
        deal(place, joint(key_refs), mine_ref, sent_ref)

    @pl.when((step >= 2 * third) & (step < 3 * third))
    def _():
        deal(place, joint(value_refs), mine_ref, sent_ref)

    @pl.when(step == 3 * third)
    def _():
        deal(place, vec_ref[...], mine_ref, sent_ref)


def late_grads(place, mixed, query, keys, values, vectors):
    rows, width = mixed[0].shape
    count = len(mixed)
    wide = 256
    third = width // wide
    groups = width // 96

    def clipped(offset):
        return lambda i: (0, jnp.clip(i - offset, 0, third - 1))

    whole = pl.BlockSpec((rows, width), lambda i: (0, 0))
    out = pl.BlockSpec((groups, 48, wide), lambda i: (0, 0, i))
    return pl.pallas_call(
        functools.partial(late_grads_kernel, count),
        grid=(3 * third + 1,),
        in_specs=[pl.BlockSpec(memory_space=pltpu.SMEM)]
        + [whole] * count
        + [pl.BlockSpec((wide, rows), lambda i: (jnp.clip(i, 0, third - 1), 0))]
        + [pl.BlockSpec((rows, wide), clipped(third))] * count
        + [pl.BlockSpec((rows, wide), clipped(2 * third))] * count
        + [pl.BlockSpec((width, wide), lambda i: (0, 0))],
        out_specs=[out, out],
        out_shape=[jax.ShapeDtypeStruct((groups, 48, wide * (3 * third + 1)), BF)] * 2,
        scratch_shapes=[pltpu.VMEM((count, width, rows), BF)],
        compiler_params=PARAMS,
        name="late_grads",
        cost_estimate=pl.CostEstimate(
            flops=2 * rows * width * width * (2 * count + 1),
            transcendentals=0,
            bytes_accessed=2 * rows * width * 4 * count + 12 * width * width,
        ),
    )(place, *mixed, query, *keys, *values, vectors)


def spread(rows, columns):
    pixel = lax.broadcasted_iota(jnp.int32, (rows, columns), 0)
    field = lax.broadcasted_iota(jnp.int32, (rows, columns), 1)
    return ((pixel // TILE_AREA) == field).astype(F32).astype(BF)


def split_two(values):
    high = values.astype(BF)
    return high, (values - high.astype(F32)).astype(BF)


def pixel_sums_kernel(f_ref, s_ref, sum_ref, first_ref, second_ref, field_ref):
    @pl.when(pl.program_id(0) == 0)
    def _():
        field_ref[...] = spread(*field_ref.shape)

    fields = field_ref[...]
    sens = s_ref[...]
    sum_ref[...] = dot(sens, fields)
    for e, out in ((0, first_ref), (1, second_ref)):
        high, rest = split_two(sens.astype(F32) * f_ref[e].astype(F32))
        out[...] = dot(high, fields) + dot(rest, fields)


def pixel_sums(forecasts, sensitivity):
    rows, pixels = sensitivity.shape
    block = math.gcd(rows, 256)
    out = pl.BlockSpec((block, 128), lambda i: (i, 0))
    return pl.pallas_call(
        pixel_sums_kernel,
        grid=(rows // block,),
        in_specs=[
            pl.BlockSpec((2, block, pixels), lambda i: (0, i, 0)),
            pl.BlockSpec((block, pixels), lambda i: (i, 0)),
        ],
        out_specs=[out] * 3,
        out_shape=[jax.ShapeDtypeStruct((rows, 128), F32)] * 3,
        scratch_shapes=[pltpu.VMEM((pixels, 128), BF)],
        compiler_params=PARAMS,
        name="pixel_sums",
        cost_estimate=pl.CostEstimate(
            flops=20 * rows * pixels * 128, transcendentals=0, bytes_accessed=6 * rows * pixels
        ),
    )(forecasts, sensitivity)


def blend_kernel(a_ref, b_ref, c_ref, f_ref, out_ref, field_ref):
    @pl.when(pl.program_id(0) == 0)
    def _():
        columns = field_ref.shape[1]
        field = lax.broadcasted_iota(jnp.int32, (256, columns), 0)
        pixel = lax.broadcasted_iota(jnp.int32, (256, columns), 1)
        field_ref[...] = ((pixel // TILE_AREA) == (field % 128)).astype(F32).astype(BF)

    fields = field_ref[...]

    def wide(ref):
        return dot(jnp.concatenate(split_two(ref[...]), axis=1), fields)

    total = wide(a_ref) * f_ref[0].astype(F32) + wide(b_ref) * f_ref[1].astype(F32)
    out_ref[...] = (total + wide(c_ref)).astype(BF)


def blend(first, second, added, forecasts):
    _, rows, pixels = forecasts.shape
    block = math.gcd(rows, 256)
    thin = pl.BlockSpec((block, 128), lambda i: (i, 0))
    return pl.pallas_call(
        blend_kernel,
        grid=(rows // block,),
        in_specs=[thin] * 3 + [pl.BlockSpec((2, block, pixels), lambda i: (0, i, 0))],
        out_specs=pl.BlockSpec((block, pixels), lambda i: (i, 0)),
        out_shape=jax.ShapeDtypeStruct((rows, pixels), BF),
        scratch_shapes=[pltpu.VMEM((256, pixels), BF)],
        compiler_params=PARAMS,
        name="blend",
        cost_estimate=pl.CostEstimate(
            flops=12 * rows * pixels * 256, transcendentals=0, bytes_accessed=6 * rows * pixels
        ),
    )(first, second, added, forecasts)


def swap(values, axis, bit):
    count = lax.axis_size(axis)
    return lax.ppermute(values, axis, [(i, i ^ bit) for i in range(count)])


def pick(values, axis, index):
    return lax.dynamic_index_in_dim(values, index, axis, keepdims=False)


def add(*terms):
    return sum(t.astype(F32) for t in terms).astype(BF)


def hold(*values):
    return lax.optimization_barrier(values)


class Halves:
    def __init__(self, values, dim, axis, bit):
        place = (lax.axis_index(axis) // bit) % 2
        self.mine = pick(values, dim, place)
        self.sent = pick(values, dim, 1 - place)
        self.axis, self.bit = axis, bit

    def finish(self):
        return add(self.mine, swap(self.sent, self.axis, self.bit))


def quarters(values):
    place = lax.axis_index("lon")
    return [pick(values, 0, place ^ k) for k in range(4)]


def join_quarters(parts):
    return add(parts[0], *[swap(parts[k], "lon", k) for k in (1, 2, 3)])


def double(values, axis, bit):
    low = (lax.axis_index(axis) // bit) % 2 == 0
    other = swap(values, axis, bit)
    return jnp.stack((jnp.where(low, values, other), jnp.where(low, other, values)))


def spread_share(values):
    values = double(values, "grp", 2)
    values = double(values, "grp", 1)
    rows = values.shape[0] * values.shape[1] * values.shape[2]
    return values.reshape(rows, values.shape[-1]).astype(F32)


def chain_gather(values):
    place = lax.axis_index("lon")
    send = functools.partial(lax.ppermute, axis_name="lon")
    right_one = send(values, perm=[(0, 1), (1, 2), (2, 3)])
    left_one = send(values, perm=[(3, 2), (2, 1), (1, 0)])
    right_two = send(right_one, perm=[(1, 2), (2, 3)])
    left_two = send(left_one, perm=[(2, 1), (1, 0)])
    right_three = send(right_two, perm=[(2, 3)])
    left_three = send(left_two, perm=[(1, 0)])
    near = jnp.where(place == 0, left_one, right_one)
    middle = jnp.where(
        place == 0, left_two, jnp.where(place == 3, right_two, left_one)
    )
    far = jnp.where(
        place == 0,
        left_three,
        jnp.where(place == 1, left_two, jnp.where(place == 2, right_two, right_three)),
    )
    return [values, near, middle, far]


def layer_norm(values):
    centred = values - jnp.mean(values, axis=-1, keepdims=True)
    inverse = lax.rsqrt(jnp.mean(centred * centred, axis=-1, keepdims=True) + EPSILON)
    return centred * inverse, inverse


def norm_back(grad_normed, normed, inverse):
    return inverse * (
        grad_normed
        - jnp.mean(grad_normed, axis=-1, keepdims=True)
        - normed * jnp.mean(grad_normed * normed, axis=-1, keepdims=True)
    )


def gelu_tanh(values):
    return jax.nn.gelu(values, approximate=True)


def pad_lanes(values):
    return jnp.pad(values, ((0, 0), (0, 128 - values.shape[1])))


def per_device(
    layer_source_tensor,
    horizon_class,
    field_selector,
    model_predictions,
    loss_sensitivity,
    gain_one,
    shift_one,
    horizon_vectors,
    w_qkv,
    w_out,
    gain_two,
    shift_two,
    w_up,
    b_up,
    w_down,
    b_down,
    w_gate,
    w_bias,
):
    frames, lat_rows, lon_cols, width = layer_source_tensor.shape
    local = lat_rows * lon_cols
    rows = frames * local
    pixels = loss_sensitivity.shape[-1]
    small = (lax.axis_size("grp"), lax.axis_size("lat"), lax.axis_size("lon")) == (4, 2, 4)

    source = layer_source_tensor.reshape(frames, local, width)
    if small:
        shards = chain_gather(source)
    else:
        parts = lax.all_gather(source, "lon", axis=1, tiled=True)
        shards = [parts]

    forecasts = jnp.transpose(model_predictions.reshape(rows, 2, pixels), (1, 0, 2))
    sensitivity = loss_sensitivity.reshape(rows, pixels)
    sum_sens, sum_first, sum_second = pixel_sums(forecasts, sensitivity)

    onehot = (horizon_class[:, None] == jnp.arange(LEADS, dtype=jnp.int32)[None, :]).astype(F32)
    lead_rows = jnp.dot(onehot, horizon_vectors, precision=HIGH)

    def mixed_of(values):
        normed, _ = layer_norm(values.astype(F32))
        return (normed * gain_one + shift_one + lead_rows[:, None, :]).astype(BF)

    wq = w_qkv[:, :width]
    wkv = w_qkv[:, width:]

    def keys_of(values):
        return dot(values.reshape(-1, width), wkv).astype(BF).reshape(frames, -1, 2 * width)

    mixed_own = mixed_of(source)
    queries = dot(mixed_own.reshape(rows, width), wq).astype(BF).reshape(frames, local, width)
    if small:
        mixed = [mixed_own, mixed_of(shards[1])]
        key_value = [keys_of(m) for m in mixed]
        queries, key_value[0], key_value[1], sum_sens = hold(
            queries, key_value[0], key_value[1], sum_sens
        )
        state = attend(queries, key_value, None, False)
        shards[2], *state = hold(shards[2], *state)
        mixed.append(mixed_of(shards[2]))
        key_value.append(keys_of(mixed[2]))
        state = attend(queries, key_value[2:], state, False)
        shards[3], *state = hold(shards[3], *state)
        mixed.append(mixed_of(shards[3]))
        key_value.append(keys_of(mixed[3]))
        attended, logs = attend(queries, key_value[3:], state, True)
    else:
        mixed = [mixed_of(shards[0])]
        key_value = [keys_of(mixed[0])]
        attended, logs = attend(queries, key_value, None, True)

    inputs = source.reshape(rows, width).astype(F32)
    attended_low = attended.reshape(rows, width)
    residual = inputs + dot(attended_low, w_out)
    normed_two, inverse_two = layer_norm(residual)
    hidden_low = (normed_two * gain_two + shift_two).astype(BF)
    up_proj = dot(hidden_low, w_up) + b_up
    activation, gelu_back = jax.vjp(gelu_tanh, up_proj)
    activation_low = activation.astype(BF)
    final = residual + dot(activation_low, w_down) + b_down
    final_low = final.astype(BF)
    logits = dot(final_low, w_gate)
    offset = dot(final_low, w_bias)
    first_logits = logits[:, :RESULT_FIELDS]
    second_logits = logits[:, RESULT_FIELDS:]
    top = jnp.maximum(first_logits, second_logits)
    first_raised = jnp.exp(first_logits - top)
    second_raised = jnp.exp(second_logits - top)
    total = first_raised + second_raised
    first_share = first_raised / total
    second_share = second_raised / total
    chosen = jnp.repeat(field_selector.astype(F32), local, axis=0)
    blending = (
        pad_lanes(chosen * first_share + (1.0 - chosen)),
        pad_lanes(chosen * second_share),
        pad_lanes(chosen * offset),
    )

    offset_low = (chosen * sum_sens[:, :RESULT_FIELDS]).astype(BF)
    first_grad = chosen * sum_first[:, :RESULT_FIELDS]
    second_grad = chosen * sum_second[:, :RESULT_FIELDS]
    mean_grad = first_share * first_grad + second_share * second_grad
    logits_low = jnp.concatenate(
        (first_share * (first_grad - mean_grad), second_share * (second_grad - mean_grad)), axis=1
    ).astype(BF)
    grad_final = dot(logits_low, w_gate, NT) + dot(offset_low, w_bias, NT)
    down_low = grad_final.astype(BF)
    grad_bdown = jnp.sum(down_low.astype(F32), axis=0)
    (grad_up_proj,) = gelu_back(dot(down_low, w_down, NT))
    up_low = grad_up_proj.astype(BF)
    grad_bup = jnp.sum(up_low.astype(F32), axis=0)
    grad_hidden = dot(up_low, w_up, NT)
    grad_gain_two = jnp.sum(grad_hidden * normed_two, axis=0)
    grad_bias_two = jnp.sum(grad_hidden, axis=0)
    grad_residual = grad_final + norm_back(grad_hidden * gain_two, normed_two, inverse_two)
    attn_low = grad_residual.astype(BF)
    grad_attended = dot(attn_low, w_out, NT).astype(BF).reshape(frames, local, width)

    fields = 3 * RESULT_FIELDS
    early_vectors = jnp.concatenate(
        (
            jnp.stack((grad_gain_two, grad_bias_two, grad_bdown)),
            grad_bup.reshape(width, -1).T,
        )
    )
    heads_low = jnp.concatenate((logits_low, offset_low), axis=1)
    normed_one, inverse_one = layer_norm(inputs)

    def back(shard, place, before, own=None):
        return attend_back(
            queries, grad_attended, attended, logs, shard, w_qkv, place, before, own
        )

    def late_vectors(sums):
        gain_column = sum(jnp.sum(s[:, 0], axis=0) for s in sums)
        column = sum(s[:, 1] for s in sums)
        lead = jnp.dot(onehot.T, column, precision=HIGH)
        return jnp.concatenate((gain_column[None], jnp.sum(column, axis=0)[None], lead))

    if small:
        core = (lax.axis_index("grp") % 2).astype(jnp.int32)[None]
        y_axis, x_axis = ("grp", 2), ("lat", 1)
        used = fields + early_vectors.shape[0]
        up_mine, up_sent = early_grads(
            core,
            hidden_low,
            attended_low,
            final_low,
            up_low,
            attn_low,
            jnp.pad(heads_low, ((0, 0), (0, 256 - fields))),
            jnp.pad(early_vectors.T, ((0, 0), (fields, 256 - used))),
        )
        down_mine, down_sent = down_grads(core, activation_low, down_low)
        grad_attended, up_sent, down_sent = hold(grad_attended, up_sent, down_sent)
        place = lax.axis_index("lon")
        send = functools.partial(lax.ppermute, axis_name="lon")
        edge = (place == 0) | (place == 3)

        grad_query, dk3, dv3, far, sums3 = back(key_value[3], shards[3], None)
        up = add(up_mine, swap(up_sent, "grp", 1)).reshape(2, 4, 2, 24, -1)
        down = add(down_mine, swap(down_sent, "grp", 1)).reshape(2, 4, 2, -1, width)
        up = Halves(up, 0, *x_axis)
        down = Halves(down, 2, *y_axis)
        grad_query, far, up.sent, down.sent = hold(grad_query, far, up.sent, down.sent)
        right = send(far, perm=[(0, 1)])
        left = send(far, perm=[(3, 2)])

        grad_query, dk2, dv2, middle, sums2 = back(key_value[2], shards[2], grad_query)
        value = jnp.where(edge, middle, add(right, left, far))
        grad_query, value = hold(grad_query, value)
        right = send(value, perm=[(0, 1), (1, 2)])
        left = send(value, perm=[(3, 2), (2, 1)])

        grad_query, dk1, dv1, near, sums1 = back(key_value[1], shards[1], grad_query)
        forth = jnp.where(place == 0, near, add(right, middle))
        back_value = add(left, near)
        up = Halves(up.finish(), 1, *y_axis)
        down = Halves(down.finish(), 0, *x_axis)
        grad_query, forth, back_value, up.sent, down.sent = hold(
            grad_query, forth, back_value, up.sent, down.sent
        )
        right = send(forth, perm=[(0, 1), (1, 2), (2, 3)])
        left = send(back_value, perm=[(3, 2), (2, 1), (1, 0)])

        query_low, dk0, dv0, own, sums0, query_term, query_sums = back(
            key_value[0], shards[0], grad_query, source
        )
        vectors = late_vectors([sums0, sums1, sums2, sums3, query_sums])
        up = quarters(up.finish())
        down = quarters(down.finish())
        query_low, *parts = hold(query_low, *up, *down)
        up, down = parts[:4], parts[4:]
        late_mine, late_sent = late_grads(
            core,
            [m.reshape(rows, width) for m in mixed],
            query_low.reshape(width, rows),
            [d.reshape(rows, width) for d in (dk0, dk1, dk2, dk3)],
            [d.reshape(rows, width) for d in (dv0, dv1, dv2, dv3)],
            jnp.pad(vectors.T, ((0, 0), (0, 256 - vectors.shape[0]))),
        )
        grad_mixed = own + query_term + right.astype(F32) + left.astype(F32)
        late = add(late_mine, swap(late_sent, "grp", 1)).reshape(2, 4, 2, 24, -1)
        first = Halves(late[:, :2], 2, *y_axis)
        second = Halves(late[:, 2:], 0, *x_axis)
        blending = hold(first.sent, second.sent, *blending)
        first.sent, second.sent = blending[:2]
        blended = blend(*blending[2:], forecasts)
        first, second, blended = hold(first.finish(), second.finish(), blended)
        first = Halves(first, 0, *x_axis)
        second = Halves(second, 1, *y_axis)
        up = join_quarters(up)
        down = join_quarters(down)
        first.sent, second.sent, up, down = hold(first.sent, second.sent, up, down)
        up_sum = spread_share(up)
        down_sum = spread_share(down)
        late = quarters(jnp.concatenate((first.finish(), second.finish())))
        late = spread_share(join_quarters(late))
        qkv_sum = late[:, : 3 * width]
        late = late[:, 3 * width : 3 * width + vectors.shape[0]].T
        hidden = w_up.shape[1]
        out_sum = up_sum[:, hidden : hidden + width]
        misc = up_sum[:, hidden + width : hidden + width + used]
        up_sum = up_sum[:, :hidden]
        heads = misc[:, :fields]
        early = misc[:, fields : fields + 3].T
        bup_sum = misc[:, fields + 3 :].reshape(-1)
    else:
        blended = blend(*blending, forecasts)
        query_low, dk, dv, term, sums, query_term, query_sums = back(
            key_value[0], shards[0], None, source
        )
        grad_mixed = query_term + lax.psum_scatter(
            term, "lon", scatter_dimension=1, tiled=True
        )

        def total_of(values, dim=0):
            share = lax.psum_scatter(values, ("lat", "lon"), scatter_dimension=dim, tiled=True)
            return lax.psum(share, "grp")

        flat = mixed[0].reshape(-1, width)
        qkv_sum = total_of(
            jnp.concatenate(
                (
                    jnp.einsum("frd,fer->de", mixed_own, query_low, preferred_element_type=F32),
                    dot(flat, dk.reshape(-1, width), TN),
                    dot(flat, dv.reshape(-1, width), TN),
                ),
                axis=1,
            )
        )
        up_sum = total_of(dot(hidden_low, up_low, TN))
        out_sum = total_of(dot(attended_low, attn_low, TN))
        down_sum = total_of(dot(activation_low, down_low, TN))
        heads = total_of(dot(final_low, heads_low, TN))
        late = total_of(late_vectors([sums, query_sums]), 1)
        early = total_of(early_vectors[:3], 1)
        bup_sum = total_of(grad_bup)

    grad_input = grad_residual + norm_back(
        grad_mixed.reshape(rows, width) * gain_one, normed_one, inverse_one
    )
    return (
        blended.reshape(frames, lat_rows, lon_cols, pixels),
        grad_input.reshape(frames, lat_rows, lon_cols, width),
        late[0],
        late[1],
        late[2:],
        qkv_sum,
        out_sum,
        early[0],
        early[1],
        up_sum,
        bup_sum,
        down_sum,
        early[2],
        heads[:, : 2 * RESULT_FIELDS],
        heads[:, 2 * RESULT_FIELDS :],
    )


def solution(mesh):
    frame = ("grp", "lat")
    share = ("lat", "lon")
    image = P(frame, None, "lon", None)
    in_specs = (
        image,
        P(frame),
        P(frame, None),
        P(frame, None, "lon", None, None),
        image,
    ) + (P(),) * 13
    vector = P(share)
    matrix = P(share, None)
    out_specs = (
        image,
        image,
        vector,
        vector,
        P(None, share),
        matrix,
        matrix,
        vector,
        vector,
        matrix,
        vector,
        matrix,
        vector,
        matrix,
        matrix,
    )
    return jax.shard_map(
        per_device, mesh=mesh, in_specs=in_specs, out_specs=out_specs, check_vma=False
    )
```

```python
import functools
import math

import jax
import jax.numpy as jnp
from jax import lax
from jax.experimental import pallas as pl
from jax.experimental.pallas import tpu as pltpu
from jax.sharding import PartitionSpec as P

H = 12
DH = 64
RESULT_FIELDS = 69
TILE_AREA = 64
LEADS = 24
EPSILON = 1e-06
HIGH = lax.Precision.HIGHEST
SCALE = 0.125
SCALE_TWO = SCALE * math.log2(math.e)
ROOT = math.sqrt(2.0 / math.pi)
CUBE = 0.044715
NN = (((1,), (0,)), ((), ()))
NT = (((1,), (1,)), ((), ()))
TN = (((0,), (0,)), ((), ()))
BF = jnp.bfloat16
F32 = jnp.float32
PARAMS = pltpu.CompilerParams(vmem_limit_bytes=60 * 1024 * 1024)


def dot(left, right, dims=NN):
    return lax.dot_general(left, right, dims, preferred_element_type=F32)


def attend_kernel(count, chained, final, *refs):
    q_ref = refs[0]
    k_refs = refs[1 : 1 + count]
    v_refs = refs[1 + count : 1 + 2 * count]
    o_ref, l_ref = refs[-2:]
    outs = []
    for h in range(2):
        part = slice(h * DH, h * DH + DH)
        q = q_ref[0, :, part]
        scores = [dot(k[0, :, part], q, NT) for k in k_refs]
        top = functools.reduce(
            jnp.maximum, [jnp.max(s, axis=0, keepdims=True) for s in scores]
        )
        top = top * SCALE_TWO
        total = None
        mixed = None
        for s, v in zip(scores, v_refs):
            raised = jnp.exp2(s * SCALE_TWO - top)
            some = jnp.sum(raised, axis=0, keepdims=True)
            term = dot(v[0, :, part], raised.astype(BF), TN)
            total = some if total is None else total + some
            mixed = term if mixed is None else mixed + term
        mixed = mixed * (1.0 / total)
        log = top + jnp.log2(total)
        if chained:
            before_ref, before_log_ref = refs[1 + 2 * count : 3 + 2 * count]
            before = before_log_ref[0, 0, h : h + 1, :]
            high = jnp.maximum(before, log)
            joint = high + jnp.log2(jnp.exp2(before - high) + jnp.exp2(log - high))
            mixed = mixed * jnp.exp2(log - joint) + before_ref[0, part, :] * jnp.exp2(
                before - joint
            )
            log = joint
        l_ref[0, 0, h : h + 1, :] = log
        if final:
            outs.append(mixed)
        else:
            o_ref[0, part, :] = mixed
    if final:
        o_ref[0] = jnp.concatenate(outs, axis=0).T.astype(BF)


def attend(queries, shards, before, final):
    frames, rows, width = queries.shape
    count = len(shards)
    keys = shards[0].shape[1]
    pairs = width // 128
    turned = pl.BlockSpec((1, 128, rows), lambda f, p: (f, p, 0))
    row = pl.BlockSpec((1, rows, 128), lambda f, p: (f, 0, p))
    log = pl.BlockSpec((1, 1, 2, rows), lambda f, p: (f, p, 0, 0))
    chained = before is not None
    return pl.pallas_call(
        functools.partial(attend_kernel, count, chained, final),
        grid=(frames, pairs),
        in_specs=[row]
        + [pl.BlockSpec((1, keys, 128), lambda f, p: (f, 0, p))] * count
        + [pl.BlockSpec((1, keys, 128), lambda f, p: (f, 0, p + pairs))] * count
        + ([turned, log] if chained else []),
        out_specs=[row if final else turned, log],
        out_shape=[
            jax.ShapeDtypeStruct((frames, rows, width), BF)
            if final
            else jax.ShapeDtypeStruct((frames, width, rows), F32),
            jax.ShapeDtypeStruct((frames, pairs, 2, rows), F32),
        ],
        compiler_params=PARAMS,
        name="attend",
        cost_estimate=pl.CostEstimate(
            flops=2 * frames * rows * count * keys * width,
            transcendentals=0,
            bytes_accessed=frames * rows * width,
        ),
    )(queries, *shards, *shards, *(before if chained else ()))


def column_sums(total, values):
    normed, _ = layer_norm(values.astype(F32))
    return jnp.concatenate(
        (
            jnp.sum(total * normed, axis=0, keepdims=True),
            jnp.sum(total, axis=0, keepdims=True),
        )
    )


def attend_back_kernel(first, last, *refs):
    q_ref, g_ref, o_ref, l_ref, k_ref, v_ref, wk_ref, wv_ref, x_ref = refs[:9]
    rest = refs[9:]
    if not first:
        before_ref, rest = rest[0], rest[1:]
    if last:
        wq_ref, own_ref = rest[:2]
        dq_ref, dk_ref, dv_ref, term_ref, sums_ref, qterm_ref, qsums_ref, qacc_ref = rest[2:]
    else:
        dq_ref, dk_ref, dv_ref, term_ref, sums_ref = rest
    pair = pl.program_id(1)
    key_terms = []
    value_terms = []
    query_terms = []
    for h in range(2):
        part = slice(h * DH, h * DH + DH)
        q = q_ref[0, :, part]
        g = g_ref[0, :, part]
        k = k_ref[0, :, part]
        v = v_ref[0, :, part]
        product = g.astype(F32) * o_ref[0, :, part].astype(F32)
        high, low = split_two(product)
        ones = jnp.ones((8, DH), BF)
        delta = (dot(ones, high, NT) + dot(ones, low, NT))[0:1]
        probs = jnp.exp2(dot(k, q, NT) * SCALE_TWO - l_ref[0, 0, h : h + 1, :])
        grad_probs = dot(v, g, NT)
        grad_scores = (probs * (grad_probs - delta)).astype(BF)
        value_terms.append(dot(probs.astype(BF), g))
        key_terms.append(dot(grad_scores, q))
        grad_query = dot(k, grad_scores, TN) * SCALE
        if not first:
            grad_query = grad_query + before_ref[0, part, :]
        query_terms.append(grad_query)
    grad_key = (jnp.concatenate(key_terms, axis=1) * SCALE).astype(BF)
    grad_value = jnp.concatenate(value_terms, axis=1).astype(BF)
    grad_query = jnp.concatenate(query_terms, axis=0).astype(dq_ref.dtype)
    lanes = pl.ds(pl.multiple_of(pair * 128, 128), 128)
    dk_ref[0, :, lanes] = grad_key
    dv_ref[0, :, lanes] = grad_value
    dq_ref[0] = grad_query

    if last:
        part = dot(grad_query, wq_ref[...], (((0,), (1,)), ((), ())))

        @pl.when(pair == 0)
        def _():
            qacc_ref[...] = part

        @pl.when(pair > 0)
        def _():
            qacc_ref[...] += part

    @pl.when(pair == pl.num_programs(1) - 1)
    def _():
        total = dot(dk_ref[0], wk_ref[...], NT) + dot(dv_ref[0], wv_ref[...], NT)
        term_ref[0] = total.astype(term_ref.dtype)
        sums_ref[0] = column_sums(total, x_ref[0])
        if last:
            total = qacc_ref[...]
            qterm_ref[0] = total
            qsums_ref[0] = column_sums(total, own_ref[0])


def attend_back(queries, grad_out, out, logs, shard, weights, source, before, own):
    frames, rows, width = queries.shape
    keys = shard.shape[1]
    pairs = width // 128
    first = before is None
    last = own is not None
    row = pl.BlockSpec((1, rows, 128), lambda f, p: (f, 0, p))
    key = pl.BlockSpec((1, keys, 128), lambda f, p: (f, 0, p))
    value = pl.BlockSpec((1, keys, 128), lambda f, p: (f, 0, p + pairs))
    turned = pl.BlockSpec((1, 128, rows), lambda f, p: (f, p, 0))
    log = pl.BlockSpec((1, 1, 2, rows), lambda f, p: (f, p, 0, 0))

    def columns(group):
        return pl.BlockSpec((width, width), lambda f, p: (0, group))

    def whole(*shape):
        return pl.BlockSpec((1,) + shape, lambda f, p: (f, 0, 0))

    in_specs = [row, row, row, log, key, value, columns(1), columns(2), whole(keys, width)]
    operands = [queries, grad_out, out, logs, shard, shard, weights, weights, source]
    aliases = {}
    if not first:
        if not last:
            aliases = {len(operands): 0}
        in_specs.append(turned)
        operands.append(before)
    out_specs = [turned, whole(keys, width), whole(keys, width), whole(keys, width), whole(2, width)]
    out_shape = [
        jax.ShapeDtypeStruct((frames, width, rows), BF if last else F32),
        jax.ShapeDtypeStruct((frames, keys, width), BF),
        jax.ShapeDtypeStruct((frames, keys, width), BF),
        jax.ShapeDtypeStruct((frames, keys, width), F32 if last else BF),
        jax.ShapeDtypeStruct((frames, 2, width), F32),
    ]
    scratch = []
    if last:
        in_specs += [pl.BlockSpec((width, 128), lambda f, p: (0, p)), whole(rows, width)]
        operands += [weights, own]
        out_specs += [whole(rows, width), whole(2, width)]
        out_shape += [
            jax.ShapeDtypeStruct((frames, rows, width), F32),
            jax.ShapeDtypeStruct((frames, 2, width), F32),
        ]
        scratch.append(pltpu.VMEM((rows, width), F32))
    return pl.pallas_call(
        functools.partial(attend_back_kernel, first, last),
        grid=(frames, pairs),
        in_specs=in_specs,
        out_specs=out_specs,
        out_shape=out_shape,
        scratch_shapes=scratch,
        input_output_aliases=aliases,
        compiler_params=PARAMS,
        name="attend_back",
        cost_estimate=pl.CostEstimate(
            flops=4 * frames * rows * keys * width,
            transcendentals=0,
            bytes_accessed=frames * rows * width,
        ),
    )(*operands)


def between_kernel(
    x_ref,
    att_ref,
    wo_ref,
    wu_ref,
    wd_ref,
    head_ref,
    gain_ref,
    shift_ref,
    bu_ref,
    bd_ref,
    mask_ref,
    sens_ref,
    one_ref,
    two_ref,
    hidden_ref,
    act_ref,
    up_ref,
    down_ref,
    final_ref,
    heads_ref,
    attn_ref,
    gres_ref,
    gatt_ref,
    first_ref,
    second_ref,
    added_ref,
    vec_ref,
    bup_ref,
    slope_ref,
):
    residual = x_ref[...].astype(F32) + dot(att_ref[...], wo_ref[...])
    normed, inverse = layer_norm(residual)
    gain = gain_ref[...]
    hidden = (normed * gain + shift_ref[...]).astype(BF)
    hidden_ref[...] = hidden
    wide = 512
    chunks = [slice(j, j + wide) for j in range(0, wu_ref.shape[1], wide)]
    final = residual + bd_ref[...]
    for part in chunks:
        up = dot(hidden, wu_ref[:, part]) + bu_ref[:, part]
        square = up * up
        tanh = jnp.tanh(ROOT * up * (1.0 + CUBE * square))
        half = 0.5 * (1.0 + tanh)
        act = (up * half).astype(BF)
        slope_ref[:, part] = half + 0.5 * up * (1.0 - tanh * tanh) * (
            ROOT + 3.0 * ROOT * CUBE * square
        )
        act_ref[:, part] = act
        final = final + dot(act, wd_ref[part, :])
    final_low = final.astype(BF)
    final_ref[...] = final_low
    logits = dot(final_low, head_ref[...], NT)
    one = logits[:, :128]
    two = logits[:, 128:256]
    offset = logits[:, 256:]
    top = jnp.maximum(one, two)
    one = jnp.exp(one - top)
    two = jnp.exp(two - top)
    total = one + two
    one = one / total
    two = two / total
    mask = mask_ref[0]
    first_ref[...] = mask * one + (1.0 - mask)
    second_ref[...] = mask * two
    added_ref[...] = mask * offset
    grad_one = mask * one_ref[...]
    grad_two = mask * two_ref[...]
    mean = one * grad_one + two * grad_two
    heads = jnp.concatenate(
        (one * (grad_one - mean), two * (grad_two - mean), mask * sens_ref[...]), axis=1
    ).astype(BF)
    heads_ref[...] = heads
    grad_final = dot(heads, head_ref[...])
    down = grad_final.astype(BF)
    down_ref[...] = down
    grad_hidden = None
    ups = []
    for part in chunks:
        grad_up = (dot(down, wd_ref[part, :], NT) * slope_ref[:, part]).astype(BF)
        up_ref[:, part] = grad_up
        ups.append(jnp.sum(grad_up.astype(F32), axis=0, keepdims=True))
        term = dot(grad_up, wu_ref[:, part], NT)
        grad_hidden = term if grad_hidden is None else grad_hidden + term
    grad_normed = grad_hidden * gain
    grad_residual = grad_final + norm_back(grad_normed, normed, inverse)
    gres_ref[...] = grad_residual
    attn = grad_residual.astype(BF)
    attn_ref[...] = attn
    gatt_ref[...] = dot(attn, wo_ref[...], NT).astype(BF)
    vectors = jnp.concatenate(
        (
            jnp.sum(grad_hidden * normed, axis=0, keepdims=True),
            jnp.sum(grad_hidden, axis=0, keepdims=True),
            jnp.sum(down.astype(F32), axis=0, keepdims=True),
        )
    )
    ups = jnp.concatenate(ups, axis=1)

    @pl.when(pl.program_id(0) == 0)
    def _():
        vec_ref[...] = vectors
        bup_ref[...] = ups

    @pl.when(pl.program_id(0) > 0)
    def _():
        vec_ref[...] += vectors
        bup_ref[...] += ups


def between(x, attended, w_out, w_up, w_down, heads, gain, shift, b_up, b_down, mask, sums, local):
    rows, width = x.shape
    hidden = w_up.shape[1]
    block = math.gcd(local, 256)

    def row(columns):
        return pl.BlockSpec((block, columns), lambda i: (i, 0))

    def whole(values):
        return pl.BlockSpec(values.shape, lambda i: (0, 0), pipeline_mode=pl.Buffered(1))

    def shape(columns, kind=BF):
        return jax.ShapeDtypeStruct((rows, columns), kind)

    fixed = [w_out, w_up, w_down, heads, gain[None], shift[None], b_up[None], b_down[None]]
    return pl.pallas_call(
        between_kernel,
        grid=(rows // block,),
        in_specs=[row(width), row(width)]
        + [whole(v) for v in fixed]
        + [pl.BlockSpec((1, 1, 128), lambda i: (i * block // local, 0, 0))]
        + [row(128)] * 3,
        out_specs=[
            row(width),
            row(hidden),
            row(hidden),
            row(width),
            row(width),
            row(384),
            row(width),
            row(width),
            row(width),
            row(128),
            row(128),
            row(128),
            pl.BlockSpec((3, width), lambda i: (0, 0)),
            pl.BlockSpec((1, hidden), lambda i: (0, 0)),
        ],
        out_shape=[
            shape(width),
            shape(hidden),
            shape(hidden),
            shape(width),
            shape(width),
            shape(384),
            shape(width),
            shape(width, F32),
            shape(width),
            shape(128, F32),
            shape(128, F32),
            shape(128, F32),
            jax.ShapeDtypeStruct((3, width), F32),
            jax.ShapeDtypeStruct((1, hidden), F32),
        ],
        scratch_shapes=[pltpu.VMEM((block, hidden), F32)],
        compiler_params=PARAMS,
        name="between",
        cost_estimate=pl.CostEstimate(
            flops=rows * width * hidden, transcendentals=0, bytes_accessed=rows * hidden
        ),
    )(x, attended, *fixed, mask, *sums)


def deal(place, result, mine_ref, sent_ref):
    halves = result.reshape(mine_ref.shape[0], 2, *mine_ref.shape[1:]).astype(BF)
    low = halves[:, 0]
    high = halves[:, 1]
    even = place == 0
    mine_ref[...] = jnp.where(even, low, high)
    sent_ref[...] = jnp.where(even, high, low)


def columns_of(vectors, start):
    count = vectors.shape[0]
    place = lax.broadcasted_iota(jnp.int32, (count, 256), 1)
    which = lax.broadcasted_iota(jnp.int32, (count, 256), 0)
    chosen = (place == which + start).astype(F32).astype(BF)
    high, rest = split_two(vectors)
    return dot(high, chosen, TN) + dot(rest, chosen, TN)


def early_grads_kernel(
    place_ref,
    h_ref,
    a_ref,
    f_ref,
    up_ref,
    attn_ref,
    head_ref,
    vec_ref,
    mine_in_ref,
    sent_in_ref,
    mine_ref,
    sent_ref,
    turn_ref,
):
    step = pl.program_id(0)
    last = pl.num_programs(0) - 1
    place = place_ref[0]
    wide = up_ref.shape[1]

    @pl.when(step == 0)
    def _():
        turn_ref[...] = h_ref[...].T

    @pl.when(step < last - 1)
    def _():
        deal(place, dot(turn_ref[...], up_ref[...]), mine_ref, sent_ref)

    @pl.when(step == last - 1)
    def _():
        turned = a_ref[...].T
        turn_ref[...] = turned
        deal(place, dot(turned, attn_ref[:, :wide]), mine_ref, sent_ref)

    @pl.when(step == last)
    def _():
        out = dot(turn_ref[...], attn_ref[:, wide:])
        heads = dot(f_ref[...].T, head_ref[...]) + columns_of(vec_ref[...], 3 * RESULT_FIELDS)
        deal(place, jnp.concatenate((out, heads), axis=1), mine_ref, sent_ref)


def early_grads(place, hidden, attended, final, up, attn, heads, vectors, mine, sent):
    rows, width = hidden.shape
    wide = 512
    steps = up.shape[1] // wide + 2
    count = width // 96
    skip = mine.shape[2] // wide - steps

    def whole(values):
        return pl.BlockSpec(values.shape, lambda i: (0, 0))

    out = pl.BlockSpec((count, 48, wide), lambda i: (0, 0, i + skip))
    untouched = pl.BlockSpec(memory_space=pl.ANY)
    return pl.pallas_call(
        early_grads_kernel,
        grid=(steps,),
        in_specs=[
            pl.BlockSpec(memory_space=pltpu.SMEM),
            whole(hidden),
            whole(attended),
            whole(final),
            pl.BlockSpec((rows, wide), lambda i: (0, jnp.minimum(i, steps - 3))),
            whole(attn),
            whole(heads),
            whole(vectors),
            untouched,
            untouched,
        ],
        out_specs=[out, out],
        out_shape=[jax.ShapeDtypeStruct(mine.shape, BF)] * 2,
        input_output_aliases={8: 0, 9: 1},
        scratch_shapes=[pltpu.VMEM((width, rows), BF)],
        compiler_params=PARAMS,
        name="early_grads",
        cost_estimate=pl.CostEstimate(
            flops=2 * rows * width * wide * steps,
            transcendentals=0,
            bytes_accessed=2 * rows * wide * steps + 2 * width * wide * steps,
        ),
    )(place, hidden, attended, final, up, attn, heads, vectors, mine, sent)


def down_grads_kernel(place_ref, act_ref, down_ref, mine_ref, sent_ref):
    result = dot(act_ref[...], down_ref[...], TN).astype(BF)
    block = result.shape[0] // 2
    piece = block // 8
    halves = []
    for c in range(2):
        groups = [
            jnp.concatenate(
                [
                    result[c * block + y * 4 * piece + g * piece :][:piece]
                    for y in range(2)
                ],
                axis=0,
            )
            for g in range(4)
        ]
        halves.append(jnp.concatenate(groups, axis=1)[None])
    even = place_ref[0] == 0
    mine_ref[...] = jnp.where(even, halves[0], halves[1])
    sent_ref[...] = jnp.where(even, halves[1], halves[0])


def down_grads(place, activation, down, columns):
    rows, width = down.shape
    block = activation.shape[1] // 8
    piece = block // 16
    out = pl.BlockSpec((1, 2 * piece, 4 * width), lambda i: (i, 0, 0))
    return pl.pallas_call(
        down_grads_kernel,
        grid=(8,),
        in_specs=[
            pl.BlockSpec(memory_space=pltpu.SMEM),
            pl.BlockSpec((rows, block), lambda i: (0, i)),
            pl.BlockSpec((rows, width), lambda i: (0, 0)),
        ],
        out_specs=[out, out],
        out_shape=[jax.ShapeDtypeStruct((8, 2 * piece, columns), BF)] * 2,
        compiler_params=PARAMS,
        name="down_grads",
        cost_estimate=pl.CostEstimate(
            flops=2 * rows * width * block, transcendentals=0, bytes_accessed=width * block
        ),
    )(place, activation, down)


def late_grads_kernel(count, place_ref, *refs):
    mixed_refs = refs[:count]
    query_ref = refs[count]
    key_refs = refs[count + 1 : 2 * count + 1]
    value_refs = refs[2 * count + 1 : 3 * count + 1]
    vec_ref, mine_ref, sent_ref, turn_ref = refs[3 * count + 1 :]
    step = pl.program_id(0)
    third = (pl.num_programs(0) - 1) // 3
    place = place_ref[0]

    @pl.when(step == 0)
    def _():
        for s in range(count):
            turn_ref[s] = mixed_refs[s][...].T

    @pl.when(step < third)
    def _():
        deal(place, dot(turn_ref[0], query_ref[...], NT), mine_ref, sent_ref)

    def joint(parts):
        return sum(dot(turn_ref[s], parts[s][...]) for s in range(count))

    @pl.when((step >= third) & (step < 2 * third))
    def _():
        deal(place, joint(key_refs), mine_ref, sent_ref)

    @pl.when((step >= 2 * third) & (step < 3 * third))
    def _():
        deal(place, joint(value_refs), mine_ref, sent_ref)

    @pl.when(step == 3 * third)
    def _():
        deal(place, columns_of(vec_ref[...], 0), mine_ref, sent_ref)


def late_grads(place, mixed, query, keys, values, vectors):
    rows, width = mixed[0].shape
    count = len(mixed)
    wide = 256
    third = width // wide
    groups = width // 96

    def clipped(offset):
        return lambda i: (0, jnp.clip(i - offset, 0, third - 1))

    whole = pl.BlockSpec((rows, width), lambda i: (0, 0))
    out = pl.BlockSpec((groups, 48, wide), lambda i: (0, 0, i))
    return pl.pallas_call(
        functools.partial(late_grads_kernel, count),
        grid=(3 * third + 1,),
        in_specs=[pl.BlockSpec(memory_space=pltpu.SMEM)]
        + [whole] * count
        + [pl.BlockSpec((wide, rows), lambda i: (jnp.clip(i, 0, third - 1), 0))]
        + [pl.BlockSpec((rows, wide), clipped(third))] * count
        + [pl.BlockSpec((rows, wide), clipped(2 * third))] * count
        + [pl.BlockSpec(vectors.shape, lambda i: (0, 0))],
        out_specs=[out, out],
        out_shape=[jax.ShapeDtypeStruct((groups, 48, wide * (3 * third + 1)), BF)] * 2,
        scratch_shapes=[pltpu.VMEM((count, width, rows), BF)],
        compiler_params=PARAMS,
        name="late_grads",
        cost_estimate=pl.CostEstimate(
            flops=2 * rows * width * width * (2 * count + 1),
            transcendentals=0,
            bytes_accessed=2 * rows * width * 4 * count + 12 * width * width,
        ),
    )(place, *mixed, query, *keys, *values, vectors)


def spread(rows, columns):
    pixel = lax.broadcasted_iota(jnp.int32, (rows, columns), 0)
    field = lax.broadcasted_iota(jnp.int32, (rows, columns), 1)
    return ((pixel // TILE_AREA) == field).astype(F32).astype(BF)


def split_two(values):
    high = values.astype(BF)
    return high, (values - high.astype(F32)).astype(BF)


def pixel_sums_kernel(f_ref, s_ref, sum_ref, first_ref, second_ref, field_ref):
    @pl.when(pl.program_id(0) == 0)
    def _():
        field_ref[...] = spread(*field_ref.shape)

    fields = field_ref[...]
    sens = s_ref[...]
    sum_ref[...] = dot(sens, fields)
    for e, out in ((0, first_ref), (1, second_ref)):
        high, rest = split_two(sens.astype(F32) * f_ref[e].astype(F32))
        out[...] = dot(high, fields) + dot(rest, fields)


def pixel_sums(forecasts, sensitivity):
    rows, pixels = sensitivity.shape
    block = math.gcd(rows, 256)
    out = pl.BlockSpec((block, 128), lambda i: (i, 0))
    return pl.pallas_call(
        pixel_sums_kernel,
        grid=(rows // block,),
        in_specs=[
            pl.BlockSpec((2, block, pixels), lambda i: (0, i, 0)),
            pl.BlockSpec((block, pixels), lambda i: (i, 0)),
        ],
        out_specs=[out] * 3,
        out_shape=[jax.ShapeDtypeStruct((rows, 128), F32)] * 3,
        scratch_shapes=[pltpu.VMEM((pixels, 128), BF)],
        compiler_params=PARAMS,
        name="pixel_sums",
        cost_estimate=pl.CostEstimate(
            flops=rows * pixels * 128, transcendentals=0, bytes_accessed=rows * pixels
        ),
    )(forecasts, sensitivity)


def blend_kernel(a_ref, b_ref, c_ref, f_ref, out_ref, field_ref):
    @pl.when(pl.program_id(0) == 0)
    def _():
        columns = field_ref.shape[1]
        field = lax.broadcasted_iota(jnp.int32, (256, columns), 0)
        pixel = lax.broadcasted_iota(jnp.int32, (256, columns), 1)
        field_ref[...] = ((pixel // TILE_AREA) == (field % 128)).astype(F32).astype(BF)

    fields = field_ref[...]

    def wide(ref):
        return dot(jnp.concatenate(split_two(ref[...]), axis=1), fields)

    total = wide(a_ref) * f_ref[0].astype(F32) + wide(b_ref) * f_ref[1].astype(F32)
    out_ref[...] = (total + wide(c_ref)).astype(BF)


def blend(first, second, added, forecasts):
    _, rows, pixels = forecasts.shape
    block = math.gcd(rows, 256)
    thin = pl.BlockSpec((block, 128), lambda i: (i, 0))
    return pl.pallas_call(
        blend_kernel,
        grid=(rows // block,),
        in_specs=[thin] * 3 + [pl.BlockSpec((2, block, pixels), lambda i: (0, i, 0))],
        out_specs=pl.BlockSpec((block, pixels), lambda i: (i, 0)),
        out_shape=jax.ShapeDtypeStruct((rows, pixels), BF),
        scratch_shapes=[pltpu.VMEM((256, pixels), BF)],
        compiler_params=PARAMS,
        name="blend",
        cost_estimate=pl.CostEstimate(
            flops=rows * pixels * 128, transcendentals=0, bytes_accessed=rows * pixels
        ),
    )(first, second, added, forecasts)


def swap(values, axis, bit):
    count = lax.axis_size(axis)
    return lax.ppermute(values, axis, [(i, i ^ bit) for i in range(count)])


def pick(values, axis, index):
    return lax.dynamic_index_in_dim(values, index, axis, keepdims=False)


def add(*terms):
    return sum(t.astype(F32) for t in terms).astype(BF)


def hold(*values):
    return lax.optimization_barrier(values)


class Halves:
    def __init__(self, terms, dim, axis, bit):
        place = (lax.axis_index(axis) // bit) % 2
        self.mine = [pick(t, dim, place) for t in terms]
        self.sent = add(*[pick(t, dim, 1 - place) for t in terms])
        self.axis, self.bit = axis, bit

    def start(self):
        self.got = swap(self.sent, self.axis, self.bit)

    def finish(self):
        return self.mine + [self.got]


def quarters(terms):
    place = lax.axis_index("lon")
    return [add(*[pick(t, 0, place ^ k) for t in terms]) for k in range(4)]


def trade_quarters(parts):
    return [parts[0]] + [swap(parts[k], "lon", k) for k in (1, 2, 3)]


def double(values, other, axis, bit):
    low = (lax.axis_index(axis) // bit) % 2 == 0
    return jnp.stack((jnp.where(low, values, other), jnp.where(low, other, values)))


def spread_core(values):
    return double(values, swap(values, "grp", 1), "grp", 1)


def layer_norm(values):
    centred = values - jnp.mean(values, axis=-1, keepdims=True)
    inverse = lax.rsqrt(jnp.mean(centred * centred, axis=-1, keepdims=True) + EPSILON)
    return centred * inverse, inverse


def norm_back(grad_normed, normed, inverse):
    return inverse * (
        grad_normed
        - jnp.mean(grad_normed, axis=-1, keepdims=True)
        - normed * jnp.mean(grad_normed * normed, axis=-1, keepdims=True)
    )


def pad_lanes(values):
    return jnp.pad(values, ((0, 0), (0, 128 - values.shape[1])))


def per_device(
    layer_source_tensor,
    horizon_class,
    field_selector,
    model_predictions,
    loss_sensitivity,
    gain_one,
    shift_one,
    horizon_vectors,
    w_qkv,
    w_out,
    gain_two,
    shift_two,
    w_up,
    b_up,
    w_down,
    b_down,
    w_gate,
    w_bias,
):
    frames, lat_rows, lon_cols, width = layer_source_tensor.shape
    local = lat_rows * lon_cols
    rows = frames * local
    pixels = loss_sensitivity.shape[-1]
    sizes = (lax.axis_size("grp"), lax.axis_size("lat"), lax.axis_size("lon"))
    small = sizes == (4, 2, 4) and frames == 1

    source = layer_source_tensor.reshape(frames, local, width)
    place = lax.axis_index("lon")
    edge = (place == 0) | (place == lax.axis_size("lon") - 1)
    send = functools.partial(lax.ppermute, axis_name="lon")
    if small:
        right = send(source, perm=[(0, 1), (1, 2), (2, 3)])
        left = send(source, perm=[(3, 2), (2, 1), (1, 0)])
    else:
        shards = [lax.all_gather(source, "lon", axis=1, tiled=True)]

    forecasts = jnp.transpose(model_predictions.reshape(rows, 2, pixels), (1, 0, 2))
    sensitivity = loss_sensitivity.reshape(rows, pixels)

    onehot = (horizon_class[:, None] == jnp.arange(LEADS, dtype=jnp.int32)[None, :]).astype(F32)
    lead_rows = jnp.dot(onehot, horizon_vectors, precision=HIGH)

    def mixed_of(values):
        normed, _ = layer_norm(values.astype(F32))
        return (normed * gain_one + shift_one + lead_rows[:, None, :]).astype(BF)

    wq = w_qkv[:, :width]
    wkv = w_qkv[:, width:]

    def keys_of(values):
        return dot(values.reshape(-1, width), wkv).astype(BF).reshape(frames, -1, 2 * width)

    mixed_own = mixed_of(source)
    queries = dot(mixed_own.reshape(rows, width), wq).astype(BF).reshape(frames, local, width)
    if small:
        key_value = [keys_of(mixed_own)]
        right, left, forecasts, queries, key_value[0] = hold(
            right, left, forecasts, queries, key_value[0]
        )
        near = jnp.where(place == 0, left, right)
        right_two = send(right, perm=[(1, 2), (2, 3)])
        left_two = send(left, perm=[(2, 1), (1, 0)])
        sums = pixel_sums(forecasts, sensitivity)
        mixed = [mixed_own, mixed_of(near)]
        key_value.append(keys_of(mixed[1]))
        right_two, left_two, key_value[1], *sums = hold(right_two, left_two, key_value[1], *sums)
        two = right_two + left_two
        three = send(two, perm=[(2, 3), (1, 0)])
        middle = jnp.where(edge, two, left)
        mixed.append(mixed_of(middle))
        key_value.append(keys_of(mixed[2]))
        state = attend(queries, key_value, None, False)
        three, *state = hold(three, *state)
        far = jnp.where(edge, three, two)
        mixed.append(mixed_of(far))
        key_value.append(keys_of(mixed[3]))
        attended, logs = attend(queries, key_value[3:], state, True)
        shards = [source, near, middle, far]
    else:
        sums = pixel_sums(forecasts, sensitivity)
        mixed = [mixed_of(shards[0])]
        key_value = [keys_of(mixed[0])]
        attended, logs = attend(queries, key_value, None, True)
    inputs = source.reshape(rows, width)
    attended_low = attended.reshape(rows, width)
    both = w_gate.T
    head_rows = jnp.concatenate(
        [
            jnp.pad(m, ((0, 128 - RESULT_FIELDS), (0, 0)))
            for m in (both[:RESULT_FIELDS], both[RESULT_FIELDS:], w_bias.T)
        ]
    )
    mask = pad_lanes(field_selector.astype(F32))[:, None]
    (
        hidden_low,
        activation_low,
        up_low,
        down_low,
        final_low,
        heads_low,
        attn_low,
        grad_residual,
        grad_attended,
        *blending,
        early_vectors,
        grad_bup,
    ) = between(
        inputs,
        attended_low,
        w_out,
        w_up,
        w_down,
        head_rows,
        gain_two,
        shift_two,
        b_up,
        b_down,
        mask,
        sums,
        local,
    )
    grad_attended = grad_attended.reshape(frames, local, width)
    fields = 3 * RESULT_FIELDS
    heads_low = jnp.concatenate(
        [heads_low[:, g * 128 : g * 128 + RESULT_FIELDS] for g in range(3)], axis=1
    )
    inputs = inputs.astype(F32)
    normed_one, inverse_one = layer_norm(inputs)

    def back(shard, place, before, own=None):
        return attend_back(
            queries, grad_attended, attended, logs, shard, w_qkv, place, before, own
        )

    def late_vectors(sums):
        gain_column = sum(jnp.sum(s[:, 0], axis=0) for s in sums)
        column = sum(s[:, 1] for s in sums)
        lead = jnp.dot(onehot.T, column, precision=HIGH)
        zeros = jnp.zeros((6, width), F32)
        return jnp.concatenate((gain_column[None], jnp.sum(column, axis=0)[None], lead, zeros))

    if small:
        bup_rows = jnp.swapaxes(grad_bup.reshape(8, 4, -1), 0, 1).reshape(4, width)
        early_vectors = jnp.concatenate(
            (early_vectors, bup_rows, jnp.zeros((1, width), F32))
        )
        core = (lax.axis_index("grp") % 2).astype(jnp.int32)[None]
        y_axis, x_axis = ("grp", 2), ("lat", 1)
        used = fields + early_vectors.shape[0]
        hidden = w_up.shape[1]
        mine, sent = down_grads(core, activation_low, down_low, 2 * hidden + width + 256)
        mine, sent = early_grads(
            core,
            hidden_low,
            attended_low,
            final_low,
            up_low,
            attn_low,
            jnp.pad(heads_low, ((0, 0), (0, 256 - fields))),
            early_vectors,
            mine,
            sent,
        )
        grad_attended, sent = hold(grad_attended, sent)
        got = swap(sent, "grp", 1)

        grad_query, dk3, dv3, far, sums3 = back(key_value[3], shards[3], None)
        terms = [t.reshape(2, 4, 2, 24, -1) for t in (mine, got)]
        middle_column = terms[0].shape[-1] // 2
        first = Halves([t[..., :middle_column] for t in terms], 0, *x_axis)
        second = Halves([t[..., middle_column:] for t in terms], 2, *y_axis)
        grad_query, far, first.sent, second.sent = hold(grad_query, far, first.sent, second.sent)
        got = send(far, perm=[(0, 1), (3, 2)])
        first.start()
        second.start()

        grad_query, dk2, dv2, middle, sums2 = back(key_value[2], shards[2], grad_query)
        value = jnp.where(edge, middle, add(got, far))
        grad_query, value = hold(grad_query, value)
        right = send(value, perm=[(0, 1), (1, 2)])
        left = send(value, perm=[(3, 2), (2, 1)])

        grad_query, dk1, dv1, near, sums1 = back(key_value[1], shards[1], grad_query)
        forth = jnp.where(place == 0, near, add(right, middle))
        back_value = add(left, near)
        first = Halves(first.finish(), 1, *y_axis)
        second = Halves(second.finish(), 0, *x_axis)
        grad_query, forth, back_value, first.sent, second.sent = hold(
            grad_query, forth, back_value, first.sent, second.sent
        )
        right = send(forth, perm=[(0, 1), (1, 2), (2, 3)])
        left = send(back_value, perm=[(3, 2), (2, 1), (1, 0)])
        first.start()
        second.start()

        query_low, dk0, dv0, own, sums0, query_term, query_sums = back(
            key_value[0], shards[0], grad_query, source
        )
        vectors = late_vectors([sums0, sums1, sums2, sums3, query_sums])
        parts = [
            jnp.concatenate(pair, axis=-1)
            for pair in zip(quarters(first.finish()), quarters(second.finish()))
        ]
        query_low, *parts = hold(query_low, *parts)
        early = trade_quarters(parts)
        late_mine, late_sent = late_grads(
            core,
            [m.reshape(rows, width) for m in mixed],
            query_low.reshape(width, rows),
            [d.reshape(rows, width) for d in (dk0, dk1, dk2, dk3)],
            [d.reshape(rows, width) for d in (dv0, dv1, dv2, dv3)],
            vectors,
        )
        got = swap(late_sent, "grp", 1)
        grad_mixed = own + query_term + right.astype(F32) + left.astype(F32)
        terms = [t.reshape(2, 4, 2, 24, -1) for t in (late_mine, got)]
        first = Halves([t[:, :2] for t in terms], 2, *y_axis)
        second = Halves([t[:, 2:] for t in terms], 0, *x_axis)
        first.sent, second.sent, *blending = hold(first.sent, second.sent, *blending)
        first.start()
        second.start()
        blended = blend(*blending, forecasts)
        first.got, second.got, blended = hold(first.got, second.got, blended)
        first = Halves(first.finish(), 0, *x_axis)
        second = Halves(second.finish(), 1, *y_axis)
        first.sent, second.sent, *early = hold(first.sent, second.sent, *early)
        first.start()
        second.start()
        early = add(*early)
        other = swap(early, "grp", 2)
        late = [jnp.concatenate(pair) for pair in zip(first.finish(), second.finish())]
        late = trade_quarters(quarters(late))
        early = spread_core(double(early, other, "grp", 2))
        late = add(*late)
        late = spread_core(double(late, swap(late, "grp", 2), "grp", 2))
        late = late.reshape(width // 8, -1).astype(F32)
        down_sum = early[..., :hidden].reshape(2, 2, 24, 4, width)
        down_sum = jnp.swapaxes(down_sum, 2, 3).reshape(-1, width).astype(F32)
        early = early.reshape(width // 8, -1)[:, hidden:].astype(F32)
        qkv_sum = late[:, : 3 * width]
        late = late[:, 3 * width : 3 * width + 2 + LEADS].T
        up_sum = early[:, :hidden]
        out_sum = early[:, hidden : hidden + width]
        misc = early[:, hidden + width : hidden + width + used]
        heads = misc[:, :fields]
        early = misc[:, fields : fields + 3].T
        bup_sum = misc[:, fields + 3 : fields + 7].T.reshape(-1)
    else:
        blended = blend(*blending, forecasts)
        query_low, dk, dv, term, sums, query_term, query_sums = back(
            key_value[0], shards[0], None, source
        )
        grad_mixed = query_term + lax.psum_scatter(
            term, "lon", scatter_dimension=1, tiled=True
        )

        def total_of(values, dim=0):
            share = lax.psum_scatter(values, ("lat", "lon"), scatter_dimension=dim, tiled=True)
            return lax.psum(share, "grp")

        flat = mixed[0].reshape(-1, width)
        qkv_sum = total_of(
            jnp.concatenate(
                (
                    jnp.einsum("frd,fer->de", mixed_own, query_low, preferred_element_type=F32),
                    dot(flat, dk.reshape(-1, width), TN),
                    dot(flat, dv.reshape(-1, width), TN),
                ),
                axis=1,
            )
        )
        up_sum = total_of(dot(hidden_low, up_low, TN))
        out_sum = total_of(dot(attended_low, attn_low, TN))
        down_sum = total_of(dot(activation_low, down_low, TN))
        heads = total_of(dot(final_low, heads_low, TN))
        late = total_of(late_vectors([sums, query_sums])[: 2 + LEADS], 1)
        early = total_of(early_vectors, 1)
        bup_sum = total_of(grad_bup[0])

    grad_input = grad_residual + norm_back(
        grad_mixed.reshape(rows, width) * gain_one, normed_one, inverse_one
    )
    return (
        blended.reshape(frames, lat_rows, lon_cols, pixels),
        grad_input.reshape(frames, lat_rows, lon_cols, width),
        late[0],
        late[1],
        late[2:],
        qkv_sum,
        out_sum,
        early[0],
        early[1],
        up_sum,
        bup_sum,
        down_sum,
        early[2],
        heads[:, : 2 * RESULT_FIELDS],
        heads[:, 2 * RESULT_FIELDS :],
    )


def solution(mesh):
    frame = ("grp", "lat")
    share = ("lat", "lon")
    image = P(frame, None, "lon", None)
    in_specs = (
        image,
        P(frame),
        P(frame, None),
        P(frame, None, "lon", None, None),
        image,
    ) + (P(),) * 13
    vector = P(share)
    matrix = P(share, None)
    out_specs = (
        image,
        image,
        vector,
        vector,
        P(None, share),
        matrix,
        matrix,
        vector,
        vector,
        matrix,
        vector,
        matrix,
        vector,
        matrix,
        matrix,
    )
    return jax.shard_map(
        per_device, mesh=mesh, in_specs=in_specs, out_specs=out_specs, check_vma=False
    )
```

```python
import functools
import math

import jax
import jax.numpy as jnp
from jax import lax
from jax.experimental import pallas as pl
from jax.experimental.pallas import tpu as pltpu
from jax.sharding import PartitionSpec as P

H = 12
DH = 64
RESULT_FIELDS = 69
TILE_AREA = 64
LEADS = 24
EPSILON = 1e-06
HIGH = lax.Precision.HIGHEST
SCALE = 0.125
SCALE_TWO = SCALE * math.log2(math.e)
ROOT = math.sqrt(2.0 / math.pi)
CUBE = 0.044715
NN = (((1,), (0,)), ((), ()))
NT = (((1,), (1,)), ((), ()))
TN = (((0,), (0,)), ((), ()))
BF = jnp.bfloat16
F32 = jnp.float32
PARAMS = pltpu.CompilerParams(vmem_limit_bytes=60 * 1024 * 1024)


def dot(left, right, dims=NN):
    return lax.dot_general(left, right, dims, preferred_element_type=F32)


def attend_kernel(count, chained, final, *refs):
    q_ref = refs[0]
    k_refs = refs[1 : 1 + count]
    v_refs = refs[1 + count : 1 + 2 * count]
    o_ref, l_ref = refs[-2:]
    outs = []
    for h in range(2):
        part = slice(h * DH, h * DH + DH)
        q = q_ref[0, :, part]
        scores = [dot(k[0, :, part], q, NT) for k in k_refs]
        top = functools.reduce(
            jnp.maximum, [jnp.max(s, axis=0, keepdims=True) for s in scores]
        )
        top = top * SCALE_TWO
        total = None
        mixed = None
        for s, v in zip(scores, v_refs):
            raised = jnp.exp2(s * SCALE_TWO - top)
            some = jnp.sum(raised, axis=0, keepdims=True)
            term = dot(v[0, :, part], raised.astype(BF), TN)
            total = some if total is None else total + some
            mixed = term if mixed is None else mixed + term
        mixed = mixed * (1.0 / total)
        log = top + jnp.log2(total)
        if chained:
            before_ref, before_log_ref = refs[1 + 2 * count : 3 + 2 * count]
            before = before_log_ref[0, 0, h : h + 1, :]
            high = jnp.maximum(before, log)
            joint = high + jnp.log2(jnp.exp2(before - high) + jnp.exp2(log - high))
            mixed = mixed * jnp.exp2(log - joint) + before_ref[0, part, :] * jnp.exp2(
                before - joint
            )
            log = joint
        l_ref[0, 0, h : h + 1, :] = log
        if final:
            outs.append(mixed)
        else:
            o_ref[0, part, :] = mixed
    if final:
        o_ref[0] = jnp.concatenate(outs, axis=0).T.astype(BF)


def attend(queries, shards, before, final):
    frames, rows, width = queries.shape
    count = len(shards)
    keys = shards[0].shape[1]
    pairs = width // 128
    turned = pl.BlockSpec((1, 128, rows), lambda f, p: (f, p, 0))
    row = pl.BlockSpec((1, rows, 128), lambda f, p: (f, 0, p))
    log = pl.BlockSpec((1, 1, 2, rows), lambda f, p: (f, p, 0, 0))
    chained = before is not None
    return pl.pallas_call(
        functools.partial(attend_kernel, count, chained, final),
        grid=(frames, pairs),
        in_specs=[row]
        + [pl.BlockSpec((1, keys, 128), lambda f, p: (f, 0, p))] * count
        + [pl.BlockSpec((1, keys, 128), lambda f, p: (f, 0, p + pairs))] * count
        + ([turned, log] if chained else []),
        out_specs=[row if final else turned, log],
        out_shape=[
            jax.ShapeDtypeStruct((frames, rows, width), BF)
            if final
            else jax.ShapeDtypeStruct((frames, width, rows), F32),
            jax.ShapeDtypeStruct((frames, pairs, 2, rows), F32),
        ],
        compiler_params=PARAMS,
        name="attend",
        cost_estimate=pl.CostEstimate(
            flops=2 * frames * rows * count * keys * width,
            transcendentals=0,
            bytes_accessed=frames * rows * width,
        ),
    )(queries, *shards, *shards, *(before if chained else ()))


def column_sums(total, values):
    normed, _ = layer_norm(values.astype(F32))
    return jnp.concatenate(
        (
            jnp.sum(total * normed, axis=0, keepdims=True),
            jnp.sum(total, axis=0, keepdims=True),
        )
    )


def attend_back_kernel(last, *refs):
    q_ref, g_ref, o_ref, l_ref, k_ref, v_ref, wk_ref, wv_ref, x_ref, before_ref = refs[:10]
    rest = refs[10:]
    if last:
        wq_ref, own_ref = rest[:2]
        dq_ref, dk_ref, dv_ref, term_ref, sums_ref, qterm_ref, qsums_ref, qacc_ref = rest[2:]
    else:
        dq_ref, dk_ref, dv_ref, term_ref, sums_ref = rest
    pair = pl.program_id(1)
    key_terms = []
    value_terms = []
    query_terms = []
    for h in range(2):
        part = slice(h * DH, h * DH + DH)
        q = q_ref[0, :, part]
        g = g_ref[0, :, part]
        k = k_ref[0, :, part]
        v = v_ref[0, :, part]
        product = g.astype(F32) * o_ref[0, :, part].astype(F32)
        high, low = split_two(product)
        ones = jnp.ones((8, DH), BF)
        delta = (dot(ones, high, NT) + dot(ones, low, NT))[0:1]
        probs = jnp.exp2(dot(k, q, NT) * SCALE_TWO - l_ref[0, 0, h : h + 1, :])
        grad_probs = dot(v, g, NT)
        grad_scores = (probs * (grad_probs - delta)).astype(BF)
        value_terms.append(dot(probs.astype(BF), g))
        key_terms.append(dot(grad_scores, q))
        grad_query = dot(k, grad_scores, TN) * SCALE + before_ref[0, part, :]
        query_terms.append(grad_query)
    grad_key = (jnp.concatenate(key_terms, axis=1) * SCALE).astype(BF)
    grad_value = jnp.concatenate(value_terms, axis=1).astype(BF)
    grad_query = jnp.concatenate(query_terms, axis=0).astype(dq_ref.dtype)
    lanes = pl.ds(pl.multiple_of(pair * 128, 128), 128)
    dk_ref[0, :, lanes] = grad_key
    dv_ref[0, :, lanes] = grad_value
    dq_ref[0] = grad_query

    if last:
        part = dot(grad_query, wq_ref[...], (((0,), (1,)), ((), ())))

        @pl.when(pair == 0)
        def _():
            qacc_ref[...] = part

        @pl.when(pair > 0)
        def _():
            qacc_ref[...] += part

    @pl.when(pair == pl.num_programs(1) - 1)
    def _():
        total = dot(dk_ref[0], wk_ref[...], NT) + dot(dv_ref[0], wv_ref[...], NT)
        term_ref[0] = total.astype(term_ref.dtype)
        sums_ref[0] = column_sums(total, x_ref[0])
        if last:
            total = qacc_ref[...]
            qterm_ref[0] = total
            qsums_ref[0] = column_sums(total, own_ref[0])


def attend_back(queries, grad_out, out, logs, shard, weights, source, before, own):
    frames, rows, width = queries.shape
    keys = shard.shape[1]
    pairs = width // 128
    last = own is not None
    row = pl.BlockSpec((1, rows, 128), lambda f, p: (f, 0, p))
    key = pl.BlockSpec((1, keys, 128), lambda f, p: (f, 0, p))
    value = pl.BlockSpec((1, keys, 128), lambda f, p: (f, 0, p + pairs))
    turned = pl.BlockSpec((1, 128, rows), lambda f, p: (f, p, 0))
    log = pl.BlockSpec((1, 1, 2, rows), lambda f, p: (f, p, 0, 0))

    def columns(group):
        return pl.BlockSpec((width, width), lambda f, p: (0, group))

    def whole(*shape):
        return pl.BlockSpec((1,) + shape, lambda f, p: (f, 0, 0))

    in_specs = [row, row, row, log, key, value, columns(1), columns(2), whole(keys, width)]
    operands = [queries, grad_out, out, logs, shard, shard, weights, weights, source]
    aliases = {} if last else {len(operands): 0}
    in_specs.append(turned)
    operands.append(before)
    out_specs = [turned, whole(keys, width), whole(keys, width), whole(keys, width), whole(2, width)]
    out_shape = [
        jax.ShapeDtypeStruct((frames, width, rows), BF if last else F32),
        jax.ShapeDtypeStruct((frames, keys, width), BF),
        jax.ShapeDtypeStruct((frames, keys, width), BF),
        jax.ShapeDtypeStruct((frames, keys, width), F32 if last else BF),
        jax.ShapeDtypeStruct((frames, 2, width), F32),
    ]
    scratch = []
    if last:
        in_specs += [pl.BlockSpec((width, 128), lambda f, p: (0, p)), whole(rows, width)]
        operands += [weights, own]
        out_specs += [whole(rows, width), whole(2, width)]
        out_shape += [
            jax.ShapeDtypeStruct((frames, rows, width), F32),
            jax.ShapeDtypeStruct((frames, 2, width), F32),
        ]
        scratch.append(pltpu.VMEM((rows, width), F32))
    return pl.pallas_call(
        functools.partial(attend_back_kernel, last),
        grid=(frames, pairs),
        in_specs=in_specs,
        out_specs=out_specs,
        out_shape=out_shape,
        scratch_shapes=scratch,
        input_output_aliases=aliases,
        compiler_params=PARAMS,
        name="attend_back",
        cost_estimate=pl.CostEstimate(
            flops=4 * frames * rows * keys * width,
            transcendentals=0,
            bytes_accessed=frames * rows * width,
        ),
    )(*operands)


def between_kernel(
    x_ref,
    att_ref,
    wo_ref,
    wu_ref,
    wd_ref,
    head_ref,
    gain_ref,
    shift_ref,
    bu_ref,
    bd_ref,
    mask_ref,
    sens_ref,
    one_ref,
    two_ref,
    hidden_ref,
    act_ref,
    up_ref,
    down_ref,
    final_ref,
    heads_ref,
    attn_ref,
    gres_ref,
    gatt_ref,
    first_ref,
    second_ref,
    added_ref,
    vec_ref,
    bup_ref,
    slope_ref,
):
    residual = x_ref[...].astype(F32) + dot(att_ref[...], wo_ref[...])
    normed, inverse = layer_norm(residual)
    gain = gain_ref[...]
    hidden = (normed * gain + shift_ref[...]).astype(BF)
    hidden_ref[...] = hidden
    wide = 512
    chunks = [slice(j, j + wide) for j in range(0, wu_ref.shape[1], wide)]
    final = residual + bd_ref[...]
    for part in chunks:
        up = dot(hidden, wu_ref[:, part]) + bu_ref[:, part]
        square = up * up
        tanh = jnp.tanh(ROOT * up * (1.0 + CUBE * square))
        half = 0.5 * (1.0 + tanh)
        act = (up * half).astype(BF)
        slope_ref[:, part] = half + 0.5 * up * (1.0 - tanh * tanh) * (
            ROOT + 3.0 * ROOT * CUBE * square
        )
        act_ref[:, part] = act
        final = final + dot(act, wd_ref[part, :])
    final_low = final.astype(BF)
    final_ref[...] = final_low
    logits = dot(final_low, head_ref[...], NT)
    one = logits[:, :128]
    two = logits[:, 128:256]
    offset = logits[:, 256:]
    top = jnp.maximum(one, two)
    one = jnp.exp(one - top)
    two = jnp.exp(two - top)
    total = one + two
    one = one / total
    two = two / total
    mask = mask_ref[0]
    first_ref[...] = mask * one + (1.0 - mask)
    second_ref[...] = mask * two
    added_ref[...] = mask * offset
    grad_one = mask * one_ref[...]
    grad_two = mask * two_ref[...]
    mean = one * grad_one + two * grad_two
    heads = jnp.concatenate(
        (one * (grad_one - mean), two * (grad_two - mean), mask * sens_ref[...]), axis=1
    ).astype(BF)
    heads_ref[...] = heads
    grad_final = dot(heads, head_ref[...])
    down = grad_final.astype(BF)
    down_ref[...] = down
    grad_hidden = None
    ups = []
    for part in chunks:
        grad_up = (dot(down, wd_ref[part, :], NT) * slope_ref[:, part]).astype(BF)
        up_ref[:, part] = grad_up
        ups.append(jnp.sum(grad_up.astype(F32), axis=0, keepdims=True))
        term = dot(grad_up, wu_ref[:, part], NT)
        grad_hidden = term if grad_hidden is None else grad_hidden + term
    grad_normed = grad_hidden * gain
    grad_residual = grad_final + norm_back(grad_normed, normed, inverse)
    gres_ref[...] = grad_residual
    attn = grad_residual.astype(BF)
    attn_ref[...] = attn
    gatt_ref[...] = dot(attn, wo_ref[...], NT).astype(BF)
    vectors = jnp.concatenate(
        (
            jnp.sum(grad_hidden * normed, axis=0, keepdims=True),
            jnp.sum(grad_hidden, axis=0, keepdims=True),
            jnp.sum(down.astype(F32), axis=0, keepdims=True),
        )
    )
    ups = jnp.concatenate(ups, axis=1)

    @pl.when(pl.program_id(0) == 0)
    def _():
        vec_ref[...] = vectors
        bup_ref[...] = ups

    @pl.when(pl.program_id(0) > 0)
    def _():
        vec_ref[...] += vectors
        bup_ref[...] += ups


def between(x, attended, w_out, w_up, w_down, heads, gain, shift, b_up, b_down, mask, sums, local):
    rows, width = x.shape
    hidden = w_up.shape[1]
    block = math.gcd(local, 256)

    def row(columns):
        return pl.BlockSpec((block, columns), lambda i: (i, 0))

    def whole(values):
        return pl.BlockSpec(values.shape, lambda i: (0, 0), pipeline_mode=pl.Buffered(1))

    def shape(columns, kind=BF):
        return jax.ShapeDtypeStruct((rows, columns), kind)

    fixed = [w_out, w_up, w_down, heads, gain[None], shift[None], b_up[None], b_down[None]]
    return pl.pallas_call(
        between_kernel,
        grid=(rows // block,),
        in_specs=[row(width), row(width)]
        + [whole(v) for v in fixed]
        + [pl.BlockSpec((1, 1, 128), lambda i: (i * block // local, 0, 0))]
        + [row(128)] * 3,
        out_specs=[
            row(width),
            row(hidden),
            row(hidden),
            row(width),
            row(width),
            row(384),
            row(width),
            row(width),
            row(width),
            row(128),
            row(128),
            row(128),
            pl.BlockSpec((3, width), lambda i: (0, 0)),
            pl.BlockSpec((1, hidden), lambda i: (0, 0)),
        ],
        out_shape=[
            shape(width),
            shape(hidden),
            shape(hidden),
            shape(width),
            shape(width),
            shape(384),
            shape(width),
            shape(width, F32),
            shape(width),
            shape(128, F32),
            shape(128, F32),
            shape(128, F32),
            jax.ShapeDtypeStruct((3, width), F32),
            jax.ShapeDtypeStruct((1, hidden), F32),
        ],
        scratch_shapes=[pltpu.VMEM((block, hidden), F32)],
        compiler_params=PARAMS,
        name="between",
        cost_estimate=pl.CostEstimate(
            flops=rows * width * hidden, transcendentals=0, bytes_accessed=rows * hidden
        ),
    )(x, attended, *fixed, mask, *sums)


def deal(place, result, mine_ref, sent_ref):
    halves = result.reshape(mine_ref.shape[0], 2, *mine_ref.shape[1:]).astype(BF)
    low = halves[:, 0]
    high = halves[:, 1]
    even = place == 0
    mine_ref[...] = jnp.where(even, low, high)
    sent_ref[...] = jnp.where(even, high, low)


def columns_of(vectors, start):
    count = vectors.shape[0]
    place = lax.broadcasted_iota(jnp.int32, (count, 256), 1)
    which = lax.broadcasted_iota(jnp.int32, (count, 256), 0)
    chosen = (place == which + start).astype(F32).astype(BF)
    high, rest = split_two(vectors)
    return dot(high, chosen, TN) + dot(rest, chosen, TN)


def early_grads_kernel(
    place_ref,
    h_ref,
    a_ref,
    f_ref,
    up_ref,
    attn_ref,
    head_ref,
    vec_ref,
    mine_in_ref,
    sent_in_ref,
    mine_ref,
    sent_ref,
    turn_ref,
):
    step = pl.program_id(0)
    last = pl.num_programs(0) - 1
    place = place_ref[0]
    wide = up_ref.shape[1]

    @pl.when(step == 0)
    def _():
        turn_ref[...] = h_ref[...].T

    @pl.when(step < last - 1)
    def _():
        deal(place, dot(turn_ref[...], up_ref[...]), mine_ref, sent_ref)

    @pl.when(step == last - 1)
    def _():
        turned = a_ref[...].T
        turn_ref[...] = turned
        deal(place, dot(turned, attn_ref[:, :wide]), mine_ref, sent_ref)

    @pl.when(step == last)
    def _():
        out = dot(turn_ref[...], attn_ref[:, wide:])
        heads = dot(f_ref[...].T, head_ref[...]) + columns_of(vec_ref[...], 3 * RESULT_FIELDS)
        deal(place, jnp.concatenate((out, heads), axis=1), mine_ref, sent_ref)


def early_grads(place, hidden, attended, final, up, attn, heads, vectors, mine, sent):
    rows, width = hidden.shape
    wide = 512
    steps = up.shape[1] // wide + 2
    count = width // 96
    skip = mine.shape[2] // wide - steps

    def whole(values):
        return pl.BlockSpec(values.shape, lambda i: (0, 0))

    out = pl.BlockSpec((count, 48, wide), lambda i: (0, 0, i + skip))
    untouched = pl.BlockSpec(memory_space=pl.ANY)
    return pl.pallas_call(
        early_grads_kernel,
        grid=(steps,),
        in_specs=[
            pl.BlockSpec(memory_space=pltpu.SMEM),
            whole(hidden),
            whole(attended),
            whole(final),
            pl.BlockSpec((rows, wide), lambda i: (0, jnp.minimum(i, steps - 3))),
            whole(attn),
            whole(heads),
            whole(vectors),
            untouched,
            untouched,
        ],
        out_specs=[out, out],
        out_shape=[jax.ShapeDtypeStruct(mine.shape, BF)] * 2,
        input_output_aliases={8: 0, 9: 1},
        scratch_shapes=[pltpu.VMEM((width, rows), BF)],
        compiler_params=PARAMS,
        name="early_grads",
        cost_estimate=pl.CostEstimate(
            flops=2 * rows * width * wide * steps,
            transcendentals=0,
            bytes_accessed=2 * rows * wide * steps + 2 * width * wide * steps,
        ),
    )(place, hidden, attended, final, up, attn, heads, vectors, mine, sent)


def down_grads_kernel(place_ref, act_ref, down_ref, mine_ref, sent_ref):
    result = dot(act_ref[...], down_ref[...], TN).astype(BF)
    block = result.shape[0] // 2
    piece = block // 8
    halves = []
    for c in range(2):
        groups = [
            jnp.concatenate(
                [
                    result[c * block + y * 4 * piece + g * piece :][:piece]
                    for y in range(2)
                ],
                axis=0,
            )
            for g in range(4)
        ]
        halves.append(jnp.concatenate(groups, axis=1)[None])
    even = place_ref[0] == 0
    mine_ref[...] = jnp.where(even, halves[0], halves[1])
    sent_ref[...] = jnp.where(even, halves[1], halves[0])


def down_grads(place, activation, down, columns):
    rows, width = down.shape
    block = activation.shape[1] // 8
    piece = block // 16
    out = pl.BlockSpec((1, 2 * piece, 4 * width), lambda i: (i, 0, 0))
    return pl.pallas_call(
        down_grads_kernel,
        grid=(8,),
        in_specs=[
            pl.BlockSpec(memory_space=pltpu.SMEM),
            pl.BlockSpec((rows, block), lambda i: (0, i)),
            pl.BlockSpec((rows, width), lambda i: (0, 0)),
        ],
        out_specs=[out, out],
        out_shape=[jax.ShapeDtypeStruct((8, 2 * piece, columns), BF)] * 2,
        compiler_params=PARAMS,
        name="down_grads",
        cost_estimate=pl.CostEstimate(
            flops=2 * rows * width * block, transcendentals=0, bytes_accessed=width * block
        ),
    )(place, activation, down)


def late_grads_kernel(count, place_ref, *refs):
    mixed_refs = refs[:count]
    query_ref = refs[count]
    key_refs = refs[count + 1 : 2 * count + 1]
    value_refs = refs[2 * count + 1 : 3 * count + 1]
    vec_ref, mine_ref, sent_ref, turn_ref = refs[3 * count + 1 :]
    step = pl.program_id(0)
    third = (pl.num_programs(0) - 1) // 3
    place = place_ref[0]

    @pl.when(step == 0)
    def _():
        for s in range(count):
            turn_ref[s] = mixed_refs[s][...].T

    @pl.when(step < third)
    def _():
        deal(place, dot(turn_ref[0], query_ref[...], NT), mine_ref, sent_ref)

    def joint(parts):
        return sum(dot(turn_ref[s], parts[s][...]) for s in range(count))

    @pl.when((step >= third) & (step < 2 * third))
    def _():
        deal(place, joint(key_refs), mine_ref, sent_ref)

    @pl.when((step >= 2 * third) & (step < 3 * third))
    def _():
        deal(place, joint(value_refs), mine_ref, sent_ref)

    @pl.when(step == 3 * third)
    def _():
        deal(place, columns_of(vec_ref[...], 0), mine_ref, sent_ref)


def late_grads(place, mixed, query, keys, values, vectors):
    rows, width = mixed[0].shape
    count = len(mixed)
    wide = 256
    third = width // wide
    groups = width // 96

    def clipped(offset):
        return lambda i: (0, jnp.clip(i - offset, 0, third - 1))

    whole = pl.BlockSpec((rows, width), lambda i: (0, 0))
    out = pl.BlockSpec((groups, 48, wide), lambda i: (0, 0, i))
    return pl.pallas_call(
        functools.partial(late_grads_kernel, count),
        grid=(3 * third + 1,),
        in_specs=[pl.BlockSpec(memory_space=pltpu.SMEM)]
        + [whole] * count
        + [pl.BlockSpec((wide, rows), lambda i: (jnp.clip(i, 0, third - 1), 0))]
        + [pl.BlockSpec((rows, wide), clipped(third))] * count
        + [pl.BlockSpec((rows, wide), clipped(2 * third))] * count
        + [pl.BlockSpec(vectors.shape, lambda i: (0, 0))],
        out_specs=[out, out],
        out_shape=[jax.ShapeDtypeStruct((groups, 48, wide * (3 * third + 1)), BF)] * 2,
        scratch_shapes=[pltpu.VMEM((count, width, rows), BF)],
        compiler_params=PARAMS,
        name="late_grads",
        cost_estimate=pl.CostEstimate(
            flops=2 * rows * width * width * (2 * count + 1),
            transcendentals=0,
            bytes_accessed=2 * rows * width * 4 * count + 12 * width * width,
        ),
    )(place, *mixed, query, *keys, *values, vectors)


def early_unpack_kernel(place_ref, *refs):
    ins = refs[:4]
    down_ref, up_ref, out_ref, misc_ref = refs[4:]
    width = down_ref.shape[1]
    hidden = up_ref.shape[1]
    for source, (c, y) in zip(ins, ((0, 0), (0, 1), (1, 0), (1, 1))):
        slot = jnp.bitwise_xor(place_ref[0], c) * 2 + jnp.bitwise_xor(place_ref[1], y)
        one = source[0].astype(F32)
        two = source[1].astype(F32)
        rows = one.shape[0]
        half = one.shape[1]
        for g in range(4):
            span = pl.ds(pl.multiple_of(slot * 4 * rows + g * rows, 8), rows)
            down_ref[span, :] = one[:, g * width : (g + 1) * width]
        span = pl.ds(pl.multiple_of(slot * rows, 8), rows)
        cut = half - 4 * width
        up_ref[span, :cut] = one[:, 4 * width :]
        up_ref[span, cut:] = two[:, : hidden - cut]
        out_ref[span, :] = two[:, hidden - cut : hidden - cut + width]
        misc_ref[span, :] = two[:, hidden - cut + width :]


def early_unpack(place, pieces, width, hidden):
    rows = pieces[0].shape[1]
    vmem = pl.BlockSpec(memory_space=pltpu.VMEM)
    return pl.pallas_call(
        early_unpack_kernel,
        in_specs=[pl.BlockSpec(memory_space=pltpu.SMEM)] + [vmem] * 4,
        out_specs=[vmem] * 4,
        out_shape=[
            jax.ShapeDtypeStruct((16 * rows, width), F32),
            jax.ShapeDtypeStruct((4 * rows, hidden), F32),
            jax.ShapeDtypeStruct((4 * rows, width), F32),
            jax.ShapeDtypeStruct((4 * rows, 256), F32),
        ],
        compiler_params=PARAMS,
        name="early_unpack",
        cost_estimate=pl.CostEstimate(flops=1 << 20, transcendentals=0, bytes_accessed=1 << 20),
    )(place, *pieces)


def late_unpack_kernel(place_ref, *refs):
    ins = refs[:4]
    main_ref, misc_ref = refs[4:]
    for source, (c, y) in zip(ins, ((0, 0), (0, 1), (1, 0), (1, 1))):
        slot = jnp.bitwise_xor(place_ref[0], c) * 2 + jnp.bitwise_xor(place_ref[1], y)
        value = source[...].astype(F32)
        rows = value.shape[0]
        span = pl.ds(pl.multiple_of(slot * rows, 8), rows)
        main_ref[span, :] = value[:, : main_ref.shape[1]]
        misc_ref[span, :] = value[:, main_ref.shape[1] :]


def late_unpack(place, pieces):
    rows, columns = pieces[0].shape
    vmem = pl.BlockSpec(memory_space=pltpu.VMEM)
    return pl.pallas_call(
        late_unpack_kernel,
        in_specs=[pl.BlockSpec(memory_space=pltpu.SMEM)] + [vmem] * 4,
        out_specs=[vmem] * 2,
        out_shape=[
            jax.ShapeDtypeStruct((4 * rows, columns - 256), F32),
            jax.ShapeDtypeStruct((4 * rows, 256), F32),
        ],
        compiler_params=PARAMS,
        name="late_unpack",
        cost_estimate=pl.CostEstimate(flops=1 << 20, transcendentals=0, bytes_accessed=1 << 20),
    )(place, *pieces)


def spread(rows, columns):
    pixel = lax.broadcasted_iota(jnp.int32, (rows, columns), 0)
    field = lax.broadcasted_iota(jnp.int32, (rows, columns), 1)
    return ((pixel // TILE_AREA) == field).astype(F32).astype(BF)


def split_two(values):
    high = values.astype(BF)
    return high, (values - high.astype(F32)).astype(BF)


def pixel_sums_kernel(f_ref, s_ref, sum_ref, first_ref, second_ref, field_ref):
    @pl.when(pl.program_id(0) == 0)
    def _():
        field_ref[...] = spread(*field_ref.shape)

    fields = field_ref[...]
    sens = s_ref[...]
    sum_ref[...] = dot(sens, fields)
    for e, out in ((0, first_ref), (1, second_ref)):
        out[...] = dot((sens.astype(F32) * f_ref[e].astype(F32)).astype(BF), fields)


def pixel_sums(forecasts, sensitivity):
    rows, pixels = sensitivity.shape
    block = math.gcd(rows, 128)
    out = pl.BlockSpec((block, 128), lambda i: (i, 0))
    return pl.pallas_call(
        pixel_sums_kernel,
        grid=(rows // block,),
        in_specs=[
            pl.BlockSpec((2, block, pixels), lambda i: (0, i, 0)),
            pl.BlockSpec((block, pixels), lambda i: (i, 0)),
        ],
        out_specs=[out] * 3,
        out_shape=[jax.ShapeDtypeStruct((rows, 128), F32)] * 3,
        scratch_shapes=[pltpu.VMEM((pixels, 128), BF)],
        compiler_params=PARAMS,
        name="pixel_sums",
        cost_estimate=pl.CostEstimate(
            flops=rows * pixels * 128, transcendentals=0, bytes_accessed=rows * pixels
        ),
    )(forecasts, sensitivity)


def blend_kernel(a_ref, b_ref, c_ref, f_ref, out_ref, field_ref):
    @pl.when(pl.program_id(0) == 0)
    def _():
        columns = field_ref.shape[1]
        field = lax.broadcasted_iota(jnp.int32, (256, columns), 0)
        pixel = lax.broadcasted_iota(jnp.int32, (256, columns), 1)
        field_ref[...] = ((pixel // TILE_AREA) == (field % 128)).astype(F32).astype(BF)

    fields = field_ref[...]

    def wide(ref):
        return dot(jnp.concatenate(split_two(ref[...]), axis=1), fields)

    total = wide(a_ref) * f_ref[0].astype(F32) + wide(b_ref) * f_ref[1].astype(F32)
    out_ref[...] = (total + wide(c_ref)).astype(BF)


def blend(first, second, added, forecasts):
    _, rows, pixels = forecasts.shape
    block = math.gcd(rows, 128)
    thin = pl.BlockSpec((block, 128), lambda i: (i, 0))
    return pl.pallas_call(
        blend_kernel,
        grid=(rows // block,),
        in_specs=[thin] * 3 + [pl.BlockSpec((2, block, pixels), lambda i: (0, i, 0))],
        out_specs=pl.BlockSpec((block, pixels), lambda i: (i, 0)),
        out_shape=jax.ShapeDtypeStruct((rows, pixels), BF),
        scratch_shapes=[pltpu.VMEM((256, pixels), BF)],
        compiler_params=PARAMS,
        name="blend",
        cost_estimate=pl.CostEstimate(
            flops=rows * pixels * 128, transcendentals=0, bytes_accessed=rows * pixels
        ),
    )(first, second, added, forecasts)


def swap(values, axis, bit):
    count = lax.axis_size(axis)
    return lax.ppermute(values, axis, [(i, i ^ bit) for i in range(count)])


def pick(values, axis, index):
    return lax.dynamic_index_in_dim(values, index, axis, keepdims=False)


def add(*terms):
    return sum(t.astype(F32) for t in terms).astype(BF)


def hold(*values):
    return lax.optimization_barrier(values)


class Halves:
    def __init__(self, terms, dim, axis, bit):
        place = (lax.axis_index(axis) // bit) % 2
        self.mine = [pick(t, dim, place) for t in terms]
        self.sent = add(*[pick(t, dim, 1 - place) for t in terms])
        self.axis, self.bit = axis, bit

    def start(self):
        self.got = swap(self.sent, self.axis, self.bit)

    def finish(self):
        return self.mine + [self.got]


def quarters(terms):
    place = lax.axis_index("lon")
    return [add(*[pick(t, 0, place ^ k) for t in terms]) for k in range(4)]


def trade_quarters(parts):
    return [parts[0]] + [swap(parts[k], "lon", k) for k in (1, 2, 3)]


def double(values, other, axis, bit):
    low = (lax.axis_index(axis) // bit) % 2 == 0
    return jnp.stack((jnp.where(low, values, other), jnp.where(low, other, values)))


def spread_core(values):
    return double(values, swap(values, "grp", 1), "grp", 1)


def layer_norm(values):
    centred = values - jnp.mean(values, axis=-1, keepdims=True)
    inverse = lax.rsqrt(jnp.mean(centred * centred, axis=-1, keepdims=True) + EPSILON)
    return centred * inverse, inverse


def norm_back(grad_normed, normed, inverse):
    return inverse * (
        grad_normed
        - jnp.mean(grad_normed, axis=-1, keepdims=True)
        - normed * jnp.mean(grad_normed * normed, axis=-1, keepdims=True)
    )


def pad_lanes(values):
    return jnp.pad(values, ((0, 0), (0, 128 - values.shape[1])))


def per_device(
    layer_source_tensor,
    horizon_class,
    field_selector,
    model_predictions,
    loss_sensitivity,
    gain_one,
    shift_one,
    horizon_vectors,
    w_qkv,
    w_out,
    gain_two,
    shift_two,
    w_up,
    b_up,
    w_down,
    b_down,
    w_gate,
    w_bias,
):
    frames, lat_rows, lon_cols, width = layer_source_tensor.shape
    local = lat_rows * lon_cols
    rows = frames * local
    pixels = loss_sensitivity.shape[-1]
    sizes = (lax.axis_size("grp"), lax.axis_size("lat"), lax.axis_size("lon"))
    small = sizes == (4, 2, 4) and frames == 1

    source = layer_source_tensor.reshape(frames, local, width)
    place = lax.axis_index("lon")
    edge = (place == 0) | (place == lax.axis_size("lon") - 1)
    send = functools.partial(lax.ppermute, axis_name="lon")
    if small:
        right = send(source, perm=[(0, 1), (1, 2), (2, 3)])
        left = send(source, perm=[(3, 2), (2, 1), (1, 0)])
    else:
        shards = [lax.all_gather(source, "lon", axis=1, tiled=True)]

    forecasts = jnp.transpose(model_predictions.reshape(rows, 2, pixels), (1, 0, 2))
    sensitivity = loss_sensitivity.reshape(rows, pixels)

    onehot = (horizon_class[:, None] == jnp.arange(LEADS, dtype=jnp.int32)[None, :]).astype(F32)
    lead_rows = jnp.dot(onehot, horizon_vectors, precision=HIGH)

    def mixed_of(values):
        normed, _ = layer_norm(values.astype(F32))
        return (normed * gain_one + shift_one + lead_rows[:, None, :]).astype(BF)

    wq = w_qkv[:, :width]
    wkv = w_qkv[:, width:]

    def keys_of(values):
        return dot(values.reshape(-1, width), wkv).astype(BF).reshape(frames, -1, 2 * width)

    mixed_own = mixed_of(source)
    queries = dot(mixed_own.reshape(rows, width), wq).astype(BF).reshape(frames, local, width)
    if small:
        key_value = [keys_of(mixed_own)]
        right, left, forecasts, queries, key_value[0] = hold(
            right, left, forecasts, queries, key_value[0]
        )
        near = jnp.where(place == 0, left, right)
        right_two = send(right, perm=[(1, 2), (2, 3)])
        left_two = send(left, perm=[(2, 1), (1, 0)])
        sums = pixel_sums(forecasts, sensitivity)
        mixed = [mixed_own, mixed_of(near)]
        key_value.append(keys_of(mixed[1]))
        right_two, left_two, key_value[1], *sums = hold(right_two, left_two, key_value[1], *sums)
        two = right_two + left_two
        three = send(two, perm=[(2, 3), (1, 0)])
        middle = jnp.where(edge, two, left)
        mixed.append(mixed_of(middle))
        key_value.append(keys_of(mixed[2]))
        state = attend(queries, key_value, None, False)
        three, *state = hold(three, *state)
        far = jnp.where(edge, three, two)
        mixed.append(mixed_of(far))
        key_value.append(keys_of(mixed[3]))
        attended, logs = attend(queries, key_value[3:], state, True)
        shards = [source, near, middle, far]
    else:
        sums = pixel_sums(forecasts, sensitivity)
        mixed = [mixed_of(shards[0])]
        key_value = [keys_of(mixed[0])]
        attended, logs = attend(queries, key_value, None, True)
    inputs = source.reshape(rows, width)
    attended_low = attended.reshape(rows, width)
    both = w_gate.T
    head_rows = jnp.concatenate(
        [
            jnp.pad(m, ((0, 128 - RESULT_FIELDS), (0, 0)))
            for m in (both[:RESULT_FIELDS], both[RESULT_FIELDS:], w_bias.T)
        ]
    )
    mask = pad_lanes(field_selector.astype(F32))[:, None]
    (
        hidden_low,
        activation_low,
        up_low,
        down_low,
        final_low,
        heads_low,
        attn_low,
        grad_residual,
        grad_attended,
        *blending,
        early_vectors,
        grad_bup,
    ) = between(
        inputs,
        attended_low,
        w_out,
        w_up,
        w_down,
        head_rows,
        gain_two,
        shift_two,
        b_up,
        b_down,
        mask,
        sums,
        local,
    )
    grad_attended = grad_attended.reshape(frames, local, width)
    fields = 3 * RESULT_FIELDS
    heads_low = jnp.concatenate(
        [heads_low[:, g * 128 : g * 128 + RESULT_FIELDS] for g in range(3)], axis=1
    )
    inputs = inputs.astype(F32)
    normed_one, inverse_one = layer_norm(inputs)

    def input_gradient(grad_mixed):
        return grad_residual + norm_back(
            grad_mixed.reshape(rows, width) * gain_one, normed_one, inverse_one
        )

    def back(shard, place, before, own=None):
        return attend_back(
            queries, grad_attended, attended, logs, shard, w_qkv, place, before, own
        )

    nothing = jnp.zeros((frames, width, local), F32)

    def late_vectors(sums):
        gain_column = sum(jnp.sum(s[:, 0], axis=0) for s in sums)
        column = sum(s[:, 1] for s in sums)
        lead = jnp.dot(onehot.T, column, precision=HIGH)
        zeros = jnp.zeros((6, width), F32)
        return jnp.concatenate((gain_column[None], jnp.sum(column, axis=0)[None], lead, zeros))

    if small:
        bup_rows = jnp.swapaxes(grad_bup.reshape(8, 4, -1), 0, 1).reshape(4, width)
        early_vectors = jnp.concatenate(
            (early_vectors, bup_rows, jnp.zeros((1, width), F32))
        )
        core = (lax.axis_index("grp") % 2).astype(jnp.int32)[None]
        y_axis, x_axis = ("grp", 2), ("lat", 1)
        used = fields + early_vectors.shape[0]
        hidden = w_up.shape[1]
        mine, sent = down_grads(core, activation_low, down_low, 2 * hidden + width + 256)
        mine, sent = early_grads(
            core,
            hidden_low,
            attended_low,
            final_low,
            up_low,
            attn_low,
            jnp.pad(heads_low, ((0, 0), (0, 256 - fields))),
            early_vectors,
            mine,
            sent,
        )
        grad_attended, sent = hold(grad_attended, sent)
        got = swap(sent, "grp", 1)

        grad_query, dk3, dv3, far, sums3 = back(key_value[3], shards[3], nothing)
        terms = [t.reshape(2, 4, 2, 24, -1) for t in (mine, got)]
        middle_column = terms[0].shape[-1] // 2
        first = Halves([t[..., :middle_column] for t in terms], 0, *x_axis)
        second = Halves([t[..., middle_column:] for t in terms], 2, *y_axis)
        grad_query, far, first.sent, second.sent = hold(grad_query, far, first.sent, second.sent)
        got = send(far, perm=[(0, 1), (3, 2)])
        first.start()
        second.start()

        grad_query, dk2, dv2, middle, sums2 = back(key_value[2], shards[2], grad_query)
        value = jnp.where(edge, middle, add(got, far))
        grad_query, value = hold(grad_query, value)
        right = send(value, perm=[(0, 1), (1, 2)])
        left = send(value, perm=[(3, 2), (2, 1)])

        grad_query, dk1, dv1, near, sums1 = back(key_value[1], shards[1], grad_query)
        forth = jnp.where(place == 0, near, add(right, middle))
        back_value = add(left, near)
        first = Halves(first.finish(), 1, *y_axis)
        second = Halves(second.finish(), 0, *x_axis)
        grad_query, forth, back_value, first.sent, second.sent = hold(
            grad_query, forth, back_value, first.sent, second.sent
        )
        right = send(forth, perm=[(0, 1), (1, 2), (2, 3)])
        left = send(back_value, perm=[(3, 2), (2, 1), (1, 0)])
        first.start()
        second.start()

        *outcome, right, left, first.got, second.got = hold(
            *back(key_value[0], shards[0], grad_query, source),
            right,
            left,
            first.got,
            second.got,
        )
        query_low, dk0, dv0, own, sums0, query_term, query_sums = outcome
        parts = [
            jnp.stack(pair) for pair in zip(quarters(first.finish()), quarters(second.finish()))
        ]
        query_low, *parts = hold(query_low, *parts)
        early = trade_quarters(parts)
        vectors = late_vectors([sums0, sums1, sums2, sums3, query_sums])
        late_mine, late_sent = late_grads(
            core,
            [m.reshape(rows, width) for m in mixed],
            query_low.reshape(width, rows),
            [d.reshape(rows, width) for d in (dk0, dk1, dk2, dk3)],
            [d.reshape(rows, width) for d in (dv0, dv1, dv2, dv3)],
            vectors,
        )
        late_mine, late_sent, own = hold(late_mine, late_sent, own)
        got = swap(late_sent, "grp", 1)
        grad_input = input_gradient(own + query_term + right.astype(F32) + left.astype(F32))
        got, grad_input, early[1] = hold(got, grad_input, early[1])
        terms = [t.reshape(2, 4, 2, 24, -1) for t in (late_mine, got)]
        first = Halves([t[:, :2] for t in terms], 2, *y_axis)
        second = Halves([t[:, 2:] for t in terms], 0, *x_axis)
        first.sent, second.sent, *blending = hold(first.sent, second.sent, *blending)
        first.start()
        second.start()
        blended = blend(*blending, forecasts)
        first.got, second.got, blended = hold(first.got, second.got, blended)
        first = Halves(first.finish(), 0, *x_axis)
        second = Halves(second.finish(), 1, *y_axis)
        first.sent, second.sent, *early = hold(first.sent, second.sent, *early)
        first.start()
        second.start()
        early = add(*early)
        first.got, second.got, early = hold(first.got, second.got, early)
        late = [jnp.concatenate(pair) for pair in zip(first.finish(), second.finish())]
        late, *early = hold(*quarters(late)[:1], early, *quarters(late)[1:])
        early, sent = early[0], early[1:]
        late = [late] + [swap(sent[k - 1], "lon", k) for k in (1, 2, 3)]
        early_y = swap(early, "grp", 2)
        early_c = swap(early, "grp", 1)
        early_y, early_c, early, *late = hold(early_y, early_c, early, *late)
        early_yc = swap(early_y, "grp", 1)
        late = add(*late)
        late_y = swap(late, "grp", 2)
        late_c = swap(late, "grp", 1)
        late_y, late_c, late, early_yc = hold(late_y, late_c, late, early_yc)
        place_two = jnp.stack((lax.axis_index("grp") % 2, lax.axis_index("grp") // 2))
        place_two = place_two.astype(jnp.int32)
        down_sum, up_sum, out_sum, misc = early_unpack(
            place_two, [early, early_y, early_c, early_yc], width, hidden
        )
        late_yc = swap(late_y, "grp", 1)
        late_yc, misc = hold(late_yc, misc)
        qkv_sum, late = late_unpack(place_two, [late, late_y, late_c, late_yc])
        late = late[:, : 2 + LEADS].T
        misc = misc[:, :used]
        heads = misc[:, :fields]
        early = misc[:, fields : fields + 3].T
        bup_sum = misc[:, fields + 3 : fields + 7].T.reshape(-1)
    else:
        blended = blend(*blending, forecasts)
        query_low, dk, dv, term, sums, query_term, query_sums = back(
            key_value[0], shards[0], nothing, source
        )
        grad_input = input_gradient(
            query_term + lax.psum_scatter(term, "lon", scatter_dimension=1, tiled=True)
        )

        def total_of(values, dim=0):
            share = lax.psum_scatter(values, ("lat", "lon"), scatter_dimension=dim, tiled=True)
            return lax.psum(share, "grp")

        flat = mixed[0].reshape(-1, width)
        qkv_sum = total_of(
            jnp.concatenate(
                (
                    jnp.einsum("frd,fer->de", mixed_own, query_low, preferred_element_type=F32),
                    dot(flat, dk.reshape(-1, width), TN),
                    dot(flat, dv.reshape(-1, width), TN),
                ),
                axis=1,
            )
        )
        up_sum = total_of(dot(hidden_low, up_low, TN))
        out_sum = total_of(dot(attended_low, attn_low, TN))
        down_sum = total_of(dot(activation_low, down_low, TN))
        heads = total_of(dot(final_low, heads_low, TN))
        late = total_of(late_vectors([sums, query_sums])[: 2 + LEADS], 1)
        early = total_of(early_vectors, 1)
        bup_sum = total_of(grad_bup[0])

    return (
        blended.reshape(frames, lat_rows, lon_cols, pixels),
        grad_input.reshape(frames, lat_rows, lon_cols, width),
        late[0],
        late[1],
        late[2:],
        qkv_sum,
        out_sum,
        early[0],
        early[1],
        up_sum,
        bup_sum,
        down_sum,
        early[2],
        heads[:, : 2 * RESULT_FIELDS],
        heads[:, 2 * RESULT_FIELDS :],
    )


def solution(mesh):
    frame = ("grp", "lat")
    share = ("lat", "lon")
    image = P(frame, None, "lon", None)
    in_specs = (
        image,
        P(frame),
        P(frame, None),
        P(frame, None, "lon", None, None),
        image,
    ) + (P(),) * 13
    vector = P(share)
    matrix = P(share, None)
    out_specs = (
        image,
        image,
        vector,
        vector,
        P(None, share),
        matrix,
        matrix,
        vector,
        vector,
        matrix,
        vector,
        matrix,
        vector,
        matrix,
        matrix,
    )
    return jax.shard_map(
        per_device, mesh=mesh, in_specs=in_specs, out_specs=out_specs, check_vma=False
    )
```

```python
import functools
import math

import jax
import jax.numpy as jnp
from jax import lax
from jax.experimental import pallas as pl
from jax.experimental.pallas import tpu as pltpu
from jax.sharding import PartitionSpec as P

H = 12
DH = 64
RESULT_FIELDS = 69
TILE_AREA = 64
LEADS = 24
EPSILON = 1e-06
HIGH = lax.Precision.HIGHEST
SCALE = 0.125
SCALE_TWO = SCALE * math.log2(math.e)
ROOT = math.sqrt(2.0 / math.pi)
CUBE = 0.044715
NN = (((1,), (0,)), ((), ()))
NT = (((1,), (1,)), ((), ()))
TN = (((0,), (0,)), ((), ()))
BF = jnp.bfloat16
F32 = jnp.float32
PARAMS = pltpu.CompilerParams(vmem_limit_bytes=60 * 1024 * 1024)


def dot(left, right, dims=NN):
    return lax.dot_general(left, right, dims, preferred_element_type=F32)


def attend_kernel(count, chained, final, *refs):
    q_ref = refs[0]
    k_refs = refs[1 : 1 + count]
    v_refs = refs[1 + count : 1 + 2 * count]
    o_ref, l_ref = refs[-2:]
    outs = []
    for h in range(2):
        part = slice(h * DH, h * DH + DH)
        q = q_ref[0, :, part]
        scores = [dot(k[0, :, part], q, NT) for k in k_refs]
        top = functools.reduce(
            jnp.maximum, [jnp.max(s, axis=0, keepdims=True) for s in scores]
        )
        top = top * SCALE_TWO
        total = None
        mixed = None
        for s, v in zip(scores, v_refs):
            raised = jnp.exp2(s * SCALE_TWO - top)
            some = jnp.sum(raised, axis=0, keepdims=True)
            term = dot(v[0, :, part], raised.astype(BF), TN)
            total = some if total is None else total + some
            mixed = term if mixed is None else mixed + term
        mixed = mixed * (1.0 / total)
        log = top + jnp.log2(total)
        if chained:
            before_ref, before_log_ref = refs[1 + 2 * count : 3 + 2 * count]
            before = before_log_ref[0, 0, h : h + 1, :]
            high = jnp.maximum(before, log)
            joint = high + jnp.log2(jnp.exp2(before - high) + jnp.exp2(log - high))
            mixed = mixed * jnp.exp2(log - joint) + before_ref[0, part, :] * jnp.exp2(
                before - joint
            )
            log = joint
        l_ref[0, 0, h : h + 1, :] = log
        if final:
            outs.append(mixed)
        else:
            o_ref[0, part, :] = mixed
    if final:
        o_ref[0] = jnp.concatenate(outs, axis=0).T.astype(BF)


def attend(queries, shards, before, final):
    frames, rows, width = queries.shape
    count = len(shards)
    keys = shards[0].shape[1]
    pairs = width // 128
    turned = pl.BlockSpec((1, 128, rows), lambda f, p: (f, p, 0))
    row = pl.BlockSpec((1, rows, 128), lambda f, p: (f, 0, p))
    log = pl.BlockSpec((1, 1, 2, rows), lambda f, p: (f, p, 0, 0))
    chained = before is not None
    return pl.pallas_call(
        functools.partial(attend_kernel, count, chained, final),
        grid=(frames, pairs),
        in_specs=[row]
        + [pl.BlockSpec((1, keys, 128), lambda f, p: (f, 0, p))] * count
        + [pl.BlockSpec((1, keys, 128), lambda f, p: (f, 0, p + pairs))] * count
        + ([turned, log] if chained else []),
        out_specs=[row if final else turned, log],
        out_shape=[
            jax.ShapeDtypeStruct((frames, rows, width), BF)
            if final
            else jax.ShapeDtypeStruct((frames, width, rows), F32),
            jax.ShapeDtypeStruct((frames, pairs, 2, rows), F32),
        ],
        compiler_params=PARAMS,
        name="attend",
        cost_estimate=pl.CostEstimate(
            flops=2 * frames * rows * count * keys * width,
            transcendentals=0,
            bytes_accessed=frames * rows * width,
        ),
    )(queries, *shards, *shards, *(before if chained else ()))


def column_sums(total, values):
    normed, _ = layer_norm(values.astype(F32))
    return jnp.concatenate(
        (
            jnp.sum(total * normed, axis=0, keepdims=True),
            jnp.sum(total, axis=0, keepdims=True),
        )
    )


def attend_back_kernel(
    q_ref,
    g_ref,
    o_ref,
    l_ref,
    k_ref,
    v_ref,
    wk_ref,
    wv_ref,
    x_ref,
    before_ref,
    dq_ref,
    dk_ref,
    dv_ref,
    term_ref,
    sums_ref,
):
    pair = pl.program_id(1)
    key_terms = []
    value_terms = []
    query_terms = []
    for h in range(2):
        part = slice(h * DH, h * DH + DH)
        q = q_ref[0, :, part]
        g = g_ref[0, :, part]
        k = k_ref[0, :, part]
        v = v_ref[0, :, part]
        product = g.astype(F32) * o_ref[0, :, part].astype(F32)
        high, low = split_two(product)
        ones = jnp.ones((8, DH), BF)
        delta = (dot(ones, high, NT) + dot(ones, low, NT))[0:1]
        probs = jnp.exp2(dot(k, q, NT) * SCALE_TWO - l_ref[0, 0, h : h + 1, :])
        grad_probs = dot(v, g, NT)
        grad_scores = (probs * (grad_probs - delta)).astype(BF)
        value_terms.append(dot(probs.astype(BF), g))
        key_terms.append(dot(grad_scores, q))
        grad_query = dot(k, grad_scores, TN) * SCALE + before_ref[0, part, :]
        query_terms.append(grad_query)
    grad_key = (jnp.concatenate(key_terms, axis=1) * SCALE).astype(BF)
    grad_value = jnp.concatenate(value_terms, axis=1).astype(BF)
    grad_query = jnp.concatenate(query_terms, axis=0).astype(dq_ref.dtype)
    lanes = pl.ds(pl.multiple_of(pair * 128, 128), 128)
    dk_ref[0, :, lanes] = grad_key
    dv_ref[0, :, lanes] = grad_value
    dq_ref[0] = grad_query

    @pl.when(pair == pl.num_programs(1) - 1)
    def _():
        total = dot(dk_ref[0], wk_ref[...], NT) + dot(dv_ref[0], wv_ref[...], NT)
        term_ref[0] = total.astype(term_ref.dtype)
        sums_ref[0] = column_sums(total, x_ref[0])


def attend_back(queries, grad_out, out, logs, shard, weights, source, before):
    frames, rows, width = queries.shape
    keys = shard.shape[1]
    pairs = width // 128
    row = pl.BlockSpec((1, rows, 128), lambda f, p: (f, 0, p))
    key = pl.BlockSpec((1, keys, 128), lambda f, p: (f, 0, p))
    value = pl.BlockSpec((1, keys, 128), lambda f, p: (f, 0, p + pairs))
    turned = pl.BlockSpec((1, 128, rows), lambda f, p: (f, p, 0))
    log = pl.BlockSpec((1, 1, 2, rows), lambda f, p: (f, p, 0, 0))

    def columns(group):
        return pl.BlockSpec((width, width), lambda f, p: (0, group))

    def whole(*shape):
        return pl.BlockSpec((1,) + shape, lambda f, p: (f, 0, 0))

    in_specs = [row, row, row, log, key, value, columns(1), columns(2), whole(keys, width)]
    operands = [queries, grad_out, out, logs, shard, shard, weights, weights, source]
    aliases = {len(operands): 0}
    in_specs.append(turned)
    operands.append(before)
    out_specs = [turned, whole(keys, width), whole(keys, width), whole(keys, width), whole(2, width)]
    out_shape = [
        jax.ShapeDtypeStruct((frames, width, rows), F32),
        jax.ShapeDtypeStruct((frames, keys, width), BF),
        jax.ShapeDtypeStruct((frames, keys, width), BF),
        jax.ShapeDtypeStruct((frames, keys, width), BF),
        jax.ShapeDtypeStruct((frames, 2, width), F32),
    ]
    return pl.pallas_call(
        attend_back_kernel,
        grid=(frames, pairs),
        in_specs=in_specs,
        out_specs=out_specs,
        out_shape=out_shape,
        input_output_aliases=aliases,
        compiler_params=PARAMS,
        name="attend_back",
        cost_estimate=pl.CostEstimate(
            flops=4 * frames * rows * keys * width,
            transcendentals=0,
            bytes_accessed=frames * rows * width,
        ),
    )(*operands)


def query_back_kernel(dq_ref, w_ref, x_ref, low_ref, term_ref, sums_ref):
    low = dq_ref[0].astype(BF)
    low_ref[0] = low
    total = dot(low, w_ref[...], (((0,), (1,)), ((), ())))
    term_ref[0] = total
    sums_ref[0] = column_sums(total, x_ref[0])


def query_back(grad_query, weights, source):
    frames, width, rows = grad_query.shape

    def whole(*shape):
        return pl.BlockSpec((1,) + shape, lambda f: (f, 0, 0))

    return pl.pallas_call(
        query_back_kernel,
        grid=(frames,),
        in_specs=[
            whole(width, rows),
            pl.BlockSpec((width, width), lambda f: (0, 0)),
            whole(rows, width),
        ],
        out_specs=[whole(width, rows), whole(rows, width), whole(2, width)],
        out_shape=[
            jax.ShapeDtypeStruct((frames, width, rows), BF),
            jax.ShapeDtypeStruct((frames, rows, width), F32),
            jax.ShapeDtypeStruct((frames, 2, width), F32),
        ],
        compiler_params=PARAMS,
        name="query_back",
        cost_estimate=pl.CostEstimate(
            flops=frames * rows * width * width, transcendentals=0, bytes_accessed=rows * width
        ),
    )(grad_query, weights, source)


def between_kernel(
    x_ref,
    att_ref,
    wo_ref,
    wu_ref,
    wd_ref,
    head_ref,
    gain_ref,
    shift_ref,
    bu_ref,
    bd_ref,
    mask_ref,
    sens_ref,
    one_ref,
    two_ref,
    hidden_ref,
    act_ref,
    up_ref,
    down_ref,
    final_ref,
    heads_ref,
    attn_ref,
    gres_ref,
    gatt_ref,
    first_ref,
    second_ref,
    added_ref,
    vec_ref,
    bup_ref,
    slope_ref,
):
    residual = x_ref[...].astype(F32) + dot(att_ref[...], wo_ref[...])
    normed, inverse = layer_norm(residual)
    gain = gain_ref[...][None]
    hidden = (normed * gain + shift_ref[...][None]).astype(BF)
    hidden_ref[...] = hidden
    wide = 512
    chunks = [slice(j, j + wide) for j in range(0, wu_ref.shape[1], wide)]
    final = residual + bd_ref[...][None]
    for part in chunks:
        up = dot(hidden, wu_ref[:, part]) + bu_ref[part][None]
        square = up * up
        tanh = jnp.tanh(ROOT * up * (1.0 + CUBE * square))
        half = 0.5 * (1.0 + tanh)
        act = (up * half).astype(BF)
        slope_ref[:, part] = half + 0.5 * up * (1.0 - tanh * tanh) * (
            ROOT + 3.0 * ROOT * CUBE * square
        )
        act_ref[:, part] = act
        final = final + dot(act, wd_ref[part, :])
    final_low = final.astype(BF)
    final_ref[...] = final_low
    logits = dot(final_low, head_ref[...], NT)
    one = logits[:, :128]
    two = logits[:, 128:256]
    offset = logits[:, 256:]
    top = jnp.maximum(one, two)
    one = jnp.exp(one - top)
    two = jnp.exp(two - top)
    total = one + two
    one = one / total
    two = two / total
    mask = mask_ref[0]
    first_ref[...] = mask * one + (1.0 - mask)
    second_ref[...] = mask * two
    added_ref[...] = mask * offset
    grad_one = mask * one_ref[...]
    grad_two = mask * two_ref[...]
    mean = one * grad_one + two * grad_two
    heads = jnp.concatenate(
        (one * (grad_one - mean), two * (grad_two - mean), mask * sens_ref[...]), axis=1
    ).astype(BF)
    heads_ref[...] = heads
    grad_final = dot(heads, head_ref[...])
    down = grad_final.astype(BF)
    down_ref[...] = down
    grad_hidden = None
    ups = []
    for part in chunks:
        grad_up = (dot(down, wd_ref[part, :], NT) * slope_ref[:, part]).astype(BF)
        up_ref[:, part] = grad_up
        ups.append(jnp.sum(grad_up.astype(F32), axis=0, keepdims=True))
        term = dot(grad_up, wu_ref[:, part], NT)
        grad_hidden = term if grad_hidden is None else grad_hidden + term
    grad_normed = grad_hidden * gain
    grad_residual = grad_final + norm_back(grad_normed, normed, inverse)
    gres_ref[...] = grad_residual
    attn = grad_residual.astype(BF)
    attn_ref[...] = attn
    gatt_ref[...] = dot(attn, wo_ref[...], NT).astype(BF)
    vectors = jnp.concatenate(
        (
            jnp.sum(grad_hidden * normed, axis=0, keepdims=True),
            jnp.sum(grad_hidden, axis=0, keepdims=True),
            jnp.sum(down.astype(F32), axis=0, keepdims=True),
        )
    )
    ups = jnp.concatenate(ups, axis=1)

    @pl.when(pl.program_id(0) == 0)
    def _():
        vec_ref[...] = vectors
        bup_ref[...] = ups

    @pl.when(pl.program_id(0) > 0)
    def _():
        vec_ref[...] += vectors
        bup_ref[...] += ups


def between(x, attended, w_out, w_up, w_down, heads, gain, shift, b_up, b_down, mask, sums, local):
    rows, width = x.shape
    hidden = w_up.shape[1]
    block = math.gcd(local, 256)

    def row(columns):
        return pl.BlockSpec((block, columns), lambda i: (i, 0))

    def whole(values):
        zeros = (0,) * values.ndim
        return pl.BlockSpec(values.shape, lambda i: zeros, pipeline_mode=pl.Buffered(1))

    def shape(columns, kind=BF):
        return jax.ShapeDtypeStruct((rows, columns), kind)

    fixed = [w_out, w_up, w_down, heads, gain, shift, b_up, b_down]
    return pl.pallas_call(
        between_kernel,
        grid=(rows // block,),
        in_specs=[row(width), row(width)]
        + [whole(v) for v in fixed]
        + [pl.BlockSpec((1, 1, 128), lambda i: (i * block // local, 0, 0))]
        + [row(128)] * 3,
        out_specs=[
            row(width),
            row(hidden),
            row(hidden),
            row(width),
            row(width),
            row(384),
            row(width),
            row(width),
            row(width),
            row(128),
            row(128),
            row(128),
            pl.BlockSpec((3, width), lambda i: (0, 0)),
            pl.BlockSpec((1, hidden), lambda i: (0, 0)),
        ],
        out_shape=[
            shape(width),
            shape(hidden),
            shape(hidden),
            shape(width),
            shape(width),
            shape(384),
            shape(width),
            shape(width, F32),
            shape(width),
            shape(128, F32),
            shape(128, F32),
            shape(128, F32),
            jax.ShapeDtypeStruct((3, width), F32),
            jax.ShapeDtypeStruct((1, hidden), F32),
        ],
        scratch_shapes=[pltpu.VMEM((block, hidden), F32)],
        compiler_params=PARAMS,
        name="between",
        cost_estimate=pl.CostEstimate(
            flops=rows * width * hidden, transcendentals=0, bytes_accessed=rows * hidden
        ),
    )(x, attended, *fixed, mask, *sums)


def deal(place, result, mine_ref, sent_ref):
    halves = result.reshape(mine_ref.shape[0], 2, *mine_ref.shape[1:]).astype(BF)
    low = halves[:, 0]
    high = halves[:, 1]
    even = place == 0
    mine_ref[...] = jnp.where(even, low, high)
    sent_ref[...] = jnp.where(even, high, low)


def columns_of(vectors, start):
    count = vectors.shape[0]
    place = lax.broadcasted_iota(jnp.int32, (count, 256), 1)
    which = lax.broadcasted_iota(jnp.int32, (count, 256), 0)
    chosen = (place == which + start).astype(F32).astype(BF)
    high, rest = split_two(vectors)
    return dot(high, chosen, TN) + dot(rest, chosen, TN)


def early_grads_kernel(
    place_ref,
    h_ref,
    a_ref,
    f_ref,
    up_ref,
    attn_ref,
    head_ref,
    vec_ref,
    mine_in_ref,
    sent_in_ref,
    mine_ref,
    sent_ref,
    turn_ref,
):
    step = pl.program_id(0)
    last = pl.num_programs(0) - 1
    place = place_ref[0]
    wide = up_ref.shape[1]

    @pl.when(step == 0)
    def _():
        turn_ref[...] = h_ref[...].T

    @pl.when(step < last - 1)
    def _():
        deal(place, dot(turn_ref[...], up_ref[...]), mine_ref, sent_ref)

    @pl.when(step == last - 1)
    def _():
        turned = a_ref[...].T
        turn_ref[...] = turned
        deal(place, dot(turned, attn_ref[:, :wide]), mine_ref, sent_ref)

    @pl.when(step == last)
    def _():
        out = dot(turn_ref[...], attn_ref[:, wide:])
        heads = dot(f_ref[...].T, head_ref[...]) + columns_of(vec_ref[...], 3 * RESULT_FIELDS)
        deal(place, jnp.concatenate((out, heads), axis=1), mine_ref, sent_ref)


def early_grads(place, hidden, attended, final, up, attn, heads, vectors, mine, sent):
    rows, width = hidden.shape
    wide = 512
    steps = up.shape[1] // wide + 2
    count = width // 96
    skip = mine.shape[2] // wide - steps

    def whole(values):
        return pl.BlockSpec(values.shape, lambda i: (0, 0))

    out = pl.BlockSpec((count, 48, wide), lambda i: (0, 0, i + skip))
    untouched = pl.BlockSpec(memory_space=pl.ANY)
    return pl.pallas_call(
        early_grads_kernel,
        grid=(steps,),
        in_specs=[
            pl.BlockSpec(memory_space=pltpu.SMEM),
            whole(hidden),
            whole(attended),
            whole(final),
            pl.BlockSpec((rows, wide), lambda i: (0, jnp.minimum(i, steps - 3))),
            whole(attn),
            whole(heads),
            whole(vectors),
            untouched,
            untouched,
        ],
        out_specs=[out, out],
        out_shape=[jax.ShapeDtypeStruct(mine.shape, BF)] * 2,
        input_output_aliases={8: 0, 9: 1},
        scratch_shapes=[pltpu.VMEM((width, rows), BF)],
        compiler_params=PARAMS,
        name="early_grads",
        cost_estimate=pl.CostEstimate(
            flops=2 * rows * width * wide * steps,
            transcendentals=0,
            bytes_accessed=2 * rows * wide * steps + 2 * width * wide * steps,
        ),
    )(place, hidden, attended, final, up, attn, heads, vectors, mine, sent)


def down_grads_kernel(place_ref, act_ref, down_ref, mine_ref, sent_ref):
    result = dot(act_ref[...], down_ref[...], TN).astype(BF)
    block = result.shape[0] // 2
    piece = block // 8
    halves = []
    for c in range(2):
        groups = [
            jnp.concatenate(
                [
                    result[c * block + y * 4 * piece + g * piece :][:piece]
                    for y in range(2)
                ],
                axis=0,
            )
            for g in range(4)
        ]
        halves.append(jnp.concatenate(groups, axis=1)[None])
    even = place_ref[0] == 0
    mine_ref[...] = jnp.where(even, halves[0], halves[1])
    sent_ref[...] = jnp.where(even, halves[1], halves[0])


def down_grads(place, activation, down, columns):
    rows, width = down.shape
    block = activation.shape[1] // 8
    piece = block // 16
    out = pl.BlockSpec((1, 2 * piece, 4 * width), lambda i: (i, 0, 0))
    return pl.pallas_call(
        down_grads_kernel,
        grid=(8,),
        in_specs=[
            pl.BlockSpec(memory_space=pltpu.SMEM),
            pl.BlockSpec((rows, block), lambda i: (0, i)),
            pl.BlockSpec((rows, width), lambda i: (0, 0)),
        ],
        out_specs=[out, out],
        out_shape=[jax.ShapeDtypeStruct((8, 2 * piece, columns), BF)] * 2,
        compiler_params=PARAMS,
        name="down_grads",
        cost_estimate=pl.CostEstimate(
            flops=2 * rows * width * block, transcendentals=0, bytes_accessed=width * block
        ),
    )(place, activation, down)


def late_grads_kernel(count, place_ref, *refs):
    mixed_refs = refs[:count]
    query_ref = refs[count]
    key_refs = refs[count + 1 : 2 * count + 1]
    value_refs = refs[2 * count + 1 : 3 * count + 1]
    vec_ref, mine_ref, sent_ref, turn_ref = refs[3 * count + 1 :]
    step = pl.program_id(0)
    third = (pl.num_programs(0) - 1) // 3
    place = place_ref[0]

    @pl.when(step == 0)
    def _():
        for s in range(count):
            turn_ref[s] = mixed_refs[s][...].T

    @pl.when(step < third)
    def _():
        deal(place, dot(turn_ref[0], query_ref[...], NT), mine_ref, sent_ref)

    def joint(parts):
        return sum(dot(turn_ref[s], parts[s][...]) for s in range(count))

    @pl.when((step >= third) & (step < 2 * third))
    def _():
        deal(place, joint(key_refs), mine_ref, sent_ref)

    @pl.when((step >= 2 * third) & (step < 3 * third))
    def _():
        deal(place, joint(value_refs), mine_ref, sent_ref)

    @pl.when(step == 3 * third)
    def _():
        deal(place, columns_of(vec_ref[...], 0), mine_ref, sent_ref)


def late_grads(place, mixed, query, keys, values, vectors):
    rows, width = mixed[0].shape
    count = len(mixed)
    wide = 256
    third = width // wide
    groups = width // 96

    def clipped(offset):
        return lambda i: (0, jnp.clip(i - offset, 0, third - 1))

    whole = pl.BlockSpec((rows, width), lambda i: (0, 0))
    out = pl.BlockSpec((groups, 48, wide), lambda i: (0, 0, i))
    return pl.pallas_call(
        functools.partial(late_grads_kernel, count),
        grid=(3 * third + 1,),
        in_specs=[pl.BlockSpec(memory_space=pltpu.SMEM)]
        + [whole] * count
        + [pl.BlockSpec((wide, rows), lambda i: (jnp.clip(i, 0, third - 1), 0))]
        + [pl.BlockSpec((rows, wide), clipped(third))] * count
        + [pl.BlockSpec((rows, wide), clipped(2 * third))] * count
        + [pl.BlockSpec(vectors.shape, lambda i: (0, 0))],
        out_specs=[out, out],
        out_shape=[jax.ShapeDtypeStruct((groups, 48, wide * (3 * third + 1)), BF)] * 2,
        scratch_shapes=[pltpu.VMEM((count, width, rows), BF)],
        compiler_params=PARAMS,
        name="late_grads",
        cost_estimate=pl.CostEstimate(
            flops=2 * rows * width * width * (2 * count + 1),
            transcendentals=0,
            bytes_accessed=2 * rows * width * 4 * count + 12 * width * width,
        ),
    )(place, *mixed, query, *keys, *values, vectors)


def block_sums_kernel(counts, dealt, where_ref, *refs):
    total_in = sum(len(group) for group in counts)
    ins, outs = refs[:total_in], refs[total_in:]
    at = 0
    for o, group in enumerate(counts):
        shape = ins[at].shape[-2:] if dealt else outs[o].shape
        value = None
        for use in group:
            term = ins[at][...].astype(F32).reshape(shape)
            if use is not None:
                term = jnp.where(use(pl.program_id(0), where_ref), term, 0.0)
            value = term if value is None else value + term
            at += 1
        if dealt:
            for k, out in enumerate(outs):

                @pl.when(pl.program_id(0) == k)
                def _(out=out, value=value, o=o):
                    out[o] = value.astype(BF)
        else:
            outs[o][...] = value.astype(BF)


def block_sums(where, steps, groups, dealt=False):
    counts = [[term[3] if len(term) > 3 else None for term in terms] for _, terms in groups]
    operands = [term[0] for _, terms in groups for term in terms]
    in_specs = [pl.BlockSpec(term[1], term[2]) for _, terms in groups for term in terms]
    if dealt:
        shape = (len(groups),) + groups[0][0]
        zeros = (0,) * len(shape)
        out_specs = [pl.BlockSpec(shape, lambda i, w: zeros)] * steps
        out_shape = [jax.ShapeDtypeStruct(shape, BF)] * steps
    else:
        out_specs = [pl.BlockSpec(out[1], out[2]) for out, _ in groups]
        out_shape = [jax.ShapeDtypeStruct(out[0], BF) for out, _ in groups]
    return pl.pallas_call(
        functools.partial(block_sums_kernel, counts, dealt),
        grid_spec=pltpu.PrefetchScalarGridSpec(
            num_scalar_prefetch=1, grid=(steps,), in_specs=in_specs, out_specs=out_specs
        ),
        out_shape=out_shape,
        compiler_params=PARAMS,
        name="block_sums",
        cost_estimate=pl.CostEstimate(flops=1 << 20, transcendentals=0, bytes_accessed=1 << 20),
    )(where, *operands)


class Reduction:
    def __init__(self, where, terms, by_columns):
        self.where = where
        self.terms = terms
        self.by_columns = by_columns
        self.depth, self.columns = terms[0].shape[3:]
        self.steps = 4 if by_columns else 2
        if by_columns:
            self.columns //= 2

    def at(self, part, x, z, y, sizes):
        block = sizes + (self.depth, self.columns)
        column = part if self.by_columns else 0
        shift = 0 if self.by_columns else 2 * part

        def index(i, w):
            return (x(w), z(i, w) + shift, y(w), 0, column)

        return [(t, block, index) for t in self.terms]

    def one(self):
        n, tail = self.steps, (self.depth, self.columns)
        ahead = lambda i, w: i
        sent = block_sums(
            self.where,
            n,
            [
                (
                    ((n, 2) + tail, (1, 2) + tail, lambda i, w: (i, 0, 0, 0)),
                    self.at(0, lambda w: 1 - w[0], ahead, lambda w: 0, (1, 1, 2)),
                ),
                (
                    ((2, n) + tail, (2, 1) + tail, lambda i, w: (0, i, 0, 0)),
                    self.at(1, lambda w: 0, ahead, lambda w: 1 - w[1], (2, 1, 1)),
                ),
            ],
        )
        return list(sent)

    def trade_one(self, sent):
        self.got_one = [swap(sent[0], "lat", 1), swap(sent[1], "grp", 2)]

    def two(self):
        n, tail = self.steps, (self.depth, self.columns)
        ahead = lambda i, w: i
        out = ((n,) + tail, (1,) + tail, lambda i, w: (i, 0, 0))
        flat = (1, 1) + tail
        sent = block_sums(
            self.where,
            n,
            [
                (
                    out,
                    self.at(0, lambda w: w[0], ahead, lambda w: 1 - w[1], (1, 1, 1))
                    + [(self.got_one[0], flat, lambda i, w: (i, 1 - w[1], 0, 0))],
                ),
                (
                    out,
                    self.at(1, lambda w: 1 - w[0], ahead, lambda w: w[1], (1, 1, 1))
                    + [(self.got_one[1], flat, lambda i, w: (1 - w[0], i, 0, 0))],
                ),
            ],
        )
        return list(sent)

    def trade_two(self, sent):
        self.got_two = [swap(sent[0], "grp", 2), swap(sent[1], "lat", 1)]

    def quarters(self):
        tail = (self.depth, self.columns)
        x = lambda w: w[0]
        y = lambda w: w[1]
        if self.by_columns:
            place = lambda i, w: w[2] ^ i
            groups = []
            for part in (0, 1):
                terms = self.at(part, x, place, y, (1, 1, 1))
                if part == 0:
                    one = lambda i, w: (w[2] ^ i, w[1], 0, 0)
                else:
                    one = lambda i, w: (w[0], w[2] ^ i, 0, 0)
                terms.append((self.got_one[part], (1, 1) + tail, one))
                terms.append((self.got_two[part], (1,) + tail, lambda i, w: (w[2] ^ i, 0, 0)))
                groups.append((tail, terms))
        else:
            low = lambda i, w: jnp.minimum(w[2] ^ i, 1)
            high = lambda i, w: jnp.maximum((w[2] ^ i) - 2, 0)
            first = lambda i, w: (w[2] ^ i) < 2
            second = lambda i, w: (w[2] ^ i) >= 2
            terms = self.at(0, x, lambda i, w: w[2] ^ i, y, (1, 1, 1))
            pair = (1, 1) + tail
            one = (1,) + tail
            terms += [
                (self.got_one[0], pair, lambda i, w: (low(i, w), w[1], 0, 0), first),
                (self.got_one[1], pair, lambda i, w: (w[0], high(i, w), 0, 0), second),
                (self.got_two[0], one, lambda i, w: (low(i, w), 0, 0), first),
                (self.got_two[1], one, lambda i, w: (high(i, w), 0, 0), second),
            ]
            groups = [(tail, terms)]
        return list(block_sums(self.where, 4, groups, True))


def early_unpack_kernel(place_ref, *refs):
    ins = refs[:4]
    down_ref, up_ref, out_ref, misc_ref = refs[4:]
    width = down_ref.shape[1]
    hidden = up_ref.shape[1]
    for source, (c, y) in zip(ins, ((0, 0), (0, 1), (1, 0), (1, 1))):
        slot = jnp.bitwise_xor(place_ref[0], c) * 2 + jnp.bitwise_xor(place_ref[1], y)
        one = source[0].astype(F32)
        two = source[1].astype(F32)
        rows = one.shape[0]
        half = one.shape[1]
        for g in range(4):
            span = pl.ds(pl.multiple_of(slot * 4 * rows + g * rows, 8), rows)
            down_ref[span, :] = one[:, g * width : (g + 1) * width]
        span = pl.ds(pl.multiple_of(slot * rows, 8), rows)
        cut = half - 4 * width
        up_ref[span, :cut] = one[:, 4 * width :]
        up_ref[span, cut:] = two[:, : hidden - cut]
        out_ref[span, :] = two[:, hidden - cut : hidden - cut + width]
        misc_ref[span, :] = two[:, hidden - cut + width :]


def early_unpack(place, pieces, width, hidden):
    rows = pieces[0].shape[1]
    vmem = pl.BlockSpec(memory_space=pltpu.VMEM)
    return pl.pallas_call(
        early_unpack_kernel,
        in_specs=[pl.BlockSpec(memory_space=pltpu.SMEM)] + [vmem] * 4,
        out_specs=[vmem] * 4,
        out_shape=[
            jax.ShapeDtypeStruct((16 * rows, width), F32),
            jax.ShapeDtypeStruct((4 * rows, hidden), F32),
            jax.ShapeDtypeStruct((4 * rows, width), F32),
            jax.ShapeDtypeStruct((4 * rows, 256), F32),
        ],
        compiler_params=PARAMS,
        name="early_unpack",
        cost_estimate=pl.CostEstimate(flops=1 << 20, transcendentals=0, bytes_accessed=1 << 20),
    )(place, *pieces)


def late_unpack_kernel(place_ref, *refs):
    ins = refs[:4]
    main_ref, misc_ref = refs[4:]
    for source, (c, y) in zip(ins, ((0, 0), (0, 1), (1, 0), (1, 1))):
        slot = jnp.bitwise_xor(place_ref[0], c) * 2 + jnp.bitwise_xor(place_ref[1], y)
        value = source[...].astype(F32)
        rows = value.shape[0]
        span = pl.ds(pl.multiple_of(slot * rows, 8), rows)
        main_ref[span, :] = value[:, : main_ref.shape[1]]
        misc_ref[span, :] = value[:, main_ref.shape[1] :]


def late_unpack(place, pieces):
    rows, columns = pieces[0].shape
    vmem = pl.BlockSpec(memory_space=pltpu.VMEM)
    return pl.pallas_call(
        late_unpack_kernel,
        in_specs=[pl.BlockSpec(memory_space=pltpu.SMEM)] + [vmem] * 4,
        out_specs=[vmem] * 2,
        out_shape=[
            jax.ShapeDtypeStruct((4 * rows, columns - 256), F32),
            jax.ShapeDtypeStruct((4 * rows, 256), F32),
        ],
        compiler_params=PARAMS,
        name="late_unpack",
        cost_estimate=pl.CostEstimate(flops=1 << 20, transcendentals=0, bytes_accessed=1 << 20),
    )(place, *pieces)


def spread(rows, columns):
    pixel = lax.broadcasted_iota(jnp.int32, (rows, columns), 0)
    field = lax.broadcasted_iota(jnp.int32, (rows, columns), 1)
    return ((pixel // TILE_AREA) == field).astype(F32).astype(BF)


def split_two(values):
    high = values.astype(BF)
    return high, (values - high.astype(F32)).astype(BF)


def pixel_sums_kernel(f_ref, s_ref, sum_ref, first_ref, second_ref, field_ref):
    @pl.when(pl.program_id(0) == 0)
    def _():
        field_ref[...] = spread(*field_ref.shape)

    fields = field_ref[...]
    sens = s_ref[...]
    sum_ref[...] = dot(sens, fields)
    for e, out in ((0, first_ref), (1, second_ref)):
        out[...] = dot((sens.astype(F32) * f_ref[e].astype(F32)).astype(BF), fields)


def pixel_sums(forecasts, sensitivity):
    rows, pixels = sensitivity.shape
    block = math.gcd(rows, 128)
    out = pl.BlockSpec((block, 128), lambda i: (i, 0))
    return pl.pallas_call(
        pixel_sums_kernel,
        grid=(rows // block,),
        in_specs=[
            pl.BlockSpec((2, block, pixels), lambda i: (0, i, 0)),
            pl.BlockSpec((block, pixels), lambda i: (i, 0)),
        ],
        out_specs=[out] * 3,
        out_shape=[jax.ShapeDtypeStruct((rows, 128), F32)] * 3,
        scratch_shapes=[pltpu.VMEM((pixels, 128), BF)],
        compiler_params=PARAMS,
        name="pixel_sums",
        cost_estimate=pl.CostEstimate(
            flops=rows * pixels * 128, transcendentals=0, bytes_accessed=rows * pixels
        ),
    )(forecasts, sensitivity)


def blend_kernel(a_ref, b_ref, c_ref, f_ref, out_ref, field_ref):
    @pl.when(pl.program_id(0) == 0)
    def _():
        columns = field_ref.shape[1]
        field = lax.broadcasted_iota(jnp.int32, (256, columns), 0)
        pixel = lax.broadcasted_iota(jnp.int32, (256, columns), 1)
        field_ref[...] = ((pixel // TILE_AREA) == (field % 128)).astype(F32).astype(BF)

    fields = field_ref[...]

    def wide(ref):
        return dot(jnp.concatenate(split_two(ref[...]), axis=1), fields)

    total = wide(a_ref) * f_ref[0].astype(F32) + wide(b_ref) * f_ref[1].astype(F32)
    out_ref[...] = (total + wide(c_ref)).astype(BF)


def blend(first, second, added, forecasts):
    _, rows, pixels = forecasts.shape
    block = math.gcd(rows, 128)
    thin = pl.BlockSpec((block, 128), lambda i: (i, 0))
    return pl.pallas_call(
        blend_kernel,
        grid=(rows // block,),
        in_specs=[thin] * 3 + [pl.BlockSpec((2, block, pixels), lambda i: (0, i, 0))],
        out_specs=pl.BlockSpec((block, pixels), lambda i: (i, 0)),
        out_shape=jax.ShapeDtypeStruct((rows, pixels), BF),
        scratch_shapes=[pltpu.VMEM((256, pixels), BF)],
        compiler_params=PARAMS,
        name="blend",
        cost_estimate=pl.CostEstimate(
            flops=rows * pixels * 128, transcendentals=0, bytes_accessed=rows * pixels
        ),
    )(first, second, added, forecasts)


def swap(values, axis, bit):
    count = lax.axis_size(axis)
    return lax.ppermute(values, axis, [(i, i ^ bit) for i in range(count)])


def add(*terms):
    return sum(t.astype(F32) for t in terms).astype(BF)


def hold(*values):
    return lax.optimization_barrier(values)


def layer_norm(values):
    centred = values - jnp.mean(values, axis=-1, keepdims=True)
    inverse = lax.rsqrt(jnp.mean(centred * centred, axis=-1, keepdims=True) + EPSILON)
    return centred * inverse, inverse


def norm_back(grad_normed, normed, inverse):
    return inverse * (
        grad_normed
        - jnp.mean(grad_normed, axis=-1, keepdims=True)
        - normed * jnp.mean(grad_normed * normed, axis=-1, keepdims=True)
    )


def pad_lanes(values):
    return jnp.pad(values, ((0, 0), (0, 128 - values.shape[1])))


def per_device(
    layer_source_tensor,
    horizon_class,
    field_selector,
    model_predictions,
    loss_sensitivity,
    gain_one,
    shift_one,
    horizon_vectors,
    w_qkv,
    w_out,
    gain_two,
    shift_two,
    w_up,
    b_up,
    w_down,
    b_down,
    w_gate,
    w_bias,
):
    frames, lat_rows, lon_cols, width = layer_source_tensor.shape
    local = lat_rows * lon_cols
    rows = frames * local
    pixels = loss_sensitivity.shape[-1]
    sizes = (lax.axis_size("grp"), lax.axis_size("lat"), lax.axis_size("lon"))
    small = sizes == (4, 2, 4) and frames == 1

    source = layer_source_tensor.reshape(frames, local, width)
    place = lax.axis_index("lon")
    edge = (place == 0) | (place == lax.axis_size("lon") - 1)
    send = functools.partial(lax.ppermute, axis_name="lon")
    if small:
        right = send(source, perm=[(0, 1), (1, 2), (2, 3)])
        left = send(source, perm=[(3, 2), (2, 1), (1, 0)])
    else:
        shards = [lax.all_gather(source, "lon", axis=1, tiled=True)]

    forecasts = jnp.transpose(model_predictions.reshape(rows, 2, pixels), (1, 0, 2))
    sensitivity = loss_sensitivity.reshape(rows, pixels)

    onehot = (horizon_class[:, None] == jnp.arange(LEADS, dtype=jnp.int32)[None, :]).astype(F32)
    lead_rows = jnp.dot(onehot, horizon_vectors, precision=HIGH)

    def mixed_of(values):
        normed, _ = layer_norm(values.astype(F32))
        return (normed * gain_one + shift_one + lead_rows[:, None, :]).astype(BF)

    wq = w_qkv[:, :width]
    wkv = w_qkv[:, width:]

    def keys_of(values):
        return dot(values.reshape(-1, width), wkv).astype(BF).reshape(frames, -1, 2 * width)

    mixed_own = mixed_of(source)
    queries = dot(mixed_own.reshape(rows, width), wq).astype(BF).reshape(frames, local, width)
    if small:
        key_value = [keys_of(mixed_own)]
        right, left, forecasts, queries, key_value[0] = hold(
            right, left, forecasts, queries, key_value[0]
        )
        near = jnp.where(place == 0, left, right)
        right_two = send(right, perm=[(1, 2), (2, 3)])
        left_two = send(left, perm=[(2, 1), (1, 0)])
        sums = pixel_sums(forecasts, sensitivity)
        mixed = [mixed_own, mixed_of(near)]
        key_value.append(keys_of(mixed[1]))
        right_two, left_two, key_value[1], *sums = hold(right_two, left_two, key_value[1], *sums)
        two = right_two + left_two
        three = send(two, perm=[(2, 3), (1, 0)])
        middle = jnp.where(edge, two, left)
        mixed.append(mixed_of(middle))
        key_value.append(keys_of(mixed[2]))
        state = attend(queries, key_value, None, False)
        three, *state = hold(three, *state)
        far = jnp.where(edge, three, two)
        mixed.append(mixed_of(far))
        key_value.append(keys_of(mixed[3]))
        attended, logs = attend(queries, key_value[3:], state, True)
        shards = [source, near, middle, far]
    else:
        sums = pixel_sums(forecasts, sensitivity)
        mixed = [mixed_of(shards[0])]
        key_value = [keys_of(mixed[0])]
        attended, logs = attend(queries, key_value, None, True)
    inputs = source.reshape(rows, width)
    attended_low = attended.reshape(rows, width)
    both = w_gate.T
    head_rows = jnp.concatenate(
        [
            jnp.pad(m, ((0, 128 - RESULT_FIELDS), (0, 0)))
            for m in (both[:RESULT_FIELDS], both[RESULT_FIELDS:], w_bias.T)
        ]
    )
    mask = pad_lanes(field_selector.astype(F32))[:, None]
    (
        hidden_low,
        activation_low,
        up_low,
        down_low,
        final_low,
        heads_low,
        attn_low,
        grad_residual,
        grad_attended,
        *blending,
        early_vectors,
        grad_bup,
    ) = between(
        inputs,
        attended_low,
        w_out,
        w_up,
        w_down,
        head_rows,
        gain_two,
        shift_two,
        b_up,
        b_down,
        mask,
        sums,
        local,
    )
    grad_attended = grad_attended.reshape(frames, local, width)
    fields = 3 * RESULT_FIELDS
    heads_low = jnp.concatenate(
        [heads_low[:, g * 128 : g * 128 + RESULT_FIELDS] for g in range(3)], axis=1
    )
    inputs = inputs.astype(F32)
    normed_one, inverse_one = layer_norm(inputs)

    def input_gradient(grad_mixed):
        return grad_residual + norm_back(
            grad_mixed.reshape(rows, width) * gain_one, normed_one, inverse_one
        )

    def back(shard, place, before):
        return attend_back(queries, grad_attended, attended, logs, shard, w_qkv, place, before)

    nothing = jnp.zeros((frames, width, local), F32)

    def late_vectors(sums):
        gain_column = sum(jnp.sum(s[:, 0], axis=0) for s in sums)
        column = sum(s[:, 1] for s in sums)
        lead = jnp.dot(onehot.T, column, precision=HIGH)
        zeros = jnp.zeros((6, width), F32)
        return jnp.concatenate((gain_column[None], jnp.sum(column, axis=0)[None], lead, zeros))

    if small:
        bup_rows = jnp.swapaxes(grad_bup.reshape(8, 4, -1), 0, 1).reshape(4, width)
        early_vectors = jnp.concatenate(
            (early_vectors, bup_rows, jnp.zeros((1, width), F32))
        )
        core = (lax.axis_index("grp") % 2).astype(jnp.int32)[None]
        where = jnp.stack(
            (lax.axis_index("lat"), lax.axis_index("grp") // 2, lax.axis_index("lon"))
        ).astype(jnp.int32)
        used = fields + early_vectors.shape[0]
        hidden = w_up.shape[1]
        mine, sent = down_grads(core, activation_low, down_low, 2 * hidden + width + 256)
        mine, sent = early_grads(
            core,
            hidden_low,
            attended_low,
            final_low,
            up_low,
            attn_low,
            jnp.pad(heads_low, ((0, 0), (0, 256 - fields))),
            early_vectors,
            mine,
            sent,
        )
        grad_attended, sent = hold(grad_attended, sent)
        got = swap(sent, "grp", 1)

        grad_query, dk3, dv3, far, sums3 = back(key_value[3], shards[3], nothing)
        early = Reduction(where, [t.reshape(2, 4, 2, 24, -1) for t in (mine, got)], True)
        grad_query, far, *sent = hold(grad_query, far, *early.one())
        got = send(far, perm=[(0, 1), (3, 2)])
        early.trade_one(sent)

        grad_query, dk2, dv2, middle, sums2 = back(key_value[2], shards[2], grad_query)
        value = jnp.where(edge, middle, add(got, far))
        grad_query, value = hold(grad_query, value)
        right = send(value, perm=[(0, 1), (1, 2)])
        left = send(value, perm=[(3, 2), (2, 1)])

        grad_query, dk1, dv1, near, sums1 = back(key_value[1], shards[1], grad_query)
        forth = jnp.where(place == 0, near, add(right, middle))
        back_value = add(left, near)
        grad_query, forth, back_value, *sent = hold(
            grad_query, forth, back_value, *early.two()
        )
        right = send(forth, perm=[(0, 1), (1, 2), (2, 3)])
        left = send(back_value, perm=[(3, 2), (2, 1), (1, 0)])
        early.trade_two(sent)

        grad_query, dk0, dv0, own, sums0, right, left, *early.got_two = hold(
            *back(key_value[0], shards[0], grad_query), right, left, *early.got_two
        )
        query_low, query_term, query_sums = query_back(grad_query, w_qkv, source)
        query_low, *parts = hold(query_low, *early.quarters())
        early = [parts[0]] + [swap(parts[k], "lon", k) for k in (1, 2, 3)]
        vectors = late_vectors([sums0, sums1, sums2, sums3, query_sums])
        late_mine, late_sent = late_grads(
            core,
            [m.reshape(rows, width) for m in mixed],
            query_low.reshape(width, rows),
            [d.reshape(rows, width) for d in (dk0, dk1, dk2, dk3)],
            [d.reshape(rows, width) for d in (dv0, dv1, dv2, dv3)],
            vectors,
        )
        late_mine, late_sent, own, early[1], early[2] = hold(
            late_mine, late_sent, own, early[1], early[2]
        )
        got = swap(late_sent, "grp", 1)
        grad_input = input_gradient(
            own.astype(F32) + query_term + right.astype(F32) + left.astype(F32)
        )
        got, grad_input = hold(got, grad_input)
        late = Reduction(where, [t.reshape(2, 4, 2, 24, -1) for t in (late_mine, got)], False)
        *sent, one, two, three = hold(*late.one(), *blending)
        late.trade_one(sent)
        blended = blend(one, two, three, forecasts)
        *late.got_one, blended = hold(*late.got_one, blended)
        late.trade_two(hold(*late.two()))
        early = add(*early)
        *late.got_two, early = hold(*late.got_two, early)
        early, *parts = hold(early, *late.quarters())
        late = [parts[0]] + [swap(parts[k], "lon", k) for k in (1, 2, 3)]
        early_y = swap(early, "grp", 2)
        early_c = swap(early, "grp", 1)
        early_y, early_c, early, *late = hold(early_y, early_c, early, *late)
        early_yc = swap(early_y, "grp", 1)
        late = add(*[part[0] for part in late])
        late_y = swap(late, "grp", 2)
        late_c = swap(late, "grp", 1)
        late_y, late_c, late, early_yc = hold(late_y, late_c, late, early_yc)
        place_two = jnp.stack((lax.axis_index("grp") % 2, lax.axis_index("grp") // 2))
        place_two = place_two.astype(jnp.int32)
        down_sum, up_sum, out_sum, misc = early_unpack(
            place_two, [early, early_y, early_c, early_yc], width, hidden
        )
        late_yc = swap(late_y, "grp", 1)
        late_yc, misc = hold(late_yc, misc)
        qkv_sum, late = late_unpack(place_two, [late, late_y, late_c, late_yc])
        late = late[:, : 2 + LEADS].T
        misc = misc[:, :used]
        heads = misc[:, :fields]
        early = misc[:, fields : fields + 3].T
        bup_sum = misc[:, fields + 3 : fields + 7].T.reshape(-1)
    else:
        blended = blend(*blending, forecasts)
        grad_query, dk, dv, term, sums = back(key_value[0], shards[0], nothing)
        query_low, query_term, query_sums = query_back(grad_query, w_qkv, source)
        grad_input = input_gradient(
            query_term + lax.psum_scatter(term.astype(F32), "lon", scatter_dimension=1, tiled=True)
        )

        def total_of(values, dim=0):
            share = lax.psum_scatter(values, ("lat", "lon"), scatter_dimension=dim, tiled=True)
            return lax.psum(share, "grp")

        flat = mixed[0].reshape(-1, width)
        qkv_sum = total_of(
            jnp.concatenate(
                (
                    jnp.einsum("frd,fer->de", mixed_own, query_low, preferred_element_type=F32),
                    dot(flat, dk.reshape(-1, width), TN),
                    dot(flat, dv.reshape(-1, width), TN),
                ),
                axis=1,
            )
        )
        up_sum = total_of(dot(hidden_low, up_low, TN))
        out_sum = total_of(dot(attended_low, attn_low, TN))
        down_sum = total_of(dot(activation_low, down_low, TN))
        heads = total_of(dot(final_low, heads_low, TN))
        late = total_of(late_vectors([sums, query_sums])[: 2 + LEADS], 1)
        early = total_of(early_vectors, 1)
        bup_sum = total_of(grad_bup[0])

    return (
        blended.reshape(frames, lat_rows, lon_cols, pixels),
        grad_input.reshape(frames, lat_rows, lon_cols, width),
        late[0],
        late[1],
        late[2:],
        qkv_sum,
        out_sum,
        early[0],
        early[1],
        up_sum,
        bup_sum,
        down_sum,
        early[2],
        heads[:, : 2 * RESULT_FIELDS],
        heads[:, 2 * RESULT_FIELDS :],
    )


def solution(mesh):
    frame = ("grp", "lat")
    share = ("lat", "lon")
    image = P(frame, None, "lon", None)
    in_specs = (
        image,
        P(frame),
        P(frame, None),
        P(frame, None, "lon", None, None),
        image,
    ) + (P(),) * 13
    vector = P(share)
    matrix = P(share, None)
    out_specs = (
        image,
        image,
        vector,
        vector,
        P(None, share),
        matrix,
        matrix,
        vector,
        vector,
        matrix,
        vector,
        matrix,
        vector,
        matrix,
        matrix,
    )
    return jax.shard_map(
        per_device, mesh=mesh, in_specs=in_specs, out_specs=out_specs, check_vma=False
    )
```

```python
import functools
import math

import jax
import jax.numpy as jnp
from jax import lax
from jax.experimental import pallas as pl
from jax.experimental.pallas import tpu as pltpu
from jax.sharding import PartitionSpec as P

H = 12
DH = 64
RESULT_FIELDS = 69
TILE_AREA = 64
LEADS = 24
EPSILON = 1e-06
HIGH = lax.Precision.HIGHEST
SCALE = 0.125
SCALE_TWO = SCALE * math.log2(math.e)
ROOT = math.sqrt(2.0 / math.pi)
CUBE = 0.044715
NN = (((1,), (0,)), ((), ()))
NT = (((1,), (1,)), ((), ()))
TN = (((0,), (0,)), ((), ()))
BF = jnp.bfloat16
F32 = jnp.float32
PARAMS = pltpu.CompilerParams(vmem_limit_bytes=60 * 1024 * 1024)


def dot(left, right, dims=NN):
    return lax.dot_general(left, right, dims, preferred_element_type=F32)


def project_kernel(own, *refs):
    if own:
        a_ref, gain_ref, shift_ref, lead_ref, wq_ref, wk_ref, wv_ref, mixed_ref, kv_ref, q_ref = refs
        value = a_ref[...]
    else:
        flag_ref, a_ref, b_ref, gain_ref, shift_ref, lead_ref, wk_ref, wv_ref = refs[:8]
        mixed_ref, kv_ref, x_ref = refs[8:]
        value = jnp.where(flag_ref[0] != 0, a_ref[...], b_ref[...])
        x_ref[...] = value
    normed, _ = layer_norm(value.astype(F32))
    mixed = (normed * gain_ref[...][None] + shift_ref[...][None] + lead_ref[...]).astype(BF)
    mixed_ref[...] = mixed
    width = mixed.shape[1]
    kv_ref[:, :width] = dot(mixed, wk_ref[...]).astype(BF)
    kv_ref[:, width:] = dot(mixed, wv_ref[...]).astype(BF)
    if own:
        q_ref[...] = dot(mixed, wq_ref[...]).astype(BF)


def project(flag, sources, gain, shift, lead, weights):
    own = flag is None
    rows, width = sources[0].shape
    block = math.gcd(rows, 256)
    row = pl.BlockSpec((block, width), lambda i: (i, 0))
    vector = pl.BlockSpec((width,), lambda i: (0,))

    def columns(group):
        return pl.BlockSpec((width, width), lambda i: (0, group))

    groups = (0, 1, 2) if own else (1, 2)
    return pl.pallas_call(
        functools.partial(project_kernel, own),
        grid=(rows // block,),
        in_specs=([] if own else [pl.BlockSpec(memory_space=pltpu.SMEM)])
        + [row] * len(sources)
        + [vector, vector, pl.BlockSpec((1, width), lambda i: (0, 0))]
        + [columns(g) for g in groups],
        out_specs=[row, pl.BlockSpec((block, 2 * width), lambda i: (i, 0)), row],
        out_shape=[
            jax.ShapeDtypeStruct((rows, width), BF),
            jax.ShapeDtypeStruct((rows, 2 * width), BF),
            jax.ShapeDtypeStruct((rows, width), BF),
        ],
        compiler_params=PARAMS,
        name="project",
        cost_estimate=pl.CostEstimate(
            flops=rows * width * width, transcendentals=0, bytes_accessed=rows * width
        ),
    )(*([] if own else [flag]), *sources, gain, shift, lead, *([weights] * len(groups)))


def attend_kernel(count, chained, final, *refs):
    q_ref = refs[0]
    k_refs = refs[1 : 1 + count]
    v_refs = refs[1 + count : 1 + 2 * count]
    o_ref, l_ref = refs[-2:]
    outs = []
    for h in range(2):
        part = slice(h * DH, h * DH + DH)
        q = q_ref[0, :, part]
        scores = [dot(k[0, :, part], q, NT) for k in k_refs]
        top = functools.reduce(
            jnp.maximum, [jnp.max(s, axis=0, keepdims=True) for s in scores]
        )
        top = top * SCALE_TWO
        total = None
        mixed = None
        for s, v in zip(scores, v_refs):
            raised = jnp.exp2(s * SCALE_TWO - top)
            some = jnp.sum(raised, axis=0, keepdims=True)
            term = dot(v[0, :, part], raised.astype(BF), TN)
            total = some if total is None else total + some
            mixed = term if mixed is None else mixed + term
        mixed = mixed * (1.0 / total)
        log = top + jnp.log2(total)
        if chained:
            before_ref, before_log_ref = refs[1 + 2 * count : 3 + 2 * count]
            before = before_log_ref[0, 0, h : h + 1, :]
            high = jnp.maximum(before, log)
            joint = high + jnp.log2(jnp.exp2(before - high) + jnp.exp2(log - high))
            mixed = mixed * jnp.exp2(log - joint) + before_ref[0, part, :] * jnp.exp2(
                before - joint
            )
            log = joint
        l_ref[0, 0, h : h + 1, :] = log
        if final:
            outs.append(mixed)
        else:
            o_ref[0, part, :] = mixed
    if final:
        o_ref[0] = jnp.concatenate(outs, axis=0).T.astype(BF)


def attend(queries, shards, before, final):
    frames, rows, width = queries.shape
    count = len(shards)
    keys = shards[0].shape[1]
    pairs = width // 128
    turned = pl.BlockSpec((1, 128, rows), lambda f, p: (f, p, 0))
    row = pl.BlockSpec((1, rows, 128), lambda f, p: (f, 0, p))
    log = pl.BlockSpec((1, 1, 2, rows), lambda f, p: (f, p, 0, 0))
    chained = before is not None
    return pl.pallas_call(
        functools.partial(attend_kernel, count, chained, final),
        grid=(frames, pairs),
        in_specs=[row]
        + [pl.BlockSpec((1, keys, 128), lambda f, p: (f, 0, p))] * count
        + [pl.BlockSpec((1, keys, 128), lambda f, p: (f, 0, p + pairs))] * count
        + ([turned, log] if chained else []),
        out_specs=[row if final else turned, log],
        out_shape=[
            jax.ShapeDtypeStruct((frames, rows, width), BF)
            if final
            else jax.ShapeDtypeStruct((frames, width, rows), F32),
            jax.ShapeDtypeStruct((frames, pairs, 2, rows), F32),
        ],
        compiler_params=PARAMS,
        name="attend",
        cost_estimate=pl.CostEstimate(
            flops=2 * frames * rows * count * keys * width,
            transcendentals=0,
            bytes_accessed=frames * rows * width,
        ),
    )(queries, *shards, *shards, *(before if chained else ()))


def column_sums(total, values):
    normed, _ = layer_norm(values.astype(F32))
    return jnp.concatenate(
        (
            jnp.sum(total * normed, axis=0, keepdims=True),
            jnp.sum(total, axis=0, keepdims=True),
        )
    )


def attend_back_kernel(
    q_ref,
    g_ref,
    o_ref,
    l_ref,
    k_ref,
    v_ref,
    wk_ref,
    wv_ref,
    x_ref,
    before_ref,
    dq_ref,
    dk_ref,
    dv_ref,
    term_ref,
    sums_ref,
):
    pair = pl.program_id(1)
    key_terms = []
    value_terms = []
    query_terms = []
    for h in range(2):
        part = slice(h * DH, h * DH + DH)
        q = q_ref[0, :, part]
        g = g_ref[0, :, part]
        k = k_ref[0, :, part]
        v = v_ref[0, :, part]
        product = g.astype(F32) * o_ref[0, :, part].astype(F32)
        high, low = split_two(product)
        ones = jnp.ones((8, DH), BF)
        delta = (dot(ones, high, NT) + dot(ones, low, NT))[0:1]
        probs = jnp.exp2(dot(k, q, NT) * SCALE_TWO - l_ref[0, 0, h : h + 1, :])
        grad_probs = dot(v, g, NT)
        grad_scores = (probs * (grad_probs - delta)).astype(BF)
        value_terms.append(dot(probs.astype(BF), g))
        key_terms.append(dot(grad_scores, q))
        grad_query = dot(k, grad_scores, TN) * SCALE + before_ref[0, part, :]
        query_terms.append(grad_query)
    grad_key = (jnp.concatenate(key_terms, axis=1) * SCALE).astype(BF)
    grad_value = jnp.concatenate(value_terms, axis=1).astype(BF)
    grad_query = jnp.concatenate(query_terms, axis=0).astype(dq_ref.dtype)
    lanes = pl.ds(pl.multiple_of(pair * 128, 128), 128)
    dk_ref[0, :, lanes] = grad_key
    dv_ref[0, :, lanes] = grad_value
    dq_ref[0] = grad_query

    @pl.when(pair == pl.num_programs(1) - 1)
    def _():
        total = dot(dk_ref[0], wk_ref[...], NT) + dot(dv_ref[0], wv_ref[...], NT)
        term_ref[0] = total.astype(term_ref.dtype)
        sums_ref[0] = column_sums(total, x_ref[0])


def attend_back(queries, grad_out, out, logs, shard, weights, source, before):
    frames, rows, width = queries.shape
    keys = shard.shape[1]
    pairs = width // 128
    row = pl.BlockSpec((1, rows, 128), lambda f, p: (f, 0, p))
    key = pl.BlockSpec((1, keys, 128), lambda f, p: (f, 0, p))
    value = pl.BlockSpec((1, keys, 128), lambda f, p: (f, 0, p + pairs))
    turned = pl.BlockSpec((1, 128, rows), lambda f, p: (f, p, 0))
    log = pl.BlockSpec((1, 1, 2, rows), lambda f, p: (f, p, 0, 0))

    def columns(group):
        return pl.BlockSpec((width, width), lambda f, p: (0, group))

    def whole(*shape):
        return pl.BlockSpec((1,) + shape, lambda f, p: (f, 0, 0))

    in_specs = [row, row, row, log, key, value, columns(1), columns(2), whole(keys, width)]
    operands = [queries, grad_out, out, logs, shard, shard, weights, weights, source]
    aliases = {len(operands): 0}
    in_specs.append(turned)
    operands.append(before)
    out_specs = [turned, whole(keys, width), whole(keys, width), whole(keys, width), whole(2, width)]
    out_shape = [
        jax.ShapeDtypeStruct((frames, width, rows), F32),
        jax.ShapeDtypeStruct((frames, keys, width), BF),
        jax.ShapeDtypeStruct((frames, keys, width), BF),
        jax.ShapeDtypeStruct((frames, keys, width), BF),
        jax.ShapeDtypeStruct((frames, 2, width), F32),
    ]
    return pl.pallas_call(
        attend_back_kernel,
        grid=(frames, pairs),
        in_specs=in_specs,
        out_specs=out_specs,
        out_shape=out_shape,
        input_output_aliases=aliases,
        compiler_params=PARAMS,
        name="attend_back",
        cost_estimate=pl.CostEstimate(
            flops=4 * frames * rows * keys * width,
            transcendentals=0,
            bytes_accessed=frames * rows * width,
        ),
    )(*operands)


def query_back_kernel(dq_ref, w_ref, x_ref, low_ref, term_ref, sums_ref):
    low = dq_ref[0].astype(BF)
    low_ref[0] = low
    total = dot(low, w_ref[...], (((0,), (1,)), ((), ())))
    term_ref[0] = total
    sums_ref[0] = column_sums(total, x_ref[0])


def query_back(grad_query, weights, source):
    frames, width, rows = grad_query.shape

    def whole(*shape):
        return pl.BlockSpec((1,) + shape, lambda f: (f, 0, 0))

    return pl.pallas_call(
        query_back_kernel,
        grid=(frames,),
        in_specs=[
            whole(width, rows),
            pl.BlockSpec((width, width), lambda f: (0, 0)),
            whole(rows, width),
        ],
        out_specs=[whole(width, rows), whole(rows, width), whole(2, width)],
        out_shape=[
            jax.ShapeDtypeStruct((frames, width, rows), BF),
            jax.ShapeDtypeStruct((frames, rows, width), F32),
            jax.ShapeDtypeStruct((frames, 2, width), F32),
        ],
        compiler_params=PARAMS,
        name="query_back",
        cost_estimate=pl.CostEstimate(
            flops=frames * rows * width * width, transcendentals=0, bytes_accessed=rows * width
        ),
    )(grad_query, weights, source)


def between_kernel(
    x_ref,
    att_ref,
    wo_ref,
    wu_ref,
    wd_ref,
    head_ref,
    gain_ref,
    shift_ref,
    bu_ref,
    bd_ref,
    mask_ref,
    sens_ref,
    one_ref,
    two_ref,
    hidden_ref,
    act_ref,
    up_ref,
    down_ref,
    final_ref,
    heads_ref,
    attn_ref,
    gres_ref,
    gatt_ref,
    first_ref,
    second_ref,
    added_ref,
    vec_ref,
    bup_ref,
    slope_ref,
):
    residual = x_ref[...].astype(F32) + dot(att_ref[...], wo_ref[...])
    normed, inverse = layer_norm(residual)
    gain = gain_ref[...][None]
    hidden = (normed * gain + shift_ref[...][None]).astype(BF)
    hidden_ref[...] = hidden
    wide = 512
    chunks = [slice(j, j + wide) for j in range(0, wu_ref.shape[1], wide)]
    final = residual + bd_ref[...][None]
    for part in chunks:
        up = dot(hidden, wu_ref[:, part]) + bu_ref[part][None]
        square = up * up
        tanh = jnp.tanh(ROOT * up * (1.0 + CUBE * square))
        half = 0.5 * (1.0 + tanh)
        act = (up * half).astype(BF)
        slope_ref[:, part] = half + 0.5 * up * (1.0 - tanh * tanh) * (
            ROOT + 3.0 * ROOT * CUBE * square
        )
        act_ref[:, part] = act
        final = final + dot(act, wd_ref[part, :])
    final_low = final.astype(BF)
    final_ref[...] = final_low
    logits = dot(final_low, head_ref[...], NT)
    one = logits[:, :128]
    two = logits[:, 128:256]
    offset = logits[:, 256:]
    top = jnp.maximum(one, two)
    one = jnp.exp(one - top)
    two = jnp.exp(two - top)
    total = one + two
    one = one / total
    two = two / total
    mask = mask_ref[0]
    first_ref[...] = mask * one + (1.0 - mask)
    second_ref[...] = mask * two
    added_ref[...] = mask * offset
    grad_one = mask * one_ref[...]
    grad_two = mask * two_ref[...]
    mean = one * grad_one + two * grad_two
    heads = jnp.concatenate(
        (one * (grad_one - mean), two * (grad_two - mean), mask * sens_ref[...]), axis=1
    ).astype(BF)
    heads_ref[...] = heads
    grad_final = dot(heads, head_ref[...])
    down = grad_final.astype(BF)
    down_ref[...] = down
    grad_hidden = None
    ups = []
    for part in chunks:
        grad_up = (dot(down, wd_ref[part, :], NT) * slope_ref[:, part]).astype(BF)
        up_ref[:, part] = grad_up
        ups.append(jnp.sum(grad_up.astype(F32), axis=0, keepdims=True))
        term = dot(grad_up, wu_ref[:, part], NT)
        grad_hidden = term if grad_hidden is None else grad_hidden + term
    grad_normed = grad_hidden * gain
    grad_residual = grad_final + norm_back(grad_normed, normed, inverse)
    gres_ref[...] = grad_residual
    attn = grad_residual.astype(BF)
    attn_ref[...] = attn
    gatt_ref[...] = dot(attn, wo_ref[...], NT).astype(BF)
    vectors = jnp.concatenate(
        (
            jnp.sum(grad_hidden * normed, axis=0, keepdims=True),
            jnp.sum(grad_hidden, axis=0, keepdims=True),
            jnp.sum(down.astype(F32), axis=0, keepdims=True),
        )
    )
    ups = jnp.concatenate(ups, axis=1)

    @pl.when(pl.program_id(0) == 0)
    def _():
        vec_ref[...] = vectors
        bup_ref[...] = ups

    @pl.when(pl.program_id(0) > 0)
    def _():
        vec_ref[...] += vectors
        bup_ref[...] += ups


def between(x, attended, w_out, w_up, w_down, heads, gain, shift, b_up, b_down, mask, sums, local):
    rows, width = x.shape
    hidden = w_up.shape[1]
    block = math.gcd(local, 256)

    def row(columns):
        return pl.BlockSpec((block, columns), lambda i: (i, 0))

    def whole(values):
        zeros = (0,) * values.ndim
        return pl.BlockSpec(values.shape, lambda i: zeros, pipeline_mode=pl.Buffered(1))

    def shape(columns, kind=BF):
        return jax.ShapeDtypeStruct((rows, columns), kind)

    fixed = [w_out, w_up, w_down, heads, gain, shift, b_up, b_down]
    return pl.pallas_call(
        between_kernel,
        grid=(rows // block,),
        in_specs=[row(width), row(width)]
        + [whole(v) for v in fixed]
        + [pl.BlockSpec((1, 1, 128), lambda i: (i * block // local, 0, 0))]
        + [row(128)] * 3,
        out_specs=[
            row(width),
            row(hidden),
            row(hidden),
            row(width),
            row(width),
            row(384),
            row(width),
            row(width),
            row(width),
            row(128),
            row(128),
            row(128),
            pl.BlockSpec((3, width), lambda i: (0, 0)),
            pl.BlockSpec((1, hidden), lambda i: (0, 0)),
        ],
        out_shape=[
            shape(width),
            shape(hidden),
            shape(hidden),
            shape(width),
            shape(width),
            shape(384),
            shape(width),
            shape(width, F32),
            shape(width),
            shape(128, F32),
            shape(128, F32),
            shape(128, F32),
            jax.ShapeDtypeStruct((3, width), F32),
            jax.ShapeDtypeStruct((1, hidden), F32),
        ],
        scratch_shapes=[pltpu.VMEM((block, hidden), F32)],
        compiler_params=PARAMS,
        name="between",
        cost_estimate=pl.CostEstimate(
            flops=rows * width * hidden, transcendentals=0, bytes_accessed=rows * hidden
        ),
    )(x, attended, *fixed, mask, *sums)


def deal(place, result, mine_ref, sent_ref):
    halves = result.reshape(mine_ref.shape[0], 2, *mine_ref.shape[1:]).astype(BF)
    low = halves[:, 0]
    high = halves[:, 1]
    even = place == 0
    mine_ref[...] = jnp.where(even, low, high)
    sent_ref[...] = jnp.where(even, high, low)


def columns_of(vectors, start):
    count = vectors.shape[0]
    place = lax.broadcasted_iota(jnp.int32, (count, 256), 1)
    which = lax.broadcasted_iota(jnp.int32, (count, 256), 0)
    chosen = (place == which + start).astype(F32).astype(BF)
    high, rest = split_two(vectors)
    return dot(high, chosen, TN) + dot(rest, chosen, TN)


def early_grads_kernel(
    place_ref,
    h_ref,
    a_ref,
    f_ref,
    up_ref,
    attn_ref,
    head_ref,
    vec_ref,
    mine_in_ref,
    sent_in_ref,
    mine_ref,
    sent_ref,
    turn_ref,
):
    step = pl.program_id(0)
    last = pl.num_programs(0) - 1
    place = place_ref[0]
    wide = up_ref.shape[1]

    @pl.when(step == 0)
    def _():
        turn_ref[...] = h_ref[...].T

    @pl.when(step < last - 1)
    def _():
        deal(place, dot(turn_ref[...], up_ref[...]), mine_ref, sent_ref)

    @pl.when(step == last - 1)
    def _():
        turned = a_ref[...].T
        turn_ref[...] = turned
        deal(place, dot(turned, attn_ref[:, :wide]), mine_ref, sent_ref)

    @pl.when(step == last)
    def _():
        out = dot(turn_ref[...], attn_ref[:, wide:])
        heads = dot(f_ref[...].T, head_ref[...]) + columns_of(vec_ref[...], 3 * RESULT_FIELDS)
        deal(place, jnp.concatenate((out, heads), axis=1), mine_ref, sent_ref)


def early_grads(place, hidden, attended, final, up, attn, heads, vectors, mine, sent):
    rows, width = hidden.shape
    wide = 512
    steps = up.shape[1] // wide + 2
    count = width // 96
    skip = mine.shape[2] // wide - steps

    def whole(values):
        return pl.BlockSpec(values.shape, lambda i: (0, 0))

    out = pl.BlockSpec((count, 48, wide), lambda i: (0, 0, i + skip))
    untouched = pl.BlockSpec(memory_space=pl.ANY)
    return pl.pallas_call(
        early_grads_kernel,
        grid=(steps,),
        in_specs=[
            pl.BlockSpec(memory_space=pltpu.SMEM),
            whole(hidden),
            whole(attended),
            whole(final),
            pl.BlockSpec((rows, wide), lambda i: (0, jnp.minimum(i, steps - 3))),
            whole(attn),
            whole(heads),
            whole(vectors),
            untouched,
            untouched,
        ],
        out_specs=[out, out],
        out_shape=[jax.ShapeDtypeStruct(mine.shape, BF)] * 2,
        input_output_aliases={8: 0, 9: 1},
        scratch_shapes=[pltpu.VMEM((width, rows), BF)],
        compiler_params=PARAMS,
        name="early_grads",
        cost_estimate=pl.CostEstimate(
            flops=2 * rows * width * wide * steps,
            transcendentals=0,
            bytes_accessed=2 * rows * wide * steps + 2 * width * wide * steps,
        ),
    )(place, hidden, attended, final, up, attn, heads, vectors, mine, sent)


def down_grads_kernel(place_ref, act_ref, down_ref, mine_ref, sent_ref):
    result = dot(act_ref[...], down_ref[...], TN).astype(BF)
    block = result.shape[0] // 2
    piece = block // 8
    halves = []
    for c in range(2):
        groups = [
            jnp.concatenate(
                [
                    result[c * block + y * 4 * piece + g * piece :][:piece]
                    for y in range(2)
                ],
                axis=0,
            )
            for g in range(4)
        ]
        halves.append(jnp.concatenate(groups, axis=1)[None])
    even = place_ref[0] == 0
    mine_ref[...] = jnp.where(even, halves[0], halves[1])
    sent_ref[...] = jnp.where(even, halves[1], halves[0])


def down_grads(place, activation, down, columns):
    rows, width = down.shape
    block = activation.shape[1] // 8
    piece = block // 16
    out = pl.BlockSpec((1, 2 * piece, 4 * width), lambda i: (i, 0, 0))
    return pl.pallas_call(
        down_grads_kernel,
        grid=(8,),
        in_specs=[
            pl.BlockSpec(memory_space=pltpu.SMEM),
            pl.BlockSpec((rows, block), lambda i: (0, i)),
            pl.BlockSpec((rows, width), lambda i: (0, 0)),
        ],
        out_specs=[out, out],
        out_shape=[jax.ShapeDtypeStruct((8, 2 * piece, columns), BF)] * 2,
        compiler_params=PARAMS,
        name="down_grads",
        cost_estimate=pl.CostEstimate(
            flops=2 * rows * width * block, transcendentals=0, bytes_accessed=width * block
        ),
    )(place, activation, down)


def late_grads_kernel(count, place_ref, *refs):
    mixed_refs = refs[:count]
    query_ref = refs[count]
    key_refs = refs[count + 1 : 2 * count + 1]
    value_refs = refs[2 * count + 1 : 3 * count + 1]
    vec_ref, mine_ref, sent_ref, turn_ref = refs[3 * count + 1 :]
    step = pl.program_id(0)
    third = (pl.num_programs(0) - 1) // 3
    place = place_ref[0]

    @pl.when(step == 0)
    def _():
        for s in range(count):
            turn_ref[s] = mixed_refs[s][...].T

    @pl.when(step < third)
    def _():
        deal(place, dot(turn_ref[0], query_ref[...], NT), mine_ref, sent_ref)

    def joint(parts):
        return sum(dot(turn_ref[s], parts[s][...]) for s in range(count))

    @pl.when((step >= third) & (step < 2 * third))
    def _():
        deal(place, joint(key_refs), mine_ref, sent_ref)

    @pl.when((step >= 2 * third) & (step < 3 * third))
    def _():
        deal(place, joint(value_refs), mine_ref, sent_ref)

    @pl.when(step == 3 * third)
    def _():
        deal(place, columns_of(vec_ref[...], 0), mine_ref, sent_ref)


def late_grads(place, mixed, query, keys, values, vectors):
    rows, width = mixed[0].shape
    count = len(mixed)
    wide = 256
    third = width // wide
    groups = width // 96

    def clipped(offset):
        return lambda i: (0, jnp.clip(i - offset, 0, third - 1))

    whole = pl.BlockSpec((rows, width), lambda i: (0, 0))
    out = pl.BlockSpec((groups, 48, wide), lambda i: (0, 0, i))
    return pl.pallas_call(
        functools.partial(late_grads_kernel, count),
        grid=(3 * third + 1,),
        in_specs=[pl.BlockSpec(memory_space=pltpu.SMEM)]
        + [whole] * count
        + [pl.BlockSpec((wide, rows), lambda i: (jnp.clip(i, 0, third - 1), 0))]
        + [pl.BlockSpec((rows, wide), clipped(third))] * count
        + [pl.BlockSpec((rows, wide), clipped(2 * third))] * count
        + [pl.BlockSpec(vectors.shape, lambda i: (0, 0))],
        out_specs=[out, out],
        out_shape=[jax.ShapeDtypeStruct((groups, 48, wide * (3 * third + 1)), BF)] * 2,
        scratch_shapes=[pltpu.VMEM((count, width, rows), BF)],
        compiler_params=PARAMS,
        name="late_grads",
        cost_estimate=pl.CostEstimate(
            flops=2 * rows * width * width * (2 * count + 1),
            transcendentals=0,
            bytes_accessed=2 * rows * width * 4 * count + 12 * width * width,
        ),
    )(place, *mixed, query, *keys, *values, vectors)


def block_sums_kernel(counts, dealt, where_ref, *refs):
    total_in = sum(len(group) for group in counts)
    ins, outs = refs[:total_in], refs[total_in:]
    at = 0
    for o, group in enumerate(counts):
        shape = ins[at].shape[-2:] if dealt else outs[o].shape
        value = None
        for use in group:
            term = ins[at][...].astype(F32).reshape(shape)
            if use is not None:
                term = jnp.where(use(pl.program_id(0), where_ref), term, 0.0)
            value = term if value is None else value + term
            at += 1
        if dealt:
            for k, out in enumerate(outs):

                @pl.when(pl.program_id(0) == k)
                def _(out=out, value=value, o=o):
                    out[o] = value.astype(BF)
        else:
            outs[o][...] = value.astype(BF)


def block_sums(where, steps, groups, dealt=False):
    counts = [[term[3] if len(term) > 3 else None for term in terms] for _, terms in groups]
    operands = [term[0] for _, terms in groups for term in terms]
    in_specs = [pl.BlockSpec(term[1], term[2]) for _, terms in groups for term in terms]
    if dealt:
        shape = (len(groups),) + groups[0][0]
        zeros = (0,) * len(shape)
        out_specs = [pl.BlockSpec(shape, lambda i, w: zeros)] * steps
        out_shape = [jax.ShapeDtypeStruct(shape, BF)] * steps
    else:
        out_specs = [pl.BlockSpec(out[1], out[2]) for out, _ in groups]
        out_shape = [jax.ShapeDtypeStruct(out[0], BF) for out, _ in groups]
    return pl.pallas_call(
        functools.partial(block_sums_kernel, counts, dealt),
        grid_spec=pltpu.PrefetchScalarGridSpec(
            num_scalar_prefetch=1, grid=(steps,), in_specs=in_specs, out_specs=out_specs
        ),
        out_shape=out_shape,
        compiler_params=PARAMS,
        name="block_sums",
        cost_estimate=pl.CostEstimate(flops=1 << 20, transcendentals=0, bytes_accessed=1 << 20),
    )(where, *operands)


class Reduction:
    def __init__(self, where, terms, by_columns):
        self.where = where
        self.terms = terms
        self.by_columns = by_columns
        self.depth, self.columns = terms[0].shape[3:]
        self.steps = 4 if by_columns else 2
        if by_columns:
            self.columns //= 2

    def at(self, part, x, z, y, sizes):
        block = sizes + (self.depth, self.columns)
        column = part if self.by_columns else 0
        shift = 0 if self.by_columns else 2 * part

        def index(i, w):
            return (x(w), z(i, w) + shift, y(w), 0, column)

        return [(t, block, index) for t in self.terms]

    def one(self):
        n, tail = self.steps, (self.depth, self.columns)
        ahead = lambda i, w: i
        sent = block_sums(
            self.where,
            n,
            [
                (
                    ((n, 2) + tail, (1, 2) + tail, lambda i, w: (i, 0, 0, 0)),
                    self.at(0, lambda w: 1 - w[0], ahead, lambda w: 0, (1, 1, 2)),
                ),
                (
                    ((2, n) + tail, (2, 1) + tail, lambda i, w: (0, i, 0, 0)),
                    self.at(1, lambda w: 0, ahead, lambda w: 1 - w[1], (2, 1, 1)),
                ),
            ],
        )
        return list(sent)

    def trade_one(self, sent):
        self.got_one = [swap(sent[0], "lat", 1), swap(sent[1], "grp", 2)]

    def two(self):
        n, tail = self.steps, (self.depth, self.columns)
        ahead = lambda i, w: i
        out = ((n,) + tail, (1,) + tail, lambda i, w: (i, 0, 0))
        flat = (1, 1) + tail
        sent = block_sums(
            self.where,
            n,
            [
                (
                    out,
                    self.at(0, lambda w: w[0], ahead, lambda w: 1 - w[1], (1, 1, 1))
                    + [(self.got_one[0], flat, lambda i, w: (i, 1 - w[1], 0, 0))],
                ),
                (
                    out,
                    self.at(1, lambda w: 1 - w[0], ahead, lambda w: w[1], (1, 1, 1))
                    + [(self.got_one[1], flat, lambda i, w: (1 - w[0], i, 0, 0))],
                ),
            ],
        )
        return list(sent)

    def trade_two(self, sent):
        self.got_two = [swap(sent[0], "grp", 2), swap(sent[1], "lat", 1)]

    def quarters(self):
        tail = (self.depth, self.columns)
        x = lambda w: w[0]
        y = lambda w: w[1]
        if self.by_columns:
            place = lambda i, w: w[2] ^ i
            groups = []
            for part in (0, 1):
                terms = self.at(part, x, place, y, (1, 1, 1))
                if part == 0:
                    one = lambda i, w: (w[2] ^ i, w[1], 0, 0)
                else:
                    one = lambda i, w: (w[0], w[2] ^ i, 0, 0)
                terms.append((self.got_one[part], (1, 1) + tail, one))
                terms.append((self.got_two[part], (1,) + tail, lambda i, w: (w[2] ^ i, 0, 0)))
                groups.append((tail, terms))
        else:
            low = lambda i, w: jnp.minimum(w[2] ^ i, 1)
            high = lambda i, w: jnp.maximum((w[2] ^ i) - 2, 0)
            first = lambda i, w: (w[2] ^ i) < 2
            second = lambda i, w: (w[2] ^ i) >= 2
            terms = self.at(0, x, lambda i, w: w[2] ^ i, y, (1, 1, 1))
            pair = (1, 1) + tail
            one = (1,) + tail
            terms += [
                (self.got_one[0], pair, lambda i, w: (low(i, w), w[1], 0, 0), first),
                (self.got_one[1], pair, lambda i, w: (w[0], high(i, w), 0, 0), second),
                (self.got_two[0], one, lambda i, w: (low(i, w), 0, 0), first),
                (self.got_two[1], one, lambda i, w: (high(i, w), 0, 0), second),
            ]
            groups = [(tail, terms)]
        return list(block_sums(self.where, 4, groups, True))


def early_unpack_kernel(place_ref, *refs):
    ins = refs[:4]
    down_ref, up_ref, out_ref, gate_ref, head_ref, gain_ref, bias_ref, bd_ref, bup_ref, misc_ref = refs[4:]
    width = down_ref.shape[1]
    hidden = up_ref.shape[1]
    for source, (c, y) in zip(ins, ((0, 0), (0, 1), (1, 0), (1, 1))):
        slot = jnp.bitwise_xor(place_ref[0], c) * 2 + jnp.bitwise_xor(place_ref[1], y)
        one = source[0].astype(F32)
        two = source[1].astype(F32)
        rows = one.shape[0]
        half = one.shape[1]
        for g in range(4):
            span = pl.ds(pl.multiple_of(slot * 4 * rows + g * rows, 8), rows)
            down_ref[span, :] = one[:, g * width : (g + 1) * width]
        span = pl.ds(pl.multiple_of(slot * rows, 8), rows)
        cut = half - 4 * width
        up_ref[span, :cut] = one[:, 4 * width :]
        up_ref[span, cut:] = two[:, : hidden - cut]
        out_ref[span, :] = two[:, hidden - cut : hidden - cut + width]
        misc_ref[span, :] = two[:, hidden - cut + width :]
    turned = misc_ref[...].T
    at = 0
    for ref in (gate_ref, head_ref, gain_ref, bias_ref, bd_ref, bup_ref):
        count = ref.shape[0]
        ref[...] = turned[at : at + count]
        at += count


def early_unpack(place, pieces, width, hidden):
    rows = pieces[0].shape[1]
    vmem = pl.BlockSpec(memory_space=pltpu.VMEM)
    return pl.pallas_call(
        early_unpack_kernel,
        in_specs=[pl.BlockSpec(memory_space=pltpu.SMEM)] + [vmem] * 4,
        out_specs=[vmem] * 9,
        out_shape=[
            jax.ShapeDtypeStruct((16 * rows, width), F32),
            jax.ShapeDtypeStruct((4 * rows, hidden), F32),
            jax.ShapeDtypeStruct((4 * rows, width), F32),
        ]
        + [
            jax.ShapeDtypeStruct((count, 4 * rows), F32)
            for count in (2 * RESULT_FIELDS, RESULT_FIELDS, 1, 1, 1, 4)
        ],
        scratch_shapes=[pltpu.VMEM((4 * rows, 256), F32)],
        compiler_params=PARAMS,
        name="early_unpack",
        cost_estimate=pl.CostEstimate(flops=1 << 20, transcendentals=0, bytes_accessed=1 << 20),
    )(place, *pieces)


def late_unpack_kernel(place_ref, *refs):
    ins = refs[:4]
    main_ref, gain_ref, bias_ref, lead_ref, misc_ref = refs[4:]
    for source, (c, y) in zip(ins, ((0, 0), (0, 1), (1, 0), (1, 1))):
        slot = jnp.bitwise_xor(place_ref[0], c) * 2 + jnp.bitwise_xor(place_ref[1], y)
        value = source[...].astype(F32)
        rows = value.shape[0]
        span = pl.ds(pl.multiple_of(slot * rows, 8), rows)
        main_ref[span, :] = value[:, : main_ref.shape[1]]
        misc_ref[span, :] = value[:, main_ref.shape[1] :]
    turned = misc_ref[...].T
    gain_ref[...] = turned[:1]
    bias_ref[...] = turned[1:2]
    lead_ref[...] = turned[2 : 2 + LEADS]


def late_unpack(place, pieces):
    rows, columns = pieces[0].shape
    vmem = pl.BlockSpec(memory_space=pltpu.VMEM)
    return pl.pallas_call(
        late_unpack_kernel,
        in_specs=[pl.BlockSpec(memory_space=pltpu.SMEM)] + [vmem] * 4,
        out_specs=[vmem] * 4,
        out_shape=[jax.ShapeDtypeStruct((4 * rows, columns - 256), F32)]
        + [jax.ShapeDtypeStruct((count, 4 * rows), F32) for count in (1, 1, LEADS)],
        scratch_shapes=[pltpu.VMEM((4 * rows, 256), F32)],
        compiler_params=PARAMS,
        name="late_unpack",
        cost_estimate=pl.CostEstimate(flops=1 << 20, transcendentals=0, bytes_accessed=1 << 20),
    )(place, *pieces)


def spread(rows, columns):
    pixel = lax.broadcasted_iota(jnp.int32, (rows, columns), 0)
    field = lax.broadcasted_iota(jnp.int32, (rows, columns), 1)
    return ((pixel // TILE_AREA) == field).astype(F32).astype(BF)


def split_two(values):
    high = values.astype(BF)
    return high, (values - high.astype(F32)).astype(BF)


def pixel_sums_kernel(f_ref, s_ref, sum_ref, first_ref, second_ref, field_ref):
    @pl.when(pl.program_id(0) == 0)
    def _():
        field_ref[...] = spread(*field_ref.shape)

    fields = field_ref[...]
    sens = s_ref[...]
    sum_ref[...] = dot(sens, fields)
    for e, out in ((0, first_ref), (1, second_ref)):
        out[...] = dot((sens.astype(F32) * f_ref[e].astype(F32)).astype(BF), fields)


def pixel_sums(forecasts, sensitivity):
    rows, pixels = sensitivity.shape
    block = math.gcd(rows, 128)
    out = pl.BlockSpec((block, 128), lambda i: (i, 0))
    return pl.pallas_call(
        pixel_sums_kernel,
        grid=(rows // block,),
        in_specs=[
            pl.BlockSpec((2, block, pixels), lambda i: (0, i, 0)),
            pl.BlockSpec((block, pixels), lambda i: (i, 0)),
        ],
        out_specs=[out] * 3,
        out_shape=[jax.ShapeDtypeStruct((rows, 128), F32)] * 3,
        scratch_shapes=[pltpu.VMEM((pixels, 128), BF)],
        compiler_params=PARAMS,
        name="pixel_sums",
        cost_estimate=pl.CostEstimate(
            flops=rows * pixels * 128, transcendentals=0, bytes_accessed=rows * pixels
        ),
    )(forecasts, sensitivity)


def blend_kernel(a_ref, b_ref, c_ref, f_ref, out_ref, field_ref):
    @pl.when(pl.program_id(0) == 0)
    def _():
        columns = field_ref.shape[1]
        field = lax.broadcasted_iota(jnp.int32, (256, columns), 0)
        pixel = lax.broadcasted_iota(jnp.int32, (256, columns), 1)
        field_ref[...] = ((pixel // TILE_AREA) == (field % 128)).astype(F32).astype(BF)

    fields = field_ref[...]

    def wide(ref):
        return dot(jnp.concatenate(split_two(ref[...]), axis=1), fields)

    total = wide(a_ref) * f_ref[0].astype(F32) + wide(b_ref) * f_ref[1].astype(F32)
    out_ref[...] = (total + wide(c_ref)).astype(BF)


def blend(first, second, added, forecasts):
    _, rows, pixels = forecasts.shape
    block = math.gcd(rows, 128)
    thin = pl.BlockSpec((block, 128), lambda i: (i, 0))
    return pl.pallas_call(
        blend_kernel,
        grid=(rows // block,),
        in_specs=[thin] * 3 + [pl.BlockSpec((2, block, pixels), lambda i: (0, i, 0))],
        out_specs=pl.BlockSpec((block, pixels), lambda i: (i, 0)),
        out_shape=jax.ShapeDtypeStruct((rows, pixels), BF),
        scratch_shapes=[pltpu.VMEM((256, pixels), BF)],
        compiler_params=PARAMS,
        name="blend",
        cost_estimate=pl.CostEstimate(
            flops=rows * pixels * 128, transcendentals=0, bytes_accessed=rows * pixels
        ),
    )(first, second, added, forecasts)


def swap(values, axis, bit):
    count = lax.axis_size(axis)
    return lax.ppermute(values, axis, [(i, i ^ bit) for i in range(count)])


def add(*terms):
    return sum(t.astype(F32) for t in terms).astype(BF)


def hold(*values):
    return lax.optimization_barrier(values)


def layer_norm(values):
    centred = values - jnp.mean(values, axis=-1, keepdims=True)
    inverse = lax.rsqrt(jnp.mean(centred * centred, axis=-1, keepdims=True) + EPSILON)
    return centred * inverse, inverse


def norm_back(grad_normed, normed, inverse):
    return inverse * (
        grad_normed
        - jnp.mean(grad_normed, axis=-1, keepdims=True)
        - normed * jnp.mean(grad_normed * normed, axis=-1, keepdims=True)
    )


def pad_lanes(values):
    return jnp.pad(values, ((0, 0), (0, 128 - values.shape[1])))


def per_device(
    layer_source_tensor,
    horizon_class,
    field_selector,
    model_predictions,
    loss_sensitivity,
    gain_one,
    shift_one,
    horizon_vectors,
    w_qkv,
    w_out,
    gain_two,
    shift_two,
    w_up,
    b_up,
    w_down,
    b_down,
    w_gate,
    w_bias,
):
    frames, lat_rows, lon_cols, width = layer_source_tensor.shape
    local = lat_rows * lon_cols
    rows = frames * local
    pixels = loss_sensitivity.shape[-1]
    sizes = (lax.axis_size("grp"), lax.axis_size("lat"), lax.axis_size("lon"))
    small = sizes == (4, 2, 4) and frames == 1

    source = layer_source_tensor.reshape(frames, local, width)
    place = lax.axis_index("lon")
    edge = (place == 0) | (place == lax.axis_size("lon") - 1)
    send = functools.partial(lax.ppermute, axis_name="lon")
    if small:
        right = send(source, perm=[(0, 1), (1, 2), (2, 3)])
        left = send(source, perm=[(3, 2), (2, 1), (1, 0)])
    else:
        shards = [lax.all_gather(source, "lon", axis=1, tiled=True)]

    forecasts = jnp.transpose(model_predictions.reshape(rows, 2, pixels), (1, 0, 2))
    sensitivity = loss_sensitivity.reshape(rows, pixels)

    onehot = (horizon_class[:, None] == jnp.arange(LEADS, dtype=jnp.int32)[None, :]).astype(F32)
    lead_rows = jnp.dot(onehot, horizon_vectors, precision=HIGH)

    def mixed_of(values):
        normed, _ = layer_norm(values.astype(F32))
        return (normed * gain_one + shift_one + lead_rows[:, None, :]).astype(BF)

    wq = w_qkv[:, :width]
    wkv = w_qkv[:, width:]

    def keys_of(values):
        return dot(values.reshape(-1, width), wkv).astype(BF).reshape(frames, -1, 2 * width)

    if small:

        def flat(values):
            return values.reshape(rows, width)

        def shard_of(flag, yes, no):
            m, kv, x = project(
                flag.astype(jnp.int32)[None],
                [flat(yes), flat(no)],
                gain_one,
                shift_one,
                lead_rows,
                w_qkv,
            )
            return m, kv[None], x[None]

        mixed_own, own_kv, queries = project(
            None, [flat(source)], gain_one, shift_one, lead_rows, w_qkv
        )
        queries = queries[None]
        mixed = [mixed_own]
        key_value = [own_kv[None]]
        right, left, forecasts, queries, key_value[0] = hold(
            right, left, forecasts, queries, key_value[0]
        )
        right_two = send(right, perm=[(1, 2), (2, 3)])
        left_two = send(left, perm=[(2, 1), (1, 0)])
        sums = pixel_sums(forecasts, sensitivity)
        m, kv, near = shard_of(place == 0, left, right)
        mixed.append(m)
        right_two, left_two, kv, *sums = hold(right_two, left_two, kv, *sums)
        key_value.append(kv)
        two = right_two + left_two
        two, middle = hold(two, left)
        three = send(two, perm=[(2, 3), (1, 0)])
        m, kv, middle = shard_of(edge, two, middle)
        mixed.append(m)
        key_value.append(kv)
        state = attend(queries, key_value, None, False)
        three, *state = hold(three, *state)
        m, kv, far = shard_of(edge, three, two)
        mixed.append(m)
        key_value.append(kv)
        attended, logs = attend(queries, key_value[3:], state, True)
        shards = [source, near, middle, far]
    else:
        mixed_own = mixed_of(source)
        queries = dot(mixed_own.reshape(rows, width), wq).astype(BF)
        queries = queries.reshape(frames, local, width)
        sums = pixel_sums(forecasts, sensitivity)
        mixed = [mixed_of(shards[0])]
        key_value = [keys_of(mixed[0])]
        attended, logs = attend(queries, key_value, None, True)
    inputs = source.reshape(rows, width)
    attended_low = attended.reshape(rows, width)
    both = w_gate.T
    head_rows = jnp.concatenate(
        [
            jnp.pad(m, ((0, 128 - RESULT_FIELDS), (0, 0)))
            for m in (both[:RESULT_FIELDS], both[RESULT_FIELDS:], w_bias.T)
        ]
    )
    mask = pad_lanes(field_selector.astype(F32))[:, None]
    (
        hidden_low,
        activation_low,
        up_low,
        down_low,
        final_low,
        heads_low,
        attn_low,
        grad_residual,
        grad_attended,
        *blending,
        early_vectors,
        grad_bup,
    ) = between(
        inputs,
        attended_low,
        w_out,
        w_up,
        w_down,
        head_rows,
        gain_two,
        shift_two,
        b_up,
        b_down,
        mask,
        sums,
        local,
    )
    grad_attended = grad_attended.reshape(frames, local, width)
    fields = 3 * RESULT_FIELDS
    heads_low = jnp.concatenate(
        [heads_low[:, g * 128 : g * 128 + RESULT_FIELDS] for g in range(3)], axis=1
    )
    inputs = inputs.astype(F32)
    normed_one, inverse_one = layer_norm(inputs)

    def input_gradient(grad_mixed):
        return grad_residual + norm_back(
            grad_mixed.reshape(rows, width) * gain_one, normed_one, inverse_one
        )

    def back(shard, place, before):
        return attend_back(queries, grad_attended, attended, logs, shard, w_qkv, place, before)

    nothing = jnp.zeros((frames, width, local), F32)

    def late_vectors(sums):
        gain_column = sum(jnp.sum(s[:, 0], axis=0) for s in sums)
        column = sum(s[:, 1] for s in sums)
        lead = jnp.dot(onehot.T, column, precision=HIGH)
        zeros = jnp.zeros((6, width), F32)
        return jnp.concatenate((gain_column[None], jnp.sum(column, axis=0)[None], lead, zeros))

    if small:
        bup_rows = jnp.swapaxes(grad_bup.reshape(8, 4, -1), 0, 1).reshape(4, width)
        early_vectors = jnp.concatenate(
            (early_vectors, bup_rows, jnp.zeros((1, width), F32))
        )
        core = (lax.axis_index("grp") % 2).astype(jnp.int32)[None]
        where = jnp.stack(
            (lax.axis_index("lat"), lax.axis_index("grp") // 2, lax.axis_index("lon"))
        ).astype(jnp.int32)
        hidden = w_up.shape[1]
        mine, sent = down_grads(core, activation_low, down_low, 2 * hidden + width + 256)
        mine, sent = early_grads(
            core,
            hidden_low,
            attended_low,
            final_low,
            up_low,
            attn_low,
            jnp.pad(heads_low, ((0, 0), (0, 256 - fields))),
            early_vectors,
            mine,
            sent,
        )
        grad_attended, sent = hold(grad_attended, sent)
        got = swap(sent, "grp", 1)

        grad_query, dk3, dv3, far, sums3 = back(key_value[3], shards[3], nothing)
        early = Reduction(where, [t.reshape(2, 4, 2, 24, -1) for t in (mine, got)], True)
        grad_query, far, *sent = hold(grad_query, far, *early.one())
        got = send(far, perm=[(0, 1), (3, 2)])
        early.trade_one(sent)

        grad_query, dk2, dv2, middle, sums2 = back(key_value[2], shards[2], grad_query)
        value = jnp.where(edge, middle, add(got, far))
        grad_query, value = hold(grad_query, value)
        right = send(value, perm=[(0, 1), (1, 2)])
        left = send(value, perm=[(3, 2), (2, 1)])

        grad_query, dk1, dv1, near, sums1 = back(key_value[1], shards[1], grad_query)
        forth = jnp.where(place == 0, near, add(right, middle))
        back_value = add(left, near)
        grad_query, forth, back_value, *sent = hold(
            grad_query, forth, back_value, *early.two()
        )
        right = send(forth, perm=[(0, 1), (1, 2), (2, 3)])
        left = send(back_value, perm=[(3, 2), (2, 1), (1, 0)])
        early.trade_two(sent)

        grad_query, dk0, dv0, own, sums0, right, left, *early.got_two = hold(
            *back(key_value[0], shards[0], grad_query), right, left, *early.got_two
        )
        query_low, query_term, query_sums = query_back(grad_query, w_qkv, source)
        vectors = late_vectors([sums0, sums1, sums2, sums3, query_sums])
        late_mine, late_sent = late_grads(
            core,
            [m.reshape(rows, width) for m in mixed],
            query_low.reshape(width, rows),
            [d.reshape(rows, width) for d in (dk0, dk1, dk2, dk3)],
            [d.reshape(rows, width) for d in (dv0, dv1, dv2, dv3)],
            vectors,
        )
        late_mine, late_sent, *early.got_two, own = hold(
            late_mine, late_sent, *early.got_two, own
        )
        got = swap(late_sent, "grp", 1)
        got, *parts = hold(got, *early.quarters())
        late = Reduction(where, [t.reshape(2, 4, 2, 24, -1) for t in (late_mine, got)], False)
        *sent, one, two, three = hold(*late.one(), *blending)
        late.trade_one(sent)
        early = [parts[0]] + [swap(parts[k], "lon", k) for k in (1, 2, 3)]
        blended = blend(one, two, three, forecasts)
        *late.got_one, blended = hold(*late.got_one, blended)
        *sent, own, early[0] = hold(*late.two(), own, early[0])
        late.trade_two(sent)
        grad_input = input_gradient(
            own.astype(F32) + query_term + right.astype(F32) + left.astype(F32)
        )
        early = add(*early)
        *late.got_two, early, grad_input = hold(*late.got_two, early, grad_input)
        early, *parts = hold(early, *late.quarters())
        late = [parts[0]] + [swap(parts[k], "lon", k) for k in (1, 2, 3)]
        early_y = swap(early, "grp", 2)
        early_c = swap(early, "grp", 1)
        early_y, early_c, early, *late = hold(early_y, early_c, early, *late)
        early_yc = swap(early_y, "grp", 1)
        late = add(*[part[0] for part in late])
        late_y = swap(late, "grp", 2)
        late_c = swap(late, "grp", 1)
        late_y, late_c, late, early_yc = hold(late_y, late_c, late, early_yc)
        place_two = jnp.stack((lax.axis_index("grp") % 2, lax.axis_index("grp") // 2))
        place_two = place_two.astype(jnp.int32)
        down_sum, up_sum, out_sum, gate_sum, head_sum, *early, bup_sum = early_unpack(
            place_two, [early, early_y, early_c, early_yc], width, hidden
        )
        late_yc = swap(late_y, "grp", 1)
        late_yc, gate_sum = hold(late_yc, gate_sum)
        qkv_sum, *late, lead_sum = late_unpack(place_two, [late, late_y, late_c, late_yc])
        early = [e.reshape(-1) for e in early]
        late = [e.reshape(-1) for e in late]
        bup_sum = bup_sum.reshape(-1)
        gate_sum = gate_sum.T
        head_sum = head_sum.T
    else:
        blended = blend(*blending, forecasts)
        grad_query, dk, dv, term, sums = back(key_value[0], shards[0], nothing)
        query_low, query_term, query_sums = query_back(grad_query, w_qkv, source)
        grad_input = input_gradient(
            query_term + lax.psum_scatter(term.astype(F32), "lon", scatter_dimension=1, tiled=True)
        )

        def total_of(values, dim=0):
            share = lax.psum_scatter(values, ("lat", "lon"), scatter_dimension=dim, tiled=True)
            return lax.psum(share, "grp")

        flat = mixed[0].reshape(-1, width)
        qkv_sum = total_of(
            jnp.concatenate(
                (
                    jnp.einsum("frd,fer->de", mixed_own, query_low, preferred_element_type=F32),
                    dot(flat, dk.reshape(-1, width), TN),
                    dot(flat, dv.reshape(-1, width), TN),
                ),
                axis=1,
            )
        )
        up_sum = total_of(dot(hidden_low, up_low, TN))
        out_sum = total_of(dot(attended_low, attn_low, TN))
        down_sum = total_of(dot(activation_low, down_low, TN))
        heads = total_of(dot(final_low, heads_low, TN))
        late = total_of(late_vectors([sums, query_sums])[: 2 + LEADS], 1)
        lead_sum = late[2:]
        gate_sum = heads[:, : 2 * RESULT_FIELDS]
        head_sum = heads[:, 2 * RESULT_FIELDS :]
        early = total_of(early_vectors, 1)
        bup_sum = total_of(grad_bup[0])

    return (
        blended.reshape(frames, lat_rows, lon_cols, pixels),
        grad_input.reshape(frames, lat_rows, lon_cols, width),
        late[0],
        late[1],
        lead_sum,
        qkv_sum,
        out_sum,
        early[0],
        early[1],
        up_sum,
        bup_sum,
        down_sum,
        early[2],
        gate_sum,
        head_sum,
    )


def solution(mesh):
    frame = ("grp", "lat")
    share = ("lat", "lon")
    image = P(frame, None, "lon", None)
    in_specs = (
        image,
        P(frame),
        P(frame, None),
        P(frame, None, "lon", None, None),
        image,
    ) + (P(),) * 13
    vector = P(share)
    matrix = P(share, None)
    out_specs = (
        image,
        image,
        vector,
        vector,
        P(None, share),
        matrix,
        matrix,
        vector,
        vector,
        matrix,
        vector,
        matrix,
        vector,
        matrix,
        matrix,
    )
    return jax.shard_map(
        per_device, mesh=mesh, in_specs=in_specs, out_specs=out_specs, check_vma=False
    )
```

```python
import functools
import math

import jax
import jax.numpy as jnp
from jax import lax
from jax.experimental import pallas as pl
from jax.experimental.pallas import tpu as pltpu
from jax.sharding import PartitionSpec as P

H = 12
DH = 64
RESULT_FIELDS = 69
TILE_AREA = 64
LEADS = 24
EPSILON = 1e-06
HIGH = lax.Precision.HIGHEST
SCALE = 0.125
SCALE_TWO = SCALE * math.log2(math.e)
ROOT = math.sqrt(2.0 / math.pi)
CUBE = 0.044715
NN = (((1,), (0,)), ((), ()))
NT = (((1,), (1,)), ((), ()))
TN = (((0,), (0,)), ((), ()))
BF = jnp.bfloat16
F32 = jnp.float32
PARAMS = pltpu.CompilerParams(vmem_limit_bytes=60 * 1024 * 1024)
FULL = pltpu.CompilerParams(vmem_limit_bytes=63 * 1024 * 1024 + 512 * 1024)


def dot(left, right, dims=NN):
    return lax.dot_general(left, right, dims, preferred_element_type=F32)


def project_kernel(own, *refs):
    if own:
        a_ref, gain_ref, shift_ref, lead_ref, wq_ref, wk_ref, wv_ref, mixed_ref, kv_ref, q_ref = refs
        value = a_ref[...]
    else:
        flag_ref, a_ref, b_ref, gain_ref, shift_ref, lead_ref, wk_ref, wv_ref = refs[:8]
        mixed_ref, kv_ref, x_ref = refs[8:]
        value = jnp.where(flag_ref[0] != 0, a_ref[...], b_ref[...])
        x_ref[...] = value
    normed, _ = layer_norm(value.astype(F32))
    mixed = (normed * gain_ref[...][None] + shift_ref[...][None] + lead_ref[...]).astype(BF)
    mixed_ref[...] = mixed
    width = mixed.shape[1]
    kv_ref[:, :width] = dot(mixed, wk_ref[...]).astype(BF)
    kv_ref[:, width:] = dot(mixed, wv_ref[...]).astype(BF)
    if own:
        q_ref[...] = dot(mixed, wq_ref[...]).astype(BF)


def project(flag, sources, gain, shift, lead, weights):
    own = flag is None
    rows, width = sources[0].shape
    block = math.gcd(rows, 256)
    row = pl.BlockSpec((block, width), lambda i: (i, 0))
    vector = pl.BlockSpec((width,), lambda i: (0,))

    def columns(group):
        return pl.BlockSpec((width, width), lambda i: (0, group))

    groups = (0, 1, 2) if own else (1, 2)
    return pl.pallas_call(
        functools.partial(project_kernel, own),
        grid=(rows // block,),
        in_specs=([] if own else [pl.BlockSpec(memory_space=pltpu.SMEM)])
        + [row] * len(sources)
        + [vector, vector, pl.BlockSpec((1, width), lambda i: (0, 0))]
        + [columns(g) for g in groups],
        out_specs=[row, pl.BlockSpec((block, 2 * width), lambda i: (i, 0)), row],
        out_shape=[
            jax.ShapeDtypeStruct((rows, width), BF),
            jax.ShapeDtypeStruct((rows, 2 * width), BF),
            jax.ShapeDtypeStruct((rows, width), BF),
        ],
        compiler_params=PARAMS,
        name="project",
        cost_estimate=pl.CostEstimate(
            flops=rows * width * width, transcendentals=0, bytes_accessed=rows * width
        ),
    )(*([] if own else [flag]), *sources, gain, shift, lead, *([weights] * len(groups)))


def attend_kernel(count, chained, final, *refs):
    q_ref = refs[0]
    k_refs = refs[1 : 1 + count]
    v_refs = refs[1 + count : 1 + 2 * count]
    o_ref, l_ref = refs[-2:]
    outs = []
    for h in range(2):
        part = slice(h * DH, h * DH + DH)
        q = q_ref[0, :, part]
        scores = [dot(k[0, :, part], q, NT) for k in k_refs]
        top = functools.reduce(
            jnp.maximum, [jnp.max(s, axis=0, keepdims=True) for s in scores]
        )
        top = top * SCALE_TWO
        total = None
        mixed = None
        for s, v in zip(scores, v_refs):
            raised = jnp.exp2(s * SCALE_TWO - top)
            some = jnp.sum(raised, axis=0, keepdims=True)
            term = dot(v[0, :, part], raised.astype(BF), TN)
            total = some if total is None else total + some
            mixed = term if mixed is None else mixed + term
        mixed = mixed * (1.0 / total)
        log = top + jnp.log2(total)
        if chained:
            before_ref, before_log_ref = refs[1 + 2 * count : 3 + 2 * count]
            before = before_log_ref[0, 0, h : h + 1, :]
            high = jnp.maximum(before, log)
            joint = high + jnp.log2(jnp.exp2(before - high) + jnp.exp2(log - high))
            mixed = mixed * jnp.exp2(log - joint) + before_ref[0, part, :] * jnp.exp2(
                before - joint
            )
            log = joint
        l_ref[0, 0, h : h + 1, :] = log
        if final:
            outs.append(mixed)
        else:
            o_ref[0, part, :] = mixed
    if final:
        o_ref[0] = jnp.concatenate(outs, axis=0).T.astype(BF)


def attend(queries, shards, before, final):
    frames, rows, width = queries.shape
    count = len(shards)
    keys = shards[0].shape[1]
    pairs = width // 128
    turned = pl.BlockSpec((1, 128, rows), lambda f, p: (f, p, 0))
    row = pl.BlockSpec((1, rows, 128), lambda f, p: (f, 0, p))
    log = pl.BlockSpec((1, 1, 2, rows), lambda f, p: (f, p, 0, 0))
    chained = before is not None
    return pl.pallas_call(
        functools.partial(attend_kernel, count, chained, final),
        grid=(frames, pairs),
        in_specs=[row]
        + [pl.BlockSpec((1, keys, 128), lambda f, p: (f, 0, p))] * count
        + [pl.BlockSpec((1, keys, 128), lambda f, p: (f, 0, p + pairs))] * count
        + ([turned, log] if chained else []),
        out_specs=[row if final else turned, log],
        out_shape=[
            jax.ShapeDtypeStruct((frames, rows, width), BF)
            if final
            else jax.ShapeDtypeStruct((frames, width, rows), F32),
            jax.ShapeDtypeStruct((frames, pairs, 2, rows), F32),
        ],
        compiler_params=PARAMS,
        name="attend",
        cost_estimate=pl.CostEstimate(
            flops=2 * frames * rows * count * keys * width,
            transcendentals=0,
            bytes_accessed=frames * rows * width,
        ),
    )(queries, *shards, *shards, *(before if chained else ()))


def column_sums(total, values):
    normed, _ = layer_norm(values.astype(F32))
    return jnp.concatenate(
        (
            jnp.sum(total * normed, axis=0, keepdims=True),
            jnp.sum(total, axis=0, keepdims=True),
        )
    )


def attend_back_kernel(
    q_ref,
    g_ref,
    o_ref,
    l_ref,
    k_ref,
    v_ref,
    wk_ref,
    wv_ref,
    x_ref,
    before_ref,
    dq_ref,
    dk_ref,
    dv_ref,
    term_ref,
    sums_ref,
):
    pair = pl.program_id(1)
    key_terms = []
    value_terms = []
    query_terms = []
    for h in range(2):
        part = slice(h * DH, h * DH + DH)
        q = q_ref[0, :, part]
        g = g_ref[0, :, part]
        k = k_ref[0, :, part]
        v = v_ref[0, :, part]
        product = g.astype(F32) * o_ref[0, :, part].astype(F32)
        high, low = split_two(product)
        ones = jnp.ones((8, DH), BF)
        delta = (dot(ones, high, NT) + dot(ones, low, NT))[0:1]
        probs = jnp.exp2(dot(k, q, NT) * SCALE_TWO - l_ref[0, 0, h : h + 1, :])
        grad_probs = dot(v, g, NT)
        grad_scores = (probs * (grad_probs - delta)).astype(BF)
        value_terms.append(dot(probs.astype(BF), g))
        key_terms.append(dot(grad_scores, q))
        grad_query = dot(k, grad_scores, TN) * SCALE + before_ref[0, part, :]
        query_terms.append(grad_query)
    grad_key = (jnp.concatenate(key_terms, axis=1) * SCALE).astype(BF)
    grad_value = jnp.concatenate(value_terms, axis=1).astype(BF)
    grad_query = jnp.concatenate(query_terms, axis=0).astype(dq_ref.dtype)
    lanes = pl.ds(pl.multiple_of(pair * 128, 128), 128)
    dk_ref[0, :, lanes] = grad_key
    dv_ref[0, :, lanes] = grad_value
    dq_ref[0] = grad_query

    @pl.when(pair == pl.num_programs(1) - 1)
    def _():
        total = dot(dk_ref[0], wk_ref[...], NT) + dot(dv_ref[0], wv_ref[...], NT)
        term_ref[0] = total.astype(term_ref.dtype)
        sums_ref[0] = column_sums(total, x_ref[0])


def attend_back(queries, grad_out, out, logs, shard, weights, source, before):
    frames, rows, width = queries.shape
    keys = shard.shape[1]
    pairs = width // 128
    row = pl.BlockSpec((1, rows, 128), lambda f, p: (f, 0, p))
    key = pl.BlockSpec((1, keys, 128), lambda f, p: (f, 0, p))
    value = pl.BlockSpec((1, keys, 128), lambda f, p: (f, 0, p + pairs))
    turned = pl.BlockSpec((1, 128, rows), lambda f, p: (f, p, 0))
    log = pl.BlockSpec((1, 1, 2, rows), lambda f, p: (f, p, 0, 0))

    def columns(group):
        return pl.BlockSpec((width, width), lambda f, p: (0, group))

    def whole(*shape):
        return pl.BlockSpec((1,) + shape, lambda f, p: (f, 0, 0))

    in_specs = [row, row, row, log, key, value, columns(1), columns(2), whole(keys, width)]
    operands = [queries, grad_out, out, logs, shard, shard, weights, weights, source]
    aliases = {len(operands): 0}
    in_specs.append(turned)
    operands.append(before)
    out_specs = [turned, whole(keys, width), whole(keys, width), whole(keys, width), whole(2, width)]
    out_shape = [
        jax.ShapeDtypeStruct((frames, width, rows), F32),
        jax.ShapeDtypeStruct((frames, keys, width), BF),
        jax.ShapeDtypeStruct((frames, keys, width), BF),
        jax.ShapeDtypeStruct((frames, keys, width), BF),
        jax.ShapeDtypeStruct((frames, 2, width), F32),
    ]
    return pl.pallas_call(
        attend_back_kernel,
        grid=(frames, pairs),
        in_specs=in_specs,
        out_specs=out_specs,
        out_shape=out_shape,
        input_output_aliases=aliases,
        compiler_params=PARAMS,
        name="attend_back",
        cost_estimate=pl.CostEstimate(
            flops=4 * frames * rows * keys * width,
            transcendentals=0,
            bytes_accessed=frames * rows * width,
        ),
    )(*operands)


def query_back_kernel(dq_ref, w_ref, x_ref, low_ref, term_ref, sums_ref):
    low = dq_ref[0].astype(BF)
    low_ref[0] = low
    total = dot(low, w_ref[...], (((0,), (1,)), ((), ())))
    term_ref[0] = total
    sums_ref[0] = column_sums(total, x_ref[0])


def query_back(grad_query, weights, source):
    frames, width, rows = grad_query.shape

    def whole(*shape):
        return pl.BlockSpec((1,) + shape, lambda f: (f, 0, 0))

    return pl.pallas_call(
        query_back_kernel,
        grid=(frames,),
        in_specs=[
            whole(width, rows),
            pl.BlockSpec((width, width), lambda f: (0, 0)),
            whole(rows, width),
        ],
        out_specs=[whole(width, rows), whole(rows, width), whole(2, width)],
        out_shape=[
            jax.ShapeDtypeStruct((frames, width, rows), BF),
            jax.ShapeDtypeStruct((frames, rows, width), F32),
            jax.ShapeDtypeStruct((frames, 2, width), F32),
        ],
        compiler_params=PARAMS,
        name="query_back",
        cost_estimate=pl.CostEstimate(
            flops=frames * rows * width * width, transcendentals=0, bytes_accessed=rows * width
        ),
    )(grad_query, weights, source)


def between_kernel(
    x_ref,
    att_ref,
    wo_ref,
    wu_ref,
    wd_ref,
    head_ref,
    gain_ref,
    shift_ref,
    bu_ref,
    bd_ref,
    mask_ref,
    sens_ref,
    one_ref,
    two_ref,
    hidden_ref,
    act_ref,
    up_ref,
    down_ref,
    final_ref,
    heads_ref,
    attn_ref,
    gres_ref,
    gatt_ref,
    first_ref,
    second_ref,
    added_ref,
    vec_ref,
    bup_ref,
    slope_ref,
):
    residual = x_ref[...].astype(F32) + dot(att_ref[...], wo_ref[...])
    normed, inverse = layer_norm(residual)
    gain = gain_ref[...][None]
    hidden = (normed * gain + shift_ref[...][None]).astype(BF)
    hidden_ref[...] = hidden
    wide = 512
    chunks = [slice(j, j + wide) for j in range(0, wu_ref.shape[1], wide)]
    final = residual + bd_ref[...][None]
    for part in chunks:
        up = dot(hidden, wu_ref[:, part]) + bu_ref[part][None]
        square = up * up
        tanh = jnp.tanh(ROOT * up * (1.0 + CUBE * square))
        half = 0.5 * (1.0 + tanh)
        act = (up * half).astype(BF)
        slope_ref[:, part] = half + 0.5 * up * (1.0 - tanh * tanh) * (
            ROOT + 3.0 * ROOT * CUBE * square
        )
        act_ref[:, part] = act
        final = final + dot(act, wd_ref[part, :])
    final_low = final.astype(BF)
    final_ref[...] = final_low
    logits = dot(final_low, head_ref[...], NT)
    one = logits[:, :128]
    two = logits[:, 128:256]
    offset = logits[:, 256:]
    top = jnp.maximum(one, two)
    one = jnp.exp(one - top)
    two = jnp.exp(two - top)
    total = one + two
    one = one / total
    two = two / total
    mask = mask_ref[0]
    first_ref[...] = mask * one + (1.0 - mask)
    second_ref[...] = mask * two
    added_ref[...] = mask * offset
    grad_one = mask * one_ref[...]
    grad_two = mask * two_ref[...]
    mean = one * grad_one + two * grad_two
    heads = jnp.concatenate(
        (one * (grad_one - mean), two * (grad_two - mean), mask * sens_ref[...]), axis=1
    ).astype(BF)
    heads_ref[...] = heads
    grad_final = dot(heads, head_ref[...])
    down = grad_final.astype(BF)
    down_ref[...] = down
    grad_hidden = None
    ups = []
    for part in chunks:
        grad_up = (dot(down, wd_ref[part, :], NT) * slope_ref[:, part]).astype(BF)
        up_ref[:, part] = grad_up
        ups.append(jnp.sum(grad_up.astype(F32), axis=0, keepdims=True))
        term = dot(grad_up, wu_ref[:, part], NT)
        grad_hidden = term if grad_hidden is None else grad_hidden + term
    grad_normed = grad_hidden * gain
    grad_residual = grad_final + norm_back(grad_normed, normed, inverse)
    gres_ref[...] = grad_residual
    attn = grad_residual.astype(BF)
    attn_ref[...] = attn
    gatt_ref[...] = dot(attn, wo_ref[...], NT).astype(BF)
    vectors = jnp.concatenate(
        (
            jnp.sum(grad_hidden * normed, axis=0, keepdims=True),
            jnp.sum(grad_hidden, axis=0, keepdims=True),
            jnp.sum(down.astype(F32), axis=0, keepdims=True),
        )
    )
    ups = jnp.concatenate(ups, axis=1)

    @pl.when(pl.program_id(0) == 0)
    def _():
        vec_ref[...] = vectors
        bup_ref[...] = ups

    @pl.when(pl.program_id(0) > 0)
    def _():
        vec_ref[...] += vectors
        bup_ref[...] += ups


def between(x, attended, w_out, w_up, w_down, heads, gain, shift, b_up, b_down, mask, sums, local):
    rows, width = x.shape
    hidden = w_up.shape[1]
    block = math.gcd(local, 256)

    def row(columns):
        return pl.BlockSpec((block, columns), lambda i: (i, 0))

    def whole(values):
        zeros = (0,) * values.ndim
        return pl.BlockSpec(values.shape, lambda i: zeros, pipeline_mode=pl.Buffered(1))

    def shape(columns, kind=BF):
        return jax.ShapeDtypeStruct((rows, columns), kind)

    fixed = [w_out, w_up, w_down, heads, gain, shift, b_up, b_down]
    return pl.pallas_call(
        between_kernel,
        grid=(rows // block,),
        in_specs=[row(width), row(width)]
        + [whole(v) for v in fixed]
        + [pl.BlockSpec((1, 1, 128), lambda i: (i * block // local, 0, 0))]
        + [row(128)] * 3,
        out_specs=[
            row(width),
            row(hidden),
            row(hidden),
            row(width),
            row(width),
            row(384),
            row(width),
            row(width),
            row(width),
            row(128),
            row(128),
            row(128),
            pl.BlockSpec((3, width), lambda i: (0, 0)),
            pl.BlockSpec((1, hidden), lambda i: (0, 0)),
        ],
        out_shape=[
            shape(width),
            shape(hidden),
            shape(hidden),
            shape(width),
            shape(width),
            shape(384),
            shape(width),
            shape(width, F32),
            shape(width),
            shape(128, F32),
            shape(128, F32),
            shape(128, F32),
            jax.ShapeDtypeStruct((3, width), F32),
            jax.ShapeDtypeStruct((1, hidden), F32),
        ],
        scratch_shapes=[pltpu.VMEM((block, hidden), F32)],
        compiler_params=PARAMS,
        name="between",
        cost_estimate=pl.CostEstimate(
            flops=rows * width * hidden, transcendentals=0, bytes_accessed=rows * hidden
        ),
    )(x, attended, *fixed, mask, *sums)


def deal(place, result, mine_ref, sent_ref):
    halves = result.reshape(mine_ref.shape[0], 2, *mine_ref.shape[1:]).astype(BF)
    low = halves[:, 0]
    high = halves[:, 1]
    even = place == 0
    mine_ref[...] = jnp.where(even, low, high)
    sent_ref[...] = jnp.where(even, high, low)


def columns_of(vectors, start):
    count = vectors.shape[0]
    place = lax.broadcasted_iota(jnp.int32, (count, 256), 1)
    which = lax.broadcasted_iota(jnp.int32, (count, 256), 0)
    chosen = (place == which + start).astype(F32).astype(BF)
    high, rest = split_two(vectors)
    return dot(high, chosen, TN) + dot(rest, chosen, TN)


def early_grads_kernel(
    place_ref,
    h_ref,
    a_ref,
    f_ref,
    up_ref,
    attn_ref,
    head_ref,
    vec_ref,
    mine_in_ref,
    sent_in_ref,
    mine_ref,
    sent_ref,
    turn_ref,
):
    step = pl.program_id(0)
    last = pl.num_programs(0) - 1
    place = place_ref[0]
    wide = up_ref.shape[1]

    @pl.when(step == 0)
    def _():
        turn_ref[...] = h_ref[...].T

    @pl.when(step < last - 1)
    def _():
        deal(place, dot(turn_ref[...], up_ref[...]), mine_ref, sent_ref)

    @pl.when(step == last - 1)
    def _():
        turned = a_ref[...].T
        turn_ref[...] = turned
        deal(place, dot(turned, attn_ref[:, :wide]), mine_ref, sent_ref)

    @pl.when(step == last)
    def _():
        out = dot(turn_ref[...], attn_ref[:, wide:])
        heads = dot(f_ref[...].T, head_ref[...]) + columns_of(vec_ref[...], 3 * RESULT_FIELDS)
        deal(place, jnp.concatenate((out, heads), axis=1), mine_ref, sent_ref)


def early_grads(place, hidden, attended, final, up, attn, heads, vectors, mine, sent):
    rows, width = hidden.shape
    wide = 512
    steps = up.shape[1] // wide + 2
    count = width // 96
    skip = mine.shape[2] // wide - steps

    def whole(values):
        return pl.BlockSpec(values.shape, lambda i: (0, 0))

    out = pl.BlockSpec((count, 48, wide), lambda i: (0, 0, i + skip))
    untouched = pl.BlockSpec(memory_space=pl.ANY)
    return pl.pallas_call(
        early_grads_kernel,
        grid=(steps,),
        in_specs=[
            pl.BlockSpec(memory_space=pltpu.SMEM),
            whole(hidden),
            whole(attended),
            whole(final),
            pl.BlockSpec((rows, wide), lambda i: (0, jnp.minimum(i, steps - 3))),
            whole(attn),
            whole(heads),
            whole(vectors),
            untouched,
            untouched,
        ],
        out_specs=[out, out],
        out_shape=[jax.ShapeDtypeStruct(mine.shape, BF)] * 2,
        input_output_aliases={8: 0, 9: 1},
        scratch_shapes=[pltpu.VMEM((width, rows), BF)],
        compiler_params=PARAMS,
        name="early_grads",
        cost_estimate=pl.CostEstimate(
            flops=2 * rows * width * wide * steps,
            transcendentals=0,
            bytes_accessed=2 * rows * wide * steps + 2 * width * wide * steps,
        ),
    )(place, hidden, attended, final, up, attn, heads, vectors, mine, sent)


def down_grads_kernel(place_ref, act_ref, down_ref, mine_ref, sent_ref):
    result = dot(act_ref[...], down_ref[...], TN).astype(BF)
    block = result.shape[0] // 2
    piece = block // 8
    halves = []
    for c in range(2):
        groups = [
            jnp.concatenate(
                [
                    result[c * block + y * 4 * piece + g * piece :][:piece]
                    for y in range(2)
                ],
                axis=0,
            )
            for g in range(4)
        ]
        halves.append(jnp.concatenate(groups, axis=1)[None])
    even = place_ref[0] == 0
    mine_ref[...] = jnp.where(even, halves[0], halves[1])
    sent_ref[...] = jnp.where(even, halves[1], halves[0])


def down_grads(place, activation, down, columns):
    rows, width = down.shape
    block = activation.shape[1] // 8
    piece = block // 16
    out = pl.BlockSpec((1, 2 * piece, 4 * width), lambda i: (i, 0, 0))
    return pl.pallas_call(
        down_grads_kernel,
        grid=(8,),
        in_specs=[
            pl.BlockSpec(memory_space=pltpu.SMEM),
            pl.BlockSpec((rows, block), lambda i: (0, i)),
            pl.BlockSpec((rows, width), lambda i: (0, 0)),
        ],
        out_specs=[out, out],
        out_shape=[jax.ShapeDtypeStruct((8, 2 * piece, columns), BF)] * 2,
        compiler_params=PARAMS,
        name="down_grads",
        cost_estimate=pl.CostEstimate(
            flops=2 * rows * width * block, transcendentals=0, bytes_accessed=width * block
        ),
    )(place, activation, down)


def late_grads_kernel(count, place_ref, *refs):
    mixed_refs = refs[:count]
    query_ref = refs[count]
    key_refs = refs[count + 1 : 2 * count + 1]
    value_refs = refs[2 * count + 1 : 3 * count + 1]
    vec_ref, mine_ref, sent_ref, turn_ref = refs[3 * count + 1 :]
    step = pl.program_id(0)
    third = (pl.num_programs(0) - 1) // 3
    place = place_ref[0]

    @pl.when(step == 0)
    def _():
        for s in range(count):
            turn_ref[s] = mixed_refs[s][...].T

    @pl.when(step < third)
    def _():
        deal(place, dot(turn_ref[0], query_ref[...], NT), mine_ref, sent_ref)

    def joint(parts):
        return sum(dot(turn_ref[s], parts[s][...]) for s in range(count))

    @pl.when((step >= third) & (step < 2 * third))
    def _():
        deal(place, joint(key_refs), mine_ref, sent_ref)

    @pl.when((step >= 2 * third) & (step < 3 * third))
    def _():
        deal(place, joint(value_refs), mine_ref, sent_ref)

    @pl.when(step == 3 * third)
    def _():
        deal(place, columns_of(vec_ref[...], 0), mine_ref, sent_ref)


def late_grads(place, mixed, query, keys, values, vectors):
    rows, width = mixed[0].shape
    count = len(mixed)
    wide = 256
    third = width // wide
    groups = width // 96

    def clipped(offset):
        return lambda i: (0, jnp.clip(i - offset, 0, third - 1))

    whole = pl.BlockSpec((rows, width), lambda i: (0, 0))
    out = pl.BlockSpec((groups, 48, wide), lambda i: (0, 0, i))
    return pl.pallas_call(
        functools.partial(late_grads_kernel, count),
        grid=(3 * third + 1,),
        in_specs=[pl.BlockSpec(memory_space=pltpu.SMEM)]
        + [whole] * count
        + [pl.BlockSpec((wide, rows), lambda i: (jnp.clip(i, 0, third - 1), 0))]
        + [pl.BlockSpec((rows, wide), clipped(third))] * count
        + [pl.BlockSpec((rows, wide), clipped(2 * third))] * count
        + [pl.BlockSpec(vectors.shape, lambda i: (0, 0))],
        out_specs=[out, out],
        out_shape=[jax.ShapeDtypeStruct((groups, 48, wide * (3 * third + 1)), BF)] * 2,
        scratch_shapes=[pltpu.VMEM((count, width, rows), BF)],
        compiler_params=PARAMS,
        name="late_grads",
        cost_estimate=pl.CostEstimate(
            flops=2 * rows * width * width * (2 * count + 1),
            transcendentals=0,
            bytes_accessed=2 * rows * width * 4 * count + 12 * width * width,
        ),
    )(place, *mixed, query, *keys, *values, vectors)


def block_sums_kernel(counts, dealt, where_ref, *refs):
    total_in = sum(len(group) for group in counts)
    ins, outs = refs[:total_in], refs[total_in:]
    at = 0
    for o, group in enumerate(counts):
        shape = ins[at].shape[-2:] if dealt else outs[o].shape
        value = None
        for use in group:
            term = ins[at][...].astype(F32).reshape(shape)
            if use is not None:
                term = jnp.where(use(pl.program_id(0), where_ref), term, 0.0)
            value = term if value is None else value + term
            at += 1
        if dealt:
            for k, out in enumerate(outs):

                @pl.when(pl.program_id(0) == k)
                def _(out=out, value=value, o=o):
                    out[o] = value.astype(BF)
        else:
            outs[o][...] = value.astype(BF)


def block_sums(where, steps, groups, dealt=False):
    counts = [[term[3] if len(term) > 3 else None for term in terms] for _, terms in groups]
    operands = [term[0] for _, terms in groups for term in terms]
    in_specs = [pl.BlockSpec(term[1], term[2]) for _, terms in groups for term in terms]
    if dealt:
        shape = (len(groups),) + groups[0][0]
        zeros = (0,) * len(shape)
        out_specs = [pl.BlockSpec(shape, lambda i, w: zeros)] * steps
        out_shape = [jax.ShapeDtypeStruct(shape, BF)] * steps
    else:
        out_specs = [pl.BlockSpec(out[1], out[2]) for out, _ in groups]
        out_shape = [jax.ShapeDtypeStruct(out[0], BF) for out, _ in groups]
    return pl.pallas_call(
        functools.partial(block_sums_kernel, counts, dealt),
        grid_spec=pltpu.PrefetchScalarGridSpec(
            num_scalar_prefetch=1, grid=(steps,), in_specs=in_specs, out_specs=out_specs
        ),
        out_shape=out_shape,
        compiler_params=FULL,
        name="block_sums",
        cost_estimate=pl.CostEstimate(flops=1 << 20, transcendentals=0, bytes_accessed=1 << 20),
    )(where, *operands)


class Reduction:
    def __init__(self, where, terms, by_columns):
        self.where = where
        self.terms = terms
        self.by_columns = by_columns
        self.depth, self.columns = terms[0].shape[3:]
        self.steps = 4 if by_columns else 2
        if by_columns:
            self.columns //= 2

    def at(self, part, x, z, y, sizes):
        block = sizes + (self.depth, self.columns)
        column = part if self.by_columns else 0
        shift = 0 if self.by_columns else 2 * part // sizes[1]

        def index(i, w):
            return (x(w), z(i, w) + shift, y(w), 0, column)

        return [(t, block, index) for t in self.terms]

    def one(self):
        n, tail = self.steps, (self.depth, self.columns)
        ahead = lambda i, w: i
        sent = block_sums(
            self.where,
            n // 2,
            [
                (
                    ((n, 2) + tail, (2, 2) + tail, lambda i, w: (i, 0, 0, 0)),
                    self.at(0, lambda w: 1 - w[0], ahead, lambda w: 0, (1, 2, 2)),
                ),
                (
                    ((2, n) + tail, (2, 2) + tail, lambda i, w: (0, i, 0, 0)),
                    self.at(1, lambda w: 0, ahead, lambda w: 1 - w[1], (2, 2, 1)),
                ),
            ],
        )
        return list(sent)

    def trade_one(self, sent):
        self.got_one = [swap(sent[0], "lat", 1), swap(sent[1], "grp", 2)]

    def two(self):
        n, tail = self.steps, (self.depth, self.columns)
        ahead = lambda i, w: i
        out = ((n,) + tail, (2,) + tail, lambda i, w: (i, 0, 0))
        sent = block_sums(
            self.where,
            n // 2,
            [
                (
                    out,
                    self.at(0, lambda w: w[0], ahead, lambda w: 1 - w[1], (1, 2, 1))
                    + [(self.got_one[0], (2, 1) + tail, lambda i, w: (i, 1 - w[1], 0, 0))],
                ),
                (
                    out,
                    self.at(1, lambda w: 1 - w[0], ahead, lambda w: w[1], (1, 2, 1))
                    + [(self.got_one[1], (1, 2) + tail, lambda i, w: (1 - w[0], i, 0, 0))],
                ),
            ],
        )
        return list(sent)

    def trade_two(self, sent):
        self.got_two = [swap(sent[0], "grp", 2), swap(sent[1], "lat", 1)]

    def quarters(self):
        tail = (self.depth, self.columns)
        x = lambda w: w[0]
        y = lambda w: w[1]
        if self.by_columns:
            place = lambda i, w: w[2] ^ i
            groups = []
            for part in (0, 1):
                terms = self.at(part, x, place, y, (1, 1, 1))
                if part == 0:
                    one = lambda i, w: (w[2] ^ i, w[1], 0, 0)
                else:
                    one = lambda i, w: (w[0], w[2] ^ i, 0, 0)
                terms.append((self.got_one[part], (1, 1) + tail, one))
                terms.append((self.got_two[part], (1,) + tail, lambda i, w: (w[2] ^ i, 0, 0)))
                groups.append((tail, terms))
        else:
            low = lambda i, w: jnp.minimum(w[2] ^ i, 1)
            high = lambda i, w: jnp.maximum((w[2] ^ i) - 2, 0)
            first = lambda i, w: (w[2] ^ i) < 2
            second = lambda i, w: (w[2] ^ i) >= 2
            terms = self.at(0, x, lambda i, w: w[2] ^ i, y, (1, 1, 1))
            pair = (1, 1) + tail
            one = (1,) + tail
            terms += [
                (self.got_one[0], pair, lambda i, w: (low(i, w), w[1], 0, 0), first),
                (self.got_one[1], pair, lambda i, w: (w[0], high(i, w), 0, 0), second),
                (self.got_two[0], one, lambda i, w: (low(i, w), 0, 0), first),
                (self.got_two[1], one, lambda i, w: (high(i, w), 0, 0), second),
            ]
            groups = [(tail, terms)]
        return list(block_sums(self.where, 4, groups, True))


def early_unpack_kernel(place_ref, *refs):
    ins = refs[:4]
    down_ref, up_ref, out_ref, gate_ref, head_ref, gain_ref, bias_ref, bd_ref, bup_ref, misc_ref = refs[4:]
    width = down_ref.shape[1]
    hidden = up_ref.shape[1]
    for source, (c, y) in zip(ins, ((0, 0), (0, 1), (1, 0), (1, 1))):
        slot = jnp.bitwise_xor(place_ref[0], c) * 2 + jnp.bitwise_xor(place_ref[1], y)
        one = source[0].astype(F32)
        two = source[1].astype(F32)
        rows = one.shape[0]
        half = one.shape[1]
        for g in range(4):
            span = pl.ds(pl.multiple_of(slot * 4 * rows + g * rows, 8), rows)
            down_ref[span, :] = one[:, g * width : (g + 1) * width]
        span = pl.ds(pl.multiple_of(slot * rows, 8), rows)
        cut = half - 4 * width
        up_ref[span, :cut] = one[:, 4 * width :]
        up_ref[span, cut:] = two[:, : hidden - cut]
        out_ref[span, :] = two[:, hidden - cut : hidden - cut + width]
        misc_ref[span, :] = two[:, hidden - cut + width :]
    turned = misc_ref[...].T
    at = 0
    for ref in (gate_ref, head_ref, gain_ref, bias_ref, bd_ref, bup_ref):
        count = ref.shape[0]
        ref[...] = turned[at : at + count]
        at += count


def early_unpack(place, pieces, width, hidden):
    rows = pieces[0].shape[1]
    vmem = pl.BlockSpec(memory_space=pltpu.VMEM)
    return pl.pallas_call(
        early_unpack_kernel,
        in_specs=[pl.BlockSpec(memory_space=pltpu.SMEM)] + [vmem] * 4,
        out_specs=[vmem] * 9,
        out_shape=[
            jax.ShapeDtypeStruct((16 * rows, width), F32),
            jax.ShapeDtypeStruct((4 * rows, hidden), F32),
            jax.ShapeDtypeStruct((4 * rows, width), F32),
        ]
        + [
            jax.ShapeDtypeStruct((count, 4 * rows), F32)
            for count in (2 * RESULT_FIELDS, RESULT_FIELDS, 1, 1, 1, 4)
        ],
        scratch_shapes=[pltpu.VMEM((4 * rows, 256), F32)],
        compiler_params=PARAMS,
        name="early_unpack",
        cost_estimate=pl.CostEstimate(flops=1 << 20, transcendentals=0, bytes_accessed=1 << 20),
    )(place, *pieces)


def late_unpack_kernel(place_ref, *refs):
    ins = refs[:4]
    main_ref, gain_ref, bias_ref, lead_ref, misc_ref = refs[4:]
    for source, (c, y) in zip(ins, ((0, 0), (0, 1), (1, 0), (1, 1))):
        slot = jnp.bitwise_xor(place_ref[0], c) * 2 + jnp.bitwise_xor(place_ref[1], y)
        value = source[...].astype(F32)
        rows = value.shape[0]
        span = pl.ds(pl.multiple_of(slot * rows, 8), rows)
        main_ref[span, :] = value[:, : main_ref.shape[1]]
        misc_ref[span, :] = value[:, main_ref.shape[1] :]
    turned = misc_ref[...].T
    gain_ref[...] = turned[:1]
    bias_ref[...] = turned[1:2]
    lead_ref[...] = turned[2 : 2 + LEADS]


def late_unpack(place, pieces):
    rows, columns = pieces[0].shape
    vmem = pl.BlockSpec(memory_space=pltpu.VMEM)
    return pl.pallas_call(
        late_unpack_kernel,
        in_specs=[pl.BlockSpec(memory_space=pltpu.SMEM)] + [vmem] * 4,
        out_specs=[vmem] * 4,
        out_shape=[jax.ShapeDtypeStruct((4 * rows, columns - 256), F32)]
        + [jax.ShapeDtypeStruct((count, 4 * rows), F32) for count in (1, 1, LEADS)],
        scratch_shapes=[pltpu.VMEM((4 * rows, 256), F32)],
        compiler_params=PARAMS,
        name="late_unpack",
        cost_estimate=pl.CostEstimate(flops=1 << 20, transcendentals=0, bytes_accessed=1 << 20),
    )(place, *pieces)


def spread(rows, columns):
    pixel = lax.broadcasted_iota(jnp.int32, (rows, columns), 0)
    field = lax.broadcasted_iota(jnp.int32, (rows, columns), 1)
    return ((pixel // TILE_AREA) == field).astype(F32).astype(BF)


def split_two(values):
    high = values.astype(BF)
    return high, (values - high.astype(F32)).astype(BF)


def pixel_sums_kernel(f_ref, s_ref, sum_ref, first_ref, second_ref, field_ref):
    @pl.when(pl.program_id(0) == 0)
    def _():
        field_ref[...] = spread(*field_ref.shape)

    fields = field_ref[...]
    sens = s_ref[...]
    sum_ref[...] = dot(sens, fields)
    for e, out in ((0, first_ref), (1, second_ref)):
        out[...] = dot((sens.astype(F32) * f_ref[e].astype(F32)).astype(BF), fields)


def pixel_sums(forecasts, sensitivity):
    rows, pixels = sensitivity.shape
    block = math.gcd(rows, 128)
    out = pl.BlockSpec((block, 128), lambda i: (i, 0))
    return pl.pallas_call(
        pixel_sums_kernel,
        grid=(rows // block,),
        in_specs=[
            pl.BlockSpec((2, block, pixels), lambda i: (0, i, 0)),
            pl.BlockSpec((block, pixels), lambda i: (i, 0)),
        ],
        out_specs=[out] * 3,
        out_shape=[jax.ShapeDtypeStruct((rows, 128), F32)] * 3,
        scratch_shapes=[pltpu.VMEM((pixels, 128), BF)],
        compiler_params=PARAMS,
        name="pixel_sums",
        cost_estimate=pl.CostEstimate(
            flops=rows * pixels * 128, transcendentals=0, bytes_accessed=rows * pixels
        ),
    )(forecasts, sensitivity)


def blend_kernel(a_ref, b_ref, c_ref, f_ref, out_ref, field_ref):
    @pl.when(pl.program_id(0) == 0)
    def _():
        columns = field_ref.shape[1]
        field = lax.broadcasted_iota(jnp.int32, (256, columns), 0)
        pixel = lax.broadcasted_iota(jnp.int32, (256, columns), 1)
        field_ref[...] = ((pixel // TILE_AREA) == (field % 128)).astype(F32).astype(BF)

    fields = field_ref[...]

    def wide(ref):
        return dot(jnp.concatenate(split_two(ref[...]), axis=1), fields)

    total = wide(a_ref) * f_ref[0].astype(F32) + wide(b_ref) * f_ref[1].astype(F32)
    out_ref[...] = (total + wide(c_ref)).astype(BF)


def blend(first, second, added, forecasts):
    _, rows, pixels = forecasts.shape
    block = math.gcd(rows, 128)
    thin = pl.BlockSpec((block, 128), lambda i: (i, 0))
    return pl.pallas_call(
        blend_kernel,
        grid=(rows // block,),
        in_specs=[thin] * 3 + [pl.BlockSpec((2, block, pixels), lambda i: (0, i, 0))],
        out_specs=pl.BlockSpec((block, pixels), lambda i: (i, 0)),
        out_shape=jax.ShapeDtypeStruct((rows, pixels), BF),
        scratch_shapes=[pltpu.VMEM((256, pixels), BF)],
        compiler_params=PARAMS,
        name="blend",
        cost_estimate=pl.CostEstimate(
            flops=rows * pixels * 128, transcendentals=0, bytes_accessed=rows * pixels
        ),
    )(first, second, added, forecasts)


def swap(values, axis, bit):
    count = lax.axis_size(axis)
    return lax.ppermute(values, axis, [(i, i ^ bit) for i in range(count)])


def add(*terms):
    return sum(t.astype(F32) for t in terms).astype(BF)


def hold(*values):
    return lax.optimization_barrier(values)


def layer_norm(values):
    centred = values - jnp.mean(values, axis=-1, keepdims=True)
    inverse = lax.rsqrt(jnp.mean(centred * centred, axis=-1, keepdims=True) + EPSILON)
    return centred * inverse, inverse


def norm_back(grad_normed, normed, inverse):
    return inverse * (
        grad_normed
        - jnp.mean(grad_normed, axis=-1, keepdims=True)
        - normed * jnp.mean(grad_normed * normed, axis=-1, keepdims=True)
    )


def pad_lanes(values):
    return jnp.pad(values, ((0, 0), (0, 128 - values.shape[1])))


def per_device(
    layer_source_tensor,
    horizon_class,
    field_selector,
    model_predictions,
    loss_sensitivity,
    gain_one,
    shift_one,
    horizon_vectors,
    w_qkv,
    w_out,
    gain_two,
    shift_two,
    w_up,
    b_up,
    w_down,
    b_down,
    w_gate,
    w_bias,
):
    frames, lat_rows, lon_cols, width = layer_source_tensor.shape
    local = lat_rows * lon_cols
    rows = frames * local
    pixels = loss_sensitivity.shape[-1]
    sizes = (lax.axis_size("grp"), lax.axis_size("lat"), lax.axis_size("lon"))
    small = sizes == (4, 2, 4) and frames == 1

    source = layer_source_tensor.reshape(frames, local, width)
    place = lax.axis_index("lon")
    edge = (place == 0) | (place == lax.axis_size("lon") - 1)
    send = functools.partial(lax.ppermute, axis_name="lon")
    if small:
        right = send(source, perm=[(0, 1), (1, 2), (2, 3)])
        left = send(source, perm=[(3, 2), (2, 1), (1, 0)])
    else:
        shards = [lax.all_gather(source, "lon", axis=1, tiled=True)]

    forecasts = jnp.transpose(model_predictions.reshape(rows, 2, pixels), (1, 0, 2))
    sensitivity = loss_sensitivity.reshape(rows, pixels)

    onehot = (horizon_class[:, None] == jnp.arange(LEADS, dtype=jnp.int32)[None, :]).astype(F32)
    lead_rows = jnp.dot(onehot, horizon_vectors, precision=HIGH)

    def mixed_of(values):
        normed, _ = layer_norm(values.astype(F32))
        return (normed * gain_one + shift_one + lead_rows[:, None, :]).astype(BF)

    wq = w_qkv[:, :width]
    wkv = w_qkv[:, width:]

    def keys_of(values):
        return dot(values.reshape(-1, width), wkv).astype(BF).reshape(frames, -1, 2 * width)

    if small:

        def flat(values):
            return values.reshape(rows, width)

        def shard_of(flag, yes, no):
            m, kv, x = project(
                flag.astype(jnp.int32)[None],
                [flat(yes), flat(no)],
                gain_one,
                shift_one,
                lead_rows,
                w_qkv,
            )
            return m, kv[None], x[None]

        mixed_own, own_kv, queries = project(
            None, [flat(source)], gain_one, shift_one, lead_rows, w_qkv
        )
        queries = queries[None]
        mixed = [mixed_own]
        key_value = [own_kv[None]]
        right, left, forecasts, queries, key_value[0] = hold(
            right, left, forecasts, queries, key_value[0]
        )
        right_two = send(right, perm=[(1, 2), (2, 3)])
        left_two = send(left, perm=[(2, 1), (1, 0)])
        sums = pixel_sums(forecasts, sensitivity)
        m, kv, near = shard_of(place == 0, left, right)
        mixed.append(m)
        right_two, left_two, kv, *sums = hold(right_two, left_two, kv, *sums)
        key_value.append(kv)
        two = right_two + left_two
        two, middle = hold(two, left)
        three = send(two, perm=[(2, 3), (1, 0)])
        m, kv, middle = shard_of(edge, two, middle)
        mixed.append(m)
        key_value.append(kv)
        state = attend(queries, key_value, None, False)
        three, *state = hold(three, *state)
        m, kv, far = shard_of(edge, three, two)
        mixed.append(m)
        key_value.append(kv)
        attended, logs = attend(queries, key_value[3:], state, True)
        shards = [source, near, middle, far]
    else:
        mixed_own = mixed_of(source)
        queries = dot(mixed_own.reshape(rows, width), wq).astype(BF)
        queries = queries.reshape(frames, local, width)
        sums = pixel_sums(forecasts, sensitivity)
        mixed = [mixed_of(shards[0])]
        key_value = [keys_of(mixed[0])]
        attended, logs = attend(queries, key_value, None, True)
    inputs = source.reshape(rows, width)
    attended_low = attended.reshape(rows, width)
    both = w_gate.T
    head_rows = jnp.concatenate(
        [
            jnp.pad(m, ((0, 128 - RESULT_FIELDS), (0, 0)))
            for m in (both[:RESULT_FIELDS], both[RESULT_FIELDS:], w_bias.T)
        ]
    )
    mask = pad_lanes(field_selector.astype(F32))[:, None]
    (
        hidden_low,
        activation_low,
        up_low,
        down_low,
        final_low,
        heads_low,
        attn_low,
        grad_residual,
        grad_attended,
        *blending,
        early_vectors,
        grad_bup,
    ) = between(
        inputs,
        attended_low,
        w_out,
        w_up,
        w_down,
        head_rows,
        gain_two,
        shift_two,
        b_up,
        b_down,
        mask,
        sums,
        local,
    )
    grad_attended = grad_attended.reshape(frames, local, width)
    fields = 3 * RESULT_FIELDS
    heads_low = jnp.concatenate(
        [heads_low[:, g * 128 : g * 128 + RESULT_FIELDS] for g in range(3)], axis=1
    )
    inputs = inputs.astype(F32)
    normed_one, inverse_one = layer_norm(inputs)

    def input_gradient(grad_mixed):
        return grad_residual + norm_back(
            grad_mixed.reshape(rows, width) * gain_one, normed_one, inverse_one
        )

    def back(shard, place, before):
        return attend_back(queries, grad_attended, attended, logs, shard, w_qkv, place, before)

    nothing = jnp.zeros((frames, width, local), F32)

    def late_vectors(sums):
        gain_column = sum(jnp.sum(s[:, 0], axis=0) for s in sums)
        column = sum(s[:, 1] for s in sums)
        lead = jnp.dot(onehot.T, column, precision=HIGH)
        zeros = jnp.zeros((6, width), F32)
        return jnp.concatenate((gain_column[None], jnp.sum(column, axis=0)[None], lead, zeros))

    if small:
        bup_rows = jnp.swapaxes(grad_bup.reshape(8, 4, -1), 0, 1).reshape(4, width)
        early_vectors = jnp.concatenate(
            (early_vectors, bup_rows, jnp.zeros((1, width), F32))
        )
        core = (lax.axis_index("grp") % 2).astype(jnp.int32)[None]
        where = jnp.stack(
            (lax.axis_index("lat"), lax.axis_index("grp") // 2, lax.axis_index("lon"))
        ).astype(jnp.int32)
        hidden = w_up.shape[1]
        mine, sent = down_grads(core, activation_low, down_low, 2 * hidden + width + 256)
        mine, sent = early_grads(
            core,
            hidden_low,
            attended_low,
            final_low,
            up_low,
            attn_low,
            jnp.pad(heads_low, ((0, 0), (0, 256 - fields))),
            early_vectors,
            mine,
            sent,
        )
        grad_attended, sent = hold(grad_attended, sent)
        got = swap(sent, "grp", 1)

        grad_query, dk3, dv3, far, sums3 = back(key_value[3], shards[3], nothing)
        early = Reduction(where, [t.reshape(2, 4, 2, 24, -1) for t in (mine, got)], True)
        grad_query, far, *sent = hold(grad_query, far, *early.one())
        got = send(far, perm=[(0, 1), (3, 2)])
        early.trade_one(sent)

        grad_query, dk2, dv2, middle, sums2 = back(key_value[2], shards[2], grad_query)
        value = jnp.where(edge, middle, add(got, far))
        grad_query, value = hold(grad_query, value)
        right = send(value, perm=[(0, 1), (1, 2)])
        left = send(value, perm=[(3, 2), (2, 1)])

        grad_query, dk1, dv1, near, sums1 = back(key_value[1], shards[1], grad_query)
        forth = jnp.where(place == 0, near, add(right, middle))
        back_value = add(left, near)
        grad_query, forth, back_value, *sent = hold(
            grad_query, forth, back_value, *early.two()
        )
        right = send(forth, perm=[(0, 1), (1, 2), (2, 3)])
        left = send(back_value, perm=[(3, 2), (2, 1), (1, 0)])
        early.trade_two(sent)

        grad_query, dk0, dv0, own, sums0, right, left, *early.got_two = hold(
            *back(key_value[0], shards[0], grad_query), right, left, *early.got_two
        )
        query_low, query_term, query_sums = query_back(grad_query, w_qkv, source)
        vectors = late_vectors([sums0, sums1, sums2, sums3, query_sums])
        late_mine, late_sent = late_grads(
            core,
            [m.reshape(rows, width) for m in mixed],
            query_low.reshape(width, rows),
            [d.reshape(rows, width) for d in (dk0, dk1, dk2, dk3)],
            [d.reshape(rows, width) for d in (dv0, dv1, dv2, dv3)],
            vectors,
        )
        late_mine, late_sent, *early.got_two, own = hold(
            late_mine, late_sent, *early.got_two, own
        )
        got = swap(late_sent, "grp", 1)
        got, *parts = hold(got, *early.quarters())
        late = Reduction(where, [t.reshape(2, 4, 2, 24, -1) for t in (late_mine, got)], False)
        *sent, one, two, three = hold(*late.one(), *blending)
        late.trade_one(sent)
        early = [parts[0]] + [swap(parts[k], "lon", k) for k in (1, 2, 3)]
        blended = blend(one, two, three, forecasts)
        *late.got_one, blended = hold(*late.got_one, blended)
        *sent, own, early[0] = hold(*late.two(), own, early[0])
        late.trade_two(sent)
        grad_input = input_gradient(
            own.astype(F32) + query_term + right.astype(F32) + left.astype(F32)
        )
        *late.got_two, grad_input = hold(*late.got_two, grad_input)
        early[0], *parts = hold(early[0], *late.quarters())
        late = [parts[0]] + [swap(parts[k], "lon", k) for k in (1, 2, 3)]
        late[1], late[2], late[3], early[0] = hold(late[1], late[2], late[3], early[0])
        late = add(*[part[0] for part in late])
        late_y = swap(late, "grp", 2)
        late_c = swap(late, "grp", 1)
        early = add(*early)
        early_y = swap(early, "grp", 2)
        early_c = swap(early, "grp", 1)
        early_y, early_c, early, late_y, late_c, late = hold(
            early_y, early_c, early, late_y, late_c, late
        )
        early_yc = swap(early_y, "grp", 1)
        late_yc = swap(late_y, "grp", 1)
        place_two = jnp.stack((lax.axis_index("grp") % 2, lax.axis_index("grp") // 2))
        place_two = place_two.astype(jnp.int32)
        down_sum, up_sum, out_sum, gate_sum, head_sum, *early, bup_sum = early_unpack(
            place_two, [early, early_y, early_c, early_yc], width, hidden
        )
        late_yc, gate_sum = hold(late_yc, gate_sum)
        qkv_sum, *late, lead_sum = late_unpack(place_two, [late, late_y, late_c, late_yc])
        early = [e.reshape(-1) for e in early]
        late = [e.reshape(-1) for e in late]
        bup_sum = bup_sum.reshape(-1)
        gate_sum = gate_sum.T
        head_sum = head_sum.T
    else:
        blended = blend(*blending, forecasts)
        grad_query, dk, dv, term, sums = back(key_value[0], shards[0], nothing)
        query_low, query_term, query_sums = query_back(grad_query, w_qkv, source)
        grad_input = input_gradient(
            query_term + lax.psum_scatter(term.astype(F32), "lon", scatter_dimension=1, tiled=True)
        )

        def total_of(values, dim=0):
            share = lax.psum_scatter(values, ("lat", "lon"), scatter_dimension=dim, tiled=True)
            return lax.psum(share, "grp")

        flat = mixed[0].reshape(-1, width)
        qkv_sum = total_of(
            jnp.concatenate(
                (
                    jnp.einsum("frd,fer->de", mixed_own, query_low, preferred_element_type=F32),
                    dot(flat, dk.reshape(-1, width), TN),
                    dot(flat, dv.reshape(-1, width), TN),
                ),
                axis=1,
            )
        )
        up_sum = total_of(dot(hidden_low, up_low, TN))
        out_sum = total_of(dot(attended_low, attn_low, TN))
        down_sum = total_of(dot(activation_low, down_low, TN))
        heads = total_of(dot(final_low, heads_low, TN))
        late = total_of(late_vectors([sums, query_sums])[: 2 + LEADS], 1)
        lead_sum = late[2:]
        gate_sum = heads[:, : 2 * RESULT_FIELDS]
        head_sum = heads[:, 2 * RESULT_FIELDS :]
        early = total_of(early_vectors, 1)
        bup_sum = total_of(grad_bup[0])

    return (
        blended.reshape(frames, lat_rows, lon_cols, pixels),
        grad_input.reshape(frames, lat_rows, lon_cols, width),
        late[0],
        late[1],
        lead_sum,
        qkv_sum,
        out_sum,
        early[0],
        early[1],
        up_sum,
        bup_sum,
        down_sum,
        early[2],
        gate_sum,
        head_sum,
    )


def solution(mesh):
    frame = ("grp", "lat")
    share = ("lat", "lon")
    image = P(frame, None, "lon", None)
    in_specs = (
        image,
        P(frame),
        P(frame, None),
        P(frame, None, "lon", None, None),
        image,
    ) + (P(),) * 13
    vector = P(share)
    matrix = P(share, None)
    out_specs = (
        image,
        image,
        vector,
        vector,
        P(None, share),
        matrix,
        matrix,
        vector,
        vector,
        matrix,
        vector,
        matrix,
        vector,
        matrix,
        matrix,
    )
    return jax.shard_map(
        per_device, mesh=mesh, in_specs=in_specs, out_specs=out_specs, check_vma=False
    )
```

```python
import functools
import math

import jax
import jax.numpy as jnp
from jax import lax
from jax.experimental import pallas as pl
from jax.experimental.pallas import tpu as pltpu
from jax.sharding import PartitionSpec as P

H = 12
DH = 64
RESULT_FIELDS = 69
TILE_AREA = 64
LEADS = 24
EPSILON = 1e-06
HIGH = lax.Precision.HIGHEST
SCALE = 0.125
SCALE_TWO = SCALE * math.log2(math.e)
ROOT = math.sqrt(2.0 / math.pi)
CUBE = 0.044715
NN = (((1,), (0,)), ((), ()))
NT = (((1,), (1,)), ((), ()))
TN = (((0,), (0,)), ((), ()))
BF = jnp.bfloat16
F32 = jnp.float32
PARAMS = pltpu.CompilerParams(vmem_limit_bytes=60 * 1024 * 1024)
FULL = pltpu.CompilerParams(vmem_limit_bytes=63 * 1024 * 1024 + 512 * 1024)


def dot(left, right, dims=NN):
    return lax.dot_general(left, right, dims, preferred_element_type=F32)


def project_kernel(own, *refs):
    if own:
        a_ref, gain_ref, shift_ref, lead_ref, wq_ref, wk_ref, wv_ref, mixed_ref, kv_ref, q_ref = refs
        value = a_ref[...]
    else:
        flag_ref, a_ref, b_ref, gain_ref, shift_ref, lead_ref, wk_ref, wv_ref = refs[:8]
        mixed_ref, kv_ref, x_ref = refs[8:]
        value = jnp.where(flag_ref[0] != 0, a_ref[...], b_ref[...])
        x_ref[...] = value
    normed, _ = layer_norm(value.astype(F32))
    mixed = (normed * gain_ref[...][None] + shift_ref[...][None] + lead_ref[...]).astype(BF)
    mixed_ref[...] = mixed
    width = mixed.shape[1]
    kv_ref[:, :width] = dot(mixed, wk_ref[...]).astype(BF)
    kv_ref[:, width:] = dot(mixed, wv_ref[...]).astype(BF)
    if own:
        q_ref[...] = dot(mixed, wq_ref[...]).astype(BF)


def project(flag, sources, gain, shift, lead, weights):
    own = flag is None
    rows, width = sources[0].shape
    block = math.gcd(rows, 256)
    row = pl.BlockSpec((block, width), lambda i: (i, 0))
    vector = pl.BlockSpec((width,), lambda i: (0,))

    def columns(group):
        return pl.BlockSpec((width, width), lambda i: (0, group))

    groups = (0, 1, 2) if own else (1, 2)
    return pl.pallas_call(
        functools.partial(project_kernel, own),
        grid=(rows // block,),
        in_specs=([] if own else [pl.BlockSpec(memory_space=pltpu.SMEM)])
        + [row] * len(sources)
        + [vector, vector, pl.BlockSpec((1, width), lambda i: (0, 0))]
        + [columns(g) for g in groups],
        out_specs=[row, pl.BlockSpec((block, 2 * width), lambda i: (i, 0)), row],
        out_shape=[
            jax.ShapeDtypeStruct((rows, width), BF),
            jax.ShapeDtypeStruct((rows, 2 * width), BF),
            jax.ShapeDtypeStruct((rows, width), BF),
        ],
        compiler_params=PARAMS,
        name="project",
        cost_estimate=pl.CostEstimate(
            flops=rows * width * width, transcendentals=0, bytes_accessed=rows * width
        ),
    )(*([] if own else [flag]), *sources, gain, shift, lead, *([weights] * len(groups)))


def attend_kernel(count, chained, final, *refs):
    q_ref = refs[0]
    k_refs = refs[1 : 1 + count]
    v_refs = refs[1 + count : 1 + 2 * count]
    o_ref, l_ref = refs[-2:]
    outs = []
    for h in range(2):
        part = slice(h * DH, h * DH + DH)
        q = q_ref[0, :, part]
        scores = [dot(k[0, :, part], q, NT) for k in k_refs]
        top = functools.reduce(
            jnp.maximum, [jnp.max(s, axis=0, keepdims=True) for s in scores]
        )
        top = top * SCALE_TWO
        total = None
        mixed = None
        for s, v in zip(scores, v_refs):
            raised = jnp.exp2(s * SCALE_TWO - top)
            some = jnp.sum(raised, axis=0, keepdims=True)
            term = dot(v[0, :, part], raised.astype(BF), TN)
            total = some if total is None else total + some
            mixed = term if mixed is None else mixed + term
        mixed = mixed * (1.0 / total)
        log = top + jnp.log2(total)
        if chained:
            before_ref, before_log_ref = refs[1 + 2 * count : 3 + 2 * count]
            before = before_log_ref[0, 0, h : h + 1, :]
            high = jnp.maximum(before, log)
            joint = high + jnp.log2(jnp.exp2(before - high) + jnp.exp2(log - high))
            mixed = mixed * jnp.exp2(log - joint) + before_ref[0, part, :] * jnp.exp2(
                before - joint
            )
            log = joint
        l_ref[0, 0, h : h + 1, :] = log
        if final:
            outs.append(mixed)
        else:
            o_ref[0, part, :] = mixed
    if final:
        o_ref[0] = jnp.concatenate(outs, axis=0).T.astype(BF)


def attend(queries, shards, before, final):
    frames, rows, width = queries.shape
    count = len(shards)
    keys = shards[0].shape[1]
    pairs = width // 128
    turned = pl.BlockSpec((1, 128, rows), lambda f, p: (f, p, 0))
    row = pl.BlockSpec((1, rows, 128), lambda f, p: (f, 0, p))
    log = pl.BlockSpec((1, 1, 2, rows), lambda f, p: (f, p, 0, 0))
    chained = before is not None
    return pl.pallas_call(
        functools.partial(attend_kernel, count, chained, final),
        grid=(frames, pairs),
        in_specs=[row]
        + [pl.BlockSpec((1, keys, 128), lambda f, p: (f, 0, p))] * count
        + [pl.BlockSpec((1, keys, 128), lambda f, p: (f, 0, p + pairs))] * count
        + ([turned, log] if chained else []),
        out_specs=[row if final else turned, log],
        out_shape=[
            jax.ShapeDtypeStruct((frames, rows, width), BF)
            if final
            else jax.ShapeDtypeStruct((frames, width, rows), F32),
            jax.ShapeDtypeStruct((frames, pairs, 2, rows), F32),
        ],
        compiler_params=PARAMS,
        name="attend",
        cost_estimate=pl.CostEstimate(
            flops=2 * frames * rows * count * keys * width,
            transcendentals=0,
            bytes_accessed=frames * rows * width,
        ),
    )(queries, *shards, *shards, *(before if chained else ()))


def column_sums(total, values):
    normed, _ = layer_norm(values.astype(F32))
    return jnp.concatenate(
        (
            jnp.sum(total * normed, axis=0, keepdims=True),
            jnp.sum(total, axis=0, keepdims=True),
        )
    )


def attend_back_kernel(
    q_ref,
    g_ref,
    o_ref,
    l_ref,
    k_ref,
    v_ref,
    wk_ref,
    wv_ref,
    x_ref,
    before_ref,
    dq_ref,
    dkv_ref,
    term_ref,
    sums_ref,
):
    pair = pl.program_id(1)
    key_terms = []
    value_terms = []
    query_terms = []
    for h in range(2):
        part = slice(h * DH, h * DH + DH)
        q = q_ref[0, :, part]
        g = g_ref[0, :, part]
        k = k_ref[0, :, part]
        v = v_ref[0, :, part]
        product = g.astype(F32) * o_ref[0, :, part].astype(F32)
        high, low = split_two(product)
        ones = jnp.ones((8, DH), BF)
        delta = (dot(ones, high, NT) + dot(ones, low, NT))[0:1]
        probs = jnp.exp2(dot(k, q, NT) * SCALE_TWO - l_ref[0, 0, h : h + 1, :])
        grad_probs = dot(v, g, NT)
        grad_scores = (probs * (grad_probs - delta)).astype(BF)
        value_terms.append(dot(probs.astype(BF), g))
        key_terms.append(dot(grad_scores, q))
        grad_query = dot(k, grad_scores, TN) * SCALE + before_ref[0, part, :]
        query_terms.append(grad_query)
    grad_key = (jnp.concatenate(key_terms, axis=1) * SCALE).astype(BF)
    grad_value = jnp.concatenate(value_terms, axis=1).astype(BF)
    grad_query = jnp.concatenate(query_terms, axis=0).astype(dq_ref.dtype)
    width = wk_ref.shape[0]
    dkv_ref[0, :, pl.ds(pl.multiple_of(pair * 128, 128), 128)] = grad_key
    dkv_ref[0, :, pl.ds(pl.multiple_of(width + pair * 128, 128), 128)] = grad_value
    dq_ref[0] = grad_query

    @pl.when(pair == pl.num_programs(1) - 1)
    def _():
        total = dot(dkv_ref[0, :, :width], wk_ref[...], NT)
        total = total + dot(dkv_ref[0, :, width:], wv_ref[...], NT)
        term_ref[0] = total.astype(term_ref.dtype)
        sums_ref[0] = column_sums(total, x_ref[0])


def attend_back(queries, grad_out, out, logs, shard, weights, source, before):
    frames, rows, width = queries.shape
    keys = shard.shape[1]
    pairs = width // 128
    row = pl.BlockSpec((1, rows, 128), lambda f, p: (f, 0, p))
    key = pl.BlockSpec((1, keys, 128), lambda f, p: (f, 0, p))
    value = pl.BlockSpec((1, keys, 128), lambda f, p: (f, 0, p + pairs))
    turned = pl.BlockSpec((1, 128, rows), lambda f, p: (f, p, 0))
    log = pl.BlockSpec((1, 1, 2, rows), lambda f, p: (f, p, 0, 0))

    def columns(group):
        return pl.BlockSpec((width, width), lambda f, p: (0, group))

    def whole(*shape):
        return pl.BlockSpec((1,) + shape, lambda f, p: (f, 0, 0))

    in_specs = [row, row, row, log, key, value, columns(1), columns(2), whole(keys, width)]
    operands = [queries, grad_out, out, logs, shard, shard, weights, weights, source]
    aliases = {len(operands): 0}
    in_specs.append(turned)
    operands.append(before)
    out_specs = [turned, whole(keys, 2 * width), whole(keys, width), whole(2, width)]
    out_shape = [
        jax.ShapeDtypeStruct((frames, width, rows), F32),
        jax.ShapeDtypeStruct((frames, keys, 2 * width), BF),
        jax.ShapeDtypeStruct((frames, keys, width), BF),
        jax.ShapeDtypeStruct((frames, 2, width), F32),
    ]
    return pl.pallas_call(
        attend_back_kernel,
        grid=(frames, pairs),
        in_specs=in_specs,
        out_specs=out_specs,
        out_shape=out_shape,
        input_output_aliases=aliases,
        compiler_params=PARAMS,
        name="attend_back",
        cost_estimate=pl.CostEstimate(
            flops=4 * frames * rows * keys * width,
            transcendentals=0,
            bytes_accessed=frames * rows * width,
        ),
    )(*operands)


def query_back_kernel(dq_ref, w_ref, x_ref, low_ref, term_ref, sums_ref):
    low = dq_ref[0].astype(BF)
    low_ref[0] = low
    total = dot(low, w_ref[...], (((0,), (1,)), ((), ())))
    term_ref[0] = total
    sums_ref[0] = column_sums(total, x_ref[0])


def query_back(grad_query, weights, source):
    frames, width, rows = grad_query.shape

    def whole(*shape):
        return pl.BlockSpec((1,) + shape, lambda f: (f, 0, 0))

    return pl.pallas_call(
        query_back_kernel,
        grid=(frames,),
        in_specs=[
            whole(width, rows),
            pl.BlockSpec((width, width), lambda f: (0, 0)),
            whole(rows, width),
        ],
        out_specs=[whole(width, rows), whole(rows, width), whole(2, width)],
        out_shape=[
            jax.ShapeDtypeStruct((frames, width, rows), BF),
            jax.ShapeDtypeStruct((frames, rows, width), F32),
            jax.ShapeDtypeStruct((frames, 2, width), F32),
        ],
        compiler_params=PARAMS,
        name="query_back",
        cost_estimate=pl.CostEstimate(
            flops=frames * rows * width * width, transcendentals=0, bytes_accessed=rows * width
        ),
    )(grad_query, weights, source)


def between_kernel(
    x_ref,
    att_ref,
    wo_ref,
    wu_ref,
    wd_ref,
    head_ref,
    gain_ref,
    shift_ref,
    bu_ref,
    bd_ref,
    mask_ref,
    sens_ref,
    one_ref,
    two_ref,
    hidden_ref,
    act_ref,
    up_ref,
    down_ref,
    final_ref,
    heads_ref,
    attn_ref,
    gres_ref,
    gatt_ref,
    first_ref,
    second_ref,
    added_ref,
    vec_ref,
    bup_ref,
    slope_ref,
    sum_ref,
    ups_ref,
):
    residual = x_ref[...].astype(F32) + dot(att_ref[...], wo_ref[...])
    normed, inverse = layer_norm(residual)
    gain = gain_ref[...][None]
    hidden = (normed * gain + shift_ref[...][None]).astype(BF)
    hidden_ref[...] = hidden
    wide = 512
    steps = wu_ref.shape[1] // wide
    sum_ref[...] = residual + bd_ref[...][None]

    def chunk(j):
        return pl.ds(pl.multiple_of(j * wide, wide), wide)

    @pl.loop(0, steps)
    def _(j):
        part = chunk(j)
        up = dot(hidden, wu_ref[:, part]) + bu_ref[part][None]
        square = up * up
        tanh = jnp.tanh(ROOT * up * (1.0 + CUBE * square))
        half = 0.5 * (1.0 + tanh)
        act = (up * half).astype(BF)
        slope_ref[:, part] = half + 0.5 * up * (1.0 - tanh * tanh) * (
            ROOT + 3.0 * ROOT * CUBE * square
        )
        act_ref[:, part] = act
        sum_ref[...] += dot(act, wd_ref[part, :])

    final = sum_ref[...]
    final_low = final.astype(BF)
    final_ref[...] = final_low
    logits = dot(final_low, head_ref[...], NT)
    one = logits[:, :128]
    two = logits[:, 128:256]
    offset = logits[:, 256:]
    top = jnp.maximum(one, two)
    one = jnp.exp(one - top)
    two = jnp.exp(two - top)
    total = one + two
    one = one / total
    two = two / total
    mask = mask_ref[0]
    first_ref[...] = mask * one + (1.0 - mask)
    second_ref[...] = mask * two
    added_ref[...] = mask * offset
    grad_one = mask * one_ref[...]
    grad_two = mask * two_ref[...]
    mean = one * grad_one + two * grad_two
    heads = jnp.concatenate(
        (one * (grad_one - mean), two * (grad_two - mean), mask * sens_ref[...]), axis=1
    ).astype(BF)
    heads_ref[...] = heads
    grad_final = dot(heads, head_ref[...])
    down = grad_final.astype(BF)
    down_ref[...] = down
    sum_ref[...] = jnp.zeros_like(sum_ref)

    @pl.loop(0, steps)
    def _(j):
        part = chunk(j)
        grad_up = (dot(down, wd_ref[part, :], NT) * slope_ref[:, part]).astype(BF)
        up_ref[:, part] = grad_up
        ups_ref[:, part] = jnp.sum(grad_up.astype(F32), axis=0, keepdims=True)
        sum_ref[...] += dot(grad_up, wu_ref[:, part], NT)

    grad_hidden = sum_ref[...]
    grad_normed = grad_hidden * gain
    grad_residual = grad_final + norm_back(grad_normed, normed, inverse)
    gres_ref[...] = grad_residual
    attn = grad_residual.astype(BF)
    attn_ref[...] = attn
    gatt_ref[...] = dot(attn, wo_ref[...], NT).astype(BF)
    vectors = jnp.concatenate(
        (
            jnp.sum(grad_hidden * normed, axis=0, keepdims=True),
            jnp.sum(grad_hidden, axis=0, keepdims=True),
            jnp.sum(down.astype(F32), axis=0, keepdims=True),
        )
    )
    ups = ups_ref[...]

    @pl.when(pl.program_id(0) == 0)
    def _():
        vec_ref[...] = vectors
        bup_ref[...] = ups

    @pl.when(pl.program_id(0) > 0)
    def _():
        vec_ref[...] += vectors
        bup_ref[...] += ups


def between(x, attended, w_out, w_up, w_down, heads, gain, shift, b_up, b_down, mask, sums, local):
    rows, width = x.shape
    hidden = w_up.shape[1]
    block = math.gcd(local, 256)

    def row(columns):
        return pl.BlockSpec((block, columns), lambda i: (i, 0))

    def whole(values):
        zeros = (0,) * values.ndim
        return pl.BlockSpec(values.shape, lambda i: zeros, pipeline_mode=pl.Buffered(1))

    def shape(columns, kind=BF):
        return jax.ShapeDtypeStruct((rows, columns), kind)

    fixed = [w_out, w_up, w_down, heads, gain, shift, b_up, b_down]
    return pl.pallas_call(
        between_kernel,
        grid=(rows // block,),
        in_specs=[row(width), row(width)]
        + [whole(v) for v in fixed]
        + [pl.BlockSpec((1, 1, 128), lambda i: (i * block // local, 0, 0))]
        + [row(128)] * 3,
        out_specs=[
            row(width),
            row(hidden),
            row(hidden),
            row(width),
            row(width),
            row(384),
            row(width),
            row(width),
            row(width),
            row(128),
            row(128),
            row(128),
            pl.BlockSpec((3, width), lambda i: (0, 0)),
            pl.BlockSpec((1, hidden), lambda i: (0, 0)),
        ],
        out_shape=[
            shape(width),
            shape(hidden),
            shape(hidden),
            shape(width),
            shape(width),
            shape(384),
            shape(width),
            shape(width, F32),
            shape(width),
            shape(128, F32),
            shape(128, F32),
            shape(128, F32),
            jax.ShapeDtypeStruct((3, width), F32),
            jax.ShapeDtypeStruct((1, hidden), F32),
        ],
        scratch_shapes=[
            pltpu.VMEM((block, hidden), F32),
            pltpu.VMEM((block, width), F32),
            pltpu.VMEM((1, hidden), F32),
        ],
        compiler_params=PARAMS,
        name="between",
        cost_estimate=pl.CostEstimate(
            flops=rows * width * hidden, transcendentals=0, bytes_accessed=rows * hidden
        ),
    )(x, attended, *fixed, mask, *sums)


def deal(place, result, mine_ref, sent_ref):
    halves = result.reshape(mine_ref.shape[0], 2, *mine_ref.shape[1:]).astype(BF)
    low = halves[:, 0]
    high = halves[:, 1]
    even = place == 0
    mine_ref[...] = jnp.where(even, low, high)
    sent_ref[...] = jnp.where(even, high, low)


def columns_of(vectors, start):
    count = vectors.shape[0]
    place = lax.broadcasted_iota(jnp.int32, (count, 256), 1)
    which = lax.broadcasted_iota(jnp.int32, (count, 256), 0)
    chosen = (place == which + start).astype(F32).astype(BF)
    high, rest = split_two(vectors)
    return dot(high, chosen, TN) + dot(rest, chosen, TN)


def early_grads_kernel(
    place_ref,
    h_ref,
    a_ref,
    f_ref,
    up_ref,
    attn_ref,
    head_ref,
    vec_ref,
    mine_in_ref,
    sent_in_ref,
    mine_ref,
    sent_ref,
    turn_ref,
):
    step = pl.program_id(0)
    last = pl.num_programs(0) - 1
    place = place_ref[0]
    wide = up_ref.shape[1]

    @pl.when(step == 0)
    def _():
        turn_ref[...] = h_ref[...].T

    @pl.when(step < last - 1)
    def _():
        deal(place, dot(turn_ref[...], up_ref[...]), mine_ref, sent_ref)

    @pl.when(step == last - 1)
    def _():
        turned = a_ref[...].T
        turn_ref[...] = turned
        deal(place, dot(turned, attn_ref[:, :wide]), mine_ref, sent_ref)

    @pl.when(step == last)
    def _():
        out = dot(turn_ref[...], attn_ref[:, wide:])
        heads = dot(f_ref[...].T, head_ref[...]) + columns_of(vec_ref[...], 3 * RESULT_FIELDS)
        deal(place, jnp.concatenate((out, heads), axis=1), mine_ref, sent_ref)


def early_grads(place, hidden, attended, final, up, attn, heads, vectors, mine, sent):
    rows, width = hidden.shape
    wide = 512
    steps = up.shape[1] // wide + 2
    count = width // 96
    skip = mine.shape[2] // wide - steps

    def whole(values):
        return pl.BlockSpec(values.shape, lambda i: (0, 0))

    out = pl.BlockSpec((count, 48, wide), lambda i: (0, 0, i + skip))
    untouched = pl.BlockSpec(memory_space=pl.ANY)
    return pl.pallas_call(
        early_grads_kernel,
        grid=(steps,),
        in_specs=[
            pl.BlockSpec(memory_space=pltpu.SMEM),
            whole(hidden),
            whole(attended),
            whole(final),
            pl.BlockSpec((rows, wide), lambda i: (0, jnp.minimum(i, steps - 3))),
            whole(attn),
            whole(heads),
            whole(vectors),
            untouched,
            untouched,
        ],
        out_specs=[out, out],
        out_shape=[jax.ShapeDtypeStruct(mine.shape, BF)] * 2,
        input_output_aliases={8: 0, 9: 1},
        scratch_shapes=[pltpu.VMEM((width, rows), BF)],
        compiler_params=PARAMS,
        name="early_grads",
        cost_estimate=pl.CostEstimate(
            flops=2 * rows * width * wide * steps,
            transcendentals=0,
            bytes_accessed=2 * rows * wide * steps + 2 * width * wide * steps,
        ),
    )(place, hidden, attended, final, up, attn, heads, vectors, mine, sent)


def down_grads_kernel(place_ref, act_ref, down_ref, mine_ref, sent_ref):
    result = dot(act_ref[...], down_ref[...], TN).astype(BF)
    block = result.shape[0] // 2
    piece = block // 8
    halves = []
    for c in range(2):
        groups = [
            jnp.concatenate(
                [
                    result[c * block + y * 4 * piece + g * piece :][:piece]
                    for y in range(2)
                ],
                axis=0,
            )
            for g in range(4)
        ]
        halves.append(jnp.concatenate(groups, axis=1)[None])
    even = place_ref[0] == 0
    mine_ref[...] = jnp.where(even, halves[0], halves[1])
    sent_ref[...] = jnp.where(even, halves[1], halves[0])


def down_grads(place, activation, down, columns):
    rows, width = down.shape
    block = activation.shape[1] // 8
    piece = block // 16
    out = pl.BlockSpec((1, 2 * piece, 4 * width), lambda i: (i, 0, 0))
    return pl.pallas_call(
        down_grads_kernel,
        grid=(8,),
        in_specs=[
            pl.BlockSpec(memory_space=pltpu.SMEM),
            pl.BlockSpec((rows, block), lambda i: (0, i)),
            pl.BlockSpec((rows, width), lambda i: (0, 0)),
        ],
        out_specs=[out, out],
        out_shape=[jax.ShapeDtypeStruct((8, 2 * piece, columns), BF)] * 2,
        compiler_params=PARAMS,
        name="down_grads",
        cost_estimate=pl.CostEstimate(
            flops=2 * rows * width * block, transcendentals=0, bytes_accessed=width * block
        ),
    )(place, activation, down)


def late_grads_kernel(count, place_ref, *refs):
    mixed_refs = refs[:count]
    query_ref = refs[count]
    both_refs = refs[count + 1 : 2 * count + 1]
    vec_ref, mine_ref, sent_ref, turn_ref = refs[2 * count + 1 :]
    step = pl.program_id(0)
    third = (pl.num_programs(0) - 1) // 3
    place = place_ref[0]

    @pl.when(step == 0)
    def _():
        for s in range(count):
            turn_ref[s] = mixed_refs[s][...].T

    @pl.when(step < third)
    def _():
        deal(place, dot(turn_ref[0], query_ref[...], NT), mine_ref, sent_ref)

    @pl.when((step >= third) & (step < 3 * third))
    def _():
        joint = sum(dot(turn_ref[s], both_refs[s][...]) for s in range(count))
        deal(place, joint, mine_ref, sent_ref)

    @pl.when(step == 3 * third)
    def _():
        deal(place, columns_of(vec_ref[...], 0), mine_ref, sent_ref)


def late_grads(place, mixed, query, both, vectors):
    rows, width = mixed[0].shape
    count = len(mixed)
    wide = 256
    third = width // wide
    groups = width // 96

    whole = pl.BlockSpec((rows, width), lambda i: (0, 0))
    out = pl.BlockSpec((groups, 48, wide), lambda i: (0, 0, i))
    return pl.pallas_call(
        functools.partial(late_grads_kernel, count),
        grid=(3 * third + 1,),
        in_specs=[pl.BlockSpec(memory_space=pltpu.SMEM)]
        + [whole] * count
        + [pl.BlockSpec((wide, rows), lambda i: (jnp.clip(i, 0, third - 1), 0))]
        + [pl.BlockSpec((rows, wide), lambda i: (0, jnp.clip(i - third, 0, 2 * third - 1)))] * count
        + [pl.BlockSpec(vectors.shape, lambda i: (0, 0))],
        out_specs=[out, out],
        out_shape=[jax.ShapeDtypeStruct((groups, 48, wide * (3 * third + 1)), BF)] * 2,
        scratch_shapes=[pltpu.VMEM((count, width, rows), BF)],
        compiler_params=PARAMS,
        name="late_grads",
        cost_estimate=pl.CostEstimate(
            flops=2 * rows * width * width * (2 * count + 1),
            transcendentals=0,
            bytes_accessed=2 * rows * width * 4 * count + 12 * width * width,
        ),
    )(place, *mixed, query, *both, vectors)


def block_sums_kernel(counts, dealt, where_ref, *refs):
    total_in = sum(len(group) for group in counts)
    ins, outs = refs[:total_in], refs[total_in:]
    at = 0
    for o, group in enumerate(counts):
        shape = ins[at].shape[-2:] if dealt else outs[o].shape
        value = None
        for use in group:
            term = ins[at][...].astype(F32).reshape(shape)
            if use is not None:
                term = jnp.where(use(pl.program_id(0), where_ref), term, 0.0)
            value = term if value is None else value + term
            at += 1
        if dealt:
            for k, out in enumerate(outs):

                @pl.when(pl.program_id(0) == k)
                def _(out=out, value=value, o=o):
                    out[o] = value.astype(BF)
        else:
            outs[o][...] = value.astype(BF)


def block_sums(where, steps, groups, dealt=False):
    counts = [[term[3] if len(term) > 3 else None for term in terms] for _, terms in groups]
    operands = [term[0] for _, terms in groups for term in terms]
    in_specs = [pl.BlockSpec(term[1], term[2]) for _, terms in groups for term in terms]
    if dealt:
        shape = (len(groups),) + groups[0][0]
        zeros = (0,) * len(shape)
        out_specs = [pl.BlockSpec(shape, lambda i, w: zeros)] * steps
        out_shape = [jax.ShapeDtypeStruct(shape, BF)] * steps
    else:
        out_specs = [pl.BlockSpec(out[1], out[2]) for out, _ in groups]
        out_shape = [jax.ShapeDtypeStruct(out[0], BF) for out, _ in groups]
    return pl.pallas_call(
        functools.partial(block_sums_kernel, counts, dealt),
        grid_spec=pltpu.PrefetchScalarGridSpec(
            num_scalar_prefetch=1, grid=(steps,), in_specs=in_specs, out_specs=out_specs
        ),
        out_shape=out_shape,
        compiler_params=FULL,
        name="block_sums",
        cost_estimate=pl.CostEstimate(flops=1 << 20, transcendentals=0, bytes_accessed=1 << 20),
    )(where, *operands)


class Reduction:
    def __init__(self, where, terms, by_columns):
        self.where = where
        self.terms = terms
        self.by_columns = by_columns
        self.depth, self.columns = terms[0].shape[3:]
        self.steps = 4 if by_columns else 2
        if by_columns:
            self.columns //= 2

    def at(self, part, x, z, y, sizes):
        block = sizes + (self.depth, self.columns)
        column = part if self.by_columns else 0
        shift = 0 if self.by_columns else 2 * part // sizes[1]

        def index(i, w):
            return (x(w), z(i, w) + shift, y(w), 0, column)

        return [(t, block, index) for t in self.terms]

    def one(self):
        n, tail = self.steps, (self.depth, self.columns)
        ahead = lambda i, w: i
        sent = block_sums(
            self.where,
            n // 2,
            [
                (
                    ((n, 2) + tail, (2, 2) + tail, lambda i, w: (i, 0, 0, 0)),
                    self.at(0, lambda w: 1 - w[0], ahead, lambda w: 0, (1, 2, 2)),
                ),
                (
                    ((2, n) + tail, (2, 2) + tail, lambda i, w: (0, i, 0, 0)),
                    self.at(1, lambda w: 0, ahead, lambda w: 1 - w[1], (2, 2, 1)),
                ),
            ],
        )
        return list(sent)

    def trade_one(self, sent):
        self.got_one = [swap(sent[0], "lat", 1), swap(sent[1], "grp", 2)]

    def two(self):
        n, tail = self.steps, (self.depth, self.columns)
        ahead = lambda i, w: i
        out = ((n,) + tail, (2,) + tail, lambda i, w: (i, 0, 0))
        sent = block_sums(
            self.where,
            n // 2,
            [
                (
                    out,
                    self.at(0, lambda w: w[0], ahead, lambda w: 1 - w[1], (1, 2, 1))
                    + [(self.got_one[0], (2, 1) + tail, lambda i, w: (i, 1 - w[1], 0, 0))],
                ),
                (
                    out,
                    self.at(1, lambda w: 1 - w[0], ahead, lambda w: w[1], (1, 2, 1))
                    + [(self.got_one[1], (1, 2) + tail, lambda i, w: (1 - w[0], i, 0, 0))],
                ),
            ],
        )
        return list(sent)

    def trade_two(self, sent):
        self.got_two = [swap(sent[0], "grp", 2), swap(sent[1], "lat", 1)]

    def quarters(self):
        tail = (self.depth, self.columns)
        x = lambda w: w[0]
        y = lambda w: w[1]
        if self.by_columns:
            place = lambda i, w: w[2] ^ i
            groups = []
            for part in (0, 1):
                terms = self.at(part, x, place, y, (1, 1, 1))
                if part == 0:
                    one = lambda i, w: (w[2] ^ i, w[1], 0, 0)
                else:
                    one = lambda i, w: (w[0], w[2] ^ i, 0, 0)
                terms.append((self.got_one[part], (1, 1) + tail, one))
                terms.append((self.got_two[part], (1,) + tail, lambda i, w: (w[2] ^ i, 0, 0)))
                groups.append((tail, terms))
        else:
            low = lambda i, w: jnp.minimum(w[2] ^ i, 1)
            high = lambda i, w: jnp.maximum((w[2] ^ i) - 2, 0)
            first = lambda i, w: (w[2] ^ i) < 2
            second = lambda i, w: (w[2] ^ i) >= 2
            terms = self.at(0, x, lambda i, w: w[2] ^ i, y, (1, 1, 1))
            pair = (1, 1) + tail
            one = (1,) + tail
            terms += [
                (self.got_one[0], pair, lambda i, w: (low(i, w), w[1], 0, 0), first),
                (self.got_one[1], pair, lambda i, w: (w[0], high(i, w), 0, 0), second),
                (self.got_two[0], one, lambda i, w: (low(i, w), 0, 0), first),
                (self.got_two[1], one, lambda i, w: (high(i, w), 0, 0), second),
            ]
            groups = [(tail, terms)]
        return list(block_sums(self.where, 4, groups, True))


def early_unpack_kernel(place_ref, *refs):
    ins = refs[:4]
    down_ref, up_ref, out_ref, gate_ref, head_ref, gain_ref, bias_ref, bd_ref, bup_ref, misc_ref = refs[4:]
    width = down_ref.shape[1]
    hidden = up_ref.shape[1]
    for source, (c, y) in zip(ins, ((0, 0), (0, 1), (1, 0), (1, 1))):
        slot = jnp.bitwise_xor(place_ref[0], c) * 2 + jnp.bitwise_xor(place_ref[1], y)
        one = source[0].astype(F32)
        two = source[1].astype(F32)
        rows = one.shape[0]
        half = one.shape[1]
        for g in range(4):
            span = pl.ds(pl.multiple_of(slot * 4 * rows + g * rows, 8), rows)
            down_ref[span, :] = one[:, g * width : (g + 1) * width]
        span = pl.ds(pl.multiple_of(slot * rows, 8), rows)
        cut = half - 4 * width
        up_ref[span, :cut] = one[:, 4 * width :]
        up_ref[span, cut:] = two[:, : hidden - cut]
        out_ref[span, :] = two[:, hidden - cut : hidden - cut + width]
        misc_ref[span, :] = two[:, hidden - cut + width :]
    turned = misc_ref[...].T
    at = 0
    for ref in (gate_ref, head_ref, gain_ref, bias_ref, bd_ref, bup_ref):
        count = ref.shape[0]
        ref[...] = turned[at : at + count]
        at += count


def early_unpack(place, pieces, width, hidden):
    rows = pieces[0].shape[1]
    vmem = pl.BlockSpec(memory_space=pltpu.VMEM)
    return pl.pallas_call(
        early_unpack_kernel,
        in_specs=[pl.BlockSpec(memory_space=pltpu.SMEM)] + [vmem] * 4,
        out_specs=[vmem] * 9,
        out_shape=[
            jax.ShapeDtypeStruct((16 * rows, width), F32),
            jax.ShapeDtypeStruct((4 * rows, hidden), F32),
            jax.ShapeDtypeStruct((4 * rows, width), F32),
        ]
        + [
            jax.ShapeDtypeStruct((count, 4 * rows), F32)
            for count in (2 * RESULT_FIELDS, RESULT_FIELDS, 1, 1, 1, 4)
        ],
        scratch_shapes=[pltpu.VMEM((4 * rows, 256), F32)],
        compiler_params=PARAMS,
        name="early_unpack",
        cost_estimate=pl.CostEstimate(flops=1 << 20, transcendentals=0, bytes_accessed=1 << 20),
    )(place, *pieces)


def late_unpack_kernel(place_ref, *refs):
    ins = refs[:4]
    main_ref, gain_ref, bias_ref, lead_ref, misc_ref = refs[4:]
    for source, (c, y) in zip(ins, ((0, 0), (0, 1), (1, 0), (1, 1))):
        slot = jnp.bitwise_xor(place_ref[0], c) * 2 + jnp.bitwise_xor(place_ref[1], y)
        value = source[...].astype(F32)
        rows = value.shape[0]
        span = pl.ds(pl.multiple_of(slot * rows, 8), rows)
        main_ref[span, :] = value[:, : main_ref.shape[1]]
        misc_ref[span, :] = value[:, main_ref.shape[1] :]
    turned = misc_ref[...].T
    gain_ref[...] = turned[:1]
    bias_ref[...] = turned[1:2]
    lead_ref[...] = turned[2 : 2 + LEADS]


def late_unpack(place, pieces):
    rows, columns = pieces[0].shape
    vmem = pl.BlockSpec(memory_space=pltpu.VMEM)
    return pl.pallas_call(
        late_unpack_kernel,
        in_specs=[pl.BlockSpec(memory_space=pltpu.SMEM)] + [vmem] * 4,
        out_specs=[vmem] * 4,
        out_shape=[jax.ShapeDtypeStruct((4 * rows, columns - 256), F32)]
        + [jax.ShapeDtypeStruct((count, 4 * rows), F32) for count in (1, 1, LEADS)],
        scratch_shapes=[pltpu.VMEM((4 * rows, 256), F32)],
        compiler_params=PARAMS,
        name="late_unpack",
        cost_estimate=pl.CostEstimate(flops=1 << 20, transcendentals=0, bytes_accessed=1 << 20),
    )(place, *pieces)


def spread(rows, columns):
    pixel = lax.broadcasted_iota(jnp.int32, (rows, columns), 0)
    field = lax.broadcasted_iota(jnp.int32, (rows, columns), 1)
    return ((pixel // TILE_AREA) == field).astype(F32).astype(BF)


def split_two(values):
    high = values.astype(BF)
    return high, (values - high.astype(F32)).astype(BF)


def pixel_sums_kernel(f_ref, s_ref, sum_ref, first_ref, second_ref, field_ref):
    @pl.when(pl.program_id(0) == 0)
    def _():
        field_ref[...] = spread(*field_ref.shape)

    fields = field_ref[...]
    sens = s_ref[...]
    sum_ref[...] = dot(sens, fields)
    for e, out in ((0, first_ref), (1, second_ref)):
        out[...] = dot((sens.astype(F32) * f_ref[e].astype(F32)).astype(BF), fields)


def pixel_sums(forecasts, sensitivity):
    rows, pixels = sensitivity.shape
    block = math.gcd(rows, 64)
    out = pl.BlockSpec((block, 128), lambda i: (i, 0))
    return pl.pallas_call(
        pixel_sums_kernel,
        grid=(rows // block,),
        in_specs=[
            pl.BlockSpec((2, block, pixels), lambda i: (0, i, 0)),
            pl.BlockSpec((block, pixels), lambda i: (i, 0)),
        ],
        out_specs=[out] * 3,
        out_shape=[jax.ShapeDtypeStruct((rows, 128), F32)] * 3,
        scratch_shapes=[pltpu.VMEM((pixels, 128), BF)],
        compiler_params=PARAMS,
        name="pixel_sums",
        cost_estimate=pl.CostEstimate(
            flops=rows * pixels * 128, transcendentals=0, bytes_accessed=rows * pixels
        ),
    )(forecasts, sensitivity)


def blend_kernel(a_ref, b_ref, c_ref, f_ref, out_ref, field_ref):
    @pl.when(pl.program_id(0) == 0)
    def _():
        columns = field_ref.shape[1]
        field = lax.broadcasted_iota(jnp.int32, (256, columns), 0)
        pixel = lax.broadcasted_iota(jnp.int32, (256, columns), 1)
        field_ref[...] = ((pixel // TILE_AREA) == (field % 128)).astype(F32).astype(BF)

    fields = field_ref[...]

    def wide(ref):
        return dot(jnp.concatenate(split_two(ref[...]), axis=1), fields)

    total = wide(a_ref) * f_ref[0].astype(F32) + wide(b_ref) * f_ref[1].astype(F32)
    out_ref[...] = (total + wide(c_ref)).astype(BF)


def blend(first, second, added, forecasts):
    _, rows, pixels = forecasts.shape
    block = math.gcd(rows, 128)
    thin = pl.BlockSpec((block, 128), lambda i: (i, 0))
    return pl.pallas_call(
        blend_kernel,
        grid=(rows // block,),
        in_specs=[thin] * 3 + [pl.BlockSpec((2, block, pixels), lambda i: (0, i, 0))],
        out_specs=pl.BlockSpec((block, pixels), lambda i: (i, 0)),
        out_shape=jax.ShapeDtypeStruct((rows, pixels), BF),
        scratch_shapes=[pltpu.VMEM((256, pixels), BF)],
        compiler_params=PARAMS,
        name="blend",
        cost_estimate=pl.CostEstimate(
            flops=rows * pixels * 128, transcendentals=0, bytes_accessed=rows * pixels
        ),
    )(first, second, added, forecasts)


def swap(values, axis, bit):
    count = lax.axis_size(axis)
    return lax.ppermute(values, axis, [(i, i ^ bit) for i in range(count)])


def add(*terms):
    return sum(t.astype(F32) for t in terms).astype(BF)


def hold(*values):
    return lax.optimization_barrier(values)


def layer_norm(values):
    centred = values - jnp.mean(values, axis=-1, keepdims=True)
    inverse = lax.rsqrt(jnp.mean(centred * centred, axis=-1, keepdims=True) + EPSILON)
    return centred * inverse, inverse


def norm_back(grad_normed, normed, inverse):
    return inverse * (
        grad_normed
        - jnp.mean(grad_normed, axis=-1, keepdims=True)
        - normed * jnp.mean(grad_normed * normed, axis=-1, keepdims=True)
    )


def pad_lanes(values):
    return jnp.pad(values, ((0, 0), (0, 128 - values.shape[1])))


def per_device(
    layer_source_tensor,
    horizon_class,
    field_selector,
    model_predictions,
    loss_sensitivity,
    gain_one,
    shift_one,
    horizon_vectors,
    w_qkv,
    w_out,
    gain_two,
    shift_two,
    w_up,
    b_up,
    w_down,
    b_down,
    w_gate,
    w_bias,
):
    frames, lat_rows, lon_cols, width = layer_source_tensor.shape
    local = lat_rows * lon_cols
    rows = frames * local
    pixels = loss_sensitivity.shape[-1]
    sizes = (lax.axis_size("grp"), lax.axis_size("lat"), lax.axis_size("lon"))
    small = sizes == (4, 2, 4) and frames == 1

    source = layer_source_tensor.reshape(frames, local, width)
    place = lax.axis_index("lon")
    edge = (place == 0) | (place == lax.axis_size("lon") - 1)
    send = functools.partial(lax.ppermute, axis_name="lon")
    if small:
        right = send(source, perm=[(0, 1), (1, 2), (2, 3)])
        left = send(source, perm=[(3, 2), (2, 1), (1, 0)])
    else:
        shards = [lax.all_gather(source, "lon", axis=1, tiled=True)]

    forecasts = jnp.transpose(model_predictions.reshape(rows, 2, pixels), (1, 0, 2))
    sensitivity = loss_sensitivity.reshape(rows, pixels)

    onehot = (horizon_class[:, None] == jnp.arange(LEADS, dtype=jnp.int32)[None, :]).astype(F32)
    lead_rows = jnp.dot(onehot, horizon_vectors, precision=HIGH)

    def mixed_of(values):
        normed, _ = layer_norm(values.astype(F32))
        return (normed * gain_one + shift_one + lead_rows[:, None, :]).astype(BF)

    wq = w_qkv[:, :width]
    wkv = w_qkv[:, width:]

    def keys_of(values):
        return dot(values.reshape(-1, width), wkv).astype(BF).reshape(frames, -1, 2 * width)

    if small:

        def flat(values):
            return values.reshape(rows, width)

        def shard_of(flag, yes, no):
            m, kv, x = project(
                flag.astype(jnp.int32)[None],
                [flat(yes), flat(no)],
                gain_one,
                shift_one,
                lead_rows,
                w_qkv,
            )
            return m, kv[None], x[None]

        mixed_own, own_kv, queries = project(
            None, [flat(source)], gain_one, shift_one, lead_rows, w_qkv
        )
        queries = queries[None]
        mixed = [mixed_own]
        key_value = [own_kv[None]]
        right, left, forecasts, queries, key_value[0] = hold(
            right, left, forecasts, queries, key_value[0]
        )
        right_two = send(right, perm=[(1, 2), (2, 3)])
        left_two = send(left, perm=[(2, 1), (1, 0)])
        sums = pixel_sums(forecasts, sensitivity)
        m, kv, near = shard_of(place == 0, left, right)
        mixed.append(m)
        right_two, left_two, kv, *sums = hold(right_two, left_two, kv, *sums)
        key_value.append(kv)
        two = right_two + left_two
        two, middle = hold(two, left)
        three = send(two, perm=[(2, 3), (1, 0)])
        m, kv, middle = shard_of(edge, two, middle)
        mixed.append(m)
        key_value.append(kv)
        state = attend(queries, key_value, None, False)
        three, *state = hold(three, *state)
        m, kv, far = shard_of(edge, three, two)
        mixed.append(m)
        key_value.append(kv)
        attended, logs = attend(queries, key_value[3:], state, True)
        shards = [source, near, middle, far]
    else:
        mixed_own = mixed_of(source)
        queries = dot(mixed_own.reshape(rows, width), wq).astype(BF)
        queries = queries.reshape(frames, local, width)
        sums = pixel_sums(forecasts, sensitivity)
        mixed = [mixed_of(shards[0])]
        key_value = [keys_of(mixed[0])]
        attended, logs = attend(queries, key_value, None, True)
    inputs = source.reshape(rows, width)
    attended_low = attended.reshape(rows, width)
    both = w_gate.T
    head_rows = jnp.concatenate(
        [
            jnp.pad(m, ((0, 128 - RESULT_FIELDS), (0, 0)))
            for m in (both[:RESULT_FIELDS], both[RESULT_FIELDS:], w_bias.T)
        ]
    )
    mask = pad_lanes(field_selector.astype(F32))[:, None]
    (
        hidden_low,
        activation_low,
        up_low,
        down_low,
        final_low,
        heads_low,
        attn_low,
        grad_residual,
        grad_attended,
        *blending,
        early_vectors,
        grad_bup,
    ) = between(
        inputs,
        attended_low,
        w_out,
        w_up,
        w_down,
        head_rows,
        gain_two,
        shift_two,
        b_up,
        b_down,
        mask,
        sums,
        local,
    )
    grad_attended = grad_attended.reshape(frames, local, width)
    fields = 3 * RESULT_FIELDS
    heads_low = jnp.concatenate(
        [heads_low[:, g * 128 : g * 128 + RESULT_FIELDS] for g in range(3)], axis=1
    )
    inputs = inputs.astype(F32)
    normed_one, inverse_one = layer_norm(inputs)

    def input_gradient(grad_mixed):
        return grad_residual + norm_back(
            grad_mixed.reshape(rows, width) * gain_one, normed_one, inverse_one
        )

    def back(shard, place, before):
        return attend_back(queries, grad_attended, attended, logs, shard, w_qkv, place, before)

    nothing = jnp.zeros((frames, width, local), F32)

    def late_vectors(sums):
        gain_column = sum(jnp.sum(s[:, 0], axis=0) for s in sums)
        column = sum(s[:, 1] for s in sums)
        lead = jnp.dot(onehot.T, column, precision=HIGH)
        zeros = jnp.zeros((6, width), F32)
        return jnp.concatenate((gain_column[None], jnp.sum(column, axis=0)[None], lead, zeros))

    if small:
        bup_rows = jnp.swapaxes(grad_bup.reshape(8, 4, -1), 0, 1).reshape(4, width)
        early_vectors = jnp.concatenate(
            (early_vectors, bup_rows, jnp.zeros((1, width), F32))
        )
        core = (lax.axis_index("grp") % 2).astype(jnp.int32)[None]
        where = jnp.stack(
            (lax.axis_index("lat"), lax.axis_index("grp") // 2, lax.axis_index("lon"))
        ).astype(jnp.int32)
        hidden = w_up.shape[1]
        mine, sent = down_grads(core, activation_low, down_low, 2 * hidden + width + 256)
        mine, sent = early_grads(
            core,
            hidden_low,
            attended_low,
            final_low,
            up_low,
            attn_low,
            jnp.pad(heads_low, ((0, 0), (0, 256 - fields))),
            early_vectors,
            mine,
            sent,
        )
        grad_attended, sent = hold(grad_attended, sent)
        got = swap(sent, "grp", 1)

        grad_query, dkv3, far, sums3 = back(key_value[3], shards[3], nothing)
        early = Reduction(where, [t.reshape(2, 4, 2, 24, -1) for t in (mine, got)], True)
        grad_query, far, *sent = hold(grad_query, far, *early.one())
        got = send(far, perm=[(0, 1), (3, 2)])
        early.trade_one(sent)

        grad_query, dkv2, middle, sums2 = back(key_value[2], shards[2], grad_query)
        value = jnp.where(edge, middle, add(got, far))
        grad_query, value = hold(grad_query, value)
        right = send(value, perm=[(0, 1), (1, 2)])
        left = send(value, perm=[(3, 2), (2, 1)])

        grad_query, dkv1, near, sums1 = back(key_value[1], shards[1], grad_query)
        forth = jnp.where(place == 0, near, add(right, middle))
        back_value = add(left, near)
        grad_query, forth, back_value, *sent = hold(
            grad_query, forth, back_value, *early.two()
        )
        right = send(forth, perm=[(0, 1), (1, 2), (2, 3)])
        left = send(back_value, perm=[(3, 2), (2, 1), (1, 0)])
        early.trade_two(sent)

        grad_query, dkv0, own, sums0, right, left, *early.got_two = hold(
            *back(key_value[0], shards[0], grad_query), right, left, *early.got_two
        )
        query_low, query_term, query_sums = query_back(grad_query, w_qkv, source)
        vectors = late_vectors([sums0, sums1, sums2, sums3, query_sums])
        late_mine, late_sent = late_grads(
            core,
            [m.reshape(rows, width) for m in mixed],
            query_low.reshape(width, rows),
            [d.reshape(rows, 2 * width) for d in (dkv0, dkv1, dkv2, dkv3)],
            vectors,
        )
        late_mine, late_sent, *early.got_two, own = hold(
            late_mine, late_sent, *early.got_two, own
        )
        got = swap(late_sent, "grp", 1)
        got, *parts = hold(got, *early.quarters())
        late = Reduction(where, [t.reshape(2, 4, 2, 24, -1) for t in (late_mine, got)], False)
        *sent, one, two, three = hold(*late.one(), *blending)
        late.trade_one(sent)
        early = [parts[0]] + [swap(parts[k], "lon", k) for k in (1, 2, 3)]
        blended = blend(one, two, three, forecasts)
        *late.got_one, blended = hold(*late.got_one, blended)
        *sent, own, early[0] = hold(*late.two(), own, early[0])
        late.trade_two(sent)
        grad_input = input_gradient(
            own.astype(F32) + query_term + right.astype(F32) + left.astype(F32)
        )
        *late.got_two, grad_input = hold(*late.got_two, grad_input)
        early[0], *parts = hold(early[0], *late.quarters())
        late = [parts[0]] + [swap(parts[k], "lon", k) for k in (1, 2, 3)]
        late[1], late[2], early[0] = hold(late[1], late[2], early[0])
        late = add(*[part[0] for part in late])
        late_y = swap(late, "grp", 2)
        late_c = swap(late, "grp", 1)
        early = add(*early)
        early_y = swap(early, "grp", 2)
        early_c = swap(early, "grp", 1)
        early_y, early_c, early, late_y, late_c, late = hold(
            early_y, early_c, early, late_y, late_c, late
        )
        early_yc = swap(early_y, "grp", 1)
        late_yc = swap(late_y, "grp", 1)
        place_two = jnp.stack((lax.axis_index("grp") % 2, lax.axis_index("grp") // 2))
        place_two = place_two.astype(jnp.int32)
        down_sum, up_sum, out_sum, gate_sum, head_sum, *early, bup_sum = early_unpack(
            place_two, [early, early_y, early_c, early_yc], width, hidden
        )
        late_yc, gate_sum = hold(late_yc, gate_sum)
        qkv_sum, *late, lead_sum = late_unpack(place_two, [late, late_y, late_c, late_yc])
        early = [e.reshape(-1) for e in early]
        late = [e.reshape(-1) for e in late]
        bup_sum = bup_sum.reshape(-1)
        gate_sum = gate_sum.T
        head_sum = head_sum.T
    else:
        blended = blend(*blending, forecasts)
        grad_query, dkv, term, sums = back(key_value[0], shards[0], nothing)
        query_low, query_term, query_sums = query_back(grad_query, w_qkv, source)
        grad_input = input_gradient(
            query_term + lax.psum_scatter(term.astype(F32), "lon", scatter_dimension=1, tiled=True)
        )

        def total_of(values, dim=0):
            share = lax.psum_scatter(values, ("lat", "lon"), scatter_dimension=dim, tiled=True)
            return lax.psum(share, "grp")

        flat = mixed[0].reshape(-1, width)
        qkv_sum = total_of(
            jnp.concatenate(
                (
                    jnp.einsum("frd,fer->de", mixed_own, query_low, preferred_element_type=F32),
                    dot(flat, dkv.reshape(-1, 2 * width), TN),
                ),
                axis=1,
            )
        )
        up_sum = total_of(dot(hidden_low, up_low, TN))
        out_sum = total_of(dot(attended_low, attn_low, TN))
        down_sum = total_of(dot(activation_low, down_low, TN))
        heads = total_of(dot(final_low, heads_low, TN))
        late = total_of(late_vectors([sums, query_sums])[: 2 + LEADS], 1)
        lead_sum = late[2:]
        gate_sum = heads[:, : 2 * RESULT_FIELDS]
        head_sum = heads[:, 2 * RESULT_FIELDS :]
        early = total_of(early_vectors, 1)
        bup_sum = total_of(grad_bup[0])

    return (
        blended.reshape(frames, lat_rows, lon_cols, pixels),
        grad_input.reshape(frames, lat_rows, lon_cols, width),
        late[0],
        late[1],
        lead_sum,
        qkv_sum,
        out_sum,
        early[0],
        early[1],
        up_sum,
        bup_sum,
        down_sum,
        early[2],
        gate_sum,
        head_sum,
    )


def solution(mesh):
    frame = ("grp", "lat")
    share = ("lat", "lon")
    image = P(frame, None, "lon", None)
    in_specs = (
        image,
        P(frame),
        P(frame, None),
        P(frame, None, "lon", None, None),
        image,
    ) + (P(),) * 13
    vector = P(share)
    matrix = P(share, None)
    out_specs = (
        image,
        image,
        vector,
        vector,
        P(None, share),
        matrix,
        matrix,
        vector,
        vector,
        matrix,
        vector,
        matrix,
        vector,
        matrix,
        matrix,
    )
    return jax.shard_map(
        per_device, mesh=mesh, in_specs=in_specs, out_specs=out_specs, check_vma=False
    )
```

```python
import functools
import math

import jax
import jax.numpy as jnp
from jax import lax
from jax.experimental import pallas as pl
from jax.experimental.pallas import tpu as pltpu
from jax.sharding import PartitionSpec as P

H = 12
DH = 64
RESULT_FIELDS = 69
TILE_AREA = 64
LEADS = 24
EPSILON = 1e-06
HIGH = lax.Precision.HIGHEST
SCALE = 0.125
SCALE_TWO = SCALE * math.log2(math.e)
ROOT = math.sqrt(2.0 / math.pi)
CUBE = 0.044715
NN = (((1,), (0,)), ((), ()))
NT = (((1,), (1,)), ((), ()))
TN = (((0,), (0,)), ((), ()))
BF = jnp.bfloat16
F32 = jnp.float32
PARAMS = pltpu.CompilerParams(vmem_limit_bytes=60 * 1024 * 1024)
FULL = pltpu.CompilerParams(vmem_limit_bytes=63 * 1024 * 1024 + 512 * 1024)


def dot(left, right, dims=NN):
    return lax.dot_general(left, right, dims, preferred_element_type=F32)


def project_kernel(own, *refs):
    if own:
        a_ref, gain_ref, shift_ref, lead_ref, wq_ref, wk_ref, wv_ref, mixed_ref, kv_ref, q_ref = refs
        value = a_ref[...]
    else:
        flag_ref, a_ref, b_ref, gain_ref, shift_ref, lead_ref, wk_ref, wv_ref = refs[:8]
        mixed_ref, kv_ref, x_ref = refs[8:]
        value = jnp.where(flag_ref[0] != 0, a_ref[...], b_ref[...])
        x_ref[...] = value
    normed, _ = layer_norm(value.astype(F32))
    mixed = (normed * gain_ref[...][None] + shift_ref[...][None] + lead_ref[...]).astype(BF)
    mixed_ref[...] = mixed
    width = mixed.shape[1]
    kv_ref[:, :width] = dot(mixed, wk_ref[...]).astype(BF)
    kv_ref[:, width:] = dot(mixed, wv_ref[...]).astype(BF)
    if own:
        q_ref[...] = dot(mixed, wq_ref[...]).astype(BF)


def project(flag, sources, gain, shift, lead, weights):
    own = flag is None
    rows, width = sources[0].shape
    block = math.gcd(rows, 256)
    row = pl.BlockSpec((block, width), lambda i: (i, 0))
    vector = pl.BlockSpec((width,), lambda i: (0,))

    def columns(group):
        return pl.BlockSpec((width, width), lambda i: (0, group))

    groups = (0, 1, 2) if own else (1, 2)
    return pl.pallas_call(
        functools.partial(project_kernel, own),
        grid=(rows // block,),
        in_specs=([] if own else [pl.BlockSpec(memory_space=pltpu.SMEM)])
        + [row] * len(sources)
        + [vector, vector, pl.BlockSpec((1, width), lambda i: (0, 0))]
        + [columns(g) for g in groups],
        out_specs=[row, pl.BlockSpec((block, 2 * width), lambda i: (i, 0)), row],
        out_shape=[
            jax.ShapeDtypeStruct((rows, width), BF),
            jax.ShapeDtypeStruct((rows, 2 * width), BF),
            jax.ShapeDtypeStruct((rows, width), BF),
        ],
        compiler_params=PARAMS,
        name="project",
        cost_estimate=pl.CostEstimate(
            flops=rows * width * width, transcendentals=0, bytes_accessed=rows * width
        ),
    )(*([] if own else [flag]), *sources, gain, shift, lead, *([weights] * len(groups)))


def attend_kernel(count, chained, final, *refs):
    q_ref = refs[0]
    k_refs = refs[1 : 1 + count]
    v_refs = refs[1 + count : 1 + 2 * count]
    o_ref, l_ref = refs[-2:]
    outs = []
    for h in range(2):
        part = slice(h * DH, h * DH + DH)
        q = q_ref[0, :, part]
        scores = [dot(k[0, :, part], q, NT) for k in k_refs]
        top = functools.reduce(
            jnp.maximum, [jnp.max(s, axis=0, keepdims=True) for s in scores]
        )
        top = top * SCALE_TWO
        total = None
        mixed = None
        for s, v in zip(scores, v_refs):
            raised = jnp.exp2(s * SCALE_TWO - top)
            some = jnp.sum(raised, axis=0, keepdims=True)
            term = dot(v[0, :, part], raised.astype(BF), TN)
            total = some if total is None else total + some
            mixed = term if mixed is None else mixed + term
        mixed = mixed * (1.0 / total)
        log = top + jnp.log2(total)
        if chained:
            before_ref, before_log_ref = refs[1 + 2 * count : 3 + 2 * count]
            before = before_log_ref[0, 0, h : h + 1, :]
            high = jnp.maximum(before, log)
            joint = high + jnp.log2(jnp.exp2(before - high) + jnp.exp2(log - high))
            mixed = mixed * jnp.exp2(log - joint) + before_ref[0, part, :] * jnp.exp2(
                before - joint
            )
            log = joint
        l_ref[0, 0, h : h + 1, :] = log
        if final:
            outs.append(mixed)
        else:
            o_ref[0, part, :] = mixed
    if final:
        o_ref[0] = jnp.concatenate(outs, axis=0).T.astype(BF)


def attend(queries, shards, before, final):
    frames, rows, width = queries.shape
    count = len(shards)
    keys = shards[0].shape[1]
    pairs = width // 128
    turned = pl.BlockSpec((1, 128, rows), lambda f, p: (f, p, 0))
    row = pl.BlockSpec((1, rows, 128), lambda f, p: (f, 0, p))
    log = pl.BlockSpec((1, 1, 2, rows), lambda f, p: (f, p, 0, 0))
    chained = before is not None
    return pl.pallas_call(
        functools.partial(attend_kernel, count, chained, final),
        grid=(frames, pairs),
        in_specs=[row]
        + [pl.BlockSpec((1, keys, 128), lambda f, p: (f, 0, p))] * count
        + [pl.BlockSpec((1, keys, 128), lambda f, p: (f, 0, p + pairs))] * count
        + ([turned, log] if chained else []),
        out_specs=[row if final else turned, log],
        out_shape=[
            jax.ShapeDtypeStruct((frames, rows, width), BF)
            if final
            else jax.ShapeDtypeStruct((frames, width, rows), F32),
            jax.ShapeDtypeStruct((frames, pairs, 2, rows), F32),
        ],
        compiler_params=PARAMS,
        name="attend",
        cost_estimate=pl.CostEstimate(
            flops=2 * frames * rows * count * keys * width,
            transcendentals=0,
            bytes_accessed=frames * rows * width,
        ),
    )(queries, *shards, *shards, *(before if chained else ()))


def column_sums(total_ref, x_ref, term_ref=None):
    rows, width = total_ref.shape
    block = math.gcd(rows, 64)

    def step(i, sums):
        span = pl.ds(pl.multiple_of(i * block, block), block)
        total = total_ref[span, :]
        if term_ref is not None:
            term_ref[span, :] = total.astype(term_ref.dtype)
        normed, _ = layer_norm(x_ref[span, :].astype(F32))
        return sums + jnp.concatenate(
            (
                jnp.sum(total * normed, axis=0, keepdims=True),
                jnp.sum(total, axis=0, keepdims=True),
            )
        )

    return lax.fori_loop(0, rows // block, step, jnp.zeros((2, width), F32))


def attend_back_kernel(
    q_ref,
    g_ref,
    o_ref,
    l_ref,
    k_ref,
    v_ref,
    wk_ref,
    wv_ref,
    x_ref,
    before_ref,
    dq_ref,
    dkv_ref,
    term_ref,
    sums_ref,
    total_ref,
):
    pair = pl.program_id(1)
    key_terms = []
    value_terms = []
    query_terms = []
    for h in range(2):
        part = slice(h * DH, h * DH + DH)
        q = q_ref[0, :, part]
        g = g_ref[0, :, part]
        k = k_ref[0, :, part]
        v = v_ref[0, :, part]
        product = g.astype(F32) * o_ref[0, :, part].astype(F32)
        high, low = split_two(product)
        ones = jnp.ones((8, DH), BF)
        delta = (dot(ones, high, NT) + dot(ones, low, NT))[0:1]
        probs = jnp.exp2(dot(k, q, NT) * SCALE_TWO - l_ref[0, 0, h : h + 1, :])
        grad_probs = dot(v, g, NT)
        grad_scores = (probs * (grad_probs - delta)).astype(BF)
        value_terms.append(dot(probs.astype(BF), g))
        key_terms.append(dot(grad_scores, q))
        grad_query = dot(k, grad_scores, TN) * SCALE + before_ref[0, part, :]
        query_terms.append(grad_query)
    grad_key = (jnp.concatenate(key_terms, axis=1) * SCALE).astype(BF)
    grad_value = jnp.concatenate(value_terms, axis=1).astype(BF)
    grad_query = jnp.concatenate(query_terms, axis=0).astype(dq_ref.dtype)
    width = wk_ref.shape[0]
    dkv_ref[0, :, pl.ds(pl.multiple_of(pair * 128, 128), 128)] = grad_key
    dkv_ref[0, :, pl.ds(pl.multiple_of(width + pair * 128, 128), 128)] = grad_value
    dq_ref[0] = grad_query

    @pl.when(pair == pl.num_programs(1) - 1)
    def _():
        total = dot(dkv_ref[0, :, :width], wk_ref[...], NT)
        total_ref[...] = total + dot(dkv_ref[0, :, width:], wv_ref[...], NT)
        sums_ref[0] = column_sums(total_ref, x_ref.at[0], term_ref.at[0])


def attend_back(queries, grad_out, out, logs, shard, weights, source, before):
    frames, rows, width = queries.shape
    keys = shard.shape[1]
    pairs = width // 128
    row = pl.BlockSpec((1, rows, 128), lambda f, p: (f, 0, p))
    key = pl.BlockSpec((1, keys, 128), lambda f, p: (f, 0, p))
    value = pl.BlockSpec((1, keys, 128), lambda f, p: (f, 0, p + pairs))
    turned = pl.BlockSpec((1, 128, rows), lambda f, p: (f, p, 0))
    log = pl.BlockSpec((1, 1, 2, rows), lambda f, p: (f, p, 0, 0))

    def columns(group):
        return pl.BlockSpec((width, width), lambda f, p: (0, group))

    def whole(*shape):
        return pl.BlockSpec((1,) + shape, lambda f, p: (f, 0, 0))

    in_specs = [row, row, row, log, key, value, columns(1), columns(2), whole(keys, width)]
    operands = [queries, grad_out, out, logs, shard, shard, weights, weights, source]
    aliases = {len(operands): 0}
    in_specs.append(turned)
    operands.append(before)
    out_specs = [turned, whole(keys, 2 * width), whole(keys, width), whole(2, width)]
    out_shape = [
        jax.ShapeDtypeStruct((frames, width, rows), F32),
        jax.ShapeDtypeStruct((frames, keys, 2 * width), BF),
        jax.ShapeDtypeStruct((frames, keys, width), BF),
        jax.ShapeDtypeStruct((frames, 2, width), F32),
    ]
    return pl.pallas_call(
        attend_back_kernel,
        grid=(frames, pairs),
        in_specs=in_specs,
        out_specs=out_specs,
        out_shape=out_shape,
        scratch_shapes=[pltpu.VMEM((keys, width), F32)],
        input_output_aliases=aliases,
        compiler_params=PARAMS,
        name="attend_back",
        cost_estimate=pl.CostEstimate(
            flops=4 * frames * rows * keys * width,
            transcendentals=0,
            bytes_accessed=frames * rows * width,
        ),
    )(*operands)


def query_back_kernel(dq_ref, w_ref, x_ref, low_ref, term_ref, sums_ref):
    low = dq_ref[0].astype(BF)
    low_ref[0] = low
    total = dot(low, w_ref[...], (((0,), (1,)), ((), ())))
    term_ref[0] = total
    sums_ref[0] = column_sums(term_ref.at[0], x_ref.at[0])


def query_back(grad_query, weights, source):
    frames, width, rows = grad_query.shape

    def whole(*shape):
        return pl.BlockSpec((1,) + shape, lambda f: (f, 0, 0))

    return pl.pallas_call(
        query_back_kernel,
        grid=(frames,),
        in_specs=[
            whole(width, rows),
            pl.BlockSpec((width, width), lambda f: (0, 0)),
            whole(rows, width),
        ],
        out_specs=[whole(width, rows), whole(rows, width), whole(2, width)],
        out_shape=[
            jax.ShapeDtypeStruct((frames, width, rows), BF),
            jax.ShapeDtypeStruct((frames, rows, width), F32),
            jax.ShapeDtypeStruct((frames, 2, width), F32),
        ],
        compiler_params=PARAMS,
        name="query_back",
        cost_estimate=pl.CostEstimate(
            flops=frames * rows * width * width, transcendentals=0, bytes_accessed=rows * width
        ),
    )(grad_query, weights, source)


def input_back_kernel(
    own_ref, query_ref, right_ref, left_ref, residual_ref, x_ref, gain_ref, out_ref
):
    total = own_ref[...].astype(F32) + query_ref[...]
    total = total + right_ref[...].astype(F32) + left_ref[...].astype(F32)
    normed, inverse = layer_norm(x_ref[...].astype(F32))
    out_ref[...] = residual_ref[...] + norm_back(total * gain_ref[...][None], normed, inverse)


def input_back(terms, residual, source, gain):
    rows, width = source.shape
    block = math.gcd(rows, 128)
    row = pl.BlockSpec((block, width), lambda i: (i, 0))
    return pl.pallas_call(
        input_back_kernel,
        grid=(rows // block,),
        in_specs=[row] * 6 + [pl.BlockSpec((width,), lambda i: (0,))],
        out_specs=row,
        out_shape=jax.ShapeDtypeStruct((rows, width), F32),
        compiler_params=PARAMS,
        name="input_back",
        cost_estimate=pl.CostEstimate(flops=1 << 20, transcendentals=0, bytes_accessed=1 << 20),
    )(*terms, residual, source, gain)


def between_kernel(
    x_ref,
    att_ref,
    wo_ref,
    wu_ref,
    wd_ref,
    head_ref,
    gain_ref,
    shift_ref,
    bu_ref,
    bd_ref,
    mask_ref,
    sens_ref,
    one_ref,
    two_ref,
    hidden_ref,
    act_ref,
    up_ref,
    down_ref,
    final_ref,
    heads_ref,
    attn_ref,
    gres_ref,
    gatt_ref,
    first_ref,
    second_ref,
    added_ref,
    vec_ref,
    bup_ref,
    slope_ref,
    sum_ref,
    ups_ref,
):
    residual = x_ref[...].astype(F32) + dot(att_ref[...], wo_ref[...])
    normed, inverse = layer_norm(residual)
    gain = gain_ref[...][None]
    hidden = (normed * gain + shift_ref[...][None]).astype(BF)
    hidden_ref[...] = hidden
    wide = 1024
    steps = wu_ref.shape[1] // wide
    sum_ref[...] = residual + bd_ref[...][None]

    def chunk(j):
        return pl.ds(pl.multiple_of(j * wide, wide), wide)

    @pl.loop(0, steps)
    def _(j):
        part = chunk(j)
        up = dot(hidden, wu_ref[:, part]) + bu_ref[part][None]
        square = up * up
        tanh = jnp.tanh(ROOT * up * (1.0 + CUBE * square))
        half = 0.5 * (1.0 + tanh)
        act = (up * half).astype(BF)
        slope_ref[:, part] = half + 0.5 * up * (1.0 - tanh * tanh) * (
            ROOT + 3.0 * ROOT * CUBE * square
        )
        act_ref[:, part] = act
        sum_ref[...] += dot(act, wd_ref[part, :])

    final = sum_ref[...]
    final_low = final.astype(BF)
    final_ref[...] = final_low
    logits = dot(final_low, head_ref[...], NT)
    one = logits[:, :128]
    two = logits[:, 128:256]
    offset = logits[:, 256:]
    top = jnp.maximum(one, two)
    one = jnp.exp(one - top)
    two = jnp.exp(two - top)
    total = one + two
    one = one / total
    two = two / total
    mask = mask_ref[0]
    first_ref[...] = mask * one + (1.0 - mask)
    second_ref[...] = mask * two
    added_ref[...] = mask * offset
    grad_one = mask * one_ref[...]
    grad_two = mask * two_ref[...]
    mean = one * grad_one + two * grad_two
    heads = jnp.concatenate(
        (one * (grad_one - mean), two * (grad_two - mean), mask * sens_ref[...]), axis=1
    ).astype(BF)
    heads_ref[...] = heads
    grad_final = dot(heads, head_ref[...])
    down = grad_final.astype(BF)
    down_ref[...] = down
    sum_ref[...] = jnp.zeros_like(sum_ref)

    @pl.loop(0, steps)
    def _(j):
        part = chunk(j)
        grad_up = (dot(down, wd_ref[part, :], NT) * slope_ref[:, part]).astype(BF)
        up_ref[:, part] = grad_up
        ups_ref[:, part] = jnp.sum(grad_up.astype(F32), axis=0, keepdims=True)
        sum_ref[...] += dot(grad_up, wu_ref[:, part], NT)

    grad_hidden = sum_ref[...]
    grad_normed = grad_hidden * gain
    grad_residual = grad_final + norm_back(grad_normed, normed, inverse)
    gres_ref[...] = grad_residual
    attn = grad_residual.astype(BF)
    attn_ref[...] = attn
    gatt_ref[...] = dot(attn, wo_ref[...], NT).astype(BF)
    vectors = jnp.concatenate(
        (
            jnp.sum(grad_hidden * normed, axis=0, keepdims=True),
            jnp.sum(grad_hidden, axis=0, keepdims=True),
            jnp.sum(down.astype(F32), axis=0, keepdims=True),
        )
    )
    ups = ups_ref[...]

    @pl.when(pl.program_id(0) == 0)
    def _():
        vec_ref[...] = vectors
        bup_ref[...] = ups

    @pl.when(pl.program_id(0) > 0)
    def _():
        vec_ref[...] += vectors
        bup_ref[...] += ups


def between(x, attended, w_out, w_up, w_down, heads, gain, shift, b_up, b_down, mask, sums, local):
    rows, width = x.shape
    hidden = w_up.shape[1]
    block = math.gcd(local, 256)

    def row(columns):
        return pl.BlockSpec((block, columns), lambda i: (i, 0))

    def whole(values):
        zeros = (0,) * values.ndim
        return pl.BlockSpec(values.shape, lambda i: zeros, pipeline_mode=pl.Buffered(1))

    def shape(columns, kind=BF):
        return jax.ShapeDtypeStruct((rows, columns), kind)

    fixed = [w_out, w_up, w_down, heads, gain, shift, b_up, b_down]
    return pl.pallas_call(
        between_kernel,
        grid=(rows // block,),
        in_specs=[row(width), row(width)]
        + [whole(v) for v in fixed]
        + [pl.BlockSpec((1, 1, 128), lambda i: (i * block // local, 0, 0))]
        + [row(128)] * 3,
        out_specs=[
            row(width),
            row(hidden),
            row(hidden),
            row(width),
            row(width),
            row(384),
            row(width),
            row(width),
            row(width),
            row(128),
            row(128),
            row(128),
            pl.BlockSpec((3, width), lambda i: (0, 0)),
            pl.BlockSpec((1, hidden), lambda i: (0, 0)),
        ],
        out_shape=[
            shape(width),
            shape(hidden),
            shape(hidden),
            shape(width),
            shape(width),
            shape(384),
            shape(width),
            shape(width, F32),
            shape(width),
            shape(128, F32),
            shape(128, F32),
            shape(128, F32),
            jax.ShapeDtypeStruct((3, width), F32),
            jax.ShapeDtypeStruct((1, hidden), F32),
        ],
        scratch_shapes=[
            pltpu.VMEM((block, hidden), F32),
            pltpu.VMEM((block, width), F32),
            pltpu.VMEM((1, hidden), F32),
        ],
        compiler_params=PARAMS,
        name="between",
        cost_estimate=pl.CostEstimate(
            flops=rows * width * hidden, transcendentals=0, bytes_accessed=rows * hidden
        ),
    )(x, attended, *fixed, mask, *sums)


def deal(place, result, mine_ref, sent_ref):
    halves = result.reshape(mine_ref.shape[0], 2, *mine_ref.shape[1:]).astype(BF)
    low = halves[:, 0]
    high = halves[:, 1]
    even = place == 0
    mine_ref[...] = jnp.where(even, low, high)
    sent_ref[...] = jnp.where(even, high, low)


def columns_of(vectors, start):
    count = vectors.shape[0]
    place = lax.broadcasted_iota(jnp.int32, (count, 256), 1)
    which = lax.broadcasted_iota(jnp.int32, (count, 256), 0)
    chosen = (place == which + start).astype(F32).astype(BF)
    high, rest = split_two(vectors)
    return dot(high, chosen, TN) + dot(rest, chosen, TN)


def early_grads_kernel(
    place_ref,
    h_ref,
    a_ref,
    f_ref,
    up_ref,
    attn_ref,
    head_ref,
    vec_ref,
    mine_in_ref,
    sent_in_ref,
    mine_ref,
    sent_ref,
    turn_ref,
):
    step = pl.program_id(0)
    last = pl.num_programs(0) - 1
    place = place_ref[0]
    wide = up_ref.shape[1]

    @pl.when(step == 0)
    def _():
        turn_ref[...] = h_ref[...].T

    @pl.when(step < last - 1)
    def _():
        deal(place, dot(turn_ref[...], up_ref[...]), mine_ref, sent_ref)

    @pl.when(step == last - 1)
    def _():
        turned = a_ref[...].T
        turn_ref[...] = turned
        deal(place, dot(turned, attn_ref[:, :wide]), mine_ref, sent_ref)

    @pl.when(step == last)
    def _():
        out = dot(turn_ref[...], attn_ref[:, wide:])
        heads = dot(f_ref[...].T, head_ref[...]) + columns_of(vec_ref[...], 3 * RESULT_FIELDS)
        deal(place, jnp.concatenate((out, heads), axis=1), mine_ref, sent_ref)


def early_grads(place, hidden, attended, final, up, attn, heads, vectors, mine, sent):
    rows, width = hidden.shape
    wide = 512
    steps = up.shape[1] // wide + 2
    count = width // 96
    skip = mine.shape[2] // wide - steps

    def whole(values):
        return pl.BlockSpec(values.shape, lambda i: (0, 0))

    out = pl.BlockSpec((count, 48, wide), lambda i: (0, 0, i + skip))
    untouched = pl.BlockSpec(memory_space=pl.ANY)
    return pl.pallas_call(
        early_grads_kernel,
        grid=(steps,),
        in_specs=[
            pl.BlockSpec(memory_space=pltpu.SMEM),
            whole(hidden),
            whole(attended),
            whole(final),
            pl.BlockSpec((rows, wide), lambda i: (0, jnp.minimum(i, steps - 3))),
            whole(attn),
            whole(heads),
            whole(vectors),
            untouched,
            untouched,
        ],
        out_specs=[out, out],
        out_shape=[jax.ShapeDtypeStruct(mine.shape, BF)] * 2,
        input_output_aliases={8: 0, 9: 1},
        scratch_shapes=[pltpu.VMEM((width, rows), BF)],
        compiler_params=PARAMS,
        name="early_grads",
        cost_estimate=pl.CostEstimate(
            flops=2 * rows * width * wide * steps,
            transcendentals=0,
            bytes_accessed=2 * rows * wide * steps + 2 * width * wide * steps,
        ),
    )(place, hidden, attended, final, up, attn, heads, vectors, mine, sent)


def down_grads_kernel(place_ref, act_ref, down_ref, mine_ref, sent_ref):
    result = dot(act_ref[...], down_ref[...], TN).astype(BF)
    block = result.shape[0] // 2
    piece = block // 8
    halves = []
    for c in range(2):
        groups = [
            jnp.concatenate(
                [
                    result[c * block + y * 4 * piece + g * piece :][:piece]
                    for y in range(2)
                ],
                axis=0,
            )
            for g in range(4)
        ]
        halves.append(jnp.concatenate(groups, axis=1)[None])
    even = place_ref[0] == 0
    mine_ref[...] = jnp.where(even, halves[0], halves[1])
    sent_ref[...] = jnp.where(even, halves[1], halves[0])


def down_grads(place, activation, down, columns):
    rows, width = down.shape
    block = activation.shape[1] // 8
    piece = block // 16
    out = pl.BlockSpec((1, 2 * piece, 4 * width), lambda i: (i, 0, 0))
    return pl.pallas_call(
        down_grads_kernel,
        grid=(8,),
        in_specs=[
            pl.BlockSpec(memory_space=pltpu.SMEM),
            pl.BlockSpec((rows, block), lambda i: (0, i)),
            pl.BlockSpec((rows, width), lambda i: (0, 0)),
        ],
        out_specs=[out, out],
        out_shape=[jax.ShapeDtypeStruct((8, 2 * piece, columns), BF)] * 2,
        compiler_params=PARAMS,
        name="down_grads",
        cost_estimate=pl.CostEstimate(
            flops=2 * rows * width * block, transcendentals=0, bytes_accessed=width * block
        ),
    )(place, activation, down)


def late_grads_kernel(count, place_ref, *refs):
    mixed_refs = refs[:count]
    query_ref = refs[count]
    both_refs = refs[count + 1 : 2 * count + 1]
    vec_ref, mine_ref, sent_ref, turn_ref = refs[2 * count + 1 :]
    step = pl.program_id(0)
    third = (pl.num_programs(0) - 1) // 3
    place = place_ref[0]

    @pl.when(step == 0)
    def _():
        for s in range(count):
            turn_ref[s] = mixed_refs[s][...].T

    @pl.when(step < third)
    def _():
        deal(place, dot(turn_ref[0], query_ref[...], NT), mine_ref, sent_ref)

    @pl.when((step >= third) & (step < 3 * third))
    def _():
        joint = sum(dot(turn_ref[s], both_refs[s][...]) for s in range(count))
        deal(place, joint, mine_ref, sent_ref)

    @pl.when(step == 3 * third)
    def _():
        deal(place, columns_of(vec_ref[...], 0), mine_ref, sent_ref)


def late_grads(place, mixed, query, both, vectors):
    rows, width = mixed[0].shape
    count = len(mixed)
    wide = 256
    third = width // wide
    groups = width // 96

    whole = pl.BlockSpec((rows, width), lambda i: (0, 0))
    out = pl.BlockSpec((groups, 48, wide), lambda i: (0, 0, i))
    return pl.pallas_call(
        functools.partial(late_grads_kernel, count),
        grid=(3 * third + 1,),
        in_specs=[pl.BlockSpec(memory_space=pltpu.SMEM)]
        + [whole] * count
        + [pl.BlockSpec((wide, rows), lambda i: (jnp.clip(i, 0, third - 1), 0))]
        + [pl.BlockSpec((rows, wide), lambda i: (0, jnp.clip(i - third, 0, 2 * third - 1)))] * count
        + [pl.BlockSpec(vectors.shape, lambda i: (0, 0))],
        out_specs=[out, out],
        out_shape=[jax.ShapeDtypeStruct((groups, 48, wide * (3 * third + 1)), BF)] * 2,
        scratch_shapes=[pltpu.VMEM((count, width, rows), BF)],
        compiler_params=PARAMS,
        name="late_grads",
        cost_estimate=pl.CostEstimate(
            flops=2 * rows * width * width * (2 * count + 1),
            transcendentals=0,
            bytes_accessed=2 * rows * width * 4 * count + 12 * width * width,
        ),
    )(place, *mixed, query, *both, vectors)


def block_sums_kernel(counts, dealt, where_ref, *refs):
    total_in = sum(len(group) for group in counts)
    ins, outs = refs[:total_in], refs[total_in:]
    at = 0
    for o, group in enumerate(counts):
        shape = ins[at].shape[-2:] if dealt else outs[o].shape
        value = None
        for use in group:
            term = ins[at][...].astype(F32).reshape(shape)
            if use is not None:
                term = jnp.where(use(pl.program_id(0), where_ref), term, 0.0)
            value = term if value is None else value + term
            at += 1
        if dealt:
            for k, out in enumerate(outs):

                @pl.when(pl.program_id(0) == k)
                def _(out=out, value=value, o=o):
                    out[o] = value.astype(BF)
        else:
            outs[o][...] = value.astype(BF)


def block_sums(where, steps, groups, dealt=False):
    counts = [[term[3] if len(term) > 3 else None for term in terms] for _, terms in groups]
    operands = [term[0] for _, terms in groups for term in terms]
    in_specs = [pl.BlockSpec(term[1], term[2]) for _, terms in groups for term in terms]
    if dealt:
        shape = (len(groups),) + groups[0][0]
        zeros = (0,) * len(shape)
        out_specs = [pl.BlockSpec(shape, lambda i, w: zeros)] * steps
        out_shape = [jax.ShapeDtypeStruct(shape, BF)] * steps
    else:
        out_specs = [pl.BlockSpec(out[1], out[2]) for out, _ in groups]
        out_shape = [jax.ShapeDtypeStruct(out[0], BF) for out, _ in groups]
    return pl.pallas_call(
        functools.partial(block_sums_kernel, counts, dealt),
        grid_spec=pltpu.PrefetchScalarGridSpec(
            num_scalar_prefetch=1, grid=(steps,), in_specs=in_specs, out_specs=out_specs
        ),
        out_shape=out_shape,
        compiler_params=FULL,
        name="block_sums",
        cost_estimate=pl.CostEstimate(flops=1 << 20, transcendentals=0, bytes_accessed=1 << 20),
    )(where, *operands)


class Reduction:
    def __init__(self, where, terms, by_columns):
        self.where = where
        self.terms = terms
        self.by_columns = by_columns
        self.depth, self.columns = terms[0].shape[3:]
        self.steps = 4 if by_columns else 2
        if by_columns:
            self.columns //= 2

    def at(self, part, x, z, y, sizes):
        block = sizes + (self.depth, self.columns)
        column = part if self.by_columns else 0
        shift = 0 if self.by_columns else 2 * part // sizes[1]

        def index(i, w):
            return (x(w), z(i, w) + shift, y(w), 0, column)

        return [(t, block, index) for t in self.terms]

    def one(self):
        n, tail = self.steps, (self.depth, self.columns)
        ahead = lambda i, w: i
        sent = block_sums(
            self.where,
            n // 2,
            [
                (
                    ((n, 2) + tail, (2, 2) + tail, lambda i, w: (i, 0, 0, 0)),
                    self.at(0, lambda w: 1 - w[0], ahead, lambda w: 0, (1, 2, 2)),
                ),
                (
                    ((2, n) + tail, (2, 2) + tail, lambda i, w: (0, i, 0, 0)),
                    self.at(1, lambda w: 0, ahead, lambda w: 1 - w[1], (2, 2, 1)),
                ),
            ],
        )
        return list(sent)

    def trade_one(self, sent):
        self.got_one = [swap(sent[0], "lat", 1), swap(sent[1], "grp", 2)]

    def two(self):
        n, tail = self.steps, (self.depth, self.columns)
        ahead = lambda i, w: i
        out = ((n,) + tail, (2,) + tail, lambda i, w: (i, 0, 0))
        sent = block_sums(
            self.where,
            n // 2,
            [
                (
                    out,
                    self.at(0, lambda w: w[0], ahead, lambda w: 1 - w[1], (1, 2, 1))
                    + [(self.got_one[0], (2, 1) + tail, lambda i, w: (i, 1 - w[1], 0, 0))],
                ),
                (
                    out,
                    self.at(1, lambda w: 1 - w[0], ahead, lambda w: w[1], (1, 2, 1))
                    + [(self.got_one[1], (1, 2) + tail, lambda i, w: (1 - w[0], i, 0, 0))],
                ),
            ],
        )
        return list(sent)

    def trade_two(self, sent):
        self.got_two = [swap(sent[0], "grp", 2), swap(sent[1], "lat", 1)]

    def quarters(self):
        tail = (self.depth, self.columns)
        x = lambda w: w[0]
        y = lambda w: w[1]
        if self.by_columns:
            place = lambda i, w: w[2] ^ i
            groups = []
            for part in (0, 1):
                terms = self.at(part, x, place, y, (1, 1, 1))
                if part == 0:
                    one = lambda i, w: (w[2] ^ i, w[1], 0, 0)
                else:
                    one = lambda i, w: (w[0], w[2] ^ i, 0, 0)
                terms.append((self.got_one[part], (1, 1) + tail, one))
                terms.append((self.got_two[part], (1,) + tail, lambda i, w: (w[2] ^ i, 0, 0)))
                groups.append((tail, terms))
        else:
            low = lambda i, w: jnp.minimum(w[2] ^ i, 1)
            high = lambda i, w: jnp.maximum((w[2] ^ i) - 2, 0)
            first = lambda i, w: (w[2] ^ i) < 2
            second = lambda i, w: (w[2] ^ i) >= 2
            terms = self.at(0, x, lambda i, w: w[2] ^ i, y, (1, 1, 1))
            pair = (1, 1) + tail
            one = (1,) + tail
            terms += [
                (self.got_one[0], pair, lambda i, w: (low(i, w), w[1], 0, 0), first),
                (self.got_one[1], pair, lambda i, w: (w[0], high(i, w), 0, 0), second),
                (self.got_two[0], one, lambda i, w: (low(i, w), 0, 0), first),
                (self.got_two[1], one, lambda i, w: (high(i, w), 0, 0), second),
            ]
            groups = [(tail, terms)]
        return list(block_sums(self.where, 4, groups, True))


def early_unpack_kernel(place_ref, *refs):
    ins = refs[:4]
    down_ref, up_ref, out_ref, gate_ref, head_ref, gain_ref, bias_ref, bd_ref, bup_ref, misc_ref = refs[4:]
    width = down_ref.shape[1]
    hidden = up_ref.shape[1]
    for source, (c, y) in zip(ins, ((0, 0), (0, 1), (1, 0), (1, 1))):
        slot = jnp.bitwise_xor(place_ref[0], c) * 2 + jnp.bitwise_xor(place_ref[1], y)
        one = source[0].astype(F32)
        two = source[1].astype(F32)
        rows = one.shape[0]
        half = one.shape[1]
        for g in range(4):
            span = pl.ds(pl.multiple_of(slot * 4 * rows + g * rows, 8), rows)
            down_ref[span, :] = one[:, g * width : (g + 1) * width]
        span = pl.ds(pl.multiple_of(slot * rows, 8), rows)
        cut = half - 4 * width
        up_ref[span, :cut] = one[:, 4 * width :]
        up_ref[span, cut:] = two[:, : hidden - cut]
        out_ref[span, :] = two[:, hidden - cut : hidden - cut + width]
        misc_ref[span, :] = two[:, hidden - cut + width :]
    turned = misc_ref[...].T
    at = 0
    for ref in (gate_ref, head_ref, gain_ref, bias_ref, bd_ref, bup_ref):
        count = ref.shape[0]
        ref[...] = turned[at : at + count]
        at += count


def early_unpack(place, pieces, width, hidden):
    rows = pieces[0].shape[1]
    vmem = pl.BlockSpec(memory_space=pltpu.VMEM)
    return pl.pallas_call(
        early_unpack_kernel,
        in_specs=[pl.BlockSpec(memory_space=pltpu.SMEM)] + [vmem] * 4,
        out_specs=[vmem] * 9,
        out_shape=[
            jax.ShapeDtypeStruct((16 * rows, width), F32),
            jax.ShapeDtypeStruct((4 * rows, hidden), F32),
            jax.ShapeDtypeStruct((4 * rows, width), F32),
        ]
        + [
            jax.ShapeDtypeStruct((count, 4 * rows), F32)
            for count in (2 * RESULT_FIELDS, RESULT_FIELDS, 1, 1, 1, 4)
        ],
        scratch_shapes=[pltpu.VMEM((4 * rows, 256), F32)],
        compiler_params=PARAMS,
        name="early_unpack",
        cost_estimate=pl.CostEstimate(flops=1 << 20, transcendentals=0, bytes_accessed=1 << 20),
    )(place, *pieces)


def late_unpack_kernel(place_ref, *refs):
    ins = refs[:4]
    main_ref, gain_ref, bias_ref, lead_ref, misc_ref = refs[4:]
    for source, (c, y) in zip(ins, ((0, 0), (0, 1), (1, 0), (1, 1))):
        slot = jnp.bitwise_xor(place_ref[0], c) * 2 + jnp.bitwise_xor(place_ref[1], y)
        value = source[...].astype(F32)
        rows = value.shape[0]
        span = pl.ds(pl.multiple_of(slot * rows, 8), rows)
        main_ref[span, :] = value[:, : main_ref.shape[1]]
        misc_ref[span, :] = value[:, main_ref.shape[1] :]
    turned = misc_ref[...].T
    gain_ref[...] = turned[:1]
    bias_ref[...] = turned[1:2]
    lead_ref[...] = turned[2 : 2 + LEADS]


def late_unpack(place, pieces):
    rows, columns = pieces[0].shape
    vmem = pl.BlockSpec(memory_space=pltpu.VMEM)
    return pl.pallas_call(
        late_unpack_kernel,
        in_specs=[pl.BlockSpec(memory_space=pltpu.SMEM)] + [vmem] * 4,
        out_specs=[vmem] * 4,
        out_shape=[jax.ShapeDtypeStruct((4 * rows, columns - 256), F32)]
        + [jax.ShapeDtypeStruct((count, 4 * rows), F32) for count in (1, 1, LEADS)],
        scratch_shapes=[pltpu.VMEM((4 * rows, 256), F32)],
        compiler_params=PARAMS,
        name="late_unpack",
        cost_estimate=pl.CostEstimate(flops=1 << 20, transcendentals=0, bytes_accessed=1 << 20),
    )(place, *pieces)


def spread(rows, columns):
    pixel = lax.broadcasted_iota(jnp.int32, (rows, columns), 0)
    field = lax.broadcasted_iota(jnp.int32, (rows, columns), 1)
    return ((pixel // TILE_AREA) == field).astype(F32).astype(BF)


def split_two(values):
    high = values.astype(BF)
    return high, (values - high.astype(F32)).astype(BF)


def pixel_sums_kernel(f_ref, s_ref, sum_ref, first_ref, second_ref, field_ref):
    @pl.when(pl.program_id(0) == 0)
    def _():
        field_ref[...] = spread(*field_ref.shape)

    fields = field_ref[...]
    sens = s_ref[...]
    sum_ref[...] = dot(sens, fields)
    for e, out in ((0, first_ref), (1, second_ref)):
        out[...] = dot((sens.astype(F32) * f_ref[e].astype(F32)).astype(BF), fields)


def pixel_sums(forecasts, sensitivity):
    rows, pixels = sensitivity.shape
    block = math.gcd(rows, 64)
    out = pl.BlockSpec((block, 128), lambda i: (i, 0))
    return pl.pallas_call(
        pixel_sums_kernel,
        grid=(rows // block,),
        in_specs=[
            pl.BlockSpec((2, block, pixels), lambda i: (0, i, 0)),
            pl.BlockSpec((block, pixels), lambda i: (i, 0)),
        ],
        out_specs=[out] * 3,
        out_shape=[jax.ShapeDtypeStruct((rows, 128), F32)] * 3,
        scratch_shapes=[pltpu.VMEM((pixels, 128), BF)],
        compiler_params=PARAMS,
        name="pixel_sums",
        cost_estimate=pl.CostEstimate(
            flops=rows * pixels * 128, transcendentals=0, bytes_accessed=rows * pixels
        ),
    )(forecasts, sensitivity)


def blend_kernel(a_ref, b_ref, c_ref, f_ref, out_ref, field_ref):
    @pl.when(pl.program_id(0) == 0)
    def _():
        columns = field_ref.shape[1]
        field = lax.broadcasted_iota(jnp.int32, (256, columns), 0)
        pixel = lax.broadcasted_iota(jnp.int32, (256, columns), 1)
        field_ref[...] = ((pixel // TILE_AREA) == (field % 128)).astype(F32).astype(BF)

    fields = field_ref[...]

    def wide(ref):
        return dot(jnp.concatenate(split_two(ref[...]), axis=1), fields)

    total = wide(a_ref) * f_ref[0].astype(F32) + wide(b_ref) * f_ref[1].astype(F32)
    out_ref[...] = (total + wide(c_ref)).astype(BF)


def blend(first, second, added, forecasts):
    _, rows, pixels = forecasts.shape
    block = math.gcd(rows, 128)
    thin = pl.BlockSpec((block, 128), lambda i: (i, 0))
    return pl.pallas_call(
        blend_kernel,
        grid=(rows // block,),
        in_specs=[thin] * 3 + [pl.BlockSpec((2, block, pixels), lambda i: (0, i, 0))],
        out_specs=pl.BlockSpec((block, pixels), lambda i: (i, 0)),
        out_shape=jax.ShapeDtypeStruct((rows, pixels), BF),
        scratch_shapes=[pltpu.VMEM((256, pixels), BF)],
        compiler_params=PARAMS,
        name="blend",
        cost_estimate=pl.CostEstimate(
            flops=rows * pixels * 128, transcendentals=0, bytes_accessed=rows * pixels
        ),
    )(first, second, added, forecasts)


def swap(values, axis, bit):
    count = lax.axis_size(axis)
    return lax.ppermute(values, axis, [(i, i ^ bit) for i in range(count)])


def add(*terms):
    return sum(t.astype(F32) for t in terms).astype(BF)


def hold(*values):
    return lax.optimization_barrier(values)


def layer_norm(values):
    centred = values - jnp.mean(values, axis=-1, keepdims=True)
    inverse = lax.rsqrt(jnp.mean(centred * centred, axis=-1, keepdims=True) + EPSILON)
    return centred * inverse, inverse


def norm_back(grad_normed, normed, inverse):
    return inverse * (
        grad_normed
        - jnp.mean(grad_normed, axis=-1, keepdims=True)
        - normed * jnp.mean(grad_normed * normed, axis=-1, keepdims=True)
    )


def pad_lanes(values):
    return jnp.pad(values, ((0, 0), (0, 128 - values.shape[1])))


def per_device(
    layer_source_tensor,
    horizon_class,
    field_selector,
    model_predictions,
    loss_sensitivity,
    gain_one,
    shift_one,
    horizon_vectors,
    w_qkv,
    w_out,
    gain_two,
    shift_two,
    w_up,
    b_up,
    w_down,
    b_down,
    w_gate,
    w_bias,
):
    frames, lat_rows, lon_cols, width = layer_source_tensor.shape
    local = lat_rows * lon_cols
    rows = frames * local
    pixels = loss_sensitivity.shape[-1]
    sizes = (lax.axis_size("grp"), lax.axis_size("lat"), lax.axis_size("lon"))
    small = sizes == (4, 2, 4) and frames == 1

    source = layer_source_tensor.reshape(frames, local, width)
    place = lax.axis_index("lon")
    edge = (place == 0) | (place == lax.axis_size("lon") - 1)
    send = functools.partial(lax.ppermute, axis_name="lon")
    if small:
        right = send(source, perm=[(0, 1), (1, 2), (2, 3)])
        left = send(source, perm=[(3, 2), (2, 1), (1, 0)])
    else:
        shards = [lax.all_gather(source, "lon", axis=1, tiled=True)]

    forecasts = jnp.transpose(model_predictions.reshape(rows, 2, pixels), (1, 0, 2))
    sensitivity = loss_sensitivity.reshape(rows, pixels)

    onehot = (horizon_class[:, None] == jnp.arange(LEADS, dtype=jnp.int32)[None, :]).astype(F32)
    lead_rows = jnp.dot(onehot, horizon_vectors, precision=HIGH)

    def mixed_of(values):
        normed, _ = layer_norm(values.astype(F32))
        return (normed * gain_one + shift_one + lead_rows[:, None, :]).astype(BF)

    wq = w_qkv[:, :width]
    wkv = w_qkv[:, width:]

    def keys_of(values):
        return dot(values.reshape(-1, width), wkv).astype(BF).reshape(frames, -1, 2 * width)

    if small:

        def flat(values):
            return values.reshape(rows, width)

        def shard_of(flag, yes, no):
            m, kv, x = project(
                flag.astype(jnp.int32)[None],
                [flat(yes), flat(no)],
                gain_one,
                shift_one,
                lead_rows,
                w_qkv,
            )
            return m, kv[None], x[None]

        mixed_own, own_kv, queries = project(
            None, [flat(source)], gain_one, shift_one, lead_rows, w_qkv
        )
        queries = queries[None]
        mixed = [mixed_own]
        key_value = [own_kv[None]]
        right, left, forecasts, queries, key_value[0] = hold(
            right, left, forecasts, queries, key_value[0]
        )
        right_two = send(right, perm=[(1, 2), (2, 3)])
        left_two = send(left, perm=[(2, 1), (1, 0)])
        sums = pixel_sums(forecasts, sensitivity)
        m, kv, near = shard_of(place == 0, left, right)
        mixed.append(m)
        right_two, left_two, kv, *sums = hold(right_two, left_two, kv, *sums)
        key_value.append(kv)
        two = right_two + left_two
        two, middle = hold(two, left)
        three = send(two, perm=[(2, 3), (1, 0)])
        m, kv, middle = shard_of(edge, two, middle)
        mixed.append(m)
        key_value.append(kv)
        state = attend(queries, key_value, None, False)
        three, *state = hold(three, *state)
        m, kv, far = shard_of(edge, three, two)
        mixed.append(m)
        key_value.append(kv)
        attended, logs = attend(queries, key_value[3:], state, True)
        shards = [source, near, middle, far]
    else:
        mixed_own = mixed_of(source)
        queries = dot(mixed_own.reshape(rows, width), wq).astype(BF)
        queries = queries.reshape(frames, local, width)
        sums = pixel_sums(forecasts, sensitivity)
        mixed = [mixed_of(shards[0])]
        key_value = [keys_of(mixed[0])]
        attended, logs = attend(queries, key_value, None, True)
    inputs = source.reshape(rows, width)
    attended_low = attended.reshape(rows, width)
    both = w_gate.T
    head_rows = jnp.concatenate(
        [
            jnp.pad(m, ((0, 128 - RESULT_FIELDS), (0, 0)))
            for m in (both[:RESULT_FIELDS], both[RESULT_FIELDS:], w_bias.T)
        ]
    )
    mask = pad_lanes(field_selector.astype(F32))[:, None]
    (
        hidden_low,
        activation_low,
        up_low,
        down_low,
        final_low,
        heads_low,
        attn_low,
        grad_residual,
        grad_attended,
        *blending,
        early_vectors,
        grad_bup,
    ) = between(
        inputs,
        attended_low,
        w_out,
        w_up,
        w_down,
        head_rows,
        gain_two,
        shift_two,
        b_up,
        b_down,
        mask,
        sums,
        local,
    )
    grad_attended = grad_attended.reshape(frames, local, width)
    fields = 3 * RESULT_FIELDS
    heads_low = jnp.concatenate(
        [heads_low[:, g * 128 : g * 128 + RESULT_FIELDS] for g in range(3)], axis=1
    )
    inputs = inputs.astype(F32)
    def input_gradient(grad_mixed):
        normed_one, inverse_one = layer_norm(inputs)
        return grad_residual + norm_back(
            grad_mixed.reshape(rows, width) * gain_one, normed_one, inverse_one
        )

    def back(shard, place, before):
        return attend_back(queries, grad_attended, attended, logs, shard, w_qkv, place, before)

    nothing = jnp.zeros((frames, width, local), F32)

    def late_vectors(sums):
        gain_column = sum(jnp.sum(s[:, 0], axis=0) for s in sums)
        column = sum(s[:, 1] for s in sums)
        lead = jnp.dot(onehot.T, column, precision=HIGH)
        zeros = jnp.zeros((6, width), F32)
        return jnp.concatenate((gain_column[None], jnp.sum(column, axis=0)[None], lead, zeros))

    if small:
        bup_rows = jnp.swapaxes(grad_bup.reshape(8, 4, -1), 0, 1).reshape(4, width)
        early_vectors = jnp.concatenate(
            (early_vectors, bup_rows, jnp.zeros((1, width), F32))
        )
        core = (lax.axis_index("grp") % 2).astype(jnp.int32)[None]
        where = jnp.stack(
            (lax.axis_index("lat"), lax.axis_index("grp") // 2, lax.axis_index("lon"))
        ).astype(jnp.int32)
        hidden = w_up.shape[1]
        mine, sent = down_grads(core, activation_low, down_low, 2 * hidden + width + 256)
        mine, sent = early_grads(
            core,
            hidden_low,
            attended_low,
            final_low,
            up_low,
            attn_low,
            jnp.pad(heads_low, ((0, 0), (0, 256 - fields))),
            early_vectors,
            mine,
            sent,
        )
        grad_attended, sent = hold(grad_attended, sent)
        got = swap(sent, "grp", 1)

        grad_query, dkv3, far, sums3 = back(key_value[3], shards[3], nothing)
        early = Reduction(where, [t.reshape(2, 4, 2, 24, -1) for t in (mine, got)], True)
        grad_query, far, *sent = hold(grad_query, far, *early.one())
        got = send(far, perm=[(0, 1), (3, 2)])
        early.trade_one(sent)

        grad_query, dkv2, middle, sums2 = back(key_value[2], shards[2], grad_query)
        value = jnp.where(edge, middle, add(got, far))
        grad_query, value = hold(grad_query, value)
        right = send(value, perm=[(0, 1), (1, 2)])
        left = send(value, perm=[(3, 2), (2, 1)])

        grad_query, dkv1, near, sums1 = back(key_value[1], shards[1], grad_query)
        forth = jnp.where(place == 0, near, add(right, middle))
        back_value = add(left, near)
        grad_query, forth, back_value, *sent = hold(
            grad_query, forth, back_value, *early.two()
        )
        right = send(forth, perm=[(0, 1), (1, 2), (2, 3)])
        left = send(back_value, perm=[(3, 2), (2, 1), (1, 0)])
        early.trade_two(sent)

        grad_query, dkv0, own, sums0, right, left, *early.got_two = hold(
            *back(key_value[0], shards[0], grad_query), right, left, *early.got_two
        )
        query_low, query_term, query_sums = query_back(grad_query, w_qkv, source)
        vectors = late_vectors([sums0, sums1, sums2, sums3, query_sums])
        late_mine, late_sent = late_grads(
            core,
            [m.reshape(rows, width) for m in mixed],
            query_low.reshape(width, rows),
            [d.reshape(rows, 2 * width) for d in (dkv0, dkv1, dkv2, dkv3)],
            vectors,
        )
        late_mine, late_sent, *early.got_two, own = hold(
            late_mine, late_sent, *early.got_two, own
        )
        got = swap(late_sent, "grp", 1)
        got, *parts = hold(got, *early.quarters())
        late = Reduction(where, [t.reshape(2, 4, 2, 24, -1) for t in (late_mine, got)], False)
        *sent, one, two, three = hold(*late.one(), *blending)
        late.trade_one(sent)
        early = [parts[0]] + [swap(parts[k], "lon", k) for k in (1, 2, 3)]
        blended = blend(one, two, three, forecasts)
        *late.got_one, blended = hold(*late.got_one, blended)
        *sent, own, early[0] = hold(*late.two(), own, early[0])
        late.trade_two(sent)
        grad_input = input_back(
            [flat(t) for t in (own, query_term, right, left)], grad_residual, flat(source), gain_one
        )
        *late.got_two, grad_input = hold(*late.got_two, grad_input)
        early[0], *parts = hold(early[0], *late.quarters())
        late = [parts[0]] + [swap(parts[k], "lon", k) for k in (1, 2, 3)]
        late[1], late[2], early[0] = hold(late[1], late[2], early[0])
        late = add(*[part[0] for part in late])
        late_y = swap(late, "grp", 2)
        late_c = swap(late, "grp", 1)
        early = add(*early)
        early_y = swap(early, "grp", 2)
        early_c = swap(early, "grp", 1)
        early_y, early_c, early, late_y, late_c, late = hold(
            early_y, early_c, early, late_y, late_c, late
        )
        early_yc = swap(early_y, "grp", 1)
        late_yc = swap(late_y, "grp", 1)
        place_two = jnp.stack((lax.axis_index("grp") % 2, lax.axis_index("grp") // 2))
        place_two = place_two.astype(jnp.int32)
        down_sum, up_sum, out_sum, gate_sum, head_sum, *early, bup_sum = early_unpack(
            place_two, [early, early_y, early_c, early_yc], width, hidden
        )
        late_yc, gate_sum = hold(late_yc, gate_sum)
        qkv_sum, *late, lead_sum = late_unpack(place_two, [late, late_y, late_c, late_yc])
        early = [e.reshape(-1) for e in early]
        late = [e.reshape(-1) for e in late]
        bup_sum = bup_sum.reshape(-1)
        gate_sum = gate_sum.T
        head_sum = head_sum.T
    else:
        blended = blend(*blending, forecasts)
        grad_query, dkv, term, sums = back(key_value[0], shards[0], nothing)
        query_low, query_term, query_sums = query_back(grad_query, w_qkv, source)
        grad_input = input_gradient(
            query_term + lax.psum_scatter(term.astype(F32), "lon", scatter_dimension=1, tiled=True)
        )

        def total_of(values, dim=0):
            share = lax.psum_scatter(values, ("lat", "lon"), scatter_dimension=dim, tiled=True)
            return lax.psum(share, "grp")

        flat = mixed[0].reshape(-1, width)
        qkv_sum = total_of(
            jnp.concatenate(
                (
                    jnp.einsum("frd,fer->de", mixed_own, query_low, preferred_element_type=F32),
                    dot(flat, dkv.reshape(-1, 2 * width), TN),
                ),
                axis=1,
            )
        )
        up_sum = total_of(dot(hidden_low, up_low, TN))
        out_sum = total_of(dot(attended_low, attn_low, TN))
        down_sum = total_of(dot(activation_low, down_low, TN))
        heads = total_of(dot(final_low, heads_low, TN))
        late = total_of(late_vectors([sums, query_sums])[: 2 + LEADS], 1)
        lead_sum = late[2:]
        gate_sum = heads[:, : 2 * RESULT_FIELDS]
        head_sum = heads[:, 2 * RESULT_FIELDS :]
        early = total_of(early_vectors, 1)
        bup_sum = total_of(grad_bup[0])

    return (
        blended.reshape(frames, lat_rows, lon_cols, pixels),
        grad_input.reshape(frames, lat_rows, lon_cols, width),
        late[0],
        late[1],
        lead_sum,
        qkv_sum,
        out_sum,
        early[0],
        early[1],
        up_sum,
        bup_sum,
        down_sum,
        early[2],
        gate_sum,
        head_sum,
    )


def solution(mesh):
    frame = ("grp", "lat")
    share = ("lat", "lon")
    image = P(frame, None, "lon", None)
    in_specs = (
        image,
        P(frame),
        P(frame, None),
        P(frame, None, "lon", None, None),
        image,
    ) + (P(),) * 13
    vector = P(share)
    matrix = P(share, None)
    out_specs = (
        image,
        image,
        vector,
        vector,
        P(None, share),
        matrix,
        matrix,
        vector,
        vector,
        matrix,
        vector,
        matrix,
        vector,
        matrix,
        matrix,
    )
    return jax.shard_map(
        per_device, mesh=mesh, in_specs=in_specs, out_specs=out_specs, check_vma=False
    )
```

```python
import functools
import math

import jax
import jax.numpy as jnp
from jax import lax
from jax.experimental import pallas as pl
from jax.experimental.pallas import tpu as pltpu
from jax.sharding import PartitionSpec as P

H = 12
DH = 64
RESULT_FIELDS = 69
TILE_AREA = 64
LEADS = 24
EPSILON = 1e-06
HIGH = lax.Precision.HIGHEST
SCALE = 0.125
SCALE_TWO = SCALE * math.log2(math.e)
ROOT = math.sqrt(2.0 / math.pi)
CUBE = 0.044715
NN = (((1,), (0,)), ((), ()))
NT = (((1,), (1,)), ((), ()))
TN = (((0,), (0,)), ((), ()))
BF = jnp.bfloat16
F32 = jnp.float32
PARAMS = pltpu.CompilerParams(vmem_limit_bytes=60 * 1024 * 1024)
FULL = pltpu.CompilerParams(vmem_limit_bytes=63 * 1024 * 1024 + 512 * 1024)


def dot(left, right, dims=NN):
    return lax.dot_general(left, right, dims, preferred_element_type=F32)


def project_kernel(own, *refs):
    if own:
        a_ref, gain_ref, shift_ref, lead_ref, wq_ref, wk_ref, wv_ref, mixed_ref, kv_ref, q_ref = refs
        value = a_ref[...]
    else:
        flag_ref, a_ref, b_ref, gain_ref, shift_ref, lead_ref, wk_ref, wv_ref = refs[:8]
        mixed_ref, kv_ref, x_ref = refs[8:]
        value = jnp.where(flag_ref[0] != 0, a_ref[...], b_ref[...])
        x_ref[...] = value
    normed, _ = layer_norm(value.astype(F32))
    mixed = (normed * gain_ref[...][None] + shift_ref[...][None] + lead_ref[...]).astype(BF)
    mixed_ref[...] = mixed
    width = mixed.shape[1]
    kv_ref[:, :width] = dot(mixed, wk_ref[...]).astype(BF)
    kv_ref[:, width:] = dot(mixed, wv_ref[...]).astype(BF)
    if own:
        q_ref[...] = dot(mixed, wq_ref[...]).astype(BF)


def project(flag, sources, gain, shift, lead, weights):
    own = flag is None
    rows, width = sources[0].shape
    block = math.gcd(rows, 256)
    row = pl.BlockSpec((block, width), lambda i: (i, 0))
    vector = pl.BlockSpec((width,), lambda i: (0,))

    def columns(group):
        return pl.BlockSpec((width, width), lambda i: (0, group))

    groups = (0, 1, 2) if own else (1, 2)
    return pl.pallas_call(
        functools.partial(project_kernel, own),
        grid=(rows // block,),
        in_specs=([] if own else [pl.BlockSpec(memory_space=pltpu.SMEM)])
        + [row] * len(sources)
        + [vector, vector, pl.BlockSpec((1, width), lambda i: (0, 0))]
        + [columns(g) for g in groups],
        out_specs=[row, pl.BlockSpec((block, 2 * width), lambda i: (i, 0)), row],
        out_shape=[
            jax.ShapeDtypeStruct((rows, width), BF),
            jax.ShapeDtypeStruct((rows, 2 * width), BF),
            jax.ShapeDtypeStruct((rows, width), BF),
        ],
        compiler_params=PARAMS,
        name="project",
        cost_estimate=pl.CostEstimate(
            flops=rows * width * width, transcendentals=0, bytes_accessed=rows * width
        ),
    )(*([] if own else [flag]), *sources, gain, shift, lead, *([weights] * len(groups)))


def attend_kernel(count, chained, final, *refs):
    q_ref = refs[0]
    k_refs = refs[1 : 1 + count]
    v_refs = refs[1 + count : 1 + 2 * count]
    o_ref, l_ref = refs[-2:]
    outs = []
    for h in range(2):
        part = slice(h * DH, h * DH + DH)
        q = q_ref[0, :, part]
        scores = [dot(k[0, :, part], q, NT) for k in k_refs]
        top = functools.reduce(
            jnp.maximum, [jnp.max(s, axis=0, keepdims=True) for s in scores]
        )
        top = top * SCALE_TWO
        total = None
        mixed = None
        for s, v in zip(scores, v_refs):
            raised = jnp.exp2(s * SCALE_TWO - top)
            some = jnp.sum(raised, axis=0, keepdims=True)
            term = dot(v[0, :, part], raised.astype(BF), TN)
            total = some if total is None else total + some
            mixed = term if mixed is None else mixed + term
        mixed = mixed * (1.0 / total)
        log = top + jnp.log2(total)
        if chained:
            before_ref, before_log_ref = refs[1 + 2 * count : 3 + 2 * count]
            before = before_log_ref[0, 0, h : h + 1, :]
            high = jnp.maximum(before, log)
            joint = high + jnp.log2(jnp.exp2(before - high) + jnp.exp2(log - high))
            mixed = mixed * jnp.exp2(log - joint) + before_ref[0, part, :] * jnp.exp2(
                before - joint
            )
            log = joint
        l_ref[0, 0, h : h + 1, :] = log
        if final:
            outs.append(mixed)
        else:
            o_ref[0, part, :] = mixed
    if final:
        o_ref[0] = jnp.concatenate(outs, axis=0).T.astype(BF)


def attend(queries, shards, before, final):
    frames, rows, width = queries.shape
    count = len(shards)
    keys = shards[0].shape[1]
    pairs = width // 128
    turned = pl.BlockSpec((1, 128, rows), lambda f, p: (f, p, 0))
    row = pl.BlockSpec((1, rows, 128), lambda f, p: (f, 0, p))
    log = pl.BlockSpec((1, 1, 2, rows), lambda f, p: (f, p, 0, 0))
    chained = before is not None
    return pl.pallas_call(
        functools.partial(attend_kernel, count, chained, final),
        grid=(frames, pairs),
        in_specs=[row]
        + [pl.BlockSpec((1, keys, 128), lambda f, p: (f, 0, p))] * count
        + [pl.BlockSpec((1, keys, 128), lambda f, p: (f, 0, p + pairs))] * count
        + ([turned, log] if chained else []),
        out_specs=[row if final else turned, log],
        out_shape=[
            jax.ShapeDtypeStruct((frames, rows, width), BF)
            if final
            else jax.ShapeDtypeStruct((frames, width, rows), F32),
            jax.ShapeDtypeStruct((frames, pairs, 2, rows), F32),
        ],
        compiler_params=PARAMS,
        name="attend",
        cost_estimate=pl.CostEstimate(
            flops=2 * frames * rows * count * keys * width,
            transcendentals=0,
            bytes_accessed=frames * rows * width,
        ),
    )(queries, *shards, *shards, *(before if chained else ()))


def column_sums(total, values):
    normed, _ = layer_norm(values.astype(F32))
    return jnp.concatenate(
        (
            jnp.sum(total * normed, axis=0, keepdims=True),
            jnp.sum(total, axis=0, keepdims=True),
        )
    )


def attend_back_kernel(
    q_ref,
    g_ref,
    o_ref,
    l_ref,
    k_ref,
    v_ref,
    wk_ref,
    wv_ref,
    x_ref,
    before_ref,
    dq_ref,
    dkv_ref,
    term_ref,
    sums_ref,
):
    pair = pl.program_id(1)
    key_terms = []
    value_terms = []
    query_terms = []
    for h in range(2):
        part = slice(h * DH, h * DH + DH)
        q = q_ref[0, :, part]
        g = g_ref[0, :, part]
        k = k_ref[0, :, part]
        v = v_ref[0, :, part]
        product = g.astype(F32) * o_ref[0, :, part].astype(F32)
        high, low = split_two(product)
        ones = jnp.ones((8, DH), BF)
        delta = (dot(ones, high, NT) + dot(ones, low, NT))[0:1]
        probs = jnp.exp2(dot(k, q, NT) * SCALE_TWO - l_ref[0, 0, h : h + 1, :])
        grad_probs = dot(v, g, NT)
        grad_scores = (probs * (grad_probs - delta)).astype(BF)
        value_terms.append(dot(probs.astype(BF), g))
        key_terms.append(dot(grad_scores, q))
        grad_query = dot(k, grad_scores, TN) * SCALE + before_ref[0, part, :]
        query_terms.append(grad_query)
    grad_key = (jnp.concatenate(key_terms, axis=1) * SCALE).astype(BF)
    grad_value = jnp.concatenate(value_terms, axis=1).astype(BF)
    grad_query = jnp.concatenate(query_terms, axis=0).astype(dq_ref.dtype)
    width = wk_ref.shape[0]
    dkv_ref[0, :, pl.ds(pl.multiple_of(pair * 128, 128), 128)] = grad_key
    dkv_ref[0, :, pl.ds(pl.multiple_of(width + pair * 128, 128), 128)] = grad_value
    dq_ref[0] = grad_query

    @pl.when(pair == pl.num_programs(1) - 1)
    def _():
        total = dot(dkv_ref[0, :, :width], wk_ref[...], NT)
        total = total + dot(dkv_ref[0, :, width:], wv_ref[...], NT)
        term_ref[0] = total.astype(term_ref.dtype)
        sums_ref[0] = column_sums(total, x_ref[0])


def attend_back(queries, grad_out, out, logs, shard, weights, source, before):
    frames, rows, width = queries.shape
    keys = shard.shape[1]
    pairs = width // 128
    row = pl.BlockSpec((1, rows, 128), lambda f, p: (f, 0, p))
    key = pl.BlockSpec((1, keys, 128), lambda f, p: (f, 0, p))
    value = pl.BlockSpec((1, keys, 128), lambda f, p: (f, 0, p + pairs))
    turned = pl.BlockSpec((1, 128, rows), lambda f, p: (f, p, 0))
    log = pl.BlockSpec((1, 1, 2, rows), lambda f, p: (f, p, 0, 0))

    def columns(group):
        return pl.BlockSpec((width, width), lambda f, p: (0, group))

    def whole(*shape):
        return pl.BlockSpec((1,) + shape, lambda f, p: (f, 0, 0))

    in_specs = [row, row, row, log, key, value, columns(1), columns(2), whole(keys, width)]
    operands = [queries, grad_out, out, logs, shard, shard, weights, weights, source]
    aliases = {len(operands): 0}
    in_specs.append(turned)
    operands.append(before)
    out_specs = [turned, whole(keys, 2 * width), whole(keys, width), whole(2, width)]
    out_shape = [
        jax.ShapeDtypeStruct((frames, width, rows), F32),
        jax.ShapeDtypeStruct((frames, keys, 2 * width), BF),
        jax.ShapeDtypeStruct((frames, keys, width), BF),
        jax.ShapeDtypeStruct((frames, 2, width), F32),
    ]
    return pl.pallas_call(
        attend_back_kernel,
        grid=(frames, pairs),
        in_specs=in_specs,
        out_specs=out_specs,
        out_shape=out_shape,
        input_output_aliases=aliases,
        compiler_params=PARAMS,
        name="attend_back",
        cost_estimate=pl.CostEstimate(
            flops=4 * frames * rows * keys * width,
            transcendentals=0,
            bytes_accessed=frames * rows * width,
        ),
    )(*operands)


def query_back_kernel(dq_ref, w_ref, x_ref, low_ref, term_ref, sums_ref):
    low = dq_ref[0].astype(BF)
    low_ref[0] = low
    total = dot(low, w_ref[...], (((0,), (1,)), ((), ())))
    term_ref[0] = total
    sums_ref[0] = column_sums(total, x_ref[0])


def query_back(grad_query, weights, source):
    frames, width, rows = grad_query.shape

    def whole(*shape):
        return pl.BlockSpec((1,) + shape, lambda f: (f, 0, 0))

    return pl.pallas_call(
        query_back_kernel,
        grid=(frames,),
        in_specs=[
            whole(width, rows),
            pl.BlockSpec((width, width), lambda f: (0, 0)),
            whole(rows, width),
        ],
        out_specs=[whole(width, rows), whole(rows, width), whole(2, width)],
        out_shape=[
            jax.ShapeDtypeStruct((frames, width, rows), BF),
            jax.ShapeDtypeStruct((frames, rows, width), F32),
            jax.ShapeDtypeStruct((frames, 2, width), F32),
        ],
        compiler_params=PARAMS,
        name="query_back",
        cost_estimate=pl.CostEstimate(
            flops=frames * rows * width * width, transcendentals=0, bytes_accessed=rows * width
        ),
    )(grad_query, weights, source)


def between_kernel(
    x_ref,
    att_ref,
    wo_ref,
    wu_ref,
    wd_ref,
    head_ref,
    gain_ref,
    shift_ref,
    bu_ref,
    bd_ref,
    mask_ref,
    sens_ref,
    one_ref,
    two_ref,
    hidden_ref,
    act_ref,
    up_ref,
    down_ref,
    final_ref,
    heads_ref,
    attn_ref,
    gres_ref,
    gatt_ref,
    first_ref,
    second_ref,
    added_ref,
    vec_ref,
    bup_ref,
    slope_ref,
    sum_ref,
    ups_ref,
):
    residual = x_ref[...].astype(F32) + dot(att_ref[...], wo_ref[...])
    normed, inverse = layer_norm(residual)
    gain = gain_ref[...][None]
    hidden = (normed * gain + shift_ref[...][None]).astype(BF)
    hidden_ref[...] = hidden
    wide = 1024
    steps = wu_ref.shape[1] // wide
    sum_ref[...] = residual + bd_ref[...][None]

    def chunk(j):
        return pl.ds(pl.multiple_of(j * wide, wide), wide)

    @pl.loop(0, steps)
    def _(j):
        part = chunk(j)
        up = dot(hidden, wu_ref[:, part]) + bu_ref[part][None]
        square = up * up
        tanh = jnp.tanh(ROOT * up * (1.0 + CUBE * square))
        half = 0.5 * (1.0 + tanh)
        act = (up * half).astype(BF)
        slope_ref[:, part] = half + 0.5 * up * (1.0 - tanh * tanh) * (
            ROOT + 3.0 * ROOT * CUBE * square
        )
        act_ref[:, part] = act
        sum_ref[...] += dot(act, wd_ref[part, :])

    final = sum_ref[...]
    final_low = final.astype(BF)
    final_ref[...] = final_low
    logits = dot(final_low, head_ref[...], NT)
    one = logits[:, :128]
    two = logits[:, 128:256]
    offset = logits[:, 256:]
    top = jnp.maximum(one, two)
    one = jnp.exp(one - top)
    two = jnp.exp(two - top)
    total = one + two
    one = one / total
    two = two / total
    mask = mask_ref[0]
    first_ref[...] = mask * one + (1.0 - mask)
    second_ref[...] = mask * two
    added_ref[...] = mask * offset
    grad_one = mask * one_ref[...]
    grad_two = mask * two_ref[...]
    mean = one * grad_one + two * grad_two
    heads = jnp.concatenate(
        (one * (grad_one - mean), two * (grad_two - mean), mask * sens_ref[...]), axis=1
    ).astype(BF)
    heads_ref[...] = heads
    grad_final = dot(heads, head_ref[...])
    down = grad_final.astype(BF)
    down_ref[...] = down
    sum_ref[...] = jnp.zeros_like(sum_ref)

    @pl.loop(0, steps)
    def _(j):
        part = chunk(j)
        grad_up = (dot(down, wd_ref[part, :], NT) * slope_ref[:, part]).astype(BF)
        up_ref[:, part] = grad_up
        ups_ref[:, part] = jnp.sum(grad_up.astype(F32), axis=0, keepdims=True)
        sum_ref[...] += dot(grad_up, wu_ref[:, part], NT)

    grad_hidden = sum_ref[...]
    grad_normed = grad_hidden * gain
    grad_residual = grad_final + norm_back(grad_normed, normed, inverse)
    gres_ref[...] = grad_residual
    attn = grad_residual.astype(BF)
    attn_ref[...] = attn
    gatt_ref[...] = dot(attn, wo_ref[...], NT).astype(BF)
    vectors = jnp.concatenate(
        (
            jnp.sum(grad_hidden * normed, axis=0, keepdims=True),
            jnp.sum(grad_hidden, axis=0, keepdims=True),
            jnp.sum(down.astype(F32), axis=0, keepdims=True),
        )
    )
    ups = ups_ref[...]

    @pl.when(pl.program_id(0) == 0)
    def _():
        vec_ref[...] = vectors
        bup_ref[...] = ups

    @pl.when(pl.program_id(0) > 0)
    def _():
        vec_ref[...] += vectors
        bup_ref[...] += ups


def between(x, attended, w_out, w_up, w_down, heads, gain, shift, b_up, b_down, mask, sums, local):
    rows, width = x.shape
    hidden = w_up.shape[1]
    block = math.gcd(local, 256)

    def row(columns):
        return pl.BlockSpec((block, columns), lambda i: (i, 0))

    def whole(values):
        zeros = (0,) * values.ndim
        return pl.BlockSpec(values.shape, lambda i: zeros, pipeline_mode=pl.Buffered(1))

    def shape(columns, kind=BF):
        return jax.ShapeDtypeStruct((rows, columns), kind)

    fixed = [w_out, w_up, w_down, heads, gain, shift, b_up, b_down]
    return pl.pallas_call(
        between_kernel,
        grid=(rows // block,),
        in_specs=[row(width), row(width)]
        + [whole(v) for v in fixed]
        + [pl.BlockSpec((1, 1, 128), lambda i: (i * block // local, 0, 0))]
        + [row(128)] * 3,
        out_specs=[
            row(width),
            row(hidden),
            row(hidden),
            row(width),
            row(width),
            row(384),
            row(width),
            row(width),
            row(width),
            row(128),
            row(128),
            row(128),
            pl.BlockSpec((3, width), lambda i: (0, 0)),
            pl.BlockSpec((1, hidden), lambda i: (0, 0)),
        ],
        out_shape=[
            shape(width),
            shape(hidden),
            shape(hidden),
            shape(width),
            shape(width),
            shape(384),
            shape(width),
            shape(width, F32),
            shape(width),
            shape(128, F32),
            shape(128, F32),
            shape(128, F32),
            jax.ShapeDtypeStruct((3, width), F32),
            jax.ShapeDtypeStruct((1, hidden), F32),
        ],
        scratch_shapes=[
            pltpu.VMEM((block, hidden), F32),
            pltpu.VMEM((block, width), F32),
            pltpu.VMEM((1, hidden), F32),
        ],
        compiler_params=PARAMS,
        name="between",
        cost_estimate=pl.CostEstimate(
            flops=rows * width * hidden, transcendentals=0, bytes_accessed=rows * hidden
        ),
    )(x, attended, *fixed, mask, *sums)


def deal(place, result, mine_ref, sent_ref):
    halves = result.reshape(mine_ref.shape[0], 2, *mine_ref.shape[1:]).astype(BF)
    low = halves[:, 0]
    high = halves[:, 1]
    even = place == 0
    mine_ref[...] = jnp.where(even, low, high)
    sent_ref[...] = jnp.where(even, high, low)


def columns_of(vectors, start):
    count = vectors.shape[0]
    place = lax.broadcasted_iota(jnp.int32, (count, 256), 1)
    which = lax.broadcasted_iota(jnp.int32, (count, 256), 0)
    chosen = (place == which + start).astype(F32).astype(BF)
    high, rest = split_two(vectors)
    return dot(high, chosen, TN) + dot(rest, chosen, TN)


def early_grads_kernel(
    place_ref,
    h_ref,
    a_ref,
    f_ref,
    up_ref,
    attn_ref,
    head_ref,
    vec_ref,
    mine_in_ref,
    sent_in_ref,
    mine_ref,
    sent_ref,
    turn_ref,
):
    step = pl.program_id(0)
    last = pl.num_programs(0) - 1
    place = place_ref[0]
    wide = up_ref.shape[1]

    @pl.when(step == 0)
    def _():
        turn_ref[...] = h_ref[...].T

    @pl.when(step < last - 1)
    def _():
        deal(place, dot(turn_ref[...], up_ref[...]), mine_ref, sent_ref)

    @pl.when(step == last - 1)
    def _():
        turned = a_ref[...].T
        turn_ref[...] = turned
        deal(place, dot(turned, attn_ref[:, :wide]), mine_ref, sent_ref)

    @pl.when(step == last)
    def _():
        out = dot(turn_ref[...], attn_ref[:, wide:])
        heads = dot(f_ref[...].T, head_ref[...]) + columns_of(vec_ref[...], 3 * RESULT_FIELDS)
        deal(place, jnp.concatenate((out, heads), axis=1), mine_ref, sent_ref)


def early_grads(place, hidden, attended, final, up, attn, heads, vectors, mine, sent):
    rows, width = hidden.shape
    wide = 512
    steps = up.shape[1] // wide + 2
    count = width // 96
    skip = mine.shape[2] // wide - steps

    def whole(values):
        return pl.BlockSpec(values.shape, lambda i: (0, 0))

    out = pl.BlockSpec((count, 48, wide), lambda i: (0, 0, i + skip))
    untouched = pl.BlockSpec(memory_space=pl.ANY)
    return pl.pallas_call(
        early_grads_kernel,
        grid=(steps,),
        in_specs=[
            pl.BlockSpec(memory_space=pltpu.SMEM),
            whole(hidden),
            whole(attended),
            whole(final),
            pl.BlockSpec((rows, wide), lambda i: (0, jnp.minimum(i, steps - 3))),
            whole(attn),
            whole(heads),
            whole(vectors),
            untouched,
            untouched,
        ],
        out_specs=[out, out],
        out_shape=[jax.ShapeDtypeStruct(mine.shape, BF)] * 2,
        input_output_aliases={8: 0, 9: 1},
        scratch_shapes=[pltpu.VMEM((width, rows), BF)],
        compiler_params=PARAMS,
        name="early_grads",
        cost_estimate=pl.CostEstimate(
            flops=2 * rows * width * wide * steps,
            transcendentals=0,
            bytes_accessed=2 * rows * wide * steps + 2 * width * wide * steps,
        ),
    )(place, hidden, attended, final, up, attn, heads, vectors, mine, sent)


def down_grads_kernel(place_ref, act_ref, down_ref, mine_ref, sent_ref):
    result = dot(act_ref[...], down_ref[...], TN).astype(BF)
    block = result.shape[0] // 2
    piece = block // 8
    halves = []
    for c in range(2):
        groups = [
            jnp.concatenate(
                [
                    result[c * block + y * 4 * piece + g * piece :][:piece]
                    for y in range(2)
                ],
                axis=0,
            )
            for g in range(4)
        ]
        halves.append(jnp.concatenate(groups, axis=1)[None])
    even = place_ref[0] == 0
    mine_ref[...] = jnp.where(even, halves[0], halves[1])
    sent_ref[...] = jnp.where(even, halves[1], halves[0])


def down_grads(place, activation, down, columns):
    rows, width = down.shape
    block = activation.shape[1] // 8
    piece = block // 16
    out = pl.BlockSpec((1, 2 * piece, 4 * width), lambda i: (i, 0, 0))
    return pl.pallas_call(
        down_grads_kernel,
        grid=(8,),
        in_specs=[
            pl.BlockSpec(memory_space=pltpu.SMEM),
            pl.BlockSpec((rows, block), lambda i: (0, i)),
            pl.BlockSpec((rows, width), lambda i: (0, 0)),
        ],
        out_specs=[out, out],
        out_shape=[jax.ShapeDtypeStruct((8, 2 * piece, columns), BF)] * 2,
        compiler_params=PARAMS,
        name="down_grads",
        cost_estimate=pl.CostEstimate(
            flops=2 * rows * width * block, transcendentals=0, bytes_accessed=width * block
        ),
    )(place, activation, down)


def late_grads_kernel(count, place_ref, *refs):
    mixed_refs = refs[:count]
    query_ref = refs[count]
    both_refs = refs[count + 1 : 2 * count + 1]
    vec_ref, mine_ref, sent_ref, turn_ref = refs[2 * count + 1 :]
    step = pl.program_id(0)
    third = (pl.num_programs(0) - 1) // 3
    place = place_ref[0]

    @pl.when(step == 0)
    def _():
        for s in range(count):
            turn_ref[s] = mixed_refs[s][...].T

    @pl.when(step < third)
    def _():
        deal(place, dot(turn_ref[0], query_ref[...], NT), mine_ref, sent_ref)

    @pl.when((step >= third) & (step < 3 * third))
    def _():
        joint = sum(dot(turn_ref[s], both_refs[s][...]) for s in range(count))
        deal(place, joint, mine_ref, sent_ref)

    @pl.when(step == 3 * third)
    def _():
        deal(place, columns_of(vec_ref[...], 0), mine_ref, sent_ref)


def late_grads(place, mixed, query, both, vectors):
    rows, width = mixed[0].shape
    count = len(mixed)
    wide = 256
    third = width // wide
    groups = width // 96

    whole = pl.BlockSpec((rows, width), lambda i: (0, 0))
    out = pl.BlockSpec((groups, 48, wide), lambda i: (0, 0, i))
    return pl.pallas_call(
        functools.partial(late_grads_kernel, count),
        grid=(3 * third + 1,),
        in_specs=[pl.BlockSpec(memory_space=pltpu.SMEM)]
        + [whole] * count
        + [pl.BlockSpec((wide, rows), lambda i: (jnp.clip(i, 0, third - 1), 0))]
        + [pl.BlockSpec((rows, wide), lambda i: (0, jnp.clip(i - third, 0, 2 * third - 1)))] * count
        + [pl.BlockSpec(vectors.shape, lambda i: (0, 0))],
        out_specs=[out, out],
        out_shape=[jax.ShapeDtypeStruct((groups, 48, wide * (3 * third + 1)), BF)] * 2,
        scratch_shapes=[pltpu.VMEM((count, width, rows), BF)],
        compiler_params=PARAMS,
        name="late_grads",
        cost_estimate=pl.CostEstimate(
            flops=2 * rows * width * width * (2 * count + 1),
            transcendentals=0,
            bytes_accessed=2 * rows * width * 4 * count + 12 * width * width,
        ),
    )(place, *mixed, query, *both, vectors)


def block_sums_kernel(counts, dealt, where_ref, *refs):
    total_in = sum(len(group) for group in counts)
    ins, outs = refs[:total_in], refs[total_in:]
    at = 0
    for o, group in enumerate(counts):
        shape = ins[at].shape[-2:] if dealt else outs[o].shape
        value = None
        for use in group:
            term = ins[at][...].astype(F32).reshape(shape)
            if use is not None:
                term = jnp.where(use(pl.program_id(0), where_ref), term, 0.0)
            value = term if value is None else value + term
            at += 1
        if dealt:
            for k, out in enumerate(outs):

                @pl.when(pl.program_id(0) == k)
                def _(out=out, value=value, o=o):
                    out[o] = value.astype(BF)
        else:
            outs[o][...] = value.astype(BF)


def block_sums(where, steps, groups, dealt=False):
    counts = [[term[3] if len(term) > 3 else None for term in terms] for _, terms in groups]
    operands = [term[0] for _, terms in groups for term in terms]
    in_specs = [pl.BlockSpec(term[1], term[2]) for _, terms in groups for term in terms]
    if dealt:
        shape = (len(groups),) + groups[0][0]
        zeros = (0,) * len(shape)
        out_specs = [pl.BlockSpec(shape, lambda i, w: zeros)] * steps
        out_shape = [jax.ShapeDtypeStruct(shape, BF)] * steps
    else:
        out_specs = [pl.BlockSpec(out[1], out[2]) for out, _ in groups]
        out_shape = [jax.ShapeDtypeStruct(out[0], BF) for out, _ in groups]
    return pl.pallas_call(
        functools.partial(block_sums_kernel, counts, dealt),
        grid_spec=pltpu.PrefetchScalarGridSpec(
            num_scalar_prefetch=1, grid=(steps,), in_specs=in_specs, out_specs=out_specs
        ),
        out_shape=out_shape,
        compiler_params=FULL,
        name="block_sums",
        cost_estimate=pl.CostEstimate(flops=1 << 20, transcendentals=0, bytes_accessed=1 << 20),
    )(where, *operands)


class Reduction:
    def __init__(self, where, terms, by_columns):
        self.where = where
        self.terms = terms
        self.by_columns = by_columns
        self.depth, self.columns = terms[0].shape[3:]
        self.steps = 4 if by_columns else 2
        if by_columns:
            self.columns //= 2

    def at(self, part, x, z, y, sizes):
        block = sizes + (self.depth, self.columns)
        column = part if self.by_columns else 0
        shift = 0 if self.by_columns else 2 * part // sizes[1]

        def index(i, w):
            return (x(w), z(i, w) + shift, y(w), 0, column)

        return [(t, block, index) for t in self.terms]

    def one(self):
        n, tail = self.steps, (self.depth, self.columns)
        ahead = lambda i, w: i
        sent = block_sums(
            self.where,
            n // 2,
            [
                (
                    ((n, 2) + tail, (2, 2) + tail, lambda i, w: (i, 0, 0, 0)),
                    self.at(0, lambda w: 1 - w[0], ahead, lambda w: 0, (1, 2, 2)),
                ),
                (
                    ((2, n) + tail, (2, 2) + tail, lambda i, w: (0, i, 0, 0)),
                    self.at(1, lambda w: 0, ahead, lambda w: 1 - w[1], (2, 2, 1)),
                ),
            ],
        )
        return list(sent)

    def trade_one(self, sent):
        self.got_one = [swap(sent[0], "lat", 1), swap(sent[1], "grp", 2)]

    def two(self):
        n, tail = self.steps, (self.depth, self.columns)
        ahead = lambda i, w: i
        out = ((n,) + tail, (2,) + tail, lambda i, w: (i, 0, 0))
        sent = block_sums(
            self.where,
            n // 2,
            [
                (
                    out,
                    self.at(0, lambda w: w[0], ahead, lambda w: 1 - w[1], (1, 2, 1))
                    + [(self.got_one[0], (2, 1) + tail, lambda i, w: (i, 1 - w[1], 0, 0))],
                ),
                (
                    out,
                    self.at(1, lambda w: 1 - w[0], ahead, lambda w: w[1], (1, 2, 1))
                    + [(self.got_one[1], (1, 2) + tail, lambda i, w: (1 - w[0], i, 0, 0))],
                ),
            ],
        )
        return list(sent)

    def trade_two(self, sent):
        self.got_two = [swap(sent[0], "grp", 2), swap(sent[1], "lat", 1)]

    def quarters(self):
        tail = (self.depth, self.columns)
        x = lambda w: w[0]
        y = lambda w: w[1]
        if self.by_columns:
            place = lambda i, w: w[2] ^ i
            groups = []
            for part in (0, 1):
                terms = self.at(part, x, place, y, (1, 1, 1))
                if part == 0:
                    one = lambda i, w: (w[2] ^ i, w[1], 0, 0)
                else:
                    one = lambda i, w: (w[0], w[2] ^ i, 0, 0)
                terms.append((self.got_one[part], (1, 1) + tail, one))
                terms.append((self.got_two[part], (1,) + tail, lambda i, w: (w[2] ^ i, 0, 0)))
                groups.append((tail, terms))
        else:
            low = lambda i, w: jnp.minimum(w[2] ^ i, 1)
            high = lambda i, w: jnp.maximum((w[2] ^ i) - 2, 0)
            first = lambda i, w: (w[2] ^ i) < 2
            second = lambda i, w: (w[2] ^ i) >= 2
            terms = self.at(0, x, lambda i, w: w[2] ^ i, y, (1, 1, 1))
            pair = (1, 1) + tail
            one = (1,) + tail
            terms += [
                (self.got_one[0], pair, lambda i, w: (low(i, w), w[1], 0, 0), first),
                (self.got_one[1], pair, lambda i, w: (w[0], high(i, w), 0, 0), second),
                (self.got_two[0], one, lambda i, w: (low(i, w), 0, 0), first),
                (self.got_two[1], one, lambda i, w: (high(i, w), 0, 0), second),
            ]
            groups = [(tail, terms)]
        return list(block_sums(self.where, 4, groups, True))


def early_unpack_kernel(place_ref, *refs):
    ins = refs[:4]
    down_ref, up_ref, out_ref, gate_ref, head_ref, gain_ref, bias_ref, bd_ref, bup_ref, misc_ref = refs[4:]
    width = down_ref.shape[1]
    hidden = up_ref.shape[1]
    for source, (c, y) in zip(ins, ((0, 0), (0, 1), (1, 0), (1, 1))):
        slot = jnp.bitwise_xor(place_ref[0], c) * 2 + jnp.bitwise_xor(place_ref[1], y)
        one = source[0].astype(F32)
        two = source[1].astype(F32)
        rows = one.shape[0]
        half = one.shape[1]
        for g in range(4):
            span = pl.ds(pl.multiple_of(slot * 4 * rows + g * rows, 8), rows)
            down_ref[span, :] = one[:, g * width : (g + 1) * width]
        span = pl.ds(pl.multiple_of(slot * rows, 8), rows)
        cut = half - 4 * width
        up_ref[span, :cut] = one[:, 4 * width :]
        up_ref[span, cut:] = two[:, : hidden - cut]
        out_ref[span, :] = two[:, hidden - cut : hidden - cut + width]
        misc_ref[span, :] = two[:, hidden - cut + width :]
    turned = misc_ref[...].T
    at = 0
    for ref in (gate_ref, head_ref, gain_ref, bias_ref, bd_ref, bup_ref):
        count = ref.shape[0]
        ref[...] = turned[at : at + count]
        at += count


def early_unpack(place, pieces, width, hidden):
    rows = pieces[0].shape[1]
    vmem = pl.BlockSpec(memory_space=pltpu.VMEM)
    return pl.pallas_call(
        early_unpack_kernel,
        in_specs=[pl.BlockSpec(memory_space=pltpu.SMEM)] + [vmem] * 4,
        out_specs=[vmem] * 9,
        out_shape=[
            jax.ShapeDtypeStruct((16 * rows, width), F32),
            jax.ShapeDtypeStruct((4 * rows, hidden), F32),
            jax.ShapeDtypeStruct((4 * rows, width), F32),
        ]
        + [
            jax.ShapeDtypeStruct((count, 4 * rows), F32)
            for count in (2 * RESULT_FIELDS, RESULT_FIELDS, 1, 1, 1, 4)
        ],
        scratch_shapes=[pltpu.VMEM((4 * rows, 256), F32)],
        compiler_params=PARAMS,
        name="early_unpack",
        cost_estimate=pl.CostEstimate(flops=1 << 20, transcendentals=0, bytes_accessed=1 << 20),
    )(place, *pieces)


def late_unpack_kernel(place_ref, *refs):
    ins = refs[:4]
    main_ref, gain_ref, bias_ref, lead_ref, misc_ref = refs[4:]
    for source, (c, y) in zip(ins, ((0, 0), (0, 1), (1, 0), (1, 1))):
        slot = jnp.bitwise_xor(place_ref[0], c) * 2 + jnp.bitwise_xor(place_ref[1], y)
        value = source[...].astype(F32)
        rows = value.shape[0]
        span = pl.ds(pl.multiple_of(slot * rows, 8), rows)
        main_ref[span, :] = value[:, : main_ref.shape[1]]
        misc_ref[span, :] = value[:, main_ref.shape[1] :]
    turned = misc_ref[...].T
    gain_ref[...] = turned[:1]
    bias_ref[...] = turned[1:2]
    lead_ref[...] = turned[2 : 2 + LEADS]


def late_unpack(place, pieces):
    rows, columns = pieces[0].shape
    vmem = pl.BlockSpec(memory_space=pltpu.VMEM)
    return pl.pallas_call(
        late_unpack_kernel,
        in_specs=[pl.BlockSpec(memory_space=pltpu.SMEM)] + [vmem] * 4,
        out_specs=[vmem] * 4,
        out_shape=[jax.ShapeDtypeStruct((4 * rows, columns - 256), F32)]
        + [jax.ShapeDtypeStruct((count, 4 * rows), F32) for count in (1, 1, LEADS)],
        scratch_shapes=[pltpu.VMEM((4 * rows, 256), F32)],
        compiler_params=PARAMS,
        name="late_unpack",
        cost_estimate=pl.CostEstimate(flops=1 << 20, transcendentals=0, bytes_accessed=1 << 20),
    )(place, *pieces)


def spread(rows, columns):
    pixel = lax.broadcasted_iota(jnp.int32, (rows, columns), 0)
    field = lax.broadcasted_iota(jnp.int32, (rows, columns), 1)
    return ((pixel // TILE_AREA) == field).astype(F32).astype(BF)


def split_two(values):
    high = values.astype(BF)
    return high, (values - high.astype(F32)).astype(BF)


def pixel_sums_kernel(f_ref, s_ref, sum_ref, first_ref, second_ref, field_ref):
    @pl.when(pl.program_id(0) == 0)
    def _():
        field_ref[...] = spread(*field_ref.shape)

    fields = field_ref[...]
    sens = s_ref[...]
    sum_ref[...] = dot(sens, fields)
    for e, out in ((0, first_ref), (1, second_ref)):
        out[...] = dot((sens.astype(F32) * f_ref[e].astype(F32)).astype(BF), fields)


def pixel_sums(forecasts, sensitivity):
    rows, pixels = sensitivity.shape
    block = math.gcd(rows, 64)
    out = pl.BlockSpec((block, 128), lambda i: (i, 0))
    return pl.pallas_call(
        pixel_sums_kernel,
        grid=(rows // block,),
        in_specs=[
            pl.BlockSpec((2, block, pixels), lambda i: (0, i, 0)),
            pl.BlockSpec((block, pixels), lambda i: (i, 0)),
        ],
        out_specs=[out] * 3,
        out_shape=[jax.ShapeDtypeStruct((rows, 128), F32)] * 3,
        scratch_shapes=[pltpu.VMEM((pixels, 128), BF)],
        compiler_params=PARAMS,
        name="pixel_sums",
        cost_estimate=pl.CostEstimate(
            flops=rows * pixels * 128, transcendentals=0, bytes_accessed=rows * pixels
        ),
    )(forecasts, sensitivity)


def blend_kernel(a_ref, b_ref, c_ref, f_ref, out_ref, field_ref):
    @pl.when(pl.program_id(0) == 0)
    def _():
        columns = field_ref.shape[1]
        field = lax.broadcasted_iota(jnp.int32, (256, columns), 0)
        pixel = lax.broadcasted_iota(jnp.int32, (256, columns), 1)
        field_ref[...] = ((pixel // TILE_AREA) == (field % 128)).astype(F32).astype(BF)

    fields = field_ref[...]

    def wide(ref):
        return dot(jnp.concatenate(split_two(ref[...]), axis=1), fields)

    total = wide(a_ref) * f_ref[0].astype(F32) + wide(b_ref) * f_ref[1].astype(F32)
    out_ref[...] = (total + wide(c_ref)).astype(BF)


def blend(first, second, added, forecasts):
    _, rows, pixels = forecasts.shape
    block = math.gcd(rows, 128)
    thin = pl.BlockSpec((block, 128), lambda i: (i, 0))
    return pl.pallas_call(
        blend_kernel,
        grid=(rows // block,),
        in_specs=[thin] * 3 + [pl.BlockSpec((2, block, pixels), lambda i: (0, i, 0))],
        out_specs=pl.BlockSpec((block, pixels), lambda i: (i, 0)),
        out_shape=jax.ShapeDtypeStruct((rows, pixels), BF),
        scratch_shapes=[pltpu.VMEM((256, pixels), BF)],
        compiler_params=PARAMS,
        name="blend",
        cost_estimate=pl.CostEstimate(
            flops=rows * pixels * 128, transcendentals=0, bytes_accessed=rows * pixels
        ),
    )(first, second, added, forecasts)


def swap(values, axis, bit):
    count = lax.axis_size(axis)
    return lax.ppermute(values, axis, [(i, i ^ bit) for i in range(count)])


def add(*terms):
    return sum(t.astype(F32) for t in terms).astype(BF)


def hold(*values):
    return lax.optimization_barrier(values)


def layer_norm(values):
    centred = values - jnp.mean(values, axis=-1, keepdims=True)
    inverse = lax.rsqrt(jnp.mean(centred * centred, axis=-1, keepdims=True) + EPSILON)
    return centred * inverse, inverse


def norm_back(grad_normed, normed, inverse):
    return inverse * (
        grad_normed
        - jnp.mean(grad_normed, axis=-1, keepdims=True)
        - normed * jnp.mean(grad_normed * normed, axis=-1, keepdims=True)
    )


def pad_lanes(values):
    return jnp.pad(values, ((0, 0), (0, 128 - values.shape[1])))


def per_device(
    layer_source_tensor,
    horizon_class,
    field_selector,
    model_predictions,
    loss_sensitivity,
    gain_one,
    shift_one,
    horizon_vectors,
    w_qkv,
    w_out,
    gain_two,
    shift_two,
    w_up,
    b_up,
    w_down,
    b_down,
    w_gate,
    w_bias,
):
    frames, lat_rows, lon_cols, width = layer_source_tensor.shape
    local = lat_rows * lon_cols
    rows = frames * local
    pixels = loss_sensitivity.shape[-1]
    sizes = (lax.axis_size("grp"), lax.axis_size("lat"), lax.axis_size("lon"))
    small = sizes == (4, 2, 4) and frames == 1

    source = layer_source_tensor.reshape(frames, local, width)
    place = lax.axis_index("lon")
    edge = (place == 0) | (place == lax.axis_size("lon") - 1)
    send = functools.partial(lax.ppermute, axis_name="lon")
    if small:
        right = send(source, perm=[(0, 1), (1, 2), (2, 3)])
        left = send(source, perm=[(3, 2), (2, 1), (1, 0)])
    else:
        shards = [lax.all_gather(source, "lon", axis=1, tiled=True)]

    forecasts = jnp.transpose(model_predictions.reshape(rows, 2, pixels), (1, 0, 2))
    sensitivity = loss_sensitivity.reshape(rows, pixels)

    onehot = (horizon_class[:, None] == jnp.arange(LEADS, dtype=jnp.int32)[None, :]).astype(F32)
    lead_rows = jnp.dot(onehot, horizon_vectors, precision=HIGH)

    def mixed_of(values):
        normed, _ = layer_norm(values.astype(F32))
        return (normed * gain_one + shift_one + lead_rows[:, None, :]).astype(BF)

    both = w_gate.T
    head_rows = jnp.concatenate(
        [
            jnp.pad(m, ((0, 128 - RESULT_FIELDS), (0, 0)))
            for m in (both[:RESULT_FIELDS], both[RESULT_FIELDS:], w_bias.T)
        ]
    )
    nothing = jnp.zeros((frames, width, local), F32)
    wq = w_qkv[:, :width]
    wkv = w_qkv[:, width:]

    def keys_of(values):
        return dot(values.reshape(-1, width), wkv).astype(BF).reshape(frames, -1, 2 * width)

    if small:

        def flat(values):
            return values.reshape(rows, width)

        def shard_of(flag, yes, no):
            m, kv, x = project(
                flag.astype(jnp.int32)[None],
                [flat(yes), flat(no)],
                gain_one,
                shift_one,
                lead_rows,
                w_qkv,
            )
            return m, kv[None], x[None]

        mixed_own, own_kv, queries = project(
            None, [flat(source)], gain_one, shift_one, lead_rows, w_qkv
        )
        queries = queries[None]
        mixed = [mixed_own]
        key_value = [own_kv[None]]
        right, left, forecasts, queries, key_value[0] = hold(
            right, left, forecasts, queries, key_value[0]
        )
        right_two = send(right, perm=[(1, 2), (2, 3)])
        left_two = send(left, perm=[(2, 1), (1, 0)])
        sums = pixel_sums(forecasts, sensitivity)
        m, kv, near = shard_of(place == 0, left, right)
        mixed.append(m)
        right_two, left_two, kv, nothing, head_rows, *sums = hold(
            right_two, left_two, kv, nothing, head_rows, *sums
        )
        key_value.append(kv)
        two = right_two + left_two
        two, middle = hold(two, left)
        three = send(two, perm=[(2, 3), (1, 0)])
        m, kv, middle = shard_of(edge, two, middle)
        mixed.append(m)
        key_value.append(kv)
        state = attend(queries, key_value, None, False)
        three, *state = hold(three, *state)
        m, kv, far = shard_of(edge, three, two)
        mixed.append(m)
        key_value.append(kv)
        attended, logs = attend(queries, key_value[3:], state, True)
        shards = [source, near, middle, far]
    else:
        mixed_own = mixed_of(source)
        queries = dot(mixed_own.reshape(rows, width), wq).astype(BF)
        queries = queries.reshape(frames, local, width)
        sums = pixel_sums(forecasts, sensitivity)
        mixed = [mixed_of(shards[0])]
        key_value = [keys_of(mixed[0])]
        attended, logs = attend(queries, key_value, None, True)
    inputs = source.reshape(rows, width)
    attended_low = attended.reshape(rows, width)
    mask = pad_lanes(field_selector.astype(F32))[:, None]
    (
        hidden_low,
        activation_low,
        up_low,
        down_low,
        final_low,
        heads_low,
        attn_low,
        grad_residual,
        grad_attended,
        *blending,
        early_vectors,
        grad_bup,
    ) = between(
        inputs,
        attended_low,
        w_out,
        w_up,
        w_down,
        head_rows,
        gain_two,
        shift_two,
        b_up,
        b_down,
        mask,
        sums,
        local,
    )
    grad_attended = grad_attended.reshape(frames, local, width)
    fields = 3 * RESULT_FIELDS
    heads_low = jnp.concatenate(
        [heads_low[:, g * 128 : g * 128 + RESULT_FIELDS] for g in range(3)], axis=1
    )
    inputs = inputs.astype(F32)
    normed_one, inverse_one = layer_norm(inputs)

    def input_gradient(grad_mixed):
        return grad_residual + norm_back(
            grad_mixed.reshape(rows, width) * gain_one, normed_one, inverse_one
        )

    def back(shard, place, before):
        return attend_back(queries, grad_attended, attended, logs, shard, w_qkv, place, before)

    def late_vectors(sums):
        gain_column = sum(jnp.sum(s[:, 0], axis=0) for s in sums)
        column = sum(s[:, 1] for s in sums)
        lead = jnp.dot(onehot.T, column, precision=HIGH)
        zeros = jnp.zeros((6, width), F32)
        return jnp.concatenate((gain_column[None], jnp.sum(column, axis=0)[None], lead, zeros))

    if small:
        bup_rows = jnp.swapaxes(grad_bup.reshape(8, 4, -1), 0, 1).reshape(4, width)
        early_vectors = jnp.concatenate(
            (early_vectors, bup_rows, jnp.zeros((1, width), F32))
        )
        core = (lax.axis_index("grp") % 2).astype(jnp.int32)[None]
        where = jnp.stack(
            (lax.axis_index("lat"), lax.axis_index("grp") // 2, lax.axis_index("lon"))
        ).astype(jnp.int32)
        hidden = w_up.shape[1]
        mine, sent = down_grads(core, activation_low, down_low, 2 * hidden + width + 256)
        mine, sent = early_grads(
            core,
            hidden_low,
            attended_low,
            final_low,
            up_low,
            attn_low,
            jnp.pad(heads_low, ((0, 0), (0, 256 - fields))),
            early_vectors,
            mine,
            sent,
        )
        grad_attended, sent = hold(grad_attended, sent)
        got = swap(sent, "grp", 1)

        grad_query, dkv3, far, sums3 = back(key_value[3], shards[3], nothing)
        early = Reduction(where, [t.reshape(2, 4, 2, 24, -1) for t in (mine, got)], True)
        grad_query, far, *sent = hold(grad_query, far, *early.one())
        got = send(far, perm=[(0, 1), (3, 2)])
        early.trade_one(sent)

        grad_query, dkv2, middle, sums2 = back(key_value[2], shards[2], grad_query)
        value = jnp.where(edge, middle, add(got, far))
        grad_query, value = hold(grad_query, value)
        right = send(value, perm=[(0, 1), (1, 2)])
        left = send(value, perm=[(3, 2), (2, 1)])

        grad_query, dkv1, near, sums1 = back(key_value[1], shards[1], grad_query)
        forth = jnp.where(place == 0, near, add(right, middle))
        back_value = add(left, near)
        grad_query, forth, back_value, *sent = hold(
            grad_query, forth, back_value, *early.two()
        )
        right = send(forth, perm=[(0, 1), (1, 2), (2, 3)])
        left = send(back_value, perm=[(3, 2), (2, 1), (1, 0)])
        early.trade_two(sent)

        grad_query, dkv0, own, sums0, right, left, *early.got_two = hold(
            *back(key_value[0], shards[0], grad_query), right, left, *early.got_two
        )
        query_low, query_term, query_sums = query_back(grad_query, w_qkv, source)
        vectors = late_vectors([sums0, sums1, sums2, sums3, query_sums])
        late_mine, late_sent = late_grads(
            core,
            [m.reshape(rows, width) for m in mixed],
            query_low.reshape(width, rows),
            [d.reshape(rows, 2 * width) for d in (dkv0, dkv1, dkv2, dkv3)],
            vectors,
        )
        late_mine, late_sent, *early.got_two, own = hold(
            late_mine, late_sent, *early.got_two, own
        )
        got = swap(late_sent, "grp", 1)
        got, *parts = hold(got, *early.quarters())
        late = Reduction(where, [t.reshape(2, 4, 2, 24, -1) for t in (late_mine, got)], False)
        *sent, one, two, three = hold(*late.one(), *blending)
        late.trade_one(sent)
        early = [parts[0]] + [swap(parts[k], "lon", k) for k in (1, 2, 3)]
        blended = blend(one, two, three, forecasts)
        *late.got_one, blended = hold(*late.got_one, blended)
        *sent, own, early[0] = hold(*late.two(), own, early[0])
        late.trade_two(sent)
        grad_input = input_gradient(
            own.astype(F32) + query_term + right.astype(F32) + left.astype(F32)
        )
        *late.got_two, grad_input = hold(*late.got_two, grad_input)
        early[0], *parts = hold(early[0], *late.quarters())
        late = [parts[0]] + [swap(parts[k], "lon", k) for k in (1, 2, 3)]
        late[1], late[2], early[0] = hold(late[1], late[2], early[0])
        late = add(*[part[0] for part in late])
        late_y = swap(late, "grp", 2)
        late_c = swap(late, "grp", 1)
        early = add(*early)
        early_y = swap(early, "grp", 2)
        early_c = swap(early, "grp", 1)
        early_y, early_c, early, late_y, late_c, late = hold(
            early_y, early_c, early, late_y, late_c, late
        )
        early_yc = swap(early_y, "grp", 1)
        late_yc = swap(late_y, "grp", 1)
        place_two = jnp.stack((lax.axis_index("grp") % 2, lax.axis_index("grp") // 2))
        place_two = place_two.astype(jnp.int32)
        down_sum, up_sum, out_sum, gate_sum, head_sum, *early, bup_sum = early_unpack(
            place_two, [early, early_y, early_c, early_yc], width, hidden
        )
        late_yc, gate_sum = hold(late_yc, gate_sum)
        qkv_sum, *late, lead_sum = late_unpack(place_two, [late, late_y, late_c, late_yc])
        early = [e.reshape(-1) for e in early]
        late = [e.reshape(-1) for e in late]
        bup_sum = bup_sum.reshape(-1)
        gate_sum = gate_sum.T
        head_sum = head_sum.T
    else:
        blended = blend(*blending, forecasts)
        grad_query, dkv, term, sums = back(key_value[0], shards[0], nothing)
        query_low, query_term, query_sums = query_back(grad_query, w_qkv, source)
        grad_input = input_gradient(
            query_term + lax.psum_scatter(term.astype(F32), "lon", scatter_dimension=1, tiled=True)
        )

        def total_of(values, dim=0):
            share = lax.psum_scatter(values, ("lat", "lon"), scatter_dimension=dim, tiled=True)
            return lax.psum(share, "grp")

        flat = mixed[0].reshape(-1, width)
        qkv_sum = total_of(
            jnp.concatenate(
                (
                    jnp.einsum("frd,fer->de", mixed_own, query_low, preferred_element_type=F32),
                    dot(flat, dkv.reshape(-1, 2 * width), TN),
                ),
                axis=1,
            )
        )
        up_sum = total_of(dot(hidden_low, up_low, TN))
        out_sum = total_of(dot(attended_low, attn_low, TN))
        down_sum = total_of(dot(activation_low, down_low, TN))
        heads = total_of(dot(final_low, heads_low, TN))
        late = total_of(late_vectors([sums, query_sums])[: 2 + LEADS], 1)
        lead_sum = late[2:]
        gate_sum = heads[:, : 2 * RESULT_FIELDS]
        head_sum = heads[:, 2 * RESULT_FIELDS :]
        early = total_of(early_vectors, 1)
        bup_sum = total_of(grad_bup[0])

    return (
        blended.reshape(frames, lat_rows, lon_cols, pixels),
        grad_input.reshape(frames, lat_rows, lon_cols, width),
        late[0],
        late[1],
        lead_sum,
        qkv_sum,
        out_sum,
        early[0],
        early[1],
        up_sum,
        bup_sum,
        down_sum,
        early[2],
        gate_sum,
        head_sum,
    )


def solution(mesh):
    frame = ("grp", "lat")
    share = ("lat", "lon")
    image = P(frame, None, "lon", None)
    in_specs = (
        image,
        P(frame),
        P(frame, None),
        P(frame, None, "lon", None, None),
        image,
    ) + (P(),) * 13
    vector = P(share)
    matrix = P(share, None)
    out_specs = (
        image,
        image,
        vector,
        vector,
        P(None, share),
        matrix,
        matrix,
        vector,
        vector,
        matrix,
        vector,
        matrix,
        vector,
        matrix,
        matrix,
    )
    return jax.shard_map(
        per_device, mesh=mesh, in_specs=in_specs, out_specs=out_specs, check_vma=False
    )
```

```python
import functools
import math

import jax
import jax.numpy as jnp
from jax import lax
from jax.experimental import pallas as pl
from jax.experimental.pallas import tpu as pltpu
from jax.sharding import PartitionSpec as P

H = 12
DH = 64
RESULT_FIELDS = 69
TILE_AREA = 64
LEADS = 24
EPSILON = 1e-06
HIGH = lax.Precision.HIGHEST
SCALE = 0.125
SCALE_TWO = SCALE * math.log2(math.e)
ROOT = math.sqrt(2.0 / math.pi)
CUBE = 0.044715
NN = (((1,), (0,)), ((), ()))
NT = (((1,), (1,)), ((), ()))
TN = (((0,), (0,)), ((), ()))
BF = jnp.bfloat16
F32 = jnp.float32
PARAMS = pltpu.CompilerParams(vmem_limit_bytes=60 * 1024 * 1024)
FULL = pltpu.CompilerParams(vmem_limit_bytes=63 * 1024 * 1024 + 512 * 1024)


def dot(left, right, dims=NN):
    return lax.dot_general(left, right, dims, preferred_element_type=F32)


def project_kernel(own, *refs):
    if own:
        a_ref, gain_ref, shift_ref, lead_ref, wq_ref, wk_ref, wv_ref, mixed_ref, kv_ref, q_ref = refs
        value = a_ref[...]
    else:
        flag_ref, a_ref, b_ref, gain_ref, shift_ref, lead_ref, wk_ref, wv_ref = refs[:8]
        mixed_ref, kv_ref, x_ref = refs[8:]
        value = jnp.where(flag_ref[0] != 0, a_ref[...], b_ref[...])
        x_ref[...] = value
    normed, _ = layer_norm(value.astype(F32))
    mixed = (normed * gain_ref[...][None] + shift_ref[...][None] + lead_ref[...]).astype(BF)
    mixed_ref[...] = mixed
    width = mixed.shape[1]
    kv_ref[:, :width] = dot(mixed, wk_ref[...]).astype(BF)
    kv_ref[:, width:] = dot(mixed, wv_ref[...]).astype(BF)
    if own:
        q_ref[...] = dot(mixed, wq_ref[...]).astype(BF)


def project(flag, sources, gain, shift, lead, weights):
    own = flag is None
    rows, width = sources[0].shape
    block = math.gcd(rows, 256)
    row = pl.BlockSpec((block, width), lambda i: (i, 0))
    vector = pl.BlockSpec((width,), lambda i: (0,))

    def columns(group):
        return pl.BlockSpec((width, width), lambda i: (0, group))

    groups = (0, 1, 2) if own else (1, 2)
    return pl.pallas_call(
        functools.partial(project_kernel, own),
        grid=(rows // block,),
        in_specs=([] if own else [pl.BlockSpec(memory_space=pltpu.SMEM)])
        + [row] * len(sources)
        + [vector, vector, pl.BlockSpec((1, width), lambda i: (0, 0))]
        + [columns(g) for g in groups],
        out_specs=[row, pl.BlockSpec((block, 2 * width), lambda i: (i, 0)), row],
        out_shape=[
            jax.ShapeDtypeStruct((rows, width), BF),
            jax.ShapeDtypeStruct((rows, 2 * width), BF),
            jax.ShapeDtypeStruct((rows, width), BF),
        ],
        compiler_params=PARAMS,
        name="project",
        cost_estimate=pl.CostEstimate(
            flops=rows * width * width, transcendentals=0, bytes_accessed=rows * width
        ),
    )(*([] if own else [flag]), *sources, gain, shift, lead, *([weights] * len(groups)))


def attend_kernel(count, chained, final, *refs):
    q_ref = refs[0]
    k_refs = refs[1 : 1 + count]
    v_refs = refs[1 + count : 1 + 2 * count]
    o_ref, l_ref = refs[-2:]
    outs = []
    for h in range(2):
        part = slice(h * DH, h * DH + DH)
        q = q_ref[0, :, part]
        scores = [dot(k[0, :, part], q, NT) for k in k_refs]
        top = functools.reduce(
            jnp.maximum, [jnp.max(s, axis=0, keepdims=True) for s in scores]
        )
        top = top * SCALE_TWO
        total = None
        mixed = None
        for s, v in zip(scores, v_refs):
            raised = jnp.exp2(s * SCALE_TWO - top)
            some = jnp.sum(raised, axis=0, keepdims=True)
            term = dot(v[0, :, part], raised.astype(BF), TN)
            total = some if total is None else total + some
            mixed = term if mixed is None else mixed + term
        mixed = mixed * (1.0 / total)
        log = top + jnp.log2(total)
        if chained:
            before_ref, before_log_ref = refs[1 + 2 * count : 3 + 2 * count]
            before = before_log_ref[0, 0, h : h + 1, :]
            high = jnp.maximum(before, log)
            joint = high + jnp.log2(jnp.exp2(before - high) + jnp.exp2(log - high))
            mixed = mixed * jnp.exp2(log - joint) + before_ref[0, part, :] * jnp.exp2(
                before - joint
            )
            log = joint
        l_ref[0, 0, h : h + 1, :] = log
        if final:
            outs.append(mixed)
        else:
            o_ref[0, part, :] = mixed
    if final:
        o_ref[0] = jnp.concatenate(outs, axis=0).T.astype(BF)


def attend(queries, shards, before, final):
    frames, rows, width = queries.shape
    count = len(shards)
    keys = shards[0].shape[1]
    pairs = width // 128
    turned = pl.BlockSpec((1, 128, rows), lambda f, p: (f, p, 0))
    row = pl.BlockSpec((1, rows, 128), lambda f, p: (f, 0, p))
    log = pl.BlockSpec((1, 1, 2, rows), lambda f, p: (f, p, 0, 0))
    chained = before is not None
    return pl.pallas_call(
        functools.partial(attend_kernel, count, chained, final),
        grid=(frames, pairs),
        in_specs=[row]
        + [pl.BlockSpec((1, keys, 128), lambda f, p: (f, 0, p))] * count
        + [pl.BlockSpec((1, keys, 128), lambda f, p: (f, 0, p + pairs))] * count
        + ([turned, log] if chained else []),
        out_specs=[row if final else turned, log],
        out_shape=[
            jax.ShapeDtypeStruct((frames, rows, width), BF)
            if final
            else jax.ShapeDtypeStruct((frames, width, rows), F32),
            jax.ShapeDtypeStruct((frames, pairs, 2, rows), F32),
        ],
        compiler_params=PARAMS,
        name="attend",
        cost_estimate=pl.CostEstimate(
            flops=2 * frames * rows * count * keys * width,
            transcendentals=0,
            bytes_accessed=frames * rows * width,
        ),
    )(queries, *shards, *shards, *(before if chained else ()))


def column_sums(total, values):
    normed, _ = layer_norm(values.astype(F32))
    return jnp.concatenate(
        (
            jnp.sum(total * normed, axis=0, keepdims=True),
            jnp.sum(total, axis=0, keepdims=True),
        )
    )


def attend_back_kernel(
    q_ref,
    g_ref,
    o_ref,
    l_ref,
    k_ref,
    v_ref,
    wk_ref,
    wv_ref,
    x_ref,
    before_ref,
    dq_ref,
    dkv_ref,
    term_ref,
    sums_ref,
):
    pair = pl.program_id(1)
    key_terms = []
    value_terms = []
    query_terms = []
    for h in range(2):
        part = slice(h * DH, h * DH + DH)
        q = q_ref[0, :, part]
        g = g_ref[0, :, part]
        k = k_ref[0, :, part]
        v = v_ref[0, :, part]
        product = g.astype(F32) * o_ref[0, :, part].astype(F32)
        high, low = split_two(product)
        ones = jnp.ones((8, DH), BF)
        delta = (dot(ones, high, NT) + dot(ones, low, NT))[0:1]
        probs = jnp.exp2(dot(k, q, NT) * SCALE_TWO - l_ref[0, 0, h : h + 1, :])
        grad_probs = dot(v, g, NT)
        grad_scores = (probs * (grad_probs - delta)).astype(BF)
        value_terms.append(dot(probs.astype(BF), g))
        key_terms.append(dot(grad_scores, q))
        grad_query = dot(k, grad_scores, TN) * SCALE + before_ref[0, part, :]
        query_terms.append(grad_query)
    grad_key = (jnp.concatenate(key_terms, axis=1) * SCALE).astype(BF)
    grad_value = jnp.concatenate(value_terms, axis=1).astype(BF)
    grad_query = jnp.concatenate(query_terms, axis=0).astype(dq_ref.dtype)
    width = wk_ref.shape[0]
    dkv_ref[0, :, pl.ds(pl.multiple_of(pair * 128, 128), 128)] = grad_key
    dkv_ref[0, :, pl.ds(pl.multiple_of(width + pair * 128, 128), 128)] = grad_value
    dq_ref[0] = grad_query

    @pl.when(pair == pl.num_programs(1) - 1)
    def _():
        total = dot(dkv_ref[0, :, :width], wk_ref[...], NT)
        total = total + dot(dkv_ref[0, :, width:], wv_ref[...], NT)
        term_ref[0] = total.astype(term_ref.dtype)
        sums_ref[0] = column_sums(total, x_ref[0])


def attend_back(queries, grad_out, out, logs, shard, weights, source, before):
    frames, rows, width = queries.shape
    keys = shard.shape[1]
    pairs = width // 128
    row = pl.BlockSpec((1, rows, 128), lambda f, p: (f, 0, p))
    key = pl.BlockSpec((1, keys, 128), lambda f, p: (f, 0, p))
    value = pl.BlockSpec((1, keys, 128), lambda f, p: (f, 0, p + pairs))
    turned = pl.BlockSpec((1, 128, rows), lambda f, p: (f, p, 0))
    log = pl.BlockSpec((1, 1, 2, rows), lambda f, p: (f, p, 0, 0))

    def columns(group):
        return pl.BlockSpec((width, width), lambda f, p: (0, group))

    def whole(*shape):
        return pl.BlockSpec((1,) + shape, lambda f, p: (f, 0, 0))

    in_specs = [row, row, row, log, key, value, columns(1), columns(2), whole(keys, width)]
    operands = [queries, grad_out, out, logs, shard, shard, weights, weights, source]
    aliases = {len(operands): 0}
    in_specs.append(turned)
    operands.append(before)
    out_specs = [turned, whole(keys, 2 * width), whole(keys, width), whole(2, width)]
    out_shape = [
        jax.ShapeDtypeStruct((frames, width, rows), F32),
        jax.ShapeDtypeStruct((frames, keys, 2 * width), BF),
        jax.ShapeDtypeStruct((frames, keys, width), BF),
        jax.ShapeDtypeStruct((frames, 2, width), F32),
    ]
    return pl.pallas_call(
        attend_back_kernel,
        grid=(frames, pairs),
        in_specs=in_specs,
        out_specs=out_specs,
        out_shape=out_shape,
        input_output_aliases=aliases,
        compiler_params=PARAMS,
        name="attend_back",
        cost_estimate=pl.CostEstimate(
            flops=4 * frames * rows * keys * width,
            transcendentals=0,
            bytes_accessed=frames * rows * width,
        ),
    )(*operands)


def query_back_kernel(dq_ref, w_ref, x_ref, low_ref, term_ref, sums_ref):
    low = dq_ref[0].astype(BF)
    low_ref[0] = low
    total = dot(low, w_ref[...], (((0,), (1,)), ((), ())))
    term_ref[0] = total
    sums_ref[0] = column_sums(total, x_ref[0])


def query_back(grad_query, weights, source):
    frames, width, rows = grad_query.shape

    def whole(*shape):
        return pl.BlockSpec((1,) + shape, lambda f: (f, 0, 0))

    return pl.pallas_call(
        query_back_kernel,
        grid=(frames,),
        in_specs=[
            whole(width, rows),
            pl.BlockSpec((width, width), lambda f: (0, 0)),
            whole(rows, width),
        ],
        out_specs=[whole(width, rows), whole(rows, width), whole(2, width)],
        out_shape=[
            jax.ShapeDtypeStruct((frames, width, rows), BF),
            jax.ShapeDtypeStruct((frames, rows, width), F32),
            jax.ShapeDtypeStruct((frames, 2, width), F32),
        ],
        compiler_params=PARAMS,
        name="query_back",
        cost_estimate=pl.CostEstimate(
            flops=frames * rows * width * width, transcendentals=0, bytes_accessed=rows * width
        ),
    )(grad_query, weights, source)


def between_kernel(
    x_ref,
    att_ref,
    wo_ref,
    wu_ref,
    wd_ref,
    head_ref,
    gain_ref,
    shift_ref,
    bu_ref,
    bd_ref,
    mask_ref,
    sens_ref,
    one_ref,
    two_ref,
    hidden_ref,
    act_ref,
    up_ref,
    down_ref,
    final_ref,
    heads_ref,
    attn_ref,
    gres_ref,
    gatt_ref,
    first_ref,
    second_ref,
    added_ref,
    vec_ref,
    bup_ref,
    slope_ref,
    sum_ref,
    ups_ref,
):
    residual = x_ref[...].astype(F32) + dot(att_ref[...], wo_ref[...])
    normed, inverse = layer_norm(residual)
    gain = gain_ref[...][None]
    hidden = (normed * gain + shift_ref[...][None]).astype(BF)
    hidden_ref[...] = hidden
    wide = 1536
    steps = wu_ref.shape[1] // wide
    sum_ref[...] = residual + bd_ref[...][None]

    def chunk(j):
        return pl.ds(pl.multiple_of(j * wide, wide), wide)

    @pl.loop(0, steps)
    def _(j):
        part = chunk(j)
        up = dot(hidden, wu_ref[:, part]) + bu_ref[part][None]
        square = up * up
        tanh = jnp.tanh(ROOT * up * (1.0 + CUBE * square))
        half = 0.5 * (1.0 + tanh)
        act = (up * half).astype(BF)
        slope_ref[:, part] = half + 0.5 * up * (1.0 - tanh * tanh) * (
            ROOT + 3.0 * ROOT * CUBE * square
        )
        act_ref[:, part] = act
        sum_ref[...] += dot(act, wd_ref[part, :])

    final = sum_ref[...]
    final_low = final.astype(BF)
    final_ref[...] = final_low
    logits = dot(final_low, head_ref[...], NT)
    one = logits[:, :128]
    two = logits[:, 128:256]
    offset = logits[:, 256:]
    top = jnp.maximum(one, two)
    one = jnp.exp(one - top)
    two = jnp.exp(two - top)
    total = one + two
    one = one / total
    two = two / total
    mask = mask_ref[0]
    first_ref[...] = mask * one + (1.0 - mask)
    second_ref[...] = mask * two
    added_ref[...] = mask * offset
    grad_one = mask * one_ref[...]
    grad_two = mask * two_ref[...]
    mean = one * grad_one + two * grad_two
    heads = jnp.concatenate(
        (one * (grad_one - mean), two * (grad_two - mean), mask * sens_ref[...]), axis=1
    ).astype(BF)
    heads_ref[...] = heads
    grad_final = dot(heads, head_ref[...])
    down = grad_final.astype(BF)
    down_ref[...] = down
    sum_ref[...] = jnp.zeros_like(sum_ref)

    @pl.loop(0, steps)
    def _(j):
        part = chunk(j)
        grad_up = (dot(down, wd_ref[part, :], NT) * slope_ref[:, part]).astype(BF)
        up_ref[:, part] = grad_up
        ups_ref[:, part] = jnp.sum(grad_up.astype(F32), axis=0, keepdims=True)
        sum_ref[...] += dot(grad_up, wu_ref[:, part], NT)

    grad_hidden = sum_ref[...]
    grad_normed = grad_hidden * gain
    grad_residual = grad_final + norm_back(grad_normed, normed, inverse)
    gres_ref[...] = grad_residual
    attn = grad_residual.astype(BF)
    attn_ref[...] = attn
    gatt_ref[...] = dot(attn, wo_ref[...], NT).astype(BF)
    vectors = jnp.concatenate(
        (
            jnp.sum(grad_hidden * normed, axis=0, keepdims=True),
            jnp.sum(grad_hidden, axis=0, keepdims=True),
            jnp.sum(down.astype(F32), axis=0, keepdims=True),
        )
    )
    ups = ups_ref[...]

    @pl.when(pl.program_id(0) == 0)
    def _():
        vec_ref[...] = vectors
        bup_ref[...] = ups

    @pl.when(pl.program_id(0) > 0)
    def _():
        vec_ref[...] += vectors
        bup_ref[...] += ups


def between(x, attended, w_out, w_up, w_down, heads, gain, shift, b_up, b_down, mask, sums, local):
    rows, width = x.shape
    hidden = w_up.shape[1]
    block = math.gcd(local, 256)

    def row(columns):
        return pl.BlockSpec((block, columns), lambda i: (i, 0))

    def whole(values):
        zeros = (0,) * values.ndim
        return pl.BlockSpec(values.shape, lambda i: zeros, pipeline_mode=pl.Buffered(1))

    def shape(columns, kind=BF):
        return jax.ShapeDtypeStruct((rows, columns), kind)

    fixed = [w_out, w_up, w_down, heads, gain, shift, b_up, b_down]
    return pl.pallas_call(
        between_kernel,
        grid=(rows // block,),
        in_specs=[row(width), row(width)]
        + [whole(v) for v in fixed]
        + [pl.BlockSpec((1, 1, 128), lambda i: (i * block // local, 0, 0))]
        + [row(128)] * 3,
        out_specs=[
            row(width),
            row(hidden),
            row(hidden),
            row(width),
            row(width),
            row(384),
            row(width),
            row(width),
            row(width),
            row(128),
            row(128),
            row(128),
            pl.BlockSpec((3, width), lambda i: (0, 0)),
            pl.BlockSpec((1, hidden), lambda i: (0, 0)),
        ],
        out_shape=[
            shape(width),
            shape(hidden),
            shape(hidden),
            shape(width),
            shape(width),
            shape(384),
            shape(width),
            shape(width, F32),
            shape(width),
            shape(128, F32),
            shape(128, F32),
            shape(128, F32),
            jax.ShapeDtypeStruct((3, width), F32),
            jax.ShapeDtypeStruct((1, hidden), F32),
        ],
        scratch_shapes=[
            pltpu.VMEM((block, hidden), F32),
            pltpu.VMEM((block, width), F32),
            pltpu.VMEM((1, hidden), F32),
        ],
        compiler_params=PARAMS,
        name="between",
        cost_estimate=pl.CostEstimate(
            flops=rows * width * hidden, transcendentals=0, bytes_accessed=rows * hidden
        ),
    )(x, attended, *fixed, mask, *sums)


def deal(place, result, mine_ref, sent_ref):
    halves = result.reshape(mine_ref.shape[0], 2, *mine_ref.shape[1:]).astype(BF)
    low = halves[:, 0]
    high = halves[:, 1]
    even = place == 0
    mine_ref[...] = jnp.where(even, low, high)
    sent_ref[...] = jnp.where(even, high, low)


def columns_of(vectors, start):
    count = vectors.shape[0]
    place = lax.broadcasted_iota(jnp.int32, (count, 256), 1)
    which = lax.broadcasted_iota(jnp.int32, (count, 256), 0)
    chosen = (place == which + start).astype(F32).astype(BF)
    high, rest = split_two(vectors)
    return dot(high, chosen, TN) + dot(rest, chosen, TN)


def early_grads_kernel(
    place_ref,
    h_ref,
    a_ref,
    f_ref,
    up_ref,
    attn_ref,
    head_ref,
    vec_ref,
    mine_in_ref,
    sent_in_ref,
    mine_ref,
    sent_ref,
    turn_ref,
):
    step = pl.program_id(0)
    last = pl.num_programs(0) - 1
    place = place_ref[0]
    wide = up_ref.shape[1]

    @pl.when(step == 0)
    def _():
        turn_ref[...] = h_ref[...].T

    @pl.when(step < last - 1)
    def _():
        deal(place, dot(turn_ref[...], up_ref[...]), mine_ref, sent_ref)

    @pl.when(step == last - 1)
    def _():
        turned = a_ref[...].T
        turn_ref[...] = turned
        deal(place, dot(turned, attn_ref[:, :wide]), mine_ref, sent_ref)

    @pl.when(step == last)
    def _():
        out = dot(turn_ref[...], attn_ref[:, wide:])
        heads = dot(f_ref[...].T, head_ref[...]) + columns_of(vec_ref[...], 3 * RESULT_FIELDS)
        deal(place, jnp.concatenate((out, heads), axis=1), mine_ref, sent_ref)


def early_grads(place, hidden, attended, final, up, attn, heads, vectors, mine, sent):
    rows, width = hidden.shape
    wide = 512
    steps = up.shape[1] // wide + 2
    count = width // 96
    skip = mine.shape[2] // wide - steps

    def whole(values):
        return pl.BlockSpec(values.shape, lambda i: (0, 0))

    out = pl.BlockSpec((count, 48, wide), lambda i: (0, 0, i + skip))
    untouched = pl.BlockSpec(memory_space=pl.ANY)
    return pl.pallas_call(
        early_grads_kernel,
        grid=(steps,),
        in_specs=[
            pl.BlockSpec(memory_space=pltpu.SMEM),
            whole(hidden),
            whole(attended),
            whole(final),
            pl.BlockSpec((rows, wide), lambda i: (0, jnp.minimum(i, steps - 3))),
            whole(attn),
            whole(heads),
            whole(vectors),
            untouched,
            untouched,
        ],
        out_specs=[out, out],
        out_shape=[jax.ShapeDtypeStruct(mine.shape, BF)] * 2,
        input_output_aliases={8: 0, 9: 1},
        scratch_shapes=[pltpu.VMEM((width, rows), BF)],
        compiler_params=PARAMS,
        name="early_grads",
        cost_estimate=pl.CostEstimate(
            flops=2 * rows * width * wide * steps,
            transcendentals=0,
            bytes_accessed=2 * rows * wide * steps + 2 * width * wide * steps,
        ),
    )(place, hidden, attended, final, up, attn, heads, vectors, mine, sent)


def down_grads_kernel(place_ref, act_ref, down_ref, mine_ref, sent_ref):
    result = dot(act_ref[...], down_ref[...], TN).astype(BF)
    block = result.shape[0] // 2
    piece = block // 8
    halves = []
    for c in range(2):
        groups = [
            jnp.concatenate(
                [
                    result[c * block + y * 4 * piece + g * piece :][:piece]
                    for y in range(2)
                ],
                axis=0,
            )
            for g in range(4)
        ]
        halves.append(jnp.concatenate(groups, axis=1)[None])
    even = place_ref[0] == 0
    mine_ref[...] = jnp.where(even, halves[0], halves[1])
    sent_ref[...] = jnp.where(even, halves[1], halves[0])


def down_grads(place, activation, down, columns):
    rows, width = down.shape
    block = activation.shape[1] // 8
    piece = block // 16
    out = pl.BlockSpec((1, 2 * piece, 4 * width), lambda i: (i, 0, 0))
    return pl.pallas_call(
        down_grads_kernel,
        grid=(8,),
        in_specs=[
            pl.BlockSpec(memory_space=pltpu.SMEM),
            pl.BlockSpec((rows, block), lambda i: (0, i)),
            pl.BlockSpec((rows, width), lambda i: (0, 0)),
        ],
        out_specs=[out, out],
        out_shape=[jax.ShapeDtypeStruct((8, 2 * piece, columns), BF)] * 2,
        compiler_params=PARAMS,
        name="down_grads",
        cost_estimate=pl.CostEstimate(
            flops=2 * rows * width * block, transcendentals=0, bytes_accessed=width * block
        ),
    )(place, activation, down)


def late_grads_kernel(count, place_ref, *refs):
    mixed_refs = refs[:count]
    query_ref = refs[count]
    both_refs = refs[count + 1 : 2 * count + 1]
    vec_ref, mine_ref, sent_ref, turn_ref = refs[2 * count + 1 :]
    step = pl.program_id(0)
    third = (pl.num_programs(0) - 1) // 3
    place = place_ref[0]

    @pl.when(step == 0)
    def _():
        for s in range(count):
            turn_ref[s] = mixed_refs[s][...].T

    @pl.when(step < third)
    def _():
        deal(place, dot(turn_ref[0], query_ref[...], NT), mine_ref, sent_ref)

    @pl.when((step >= third) & (step < 3 * third))
    def _():
        joint = sum(dot(turn_ref[s], both_refs[s][...]) for s in range(count))
        deal(place, joint, mine_ref, sent_ref)

    @pl.when(step == 3 * third)
    def _():
        deal(place, columns_of(vec_ref[...], 0), mine_ref, sent_ref)


def late_grads(place, mixed, query, both, vectors):
    rows, width = mixed[0].shape
    count = len(mixed)
    wide = 256
    third = width // wide
    groups = width // 96

    whole = pl.BlockSpec((rows, width), lambda i: (0, 0))
    out = pl.BlockSpec((groups, 48, wide), lambda i: (0, 0, i))
    return pl.pallas_call(
        functools.partial(late_grads_kernel, count),
        grid=(3 * third + 1,),
        in_specs=[pl.BlockSpec(memory_space=pltpu.SMEM)]
        + [whole] * count
        + [pl.BlockSpec((wide, rows), lambda i: (jnp.clip(i, 0, third - 1), 0))]
        + [pl.BlockSpec((rows, wide), lambda i: (0, jnp.clip(i - third, 0, 2 * third - 1)))] * count
        + [pl.BlockSpec(vectors.shape, lambda i: (0, 0))],
        out_specs=[out, out],
        out_shape=[jax.ShapeDtypeStruct((groups, 48, wide * (3 * third + 1)), BF)] * 2,
        scratch_shapes=[pltpu.VMEM((count, width, rows), BF)],
        compiler_params=PARAMS,
        name="late_grads",
        cost_estimate=pl.CostEstimate(
            flops=2 * rows * width * width * (2 * count + 1),
            transcendentals=0,
            bytes_accessed=2 * rows * width * 4 * count + 12 * width * width,
        ),
    )(place, *mixed, query, *both, vectors)


def block_sums_kernel(counts, dealt, where_ref, *refs):
    total_in = sum(len(group) for group in counts)
    ins, outs = refs[:total_in], refs[total_in:]
    at = 0
    for o, group in enumerate(counts):
        shape = ins[at].shape[-2:] if dealt else outs[o].shape
        value = None
        for use in group:
            term = ins[at][...].astype(F32).reshape(shape)
            if use is not None:
                term = jnp.where(use(pl.program_id(0), where_ref), term, 0.0)
            value = term if value is None else value + term
            at += 1
        if dealt:
            for k, out in enumerate(outs):

                @pl.when(pl.program_id(0) == k)
                def _(out=out, value=value, o=o):
                    out[o] = value.astype(BF)
        else:
            outs[o][...] = value.astype(BF)


def block_sums(where, steps, groups, dealt=False):
    counts = [[term[3] if len(term) > 3 else None for term in terms] for _, terms in groups]
    operands = [term[0] for _, terms in groups for term in terms]
    in_specs = [pl.BlockSpec(term[1], term[2]) for _, terms in groups for term in terms]
    if dealt:
        shape = (len(groups),) + groups[0][0]
        zeros = (0,) * len(shape)
        out_specs = [pl.BlockSpec(shape, lambda i, w: zeros)] * steps
        out_shape = [jax.ShapeDtypeStruct(shape, BF)] * steps
    else:
        out_specs = [pl.BlockSpec(out[1], out[2]) for out, _ in groups]
        out_shape = [jax.ShapeDtypeStruct(out[0], BF) for out, _ in groups]
    return pl.pallas_call(
        functools.partial(block_sums_kernel, counts, dealt),
        grid_spec=pltpu.PrefetchScalarGridSpec(
            num_scalar_prefetch=1, grid=(steps,), in_specs=in_specs, out_specs=out_specs
        ),
        out_shape=out_shape,
        compiler_params=FULL,
        name="block_sums",
        cost_estimate=pl.CostEstimate(flops=1 << 20, transcendentals=0, bytes_accessed=1 << 20),
    )(where, *operands)


class Reduction:
    def __init__(self, where, terms, by_columns):
        self.where = where
        self.terms = terms
        self.by_columns = by_columns
        self.depth, self.columns = terms[0].shape[3:]
        self.steps = 4 if by_columns else 2
        if by_columns:
            self.columns //= 2

    def at(self, part, x, z, y, sizes):
        block = sizes + (self.depth, self.columns)
        column = part if self.by_columns else 0
        shift = 0 if self.by_columns else 2 * part // sizes[1]

        def index(i, w):
            return (x(w), z(i, w) + shift, y(w), 0, column)

        return [(t, block, index) for t in self.terms]

    def one(self):
        n, tail = self.steps, (self.depth, self.columns)
        ahead = lambda i, w: i
        sent = block_sums(
            self.where,
            n // 2,
            [
                (
                    ((n, 2) + tail, (2, 2) + tail, lambda i, w: (i, 0, 0, 0)),
                    self.at(0, lambda w: 1 - w[0], ahead, lambda w: 0, (1, 2, 2)),
                ),
                (
                    ((2, n) + tail, (2, 2) + tail, lambda i, w: (0, i, 0, 0)),
                    self.at(1, lambda w: 0, ahead, lambda w: 1 - w[1], (2, 2, 1)),
                ),
            ],
        )
        return list(sent)

    def trade_one(self, sent):
        self.got_one = [swap(sent[0], "lat", 1), swap(sent[1], "grp", 2)]

    def two(self):
        n, tail = self.steps, (self.depth, self.columns)
        ahead = lambda i, w: i
        out = ((n,) + tail, (2,) + tail, lambda i, w: (i, 0, 0))
        sent = block_sums(
            self.where,
            n // 2,
            [
                (
                    out,
                    self.at(0, lambda w: w[0], ahead, lambda w: 1 - w[1], (1, 2, 1))
                    + [(self.got_one[0], (2, 1) + tail, lambda i, w: (i, 1 - w[1], 0, 0))],
                ),
                (
                    out,
                    self.at(1, lambda w: 1 - w[0], ahead, lambda w: w[1], (1, 2, 1))
                    + [(self.got_one[1], (1, 2) + tail, lambda i, w: (1 - w[0], i, 0, 0))],
                ),
            ],
        )
        return list(sent)

    def trade_two(self, sent):
        self.got_two = [swap(sent[0], "grp", 2), swap(sent[1], "lat", 1)]

    def quarters(self):
        tail = (self.depth, self.columns)
        x = lambda w: w[0]
        y = lambda w: w[1]
        if self.by_columns:
            place = lambda i, w: w[2] ^ i
            groups = []
            for part in (0, 1):
                terms = self.at(part, x, place, y, (1, 1, 1))
                if part == 0:
                    one = lambda i, w: (w[2] ^ i, w[1], 0, 0)
                else:
                    one = lambda i, w: (w[0], w[2] ^ i, 0, 0)
                terms.append((self.got_one[part], (1, 1) + tail, one))
                terms.append((self.got_two[part], (1,) + tail, lambda i, w: (w[2] ^ i, 0, 0)))
                groups.append((tail, terms))
        else:
            low = lambda i, w: jnp.minimum(w[2] ^ i, 1)
            high = lambda i, w: jnp.maximum((w[2] ^ i) - 2, 0)
            first = lambda i, w: (w[2] ^ i) < 2
            second = lambda i, w: (w[2] ^ i) >= 2
            terms = self.at(0, x, lambda i, w: w[2] ^ i, y, (1, 1, 1))
            pair = (1, 1) + tail
            one = (1,) + tail
            terms += [
                (self.got_one[0], pair, lambda i, w: (low(i, w), w[1], 0, 0), first),
                (self.got_one[1], pair, lambda i, w: (w[0], high(i, w), 0, 0), second),
                (self.got_two[0], one, lambda i, w: (low(i, w), 0, 0), first),
                (self.got_two[1], one, lambda i, w: (high(i, w), 0, 0), second),
            ]
            groups = [(tail, terms)]
        return list(block_sums(self.where, 4, groups, True))


def early_unpack_kernel(place_ref, *refs):
    ins = refs[:4]
    down_ref, up_ref, out_ref, gate_ref, head_ref, gain_ref, bias_ref, bd_ref, bup_ref, misc_ref = refs[4:]
    width = down_ref.shape[1]
    hidden = up_ref.shape[1]
    for source, (c, y) in zip(ins, ((0, 0), (0, 1), (1, 0), (1, 1))):
        slot = jnp.bitwise_xor(place_ref[0], c) * 2 + jnp.bitwise_xor(place_ref[1], y)
        one = source[0].astype(F32)
        two = source[1].astype(F32)
        rows = one.shape[0]
        half = one.shape[1]
        for g in range(4):
            span = pl.ds(pl.multiple_of(slot * 4 * rows + g * rows, 8), rows)
            down_ref[span, :] = one[:, g * width : (g + 1) * width]
        span = pl.ds(pl.multiple_of(slot * rows, 8), rows)
        cut = half - 4 * width
        up_ref[span, :cut] = one[:, 4 * width :]
        up_ref[span, cut:] = two[:, : hidden - cut]
        out_ref[span, :] = two[:, hidden - cut : hidden - cut + width]
        misc_ref[span, :] = two[:, hidden - cut + width :]
    turned = misc_ref[...].T
    at = 0
    for ref in (gate_ref, head_ref, gain_ref, bias_ref, bd_ref, bup_ref):
        count = ref.shape[0]
        ref[...] = turned[at : at + count]
        at += count


def early_unpack(place, pieces, width, hidden):
    rows = pieces[0].shape[1]
    vmem = pl.BlockSpec(memory_space=pltpu.VMEM)
    return pl.pallas_call(
        early_unpack_kernel,
        in_specs=[pl.BlockSpec(memory_space=pltpu.SMEM)] + [vmem] * 4,
        out_specs=[vmem] * 9,
        out_shape=[
            jax.ShapeDtypeStruct((16 * rows, width), F32),
            jax.ShapeDtypeStruct((4 * rows, hidden), F32),
            jax.ShapeDtypeStruct((4 * rows, width), F32),
        ]
        + [
            jax.ShapeDtypeStruct((count, 4 * rows), F32)
            for count in (2 * RESULT_FIELDS, RESULT_FIELDS, 1, 1, 1, 4)
        ],
        scratch_shapes=[pltpu.VMEM((4 * rows, 256), F32)],
        compiler_params=FULL,
        name="early_unpack",
        cost_estimate=pl.CostEstimate(flops=1 << 20, transcendentals=0, bytes_accessed=1 << 20),
    )(place, *pieces)


def late_unpack_kernel(place_ref, *refs):
    ins = refs[:4]
    main_ref, gain_ref, bias_ref, lead_ref, misc_ref = refs[4:]
    for source, (c, y) in zip(ins, ((0, 0), (0, 1), (1, 0), (1, 1))):
        slot = jnp.bitwise_xor(place_ref[0], c) * 2 + jnp.bitwise_xor(place_ref[1], y)
        value = source[...].astype(F32)
        rows = value.shape[0]
        span = pl.ds(pl.multiple_of(slot * rows, 8), rows)
        main_ref[span, :] = value[:, : main_ref.shape[1]]
        misc_ref[span, :] = value[:, main_ref.shape[1] :]
    turned = misc_ref[...].T
    gain_ref[...] = turned[:1]
    bias_ref[...] = turned[1:2]
    lead_ref[...] = turned[2 : 2 + LEADS]


def late_unpack(place, pieces):
    rows, columns = pieces[0].shape
    vmem = pl.BlockSpec(memory_space=pltpu.VMEM)
    return pl.pallas_call(
        late_unpack_kernel,
        in_specs=[pl.BlockSpec(memory_space=pltpu.SMEM)] + [vmem] * 4,
        out_specs=[vmem] * 4,
        out_shape=[jax.ShapeDtypeStruct((4 * rows, columns - 256), F32)]
        + [jax.ShapeDtypeStruct((count, 4 * rows), F32) for count in (1, 1, LEADS)],
        scratch_shapes=[pltpu.VMEM((4 * rows, 256), F32)],
        compiler_params=PARAMS,
        name="late_unpack",
        cost_estimate=pl.CostEstimate(flops=1 << 20, transcendentals=0, bytes_accessed=1 << 20),
    )(place, *pieces)


def spread(rows, columns):
    pixel = lax.broadcasted_iota(jnp.int32, (rows, columns), 0)
    field = lax.broadcasted_iota(jnp.int32, (rows, columns), 1)
    return ((pixel // TILE_AREA) == field).astype(F32).astype(BF)


def split_two(values):
    high = values.astype(BF)
    return high, (values - high.astype(F32)).astype(BF)


def pixel_sums_kernel(f_ref, s_ref, sum_ref, first_ref, second_ref, field_ref):
    @pl.when(pl.program_id(0) == 0)
    def _():
        field_ref[...] = spread(*field_ref.shape)

    fields = field_ref[...]
    sens = s_ref[...]
    sum_ref[...] = dot(sens, fields)
    for e, out in ((0, first_ref), (1, second_ref)):
        out[...] = dot((sens.astype(F32) * f_ref[e].astype(F32)).astype(BF), fields)


def pixel_sums(forecasts, sensitivity):
    rows, pixels = sensitivity.shape
    block = math.gcd(rows, 64)
    out = pl.BlockSpec((block, 128), lambda i: (i, 0))
    return pl.pallas_call(
        pixel_sums_kernel,
        grid=(rows // block,),
        in_specs=[
            pl.BlockSpec((2, block, pixels), lambda i: (0, i, 0)),
            pl.BlockSpec((block, pixels), lambda i: (i, 0)),
        ],
        out_specs=[out] * 3,
        out_shape=[jax.ShapeDtypeStruct((rows, 128), F32)] * 3,
        scratch_shapes=[pltpu.VMEM((pixels, 128), BF)],
        compiler_params=PARAMS,
        name="pixel_sums",
        cost_estimate=pl.CostEstimate(
            flops=rows * pixels * 128, transcendentals=0, bytes_accessed=rows * pixels
        ),
    )(forecasts, sensitivity)


def blend_kernel(a_ref, b_ref, c_ref, f_ref, out_ref, field_ref):
    @pl.when(pl.program_id(0) == 0)
    def _():
        columns = field_ref.shape[1]
        field = lax.broadcasted_iota(jnp.int32, (256, columns), 0)
        pixel = lax.broadcasted_iota(jnp.int32, (256, columns), 1)
        field_ref[...] = ((pixel // TILE_AREA) == (field % 128)).astype(F32).astype(BF)

    fields = field_ref[...]

    def wide(ref):
        return dot(jnp.concatenate(split_two(ref[...]), axis=1), fields)

    total = wide(a_ref) * f_ref[0].astype(F32) + wide(b_ref) * f_ref[1].astype(F32)
    out_ref[...] = (total + wide(c_ref)).astype(BF)


def blend(first, second, added, forecasts):
    _, rows, pixels = forecasts.shape
    block = math.gcd(rows, 128)
    thin = pl.BlockSpec((block, 128), lambda i: (i, 0))
    return pl.pallas_call(
        blend_kernel,
        grid=(rows // block,),
        in_specs=[thin] * 3 + [pl.BlockSpec((2, block, pixels), lambda i: (0, i, 0))],
        out_specs=pl.BlockSpec((block, pixels), lambda i: (i, 0)),
        out_shape=jax.ShapeDtypeStruct((rows, pixels), BF),
        scratch_shapes=[pltpu.VMEM((256, pixels), BF)],
        compiler_params=PARAMS,
        name="blend",
        cost_estimate=pl.CostEstimate(
            flops=rows * pixels * 128, transcendentals=0, bytes_accessed=rows * pixels
        ),
    )(first, second, added, forecasts)


def swap(values, axis, bit):
    count = lax.axis_size(axis)
    return lax.ppermute(values, axis, [(i, i ^ bit) for i in range(count)])


def add(*terms):
    return sum(t.astype(F32) for t in terms).astype(BF)


def hold(*values):
    return lax.optimization_barrier(values)


def layer_norm(values):
    centred = values - jnp.mean(values, axis=-1, keepdims=True)
    inverse = lax.rsqrt(jnp.mean(centred * centred, axis=-1, keepdims=True) + EPSILON)
    return centred * inverse, inverse


def norm_back(grad_normed, normed, inverse):
    return inverse * (
        grad_normed
        - jnp.mean(grad_normed, axis=-1, keepdims=True)
        - normed * jnp.mean(grad_normed * normed, axis=-1, keepdims=True)
    )


def pad_lanes(values):
    return jnp.pad(values, ((0, 0), (0, 128 - values.shape[1])))


def per_device(
    layer_source_tensor,
    horizon_class,
    field_selector,
    model_predictions,
    loss_sensitivity,
    gain_one,
    shift_one,
    horizon_vectors,
    w_qkv,
    w_out,
    gain_two,
    shift_two,
    w_up,
    b_up,
    w_down,
    b_down,
    w_gate,
    w_bias,
):
    frames, lat_rows, lon_cols, width = layer_source_tensor.shape
    local = lat_rows * lon_cols
    rows = frames * local
    pixels = loss_sensitivity.shape[-1]
    sizes = (lax.axis_size("grp"), lax.axis_size("lat"), lax.axis_size("lon"))
    small = sizes == (4, 2, 4) and frames == 1

    source = layer_source_tensor.reshape(frames, local, width)
    place = lax.axis_index("lon")
    edge = (place == 0) | (place == lax.axis_size("lon") - 1)
    send = functools.partial(lax.ppermute, axis_name="lon")
    if small:
        right = send(source, perm=[(0, 1), (1, 2), (2, 3)])
        left = send(source, perm=[(3, 2), (2, 1), (1, 0)])
    else:
        shards = [lax.all_gather(source, "lon", axis=1, tiled=True)]

    forecasts = jnp.transpose(model_predictions.reshape(rows, 2, pixels), (1, 0, 2))
    sensitivity = loss_sensitivity.reshape(rows, pixels)

    onehot = (horizon_class[:, None] == jnp.arange(LEADS, dtype=jnp.int32)[None, :]).astype(F32)
    lead_rows = jnp.dot(onehot, horizon_vectors, precision=HIGH)

    def mixed_of(values):
        normed, _ = layer_norm(values.astype(F32))
        return (normed * gain_one + shift_one + lead_rows[:, None, :]).astype(BF)

    both = w_gate.T
    head_rows = jnp.concatenate(
        [
            jnp.pad(m, ((0, 128 - RESULT_FIELDS), (0, 0)))
            for m in (both[:RESULT_FIELDS], both[RESULT_FIELDS:], w_bias.T)
        ]
    )
    nothing = jnp.zeros((frames, width, local), F32)
    wq = w_qkv[:, :width]
    wkv = w_qkv[:, width:]

    def keys_of(values):
        return dot(values.reshape(-1, width), wkv).astype(BF).reshape(frames, -1, 2 * width)

    if small:

        def flat(values):
            return values.reshape(rows, width)

        def shard_of(flag, yes, no):
            m, kv, x = project(
                flag.astype(jnp.int32)[None],
                [flat(yes), flat(no)],
                gain_one,
                shift_one,
                lead_rows,
                w_qkv,
            )
            return m, kv[None], x[None]

        mixed_own, own_kv, queries = project(
            None, [flat(source)], gain_one, shift_one, lead_rows, w_qkv
        )
        queries = queries[None]
        mixed = [mixed_own]
        key_value = [own_kv[None]]
        right, left, forecasts, queries, key_value[0] = hold(
            right, left, forecasts, queries, key_value[0]
        )
        right_two = send(right, perm=[(1, 2), (2, 3)])
        left_two = send(left, perm=[(2, 1), (1, 0)])
        sums = pixel_sums(forecasts, sensitivity)
        m, kv, near = shard_of(place == 0, left, right)
        mixed.append(m)
        right_two, left_two, kv, nothing, head_rows, *sums = hold(
            right_two, left_two, kv, nothing, head_rows, *sums
        )
        key_value.append(kv)
        two = right_two + left_two
        two, middle = hold(two, left)
        three = send(two, perm=[(2, 3), (1, 0)])
        m, kv, middle = shard_of(edge, two, middle)
        mixed.append(m)
        key_value.append(kv)
        state = attend(queries, key_value, None, False)
        three, *state = hold(three, *state)
        m, kv, far = shard_of(edge, three, two)
        mixed.append(m)
        key_value.append(kv)
        attended, logs = attend(queries, key_value[3:], state, True)
        shards = [source, near, middle, far]
    else:
        mixed_own = mixed_of(source)
        queries = dot(mixed_own.reshape(rows, width), wq).astype(BF)
        queries = queries.reshape(frames, local, width)
        sums = pixel_sums(forecasts, sensitivity)
        mixed = [mixed_of(shards[0])]
        key_value = [keys_of(mixed[0])]
        attended, logs = attend(queries, key_value, None, True)
    inputs = source.reshape(rows, width)
    attended_low = attended.reshape(rows, width)
    mask = pad_lanes(field_selector.astype(F32))[:, None]
    (
        hidden_low,
        activation_low,
        up_low,
        down_low,
        final_low,
        heads_low,
        attn_low,
        grad_residual,
        grad_attended,
        *blending,
        early_vectors,
        grad_bup,
    ) = between(
        inputs,
        attended_low,
        w_out,
        w_up,
        w_down,
        head_rows,
        gain_two,
        shift_two,
        b_up,
        b_down,
        mask,
        sums,
        local,
    )
    grad_attended = grad_attended.reshape(frames, local, width)
    fields = 3 * RESULT_FIELDS
    heads_low = jnp.concatenate(
        [heads_low[:, g * 128 : g * 128 + RESULT_FIELDS] for g in range(3)], axis=1
    )
    inputs = inputs.astype(F32)
    normed_one, inverse_one = layer_norm(inputs)

    def input_gradient(grad_mixed):
        return grad_residual + norm_back(
            grad_mixed.reshape(rows, width) * gain_one, normed_one, inverse_one
        )

    def back(shard, place, before):
        return attend_back(queries, grad_attended, attended, logs, shard, w_qkv, place, before)

    def late_vectors(sums):
        gain_column = sum(jnp.sum(s[:, 0], axis=0) for s in sums)
        column = sum(s[:, 1] for s in sums)
        lead = jnp.dot(onehot.T, column, precision=HIGH)
        zeros = jnp.zeros((6, width), F32)
        return jnp.concatenate((gain_column[None], jnp.sum(column, axis=0)[None], lead, zeros))

    if small:
        bup_rows = jnp.swapaxes(grad_bup.reshape(8, 4, -1), 0, 1).reshape(4, width)
        early_vectors = jnp.concatenate(
            (early_vectors, bup_rows, jnp.zeros((1, width), F32))
        )
        core = (lax.axis_index("grp") % 2).astype(jnp.int32)[None]
        where = jnp.stack(
            (lax.axis_index("lat"), lax.axis_index("grp") // 2, lax.axis_index("lon"))
        ).astype(jnp.int32)
        hidden = w_up.shape[1]
        mine, sent = down_grads(core, activation_low, down_low, 2 * hidden + width + 256)
        mine, sent = early_grads(
            core,
            hidden_low,
            attended_low,
            final_low,
            up_low,
            attn_low,
            jnp.pad(heads_low, ((0, 0), (0, 256 - fields))),
            early_vectors,
            mine,
            sent,
        )
        grad_attended, sent = hold(grad_attended, sent)
        got = swap(sent, "grp", 1)

        grad_query, dkv3, far, sums3 = back(key_value[3], shards[3], nothing)
        early = Reduction(where, [t.reshape(2, 4, 2, 24, -1) for t in (mine, got)], True)
        grad_query, far, *sent = hold(grad_query, far, *early.one())
        got = send(far, perm=[(0, 1), (3, 2)])
        early.trade_one(sent)

        grad_query, dkv2, middle, sums2 = back(key_value[2], shards[2], grad_query)
        value = jnp.where(edge, middle, add(got, far))
        grad_query, value = hold(grad_query, value)
        right = send(value, perm=[(0, 1), (1, 2)])
        left = send(value, perm=[(3, 2), (2, 1)])

        grad_query, dkv1, near, sums1 = back(key_value[1], shards[1], grad_query)
        forth = jnp.where(place == 0, near, add(right, middle))
        back_value = add(left, near)
        grad_query, forth, back_value, *sent = hold(
            grad_query, forth, back_value, *early.two()
        )
        right = send(forth, perm=[(0, 1), (1, 2), (2, 3)])
        left = send(back_value, perm=[(3, 2), (2, 1), (1, 0)])
        early.trade_two(sent)

        grad_query, dkv0, own, sums0, right, left, *early.got_two = hold(
            *back(key_value[0], shards[0], grad_query), right, left, *early.got_two
        )
        query_low, query_term, query_sums = query_back(grad_query, w_qkv, source)
        vectors = late_vectors([sums0, sums1, sums2, sums3, query_sums])
        late_mine, late_sent = late_grads(
            core,
            [m.reshape(rows, width) for m in mixed],
            query_low.reshape(width, rows),
            [d.reshape(rows, 2 * width) for d in (dkv0, dkv1, dkv2, dkv3)],
            vectors,
        )
        late_mine, late_sent, *early.got_two, own = hold(
            late_mine, late_sent, *early.got_two, own
        )
        got = swap(late_sent, "grp", 1)
        got, *parts = hold(got, *early.quarters())
        late = Reduction(where, [t.reshape(2, 4, 2, 24, -1) for t in (late_mine, got)], False)
        *sent, one, two, three = hold(*late.one(), *blending)
        late.trade_one(sent)
        early = [parts[0]] + [swap(parts[k], "lon", k) for k in (1, 2, 3)]
        blended = blend(one, two, three, forecasts)
        *late.got_one, blended = hold(*late.got_one, blended)
        *sent, own, early[0] = hold(*late.two(), own, early[0])
        late.trade_two(sent)
        grad_input = input_gradient(
            own.astype(F32) + query_term + right.astype(F32) + left.astype(F32)
        )
        *late.got_two, grad_input = hold(*late.got_two, grad_input)
        early[0], *parts = hold(early[0], *late.quarters())
        late = [parts[0]] + [swap(parts[k], "lon", k) for k in (1, 2, 3)]
        late[1], late[2], early[0] = hold(late[1], late[2], early[0])
        late = add(*[part[0] for part in late])
        late_y = swap(late, "grp", 2)
        late_c = swap(late, "grp", 1)
        early = add(*early)
        early_y = swap(early, "grp", 2)
        early_c = swap(early, "grp", 1)
        early_y, early_c, early, late_y, late_c, late = hold(
            early_y, early_c, early, late_y, late_c, late
        )
        early_yc = swap(early_y, "grp", 1)
        late_yc = swap(late_y, "grp", 1)
        place_two = jnp.stack((lax.axis_index("grp") % 2, lax.axis_index("grp") // 2))
        place_two = place_two.astype(jnp.int32)
        down_sum, up_sum, out_sum, gate_sum, head_sum, *early, bup_sum = early_unpack(
            place_two, [early, early_y, early_c, early_yc], width, hidden
        )
        late_yc, gate_sum = hold(late_yc, gate_sum)
        qkv_sum, *late, lead_sum = late_unpack(place_two, [late, late_y, late_c, late_yc])
        early = [e.reshape(-1) for e in early]
        late = [e.reshape(-1) for e in late]
        bup_sum = bup_sum.reshape(-1)
        gate_sum = gate_sum.T
        head_sum = head_sum.T
    else:
        blended = blend(*blending, forecasts)
        grad_query, dkv, term, sums = back(key_value[0], shards[0], nothing)
        query_low, query_term, query_sums = query_back(grad_query, w_qkv, source)
        grad_input = input_gradient(
            query_term + lax.psum_scatter(term.astype(F32), "lon", scatter_dimension=1, tiled=True)
        )

        def total_of(values, dim=0):
            share = lax.psum_scatter(values, ("lat", "lon"), scatter_dimension=dim, tiled=True)
            return lax.psum(share, "grp")

        flat = mixed[0].reshape(-1, width)
        qkv_sum = total_of(
            jnp.concatenate(
                (
                    jnp.einsum("frd,fer->de", mixed_own, query_low, preferred_element_type=F32),
                    dot(flat, dkv.reshape(-1, 2 * width), TN),
                ),
                axis=1,
            )
        )
        up_sum = total_of(dot(hidden_low, up_low, TN))
        out_sum = total_of(dot(attended_low, attn_low, TN))
        down_sum = total_of(dot(activation_low, down_low, TN))
        heads = total_of(dot(final_low, heads_low, TN))
        late = total_of(late_vectors([sums, query_sums])[: 2 + LEADS], 1)
        lead_sum = late[2:]
        gate_sum = heads[:, : 2 * RESULT_FIELDS]
        head_sum = heads[:, 2 * RESULT_FIELDS :]
        early = total_of(early_vectors, 1)
        bup_sum = total_of(grad_bup[0])

    return (
        blended.reshape(frames, lat_rows, lon_cols, pixels),
        grad_input.reshape(frames, lat_rows, lon_cols, width),
        late[0],
        late[1],
        lead_sum,
        qkv_sum,
        out_sum,
        early[0],
        early[1],
        up_sum,
        bup_sum,
        down_sum,
        early[2],
        gate_sum,
        head_sum,
    )


def solution(mesh):
    frame = ("grp", "lat")
    share = ("lat", "lon")
    image = P(frame, None, "lon", None)
    in_specs = (
        image,
        P(frame),
        P(frame, None),
        P(frame, None, "lon", None, None),
        image,
    ) + (P(),) * 13
    vector = P(share)
    matrix = P(share, None)
    out_specs = (
        image,
        image,
        vector,
        vector,
        P(None, share),
        matrix,
        matrix,
        vector,
        vector,
        matrix,
        vector,
        matrix,
        vector,
        matrix,
        matrix,
    )
    return jax.shard_map(
        per_device, mesh=mesh, in_specs=in_specs, out_specs=out_specs, check_vma=False
    )
```
